32 devices in a mesh: dp: 8 (over y, x, core), sp: 4 (over z).
Axes of the slice: x: 2, y: 2, z: 4, core: 2. Of those that a mesh axis runs over, the one named last changes fastest.
Arguments:
- tokens: float32 [2, 8, 4096, 512], P(None, 'dp', 'sp'), may hold values from -6 to 6
- segment_ids: int32 [2, 8, 4096], P(None, 'dp'), may hold values from 0 to 127, never falling along the last dimension, each value on 1 to 1024 neighbouring positions
- norm_gains: bfloat16 [2, 512], P(None, 'dp'), may hold values from 0.099609375 to 1.8984375
- norm_biases: bfloat16 [2, 512], P(None, 'dp'), may hold values from -1.5 to 1.5
- qkv_weight: bfloat16 [3, 512, 512], P(None, 'dp'), may hold values from -0.25 to 0.25
- out_weight: bfloat16 [512, 512], P('dp'), may hold values from -0.75 to 0.75
- in_weight: bfloat16 [512, 2048], P('dp'), may hold values from -0.25 to 0.25
- in_bias: bfloat16 [2048], P('dp'), may hold values from -1.5 to 1.5
- down_weight: bfloat16 [2048, 512], P('dp'), may hold values from -0.125 to 0.125
- down_bias: bfloat16 [512], P('dp'), may hold values from -1.5 to 1.5
- cotangent: float32 [2, 8, 4096, 512], P(None, 'dp', 'sp'), may hold values from -6 to 6
Outputs:
- outputs: float32 [2, 8, 4096, 512], P(None, 'dp', 'sp')
- input_grad: float32 [2, 8, 4096, 512], P(None, 'dp', 'sp')
- grad_norm_gains: float32 [2, 512], P(None, 'dp')
- grad_norm_biases: float32 [2, 512], P(None, 'dp')
- grad_qkv_weight: float32 [3, 512, 512], P(None, 'dp')
- grad_out_weight: float32 [512, 512], P('dp')
- grad_in_weight: float32 [512, 2048], P('dp')
- grad_in_bias: float32 [2048], P('dp')
- grad_down_weight: float32 [2048, 512], P('dp')
- grad_down_bias: float32 [512], P('dp')
The draws below stay inside these ranges and needn't reach their ends.
Inputs may be any that keep to these rules, and one draw needn't show every extreme that they name: `segment_ids`: within each sequence the ids never fall and count documents from 0; a document has 1 to 1024 tokens, and one has exactly 1024.
All inputs are finite; a program needn't handle non-finite values.
Results may differ from the reference program's by a relative error of at most 0.013.
Values may be sent and summed in bfloat16 or wider, within the bound.
No kernel may reach another device: no remote copies, remote signals or barrier semaphores. Data moves between devices by JAX's collectives and lax.ppermute only.
A program may use at most 384 MiB of HBM per device.

```python
import math
from functools import reduce
import jax
import jax.numpy as jnp
import numpy as np
from jax import lax

HEADS = 8
HEAD_DIM = 64
FF = 2048
BLOCK = 16
LEVELS = 8
MICRO = 2
D = 512
SEQ = 4096
BATCH = 8


def spiked(drawn, key, source, target, blocks, factor):
    owner, partner = [(jnp.arange(drawn.shape[axis_at]) // (drawn.shape[axis_at] // blocks)).reshape([-1 if axis == axis_at else 1 for axis in range(drawn.ndim)]) for axis_at in (source, target)]
    chosen = jax.random.permutation(key, blocks)[partner]
    strong = (owner == chosen) | (owner == (partner + blocks // 2) % blocks)
    return jnp.where(strong, factor * drawn, drawn)


def block_levels(rng, dims, split, least, high):
    loudness = 1.0
    for position, shards_of in split:
        heights = jax.random.uniform(jax.random.fold_in(jax.random.fold_in(rng, 6), position), (shards_of,), jnp.float32, least / len(split), high / len(split))
        loudness = loudness * jnp.repeat(jnp.exp(heights), dims[position] // shards_of).reshape((-1,) + (1,) * (len(dims) - 1 - position))
    return loudness


def split_up(number_of, total, reach, slope):
    portions = [(1 << 20) // math.isqrt(grade ** slope) + 1 for grade in range(2, number_of + 1)]
    rest, counts = total - reach - (number_of - 1), [1] * (number_of - 1)
    while rest > 0:
        candidates = [i for i in range(number_of - 1) if counts[i] < reach]
        pool, remaining = sum([portions[i] for i in candidates]), rest
        for i in candidates:
            addition = min(reach - counts[i], max(1, remaining * portions[i] // pool), rest)
            counts[i] = counts[i] + addition
            rest = rest - addition
    return np.array([reach] + counts)


def ragged_sizes(own_key, number_of, total, reach, slope):
    if number_of == 2:
        one = jax.random.randint(own_key, (), max(1, total - reach), min(reach, total - 1) + 1)
        return jnp.stack([one, total - one])
    tallies = jnp.asarray(split_up(number_of, total, reach, slope), jnp.int32)
    twos = (number_of - 1) // 2
    source_of, taker = tallies[1:1 + 2 * twos:2], tallies[2:2 + 2 * twos:2]
    room = jnp.minimum(source_of - 1, reach - taker)
    shifted = jax.random.randint(jax.random.fold_in(own_key, 1), (twos,), 0, 1 << 20) % (room + 1)
    tallies = tallies.at[1:1 + 2 * twos:2].set(source_of - shifted).at[2:2 + 2 * twos:2].set(taker + shifted)
    return tallies[jax.random.permutation(jax.random.fold_in(own_key, 2), number_of)]


def centred(key, shape, deviation, bound, split=(), kind=jnp.bfloat16):
    drawn = deviation * jax.random.normal(key, shape, jnp.float32)
    if split:
        drawn = drawn * block_levels(key, shape, split, -0.22, 0.18)
    return jnp.clip(drawn, -bound, bound).astype(kind)


def gaussian_with(rng, dims, scale, bound, shards, heavy, kind=jnp.bfloat16):
    array = scale * jax.random.normal(rng, dims, jnp.float32)
    if shards:
        array = array * block_levels(rng, dims, shards, -0.22, 0.18)
    return jnp.clip(spiked(array, jax.random.fold_in(rng, 3), *heavy), -bound, bound).astype(kind)


def setup_inputs(seed: int = 0) -> dict:
    arg_keys = jax.random.split(jax.random.key(seed), 12)
    return {
        "tokens": centred(arg_keys[0], (MICRO, BATCH, SEQ, D), 1.0, 6.0, ((1, 8), (2, 4)), jnp.float32),
        "segment_ids": jax.vmap(lambda own: jnp.searchsorted(jnp.cumsum(ragged_sizes(own, SEQ // 32, SEQ, SEQ // 4, 2)), jnp.arange(SEQ), side="right"))(jax.random.split(arg_keys[1], MICRO * BATCH)).reshape((MICRO, BATCH, SEQ)).astype(jnp.int32),
        "norm_gains": jnp.clip(1.0 + 0.18 * jax.random.normal(arg_keys[2], (2, D), jnp.float32), 0.099609375, 1.8984375).astype(jnp.bfloat16),
        "norm_biases": centred(arg_keys[3], (2, D), 0.3, 1.5, ((1, 8),)),
        "qkv_weight": centred(arg_keys[4], (3, D, D), D ** -0.5, 0.25, ((1, 8),)),
        "out_weight": centred(arg_keys[5], (D, D), HEAD_DIM ** -0.5, 0.75, ((0, 8),)),
        "in_weight": centred(arg_keys[6], (D, FF), D ** -0.5, 0.25, ((0, 8),)),
        "in_bias": centred(arg_keys[7], (FF,), 0.3, 1.5, ((0, 8),)),
        "down_weight": centred(arg_keys[8], (FF, D), FF ** -0.5, 0.125, ((0, 8),)),
        "down_bias": centred(arg_keys[9], (D,), 0.3, 1.5, ((0, 8),)),
        "cotangent": gaussian_with(arg_keys[10], (MICRO, BATCH, SEQ, D), 1.0, 6.0, ((1, 8), (2, 4)), (1, 3, 8, 2.0), jnp.float32),
    }


@jax.custom_vjp
def low(v):
    return lax.optimization_barrier(v.astype(jnp.bfloat16)).astype(jnp.float32)

@jax.custom_vjp
def low_back(v):
    return v

def low_keep(v):
    return (low(v), None)

def low_pass(kept, grad):
    return (grad,)

def back_keep(v):
    return (v, None)

def back_low(kept, grad):
    return (low(grad),)
low.defvjp(low_keep, low_pass)
low_back.defvjp(back_keep, back_low)

def layer_norm(values, scale_gain, offset):
    center = values - lax.optimization_barrier(jnp.mean(values, axis=-1, keepdims=True))
    spread = lax.optimization_barrier(jnp.mean(center * center, axis=-1, keepdims=True))
    return center * lax.rsqrt(spread + 1e-05) * scale_gain + offset

def coarse_ids(seg_row, cell_size, filler):
    grouped = seg_row.reshape(-1, cell_size)
    lowest = lax.optimization_barrier(jnp.min(grouped, axis=1))
    highest = lax.optimization_barrier(jnp.max(grouped, axis=1))
    return jnp.where(lowest == highest, lowest, filler).astype(jnp.int32)

def level_mask(level_index):
    if level_index == 0:
        return np.ones((BLOCK, 3 * BLOCK), dtype=bool)
    row_pos = np.arange(BLOCK)[:, None]
    col_pos = np.arange(2 * BLOCK)[None, :]
    half_block = BLOCK // 2
    left_side = (col_pos < BLOCK) & ~((row_pos < half_block) & (col_pos >= half_block))
    right_side = (col_pos >= BLOCK) & ~((row_pos >= half_block) & (col_pos - BLOCK < half_block))
    return left_side | right_side

def around_blocks(padded, level_index):
    if level_index == 0:
        return jnp.concatenate([padded[:-2], padded[1:-1], padded[2:]], axis=1)
    return jnp.concatenate([padded[:-2], padded[2:]], axis=1)

def head_attention(query, key_in, value_in, seg_row):
    seq_length, head_width = query.shape
    scale_factor = 1.0 / math.sqrt(head_width)
    level_tops = []
    level_totals = []
    level_sums = []
    for level_index in range(LEVELS):
        cell_size = 2 ** level_index
        cell_count = seq_length // cell_size
        block_count = cell_count // BLOCK

        def coarse(values):
            return lax.optimization_barrier(jnp.mean(values.reshape(cell_count, cell_size, head_width), axis=1)).reshape(block_count, BLOCK, head_width)
        coarse_query = coarse(query)
        coarse_key = coarse(key_in)
        coarse_value = coarse(value_in)
        query_ids = coarse_ids(seg_row, cell_size, -1).reshape(block_count, BLOCK)
        key_ids = coarse_ids(seg_row, cell_size, -2).reshape(block_count, BLOCK)
        near_keys = around_blocks(jnp.pad(coarse_key, ((1, 1), (0, 0), (0, 0))), level_index)
        near_values = around_blocks(jnp.pad(coarse_value, ((1, 1), (0, 0), (0, 0))), level_index)
        near_ids = around_blocks(jnp.pad(key_ids, ((1, 1), (0, 0)), constant_values=-3), level_index)
        scores = jnp.einsum('bid,bjd->bij', coarse_query, near_keys, precision=lax.Precision.HIGHEST) * scale_factor + math.log(cell_size)
        allowed = (query_ids[:, :, None] == near_ids[:, None, :]) & jnp.asarray(level_mask(level_index))[None]
        masked = jnp.where(allowed, scores, -1e+30)
        row_top = lax.optimization_barrier(jnp.max(masked, axis=2))
        weights = jnp.where(allowed, jnp.exp(masked - row_top[:, :, None]), 0.0)
        weighted = jnp.einsum('bij,bjd->bid', weights, near_values, precision=lax.Precision.HIGHEST)
        level_tops.append(jnp.repeat(row_top.reshape(cell_count), cell_size))
        level_totals.append(jnp.repeat(lax.optimization_barrier(jnp.sum(weights, axis=2)).reshape(cell_count), cell_size))
        level_sums.append(jnp.repeat(weighted.reshape(cell_count, head_width), cell_size, axis=0))
    overall = reduce(jnp.maximum, level_tops)
    denominator = jnp.zeros((seq_length,), jnp.float32)
    numerator = jnp.zeros((seq_length, head_width), jnp.float32)
    for level_index in range(LEVELS):
        factor = jnp.exp(level_tops[level_index] - overall)
        denominator = denominator + level_totals[level_index] * factor
        numerator = numerator + level_sums[level_index] * factor[:, None]
    return numerator / denominator[:, None]

def group_attention(query, key_in, value_in, seg_row):
    return jax.vmap(head_attention, in_axes=(1, 1, 1, None), out_axes=1)(query, key_in, value_in, seg_row)

def layer(token_rows, seg_row, params):
    norm_scale, norm_shift, qkv_full, out_full, in_full, in_shift, down_full, down_shift = params
    seq_length, model_width = token_rows.shape
    normed = low(layer_norm(token_rows, norm_scale[0], norm_shift[0]))
    projected = low(low_back(jnp.einsum('sd,tde->tse', normed, qkv_full, precision=lax.Precision.HIGHEST)))
    split_heads = projected.reshape(3, seq_length, HEADS, model_width // HEADS)
    mixed = group_attention(split_heads[0], split_heads[1], split_heads[2], seg_row)
    mixed = low(low_back(mixed.reshape(seq_length, model_width)))
    middle = token_rows + low_back(jnp.dot(mixed, out_full, precision=lax.Precision.HIGHEST))
    second = low(layer_norm(middle, norm_scale[1], norm_shift[1]))
    pre_act = low_back(jnp.dot(second, in_full, precision=lax.Precision.HIGHEST) + in_shift)
    activ = low(jax.nn.gelu(pre_act, approximate=True))
    return middle + low_back(jnp.dot(activ, down_full, precision=lax.Precision.HIGHEST) + down_shift)

def reference(tokens, segment_ids, norm_gains, norm_biases, qkv_weight, out_weight, in_weight, in_bias, down_weight, down_bias, cotangent):
    params = tuple((value.astype(jnp.float32) for value in (norm_gains, norm_biases, qkv_weight, out_weight, in_weight, in_bias, down_weight, down_bias)))
    seq_length = tokens.shape[2]
    model_width = tokens.shape[3]
    sequences = tokens.reshape(-1, seq_length, model_width)
    seg_rows = segment_ids.reshape(-1, seq_length)
    cot_rows = cotangent.reshape(-1, seq_length, model_width)

    def one_sequence(running, sample):
        token_rows, seg_row, cot_row = sample
        result, pullback = jax.vjp(lambda inputs, weights: layer(inputs, seg_row, weights), token_rows, params)
        grad_inputs, grad_params = pullback(cot_row)
        running = jax.tree.map(lambda held, added: held + added, running, grad_params)
        return (running, (result, grad_inputs))
    zeros_start = tuple((jnp.zeros_like(value) for value in params))
    totals, (results, grad_rows) = lax.scan(one_sequence, zeros_start, (sequences, seg_rows, cot_rows))
    return (results.reshape(tokens.shape), grad_rows.reshape(tokens.shape), totals[0], totals[1], totals[2], totals[3], totals[4], totals[5], totals[6], totals[7])
```

```python
import math

import jax
import jax.numpy as jnp
import numpy as np
from jax import lax
from jax.experimental import pallas as pl
from jax.experimental.pallas import tpu as pltpu
from jax.sharding import PartitionSpec as P

HEADS = 8
HEAD_DIM = 64
BLOCK = 16
LEVELS = 8
HALO = 16
TILE = 64
QUAD = 4
QL = QUAD * HEAD_DIM
NEG = -1e30
FINE = 3
ROWS = 1024
EDGE = 112
F32 = jnp.float32
BF16 = jnp.bfloat16

CELLS = [ROWS >> level for level in range(LEVELS)]
OFF = [2 * ROWS - (2 * ROWS >> level) for level in range(LEVELS)]
POFF = []
_at = 0
for _level in range(LEVELS - 1):
    POFF.append(_at)
    _at += CELLS[_level] + 2 * HALO
POFF.append(_at)
PIECE7 = CELLS[LEVELS - 1]
PADDED = _at + 4 * PIECE7
FINE_TILES = ROWS // TILE
COARSE_TILES = ROWS // 8 // TILE
FINE_KEYS = 192
COARSE_KEYS = 256
LN_EPS = 1e-05
VMEM_LIMIT = 62 * 1024 * 1024


def _counts(level, query, key):
    query = query[None, :]
    key = key[:, None]
    near = np.abs(query // 16 - key // 16)
    if level == 0:
        return near <= 1
    return (near == 1) & (np.abs(query // 8 - key // 8) >= 2)


def _bias(parts):
    rows = []
    for level, allowed in parts:
        rows.append(np.where(allowed, np.float32(level * math.log(2.0)), np.float32(NEG)))
    block = np.concatenate(rows, axis=0).astype(np.float32)
    return np.tile(block, (1, QUAD))


def _two_blocks():
    return np.concatenate([np.arange(16) - 16, np.arange(16) + 16])


def fine_bias():
    token = np.arange(TILE)
    return _bias(
        [
            (0, _counts(0, token, np.arange(96) - 16)),
            (1, _counts(1, token // 2, np.arange(64) - 16)),
            (2, _counts(2, token // 4, _two_blocks())),
        ]
    )


def coarse_bias():
    cell = np.arange(TILE)
    out = []
    for tile in range(COARSE_TILES):
        out.append(
            _bias(
                [
                    (3, _counts(3, cell, np.arange(96) - 16)),
                    (4, _counts(4, cell // 2, np.arange(64) - 16)),
                    (5, _counts(5, cell // 4, _two_blocks())),
                    (6, _counts(6, 8 * tile + cell // 8, _two_blocks())),
                    (7, np.ones((4 * PIECE7, TILE), bool)),
                ]
            )
        )
    return np.stack(out)


def averaging(cell, count):
    at = np.arange(count) // cell
    return (at[:, None] == at[None, :]).astype(np.float32) / cell


def mean_rows(cell, count):
    return (np.arange(count)[None, :] // cell == np.arange(count // cell)[:, None]).astype(
        np.float32
    ) / cell


def spread_matrix():
    out = np.zeros((QUAD, TILE, 8, QUAD, TILE), np.float32)
    for part in range(8):
        for token in range(TILE):
            for head in range(QUAD):
                out[head, 8 * part + token // 8, part, head, token] = 1.0
    return out.reshape(QL, 8 * QL)


def constants():
    query_means = np.concatenate([averaging(1 << r, TILE) for r in range(5)]) * 0.125
    grad_means = np.stack([np.kron(np.eye(QUAD), averaging(1 << r, TILE)) for r in range(1, 5)])
    head_mask = np.kron(np.eye(QUAD), np.ones((TILE, HEAD_DIM)))
    means_low = np.concatenate([mean_rows(1 << level, 256) for level in range(1, 5)])
    means_high = np.concatenate(
        [mean_rows(1 << level, ROWS) for level in range(5, 8)] + [np.zeros((8, ROWS))]
    )
    as_low = lambda value: jnp.asarray(value.astype(np.float32)).astype(BF16)
    return dict(
        fine=jnp.asarray(fine_bias()),
        coarse=jnp.asarray(coarse_bias()),
        query_means=as_low(query_means),
        grad_means=as_low(grad_means),
        head_mask=as_low(head_mask),
        means_low=as_low(means_low),
        means_high=as_low(means_high),
        means_low_t=as_low(means_low.T),
        means_high_t=as_low(means_high.T),
        spread=as_low(spread_matrix()),
        spread_t=as_low(spread_matrix().T),
    )


def dot_nn(left, right):
    return jnp.dot(left, right, preferred_element_type=F32)


def dot_nt(left, right):
    return lax.dot_general(left, right, (((1,), (1,)), ((), ())), preferred_element_type=F32)


def dot_tn(left, right):
    return lax.dot_general(left, right, (((0,), (0,)), ((), ())), preferred_element_type=F32)


def at(start, size):
    return pl.ds(pl.multiple_of(start, 16), size)


def whole(shape):
    zeros = (0,) * len(shape)
    return pl.BlockSpec(shape, lambda *_: zeros)


def per_micro(shape):
    zeros = (0,) * len(shape)
    return pl.BlockSpec((1,) + shape, lambda m: (m,) + zeros)


def params(steps):
    return pltpu.CompilerParams(
        dimension_semantics=("arbitrary",) * steps, vmem_limit_bytes=VMEM_LIMIT
    )


def normalised(rows):
    center = rows - jnp.mean(rows, axis=-1, keepdims=True)
    spread = jnp.mean(center * center, axis=-1, keepdims=True)
    rate = lax.rsqrt(spread + LN_EPS)
    return center * rate, rate


def norm_back(grad, unit, rate):
    mean_grad = jnp.mean(grad, axis=-1, keepdims=True)
    mean_dot = jnp.mean(grad * unit, axis=-1, keepdims=True)
    return rate * (grad - mean_grad - unit * mean_dot)


def fold_rows(value):
    return jnp.sum(value.reshape(-1, 8, value.shape[-1]), axis=0)


def project_kernel(
    tok_ref, gain_ref, off_ref, w_ref, low_ref, high_ref, q_ref, q3_ref, kv_ref, left_ref, right_ref
):
    for chunk in range(ROWS // 256):
        rows = pl.ds(256 * chunk, 256)
        unit, _ = normalised(tok_ref[0, rows, :])
        normed = (unit * gain_ref[...] + off_ref[...]).astype(BF16)
        query = dot_nn(normed, w_ref[0]).astype(BF16)
        q_ref[0, rows, :] = query
        q3_ref[0, pl.ds(32 * chunk, 32), :] = dot_nn(low_ref[192:224, :], query).astype(BF16)
        for part in range(2):
            lanes = pl.ds(512 * part, 512)
            value = dot_nn(normed, w_ref[1 + part]).astype(BF16)
            kv_ref[0, rows, lanes] = value
            cells = dot_nn(low_ref[...], value).astype(BF16)
            start = 0
            for level in range(1, 5):
                count = 256 >> level
                kv_ref[0, pl.ds(OFF[level] + count * chunk, count), lanes] = cells[
                    start : start + count
                ]
                start += count
    for part in range(2):
        lanes = pl.ds(512 * part, 512)
        kv_ref[0, pl.ds(OFF[5], 64), lanes] = dot_nn(
            high_ref[...], kv_ref[0, pl.ds(0, ROWS), lanes]
        ).astype(BF16)
    for level in range(LEVELS - 1):
        edge = pl.ds(HALO * level, HALO)
        left_ref[0, edge, :] = kv_ref[0, pl.ds(OFF[level], HALO), :]
        right_ref[0, edge, :] = kv_ref[0, pl.ds(OFF[level] + CELLS[level] - HALO, HALO), :]


def project(tokens, gain, offset, weight, const):
    micro = tokens.shape[0]
    width = tokens.shape[2]
    shape = jax.ShapeDtypeStruct
    return pl.pallas_call(
        project_kernel,
        grid=(micro,),
        in_specs=[
            per_micro((ROWS, width)),
            whole((1, width)),
            whole((1, width)),
            whole((3, width, width)),
            whole((240, 256)),
            whole((64, ROWS)),
        ],
        out_specs=[
            per_micro((ROWS, width)),
            per_micro((ROWS // 8, width)),
            per_micro((2 * ROWS, 2 * width)),
            per_micro((EDGE, 2 * width)),
            per_micro((EDGE, 2 * width)),
        ],
        out_shape=[
            shape((micro, ROWS, width), BF16),
            shape((micro, ROWS // 8, width), BF16),
            shape((micro, 2 * ROWS, 2 * width), BF16),
            shape((micro, EDGE, 2 * width), BF16),
            shape((micro, EDGE, 2 * width), BF16),
        ],
        compiler_params=params(1),
        name="project",
    )(tokens, gain, offset, weight, const["means_low"], const["means_high"])


def fine_windows(tile):
    return [
        (POFF[0] + 64 * tile, 96),
        (POFF[1] + 32 * tile, 64),
        (POFF[2] + 16 * tile, 16),
        (POFF[2] + 16 * tile + 32, 16),
    ]


def coarse_windows(tile):
    return [
        (POFF[3] + 64 * tile, 96),
        (POFF[4] + 32 * tile, 64),
        (POFF[5] + 16 * tile, 16),
        (POFF[5] + 16 * tile + 32, 16),
        (POFF[6], 16),
        (POFF[6] + 32, 16),
        (POFF[7], 32),
    ]


FINE_LEVELS = [96, 64, 32]
COARSE_LEVELS = [96, 64, 32, 32, 32]


def gather_rows(ref, windows, lanes):
    return jnp.concatenate([ref[0, at(start, size), lanes] for start, size in windows], axis=0)


def tile_bias(kid_ref, qid_ref, row, windows, levels, bias):
    keys = jnp.concatenate([kid_ref[0, at(start, size), :] for start, size in windows], axis=0)
    keys = jnp.concatenate([keys, keys], axis=1)
    out = []
    start = 0
    for index, count in enumerate(levels):
        part = slice(start, start + count)
        owner = qid_ref[0, pl.ds(row + index, 1), :]
        out.append(jnp.where(keys[part] == owner, bias[part], NEG))
        start += count
    return jnp.concatenate(out, axis=0)


def head_stack(value, mask):
    return jnp.concatenate([value] * QUAD, axis=0) * mask


def head_pick(stacked):
    lane = lax.broadcasted_iota(jnp.int32, (TILE, QL), 1) // HEAD_DIM
    out = stacked[0:TILE]
    for head in range(1, QUAD):
        out = jnp.where(lane == head, stacked[TILE * head : TILE * (head + 1)], out)
    return out


def tile_scores(keys, queries, mask, levels):
    out = []
    start = 0
    for index, count in enumerate(levels):
        stacked = head_stack(queries[TILE * index : TILE * (index + 1)], mask)
        out.append(dot_nt(keys[start : start + count], stacked))
        start += count
    return jnp.concatenate(out, axis=0)


def three_terms(row):
    high = row.astype(BF16)
    rest = row - high.astype(F32)
    middle = rest.astype(BF16)
    low = (rest - middle.astype(F32)).astype(BF16)
    return high, middle, low


def own_cell(tile):
    cell = lax.broadcasted_iota(jnp.int32, (16, QL), 0)
    token = lax.broadcasted_iota(jnp.int32, (16, QL), 1) % TILE
    return cell == 8 * (tile % 2) + token // 8


def attend_kernel(
    q_ref,
    q3_ref,
    kv_ref,
    left_ref,
    right_ref,
    top_ref,
    kid_ref,
    qidf_ref,
    qidc_ref,
    fine_ref,
    coarse_ref,
    means_ref,
    mask_ref,
    spread_ref,
    mixed_ref,
    kvp_ref,
    lse_ref,
    lsec_ref,
    lsex_ref,
    oc_ref,
):
    for level in range(LEVELS - 1):
        base = POFF[level]
        count = CELLS[level]
        edge = pl.ds(HALO * level, HALO)
        kvp_ref[0, pl.ds(base, HALO), :] = left_ref[0, edge, :]
        kvp_ref[0, pl.ds(base + HALO, count), :] = kv_ref[0, pl.ds(OFF[level], count), :]
        kvp_ref[0, pl.ds(base + HALO + count, HALO), :] = right_ref[0, edge, :]
    kvp_ref[0, pl.ds(POFF[7], 4 * PIECE7), :] = top_ref[0]
    mask = mask_ref[...]

    def coarse_tile(tile, carry):
        windows = coarse_windows(tile)
        bias = tile_bias(kid_ref, qidc_ref, 8 * tile, windows, COARSE_LEVELS, coarse_ref[tile])
        rows = at(TILE * tile, TILE)
        for quad in range(2):
            lanes = pl.ds(QL * quad, QL)
            vlanes = pl.ds(512 + QL * quad, QL)
            queries = dot_nn(means_ref[...], q3_ref[0, rows, lanes]).astype(BF16)
            keys = gather_rows(kvp_ref, windows, lanes)
            scores = tile_scores(keys, queries, mask, COARSE_LEVELS) + bias
            top = jnp.max(scores, axis=0, keepdims=True)
            share = jnp.exp(scores - top)
            total = jnp.sum(share, axis=0, keepdims=True)
            lse = top + jnp.log(total)
            lsec_ref[0, pl.ds(2 * tile + quad, 1), :] = lse
            share = (share * (1.0 / total)).astype(BF16)
            values = gather_rows(kvp_ref, windows, vlanes)
            oc_ref[0, rows, lanes] = head_pick(dot_tn(share, values)).astype(BF16)
            high, middle, low = three_terms(lse)
            terms = jnp.concatenate([high, middle, low, low, low, low, low, low], axis=0)
            terms = dot_nn(terms, spread_ref[...])
            lsex_ref[0, pl.ds(2 * tile + quad, 1), :] = terms[0:1] + terms[1:2] + terms[2:3]
        return carry

    lax.fori_loop(0, COARSE_TILES, coarse_tile, 0)

    def fine_tile(tile, carry):
        windows = fine_windows(tile)
        bias = tile_bias(kid_ref, qidf_ref, 8 * tile, windows, FINE_LEVELS, fine_ref[...])
        rows = at(TILE * tile, TILE)
        own = own_cell(tile)
        for quad in range(2):
            lanes = pl.ds(QL * quad, QL)
            vlanes = pl.ds(512 + QL * quad, QL)
            queries = dot_nn(means_ref[0 : FINE * TILE, :], q_ref[0, rows, lanes]).astype(BF16)
            keys = gather_rows(kvp_ref, windows, lanes)
            scores = tile_scores(keys, queries, mask, FINE_LEVELS) + bias
            far = lsex_ref[
                0, pl.ds(2 * (tile // 8) + quad, 1), pl.ds(pl.multiple_of(QL * (tile % 8), QL), QL)
            ]
            top = jnp.maximum(jnp.max(scores, axis=0, keepdims=True), far)
            share = jnp.exp(scores - top)
            far_share = jnp.exp(far - top)
            total = jnp.sum(share, axis=0, keepdims=True) + far_share
            lse_ref[0, pl.ds(2 * tile + quad, 1), :] = top + jnp.log(total)
            inverse = 1.0 / total
            share = jnp.concatenate(
                [share * inverse, jnp.where(own, far_share * inverse, 0.0)], axis=0
            ).astype(BF16)
            values = jnp.concatenate(
                [
                    gather_rows(kvp_ref, windows, vlanes),
                    oc_ref[0, at(16 * (tile // 2), 16), lanes],
                ],
                axis=0,
            )
            mixed_ref[0, rows, lanes] = head_pick(dot_tn(share, values)).astype(BF16)
        return carry

    lax.fori_loop(0, FINE_TILES, fine_tile, 0)


def attend(q, q3, kv, left, right, top, ids, const):
    micro, _, width = q.shape
    shape = jax.ShapeDtypeStruct
    return pl.pallas_call(
        attend_kernel,
        grid=(micro,),
        in_specs=[
            per_micro((ROWS, width)),
            per_micro((ROWS // 8, width)),
            per_micro((2 * ROWS, 2 * width)),
            per_micro((EDGE, 2 * width)),
            per_micro((EDGE, 2 * width)),
            per_micro((4 * PIECE7, 2 * width)),
            per_micro((PADDED, 128)),
            per_micro((8 * FINE_TILES, QL)),
            per_micro((8 * COARSE_TILES, QL)),
            whole((FINE_KEYS, QL)),
            whole((COARSE_TILES, COARSE_KEYS, QL)),
            whole((5 * TILE, TILE)),
            whole((QL, QL)),
            whole((QL, 8 * QL)),
        ],
        out_specs=[
            per_micro((ROWS, width)),
            per_micro((PADDED, 2 * width)),
            per_micro((2 * FINE_TILES, QL)),
            per_micro((2 * COARSE_TILES, QL)),
            per_micro((2 * COARSE_TILES, 8 * QL)),
            per_micro((ROWS // 8, width)),
        ],
        out_shape=[
            shape((micro, ROWS, width), BF16),
            shape((micro, PADDED, 2 * width), BF16),
            shape((micro, 2 * FINE_TILES, QL), F32),
            shape((micro, 2 * COARSE_TILES, QL), F32),
            shape((micro, 2 * COARSE_TILES, 8 * QL), F32),
            shape((micro, ROWS // 8, width), BF16),
        ],
        compiler_params=params(1),
        name="attend",
    )(
        q,
        q3,
        kv,
        left,
        right,
        top,
        ids["key"],
        ids["fine"],
        ids["coarse"],
        const["fine"],
        const["coarse"],
        const["query_means"],
        const["head_mask"],
        const["spread"],
    )


def add_rows(ref, windows, lanes, value):
    start = 0
    for base, count in windows:
        rows = at(base, count)
        ref[rows, lanes] = ref[rows, lanes] + value[start : start + count]
        start += count


def mean_scores(grads, means_ref, levels):
    out = [grads[0 : levels[0]]]
    start = levels[0]
    for index, count in enumerate(levels[1:]):
        out.append(dot_nn(grads[start : start + count], means_ref[index]).astype(BF16))
        start += count
    return jnp.concatenate(out, axis=0)


def attend_back_kernel(
    q_ref,
    q3_ref,
    kvp_ref,
    lse_ref,
    lsec_ref,
    lsex_ref,
    oc_ref,
    dout_ref,
    kid_ref,
    qidf_ref,
    qidc_ref,
    fine_ref,
    coarse_ref,
    means_ref,
    grad_means_ref,
    mask_ref,
    spread_t_ref,
    dq_ref,
    dq3_ref,
    dkv_ref,
    left_ref,
    right_ref,
    top_ref,
    acc_ref,
    dcell_ref,
    delta_ref,
):
    acc_ref[...] = jnp.zeros(acc_ref.shape, F32)
    dcell_ref[...] = jnp.zeros(dcell_ref.shape, F32)
    mask = mask_ref[...]

    def fine_tile(tile, carry):
        windows = fine_windows(tile)
        bias = tile_bias(kid_ref, qidf_ref, 8 * tile, windows, FINE_LEVELS, fine_ref[...])
        rows = at(TILE * tile, TILE)
        own = own_cell(tile)
        cells = at(16 * (tile // 2), 16)
        for quad in range(2):
            lanes = pl.ds(QL * quad, QL)
            vlanes = pl.ds(512 + QL * quad, QL)
            query = q_ref[0, rows, lanes]
            queries = dot_nn(means_ref[0 : FINE * TILE, :], query).astype(BF16)
            keys = gather_rows(kvp_ref, windows, lanes)
            lse = lse_ref[0, pl.ds(2 * tile + quad, 1), :]
            wide = pl.ds(pl.multiple_of(QL * (tile % 8), QL), QL)
            coarse_row = pl.ds(2 * (tile // 8) + quad, 1)
            far_share = jnp.exp(lsex_ref[0, coarse_row, wide] - lse)
            share = jnp.exp(tile_scores(keys, queries, mask, FINE_LEVELS) + bias - lse)
            share = jnp.concatenate([share, jnp.where(own, far_share, 0.0)], axis=0)
            values = jnp.concatenate(
                [gather_rows(kvp_ref, windows, vlanes), oc_ref[0, cells, lanes]], axis=0
            )
            dout = head_stack(dout_ref[0, rows, lanes], mask)
            weighted = share * dot_nt(values, dout)
            delta = jnp.sum(weighted, axis=0, keepdims=True)
            delta_ref[coarse_row, wide] = far_share * delta
            grads = (weighted[0:FINE_KEYS] - share[0:FINE_KEYS] * delta).astype(BF16)
            dvalues = dot_nn(share.astype(BF16), dout)
            add_rows(acc_ref, windows, vlanes, dvalues)
            dcell_ref[cells, lanes] = dcell_ref[cells, lanes] + dvalues[FINE_KEYS:]
            grads = mean_scores(grads, grad_means_ref, FINE_LEVELS)
            add_rows(acc_ref, windows, lanes, dot_nn(grads, head_stack(query, mask)))
            dq_ref[0, rows, lanes] = (head_pick(dot_tn(grads, keys)) * 0.125).astype(BF16)
        return carry

    lax.fori_loop(0, FINE_TILES, fine_tile, 0)

    def coarse_tile(tile, carry):
        windows = coarse_windows(tile)
        bias = tile_bias(kid_ref, qidc_ref, 8 * tile, windows, COARSE_LEVELS, coarse_ref[tile])
        rows = at(TILE * tile, TILE)
        for quad in range(2):
            lanes = pl.ds(QL * quad, QL)
            vlanes = pl.ds(512 + QL * quad, QL)
            row = pl.ds(2 * tile + quad, 1)
            query = q3_ref[0, rows, lanes]
            queries = dot_nn(means_ref[...], query).astype(BF16)
            keys = gather_rows(kvp_ref, windows, lanes)
            lse = lsec_ref[0, row, :]
            share = jnp.exp(tile_scores(keys, queries, mask, COARSE_LEVELS) + bias - lse)
            high, middle, low = three_terms(delta_ref[row, :])
            terms = jnp.concatenate([high, middle, low, low, low, low, low, low], axis=0)
            terms = dot_nn(terms, spread_t_ref[...])
            delta = terms[0:1] + terms[1:2] + terms[2:3]
            values = gather_rows(kvp_ref, windows, vlanes)
            dout = head_stack(dcell_ref[rows, lanes].astype(BF16), mask)
            grads = (share * (dot_nt(values, dout) - delta)).astype(BF16)
            add_rows(acc_ref, windows, vlanes, dot_nn(share.astype(BF16), dout))
            grads = mean_scores(grads, grad_means_ref, COARSE_LEVELS)
            add_rows(acc_ref, windows, lanes, dot_nn(grads, head_stack(query, mask)))
            dq3_ref[0, rows, lanes] = (head_pick(dot_tn(grads, keys)) * 0.125).astype(BF16)
        return carry

    lax.fori_loop(0, COARSE_TILES, coarse_tile, 0)

    scale = jnp.where(lax.broadcasted_iota(jnp.int32, (1, acc_ref.shape[1]), 1) < 512, 0.125, 1.0)

    def low(start, count):
        return (acc_ref[pl.ds(start, count), :] * scale).astype(BF16)

    for level in range(LEVELS - 1):
        base = POFF[level]
        count = CELLS[level]
        edge = pl.ds(HALO * level, HALO)
        left_ref[0, edge, :] = low(base, HALO)
        dkv_ref[0, pl.ds(OFF[level], count), :] = low(base + HALO, count)
        right_ref[0, edge, :] = low(base + HALO + count, HALO)
    dkv_ref[0, pl.ds(OFF[7], 16), :] = jnp.zeros((16, acc_ref.shape[1]), BF16)
    top_ref[0] = low(POFF[7], 4 * PIECE7)


def attend_back(q, q3, kvp, stats, dout, ids, const):
    micro, _, width = q.shape
    lse, lsec, lsex, oc = stats
    shape = jax.ShapeDtypeStruct
    return pl.pallas_call(
        attend_back_kernel,
        grid=(micro,),
        in_specs=[
            per_micro((ROWS, width)),
            per_micro((ROWS // 8, width)),
            per_micro((PADDED, 2 * width)),
            per_micro((2 * FINE_TILES, QL)),
            per_micro((2 * COARSE_TILES, QL)),
            per_micro((2 * COARSE_TILES, 8 * QL)),
            per_micro((ROWS // 8, width)),
            per_micro((ROWS, width)),
            per_micro((PADDED, 128)),
            per_micro((8 * FINE_TILES, QL)),
            per_micro((8 * COARSE_TILES, QL)),
            whole((FINE_KEYS, QL)),
            whole((COARSE_TILES, COARSE_KEYS, QL)),
            whole((5 * TILE, TILE)),
            whole((4, QL, QL)),
            whole((QL, QL)),
            whole((8 * QL, QL)),
        ],
        out_specs=[
            per_micro((ROWS, width)),
            per_micro((ROWS // 8, width)),
            per_micro((2 * ROWS, 2 * width)),
            per_micro((EDGE, 2 * width)),
            per_micro((EDGE, 2 * width)),
            per_micro((4 * PIECE7, 2 * width)),
        ],
        out_shape=[
            shape((micro, ROWS, width), BF16),
            shape((micro, ROWS // 8, width), BF16),
            shape((micro, 2 * ROWS, 2 * width), BF16),
            shape((micro, EDGE, 2 * width), BF16),
            shape((micro, EDGE, 2 * width), BF16),
            shape((micro, 4 * PIECE7, 2 * width), BF16),
        ],
        scratch_shapes=[
            pltpu.VMEM((PADDED, 2 * width), F32),
            pltpu.VMEM((ROWS // 8, width), F32),
            pltpu.VMEM((2 * COARSE_TILES, 8 * QL), F32),
        ],
        compiler_params=params(1),
        name="attend_back",
    )(
        q,
        q3,
        kvp,
        lse,
        lsec,
        lsex,
        oc,
        dout,
        ids["key"],
        ids["fine"],
        ids["coarse"],
        const["fine"],
        const["coarse"],
        const["query_means"],
        const["grad_means"],
        const["head_mask"],
        const["spread_t"],
    )


MID_ROWS = 512
FF_CHUNK = 512
ROOT = math.sqrt(2.0 / math.pi)


def middle_kernel(
    tok_ref,
    cot_ref,
    mixed_ref,
    gain_ref,
    off_ref,
    wo_ref,
    wi_ref,
    bi_ref,
    wd_ref,
    bd_ref,
    out_ref,
    dmid_ref,
    dmix_ref,
    gwo_ref,
    gwi_ref,
    gwd_ref,
    gbi_ref,
    gsmall_ref,
    acc_o,
    acc_i,
    acc_d,
):
    step = pl.program_id(0)

    @pl.when(step == 0)
    def _():
        acc_o[...] = jnp.zeros(acc_o.shape, F32)
        acc_i[...] = jnp.zeros(acc_i.shape, F32)
        acc_d[...] = jnp.zeros(acc_d.shape, F32)
        gbi_ref[...] = jnp.zeros(gbi_ref.shape, F32)
        gsmall_ref[...] = jnp.zeros(gsmall_ref.shape, F32)

    cot = cot_ref[...]
    top = cot.astype(BF16)
    mixed = mixed_ref[...]
    middle = tok_ref[...] + dot_nn(mixed, wo_ref[...])
    unit, rate = normalised(middle)
    second = (unit * gain_ref[...] + off_ref[...]).astype(BF16)
    gsmall_ref[0:8, :] = gsmall_ref[0:8, :] + fold_rows(top.astype(F32))
    result = middle + bd_ref[...]
    back = jnp.zeros(cot.shape, F32)
    hidden = wi_ref.shape[1]
    for part in range(hidden // FF_CHUNK):
        cols = pl.ds(FF_CHUNK * part, FF_CHUNK)
        wi = wi_ref[:, cols]
        wd = wd_ref[cols, :]
        pre = dot_nn(second, wi) + bi_ref[:, cols]
        square = pre * pre
        tanh = jnp.tanh(ROOT * pre * (1.0 + 0.044715 * square))
        half = 0.5 * (1.0 + tanh)
        activ = (pre * half).astype(BF16)
        slope = half + (0.5 * ROOT) * pre * (1.0 - tanh * tanh) * (1.0 + 3 * 0.044715 * square)
        result = result + dot_nn(activ, wd)
        grad = dot_nt(top, wd) * slope
        grad_low = grad.astype(BF16)
        gbi_ref[:, cols] = gbi_ref[:, cols] + fold_rows(grad_low.astype(F32))
        back = back + dot_nt(grad_low, wi)
        acc_d[cols, :] = acc_d[cols, :] + dot_tn(activ, top)
        acc_i[:, cols] = acc_i[:, cols] + dot_tn(second, grad_low)
    out_ref[...] = result
    gsmall_ref[8:16, :] = gsmall_ref[8:16, :] + fold_rows(back * unit)
    gsmall_ref[16:24, :] = gsmall_ref[16:24, :] + fold_rows(back)
    dmid = cot + norm_back(back * gain_ref[...], unit, rate)
    dmid_ref[...] = dmid
    branch = dmid.astype(BF16)
    dmix_ref[...] = dot_nt(branch, wo_ref[...]).astype(BF16)
    acc_o[...] = acc_o[...] + dot_tn(mixed, branch)

    @pl.when(step == pl.num_programs(0) - 1)
    def _():
        gwo_ref[...] = acc_o[...].astype(BF16)
        gwi_ref[...] = acc_i[...].astype(BF16)
        gwd_ref[...] = acc_d[...].astype(BF16)


def middle_part(tokens, cot, mixed, gain, offset, wo, wi, bi, wd, bd):
    rows, width = tokens.shape
    hidden = wi.shape[1]
    shape = jax.ShapeDtypeStruct
    tiled = pl.BlockSpec((MID_ROWS, width), lambda r: (r, 0))
    return pl.pallas_call(
        middle_kernel,
        grid=(rows // MID_ROWS,),
        in_specs=[
            tiled,
            tiled,
            tiled,
            whole((1, width)),
            whole((1, width)),
            whole((width, width)),
            whole((width, hidden)),
            whole((1, hidden)),
            whole((hidden, width)),
            whole((1, width)),
        ],
        out_specs=[
            tiled,
            tiled,
            tiled,
            whole((width, width)),
            whole((width, hidden)),
            whole((hidden, width)),
            whole((8, hidden)),
            whole((24, width)),
        ],
        out_shape=[
            shape((rows, width), F32),
            shape((rows, width), F32),
            shape((rows, width), BF16),
            shape((width, width), BF16),
            shape((width, hidden), BF16),
            shape((hidden, width), BF16),
            shape((8, hidden), F32),
            shape((24, width), F32),
        ],
        scratch_shapes=[
            pltpu.VMEM((width, width), F32),
            pltpu.VMEM((width, hidden), F32),
            pltpu.VMEM((hidden, width), F32),
        ],
        compiler_params=params(1),
        name="middle",
    )(tokens, cot, mixed, gain, offset, wo, wi, bi, wd, bd)


def finish_kernel(
    tok_ref,
    dmid_ref,
    dq_ref,
    dq3_ref,
    dkv_ref,
    left_ref,
    right_ref,
    top_ref,
    gain_ref,
    off_ref,
    w_ref,
    low_ref,
    high_ref,
    grad_ref,
    gw_ref,
    gsmall_ref,
    cells_ref,
    acc_ref,
):
    step = pl.program_id(0)

    @pl.when(step == 0)
    def _():
        acc_ref[...] = jnp.zeros(acc_ref.shape, F32)
        gsmall_ref[...] = jnp.zeros(gsmall_ref.shape, F32)

    cells_ref[...] = dkv_ref[0]

    def add(start, value):
        rows = pl.ds(start, HALO)
        cells_ref[rows, :] = (cells_ref[rows, :].astype(F32) + value.astype(F32)).astype(BF16)

    for level in range(LEVELS - 1):
        edge = pl.ds(HALO * level, HALO)
        add(OFF[level], left_ref[0, edge, :])
        add(OFF[level] + CELLS[level] - HALO, right_ref[0, edge, :])
    add(OFF[7], top_ref[0])

    for chunk in range(ROWS // 256):
        rows = pl.ds(256 * chunk, 256)
        unit, rate = normalised(tok_ref[0, rows, :])
        normed = (unit * gain_ref[...] + off_ref[...]).astype(BF16)
        cells = jnp.concatenate(
            [
                cells_ref[pl.ds(OFF[level] + (256 >> level) * chunk, 256 >> level), :]
                for level in range(1, 5)
            ],
            axis=0,
        )
        dkv = (
            cells_ref[rows, :].astype(F32)
            + dot_nn(low_ref[...], cells)
            + dot_nn(high_ref[rows, :], cells_ref[pl.ds(OFF[5], 64), :])
        ).astype(BF16)
        dq = (
            dq_ref[0, rows, :].astype(F32)
            + dot_nn(low_ref[:, 192:224], dq3_ref[0, pl.ds(32 * chunk, 32), :])
        ).astype(BF16)
        parts = [dq, dkv[:, 0:512], dkv[:, 512:1024]]
        back = jnp.zeros(unit.shape, F32)
        for index in range(3):
            back = back + dot_nt(parts[index], w_ref[index])
            acc_ref[index] = acc_ref[index] + dot_tn(normed, parts[index])
        gsmall_ref[0:8, :] = gsmall_ref[0:8, :] + fold_rows(back * unit)
        gsmall_ref[8:16, :] = gsmall_ref[8:16, :] + fold_rows(back)
        grad_ref[0, rows, :] = dmid_ref[0, rows, :] + norm_back(back * gain_ref[...], unit, rate)

    @pl.when(step == pl.num_programs(0) - 1)
    def _():
        gw_ref[...] = acc_ref[...].astype(BF16)


def finish(tokens, dmid, dq, dq3, dkv, left, right, top, gain, offset, weight, const):
    micro, _, width = tokens.shape
    shape = jax.ShapeDtypeStruct
    return pl.pallas_call(
        finish_kernel,
        grid=(micro,),
        in_specs=[
            per_micro((ROWS, width)),
            per_micro((ROWS, width)),
            per_micro((ROWS, width)),
            per_micro((ROWS // 8, width)),
            per_micro((2 * ROWS, 2 * width)),
            per_micro((EDGE, 2 * width)),
            per_micro((EDGE, 2 * width)),
            per_micro((16, 2 * width)),
            whole((1, width)),
            whole((1, width)),
            whole((3, width, width)),
            whole((256, 240)),
            whole((ROWS, 64)),
        ],
        out_specs=[
            per_micro((ROWS, width)),
            whole((3, width, width)),
            whole((16, width)),
        ],
        out_shape=[
            shape((micro, ROWS, width), F32),
            shape((3, width, width), BF16),
            shape((16, width), F32),
        ],
        scratch_shapes=[
            pltpu.VMEM((2 * ROWS, 2 * width), BF16),
            pltpu.VMEM((3, width, width), F32),
        ],
        compiler_params=params(1),
        name="finish",
    )(
        tokens,
        dmid,
        dq,
        dq3,
        dkv,
        left,
        right,
        top,
        gain,
        offset,
        weight,
        const["means_low_t"],
        const["means_high_t"],
    )


def cell_documents(segments, piece):
    micro, length = segments.shape
    keys = []
    fine = []
    coarse = []
    for level in range(LEVELS):
        cell = 1 << level
        grouped = segments.reshape(micro, length // cell, cell)
        lowest = grouped[:, :, 0]
        highest = grouped[:, :, cell - 1]
        same = lowest == highest
        key = jnp.where(same, lowest, -2)
        query = jnp.where(same, lowest, -1)
        own = lax.dynamic_slice_in_dim(query, piece * CELLS[level], CELLS[level], axis=1)
        if level < LEVELS - 1:
            padded = jnp.pad(key, ((0, 0), (HALO, HALO)), constant_values=-3)
            keys.append(
                lax.dynamic_slice_in_dim(
                    padded, piece * CELLS[level], CELLS[level] + 2 * HALO, axis=1
                )
            )
        else:
            owner = jnp.arange(key.shape[1]) // PIECE7
            counted = (jnp.abs(owner // 2 - piece // 2) == 1) & (jnp.abs(owner - piece) >= 2)
            keys.append(jnp.where(counted[None], key, -3))
        if level < FINE:
            fine.append(jnp.repeat(own, cell, axis=1).reshape(micro, FINE_TILES, 1, TILE))
        else:
            coarse.append(jnp.repeat(own, cell // 8, axis=1).reshape(micro, COARSE_TILES, 1, TILE))

    def rows(parts):
        value = jnp.concatenate(parts, axis=2)
        value = jnp.pad(value, ((0, 0), (0, 0), (0, 8 - len(parts)), (0, 0)))
        return jnp.tile(value, (1, 1, 1, QUAD)).reshape(micro, -1, QL)

    key = jnp.concatenate(keys, axis=1)
    return dict(
        key=jnp.broadcast_to(key[:, :, None], key.shape + (128,)),
        fine=rows(fine),
        coarse=rows(coarse),
    )


def body(
    tokens,
    segment_ids,
    norm_gains,
    norm_biases,
    qkv_weight,
    out_weight,
    in_weight,
    in_bias,
    down_weight,
    down_bias,
    cotangent,
):
    micro, _, row_count, width = tokens.shape
    pieces = lax.axis_size("sp")
    piece = lax.axis_index("sp")
    assert row_count == ROWS and pieces == 4
    const = constants()
    tokens = tokens[:, 0]
    cotangent = cotangent[:, 0]

    gains = lax.all_gather(norm_gains, "dp", axis=1, tiled=True).astype(F32)
    offsets = lax.all_gather(norm_biases, "dp", axis=1, tiled=True).astype(F32)
    wqkv = lax.all_gather(qkv_weight, "dp", axis=1, tiled=True)
    wo = lax.all_gather(out_weight, "dp", axis=0, tiled=True)
    wi = lax.all_gather(in_weight, "dp", axis=0, tiled=True)
    bi = lax.all_gather(in_bias, "dp", axis=0, tiled=True).astype(F32)
    wd = lax.all_gather(down_weight, "dp", axis=0, tiled=True)
    bd = lax.all_gather(down_bias, "dp", axis=0, tiled=True).astype(F32)

    ids = cell_documents(segment_ids[:, 0], piece)

    rightward = [(p, p + 1) for p in range(pieces - 1)]
    leftward = [(p + 1, p) for p in range(pieces - 1)]
    across = [(p, (p + 2) % pieces) for p in range(pieces)]
    ends = [(0, pieces - 1), (pieces - 1, 0)]
    move = lambda value, perm: lax.ppermute(value, "sp", perm)

    q, q3, kv, to_left, to_right = project(tokens, gains[0:1], offsets[0:1], wqkv, const)
    from_left = move(to_right, rightward)
    from_right = move(to_left, leftward)
    top = kv[:, OFF[7] : OFF[7] + PIECE7]
    top_across = move(top, across)
    top_ends = move(top, ends)
    owner = jnp.arange(pieces)[None, :, None, None]
    tops = jnp.where(
        owner == (piece + 2) % pieces,
        top_across[:, None],
        jnp.where(owner == pieces - 1 - piece, top_ends[:, None], jnp.zeros((), BF16)),
    ).reshape(micro, pieces * PIECE7, 2 * width)

    mixed, kvp, *stats = attend(q, q3, kv, from_left, from_right, tops, ids, const)

    flat = lambda value: value.reshape(micro * ROWS, width)
    outputs, dmid, dmix, gwo, gwi, gwd, gbi, gsmall_two = middle_part(
        flat(tokens),
        flat(cotangent),
        flat(mixed),
        gains[1:2],
        offsets[1:2],
        wo,
        wi,
        bi[None],
        wd,
        bd[None],
    )
    split = lambda value: value.reshape(micro, ROWS, width)

    dq, dq3, dkv, dleft, dright, dtop = attend_back(
        q, q3, kvp, stats, split(dmix), ids, const
    )
    dfrom_left = move(dright, rightward)
    dfrom_right = move(dleft, leftward)
    dtop = dtop.reshape(micro, pieces, PIECE7, 2 * width)
    pick = lambda index: lax.dynamic_index_in_dim(dtop, index, axis=1, keepdims=False)
    dtop_own = move(pick((piece + 2) % pieces), across).astype(F32) + move(
        pick(pieces - 1 - piece), ends
    ).astype(F32)
    dtop_own = jnp.pad(dtop_own.astype(BF16), ((0, 0), (0, 16 - PIECE7), (0, 0)))

    input_grad, gwqkv, gsmall_one = finish(
        tokens,
        split(dmid),
        dq,
        dq3,
        dkv,
        dfrom_left,
        dfrom_right,
        dtop_own,
        gains[0:1],
        offsets[0:1],
        wqkv,
        const,
    )

    fold = lambda value, index: jnp.sum(value[8 * index : 8 * index + 8], axis=0)

    def reduced(value, dimension):
        value = lax.psum_scatter(
            value.astype(BF16), "dp", scatter_dimension=dimension, tiled=True
        )
        return lax.psum(value, "sp").astype(F32)

    return (
        outputs.reshape(micro, 1, ROWS, width),
        input_grad[:, None],
        reduced(jnp.stack([fold(gsmall_one, 0), fold(gsmall_two, 1)]), 1),
        reduced(jnp.stack([fold(gsmall_one, 1), fold(gsmall_two, 2)]), 1),
        reduced(gwqkv, 1),
        reduced(gwo, 0),
        reduced(gwi, 0),
        reduced(fold(gbi, 0), 0),
        reduced(gwd, 0),
        reduced(fold(gsmall_two, 0), 0),
    )


def solution(mesh):
    in_specs = (
        P(None, "dp", "sp", None),
        P(None, "dp", None),
        P(None, "dp"),
        P(None, "dp"),
        P(None, "dp", None),
        P("dp", None),
        P("dp", None),
        P("dp"),
        P("dp", None),
        P("dp"),
        P(None, "dp", "sp", None),
    )
    out_specs = (
        P(None, "dp", "sp", None),
        P(None, "dp", "sp", None),
        P(None, "dp"),
        P(None, "dp"),
        P(None, "dp", None),
        P("dp", None),
        P("dp", None),
        P("dp"),
        P("dp", None),
        P("dp"),
    )
    return jax.shard_map(body, mesh=mesh, in_specs=in_specs, out_specs=out_specs, check_vma=False)
```

```python
import math

import jax
import jax.numpy as jnp
import numpy as np
from jax import lax
from jax.experimental import pallas as pl
from jax.experimental.pallas import tpu as pltpu
from jax.sharding import PartitionSpec as P

HEADS = 8
HEAD_DIM = 64
BLOCK = 16
LEVELS = 8
HALO = 16
TILE = 64
QUAD = 4
QL = QUAD * HEAD_DIM
NEG = -1e30
FINE = 3
ROWS = 1024
EDGE = 112
EDGES = 128
F32 = jnp.float32
BF16 = jnp.bfloat16

CELLS = [ROWS >> level for level in range(LEVELS)]
OFF = [2 * ROWS - (2 * ROWS >> level) for level in range(LEVELS)]
POFF = []
_at = 0
for _level in range(LEVELS - 1):
    POFF.append(_at)
    _at += CELLS[_level] + 2 * HALO
POFF.append(_at)
PIECE7 = CELLS[LEVELS - 1]
PADDED = _at + 4 * PIECE7
FINE_TILES = ROWS // TILE
COARSE_TILES = ROWS // 8 // TILE
FINE_KEYS = 192
COARSE_KEYS = 256
LN_EPS = 1e-05
VMEM_LIMIT = 62 * 1024 * 1024


def _counts(level, query, key):
    query = query[None, :]
    key = key[:, None]
    near = np.abs(query // 16 - key // 16)
    if level == 0:
        return near <= 1
    return (near == 1) & (np.abs(query // 8 - key // 8) >= 2)


def _bias(parts):
    rows = []
    for level, allowed in parts:
        rows.append(np.where(allowed, np.float32(level * math.log(2.0)), np.float32(NEG)))
    block = np.concatenate(rows, axis=0).astype(np.float32)
    return np.tile(block, (1, QUAD))


def _two_blocks():
    return np.concatenate([np.arange(16) - 16, np.arange(16) + 16])


def fine_bias():
    token = np.arange(TILE)
    return _bias(
        [
            (0, _counts(0, token, np.arange(96) - 16)),
            (1, _counts(1, token // 2, np.arange(64) - 16)),
            (2, _counts(2, token // 4, _two_blocks())),
        ]
    )


def coarse_bias():
    cell = np.arange(TILE)
    out = []
    for tile in range(COARSE_TILES):
        out.append(
            _bias(
                [
                    (3, _counts(3, cell, np.arange(96) - 16)),
                    (4, _counts(4, cell // 2, np.arange(64) - 16)),
                    (5, _counts(5, cell // 4, _two_blocks())),
                    (6, _counts(6, 8 * tile + cell // 8, _two_blocks())),
                    (7, np.ones((4 * PIECE7, TILE), bool)),
                ]
            )
        )
    return np.stack(out)


def averaging(cell, count):
    at = np.arange(count) // cell
    return (at[:, None] == at[None, :]).astype(np.float32) / cell


def mean_rows(cell, count):
    return (np.arange(count)[None, :] // cell == np.arange(count // cell)[:, None]).astype(
        np.float32
    ) / cell


def spread_matrix():
    out = np.zeros((QUAD, TILE, 8, QUAD, TILE), np.float32)
    for part in range(8):
        for token in range(TILE):
            for head in range(QUAD):
                out[head, 8 * part + token // 8, part, head, token] = 1.0
    return out.reshape(QL, 8 * QL)


def constants():
    query_means = np.concatenate([averaging(1 << r, TILE) for r in range(5)]) * 0.125
    grad_means = np.stack([np.kron(np.eye(QUAD), averaging(1 << r, TILE)) for r in range(1, 5)])
    head_mask = np.kron(np.eye(QUAD), np.ones((TILE, HEAD_DIM)))
    means_low = np.concatenate([mean_rows(1 << level, 256) for level in range(1, 5)])
    means_high = np.concatenate(
        [mean_rows(1 << level, ROWS) for level in range(5, 8)] + [np.zeros((8, ROWS))]
    )
    as_low = lambda value: jnp.asarray(value.astype(np.float32)).astype(BF16)
    return dict(
        fine=jnp.asarray(fine_bias()),
        coarse=jnp.asarray(coarse_bias()),
        query_means=as_low(query_means),
        grad_means=as_low(grad_means),
        head_mask=as_low(head_mask),
        means_low=as_low(means_low),
        means_high=as_low(means_high),
        means_low_t=as_low(means_low.T),
        means_high_t=as_low(means_high.T),
        spread=as_low(spread_matrix()),
        spread_t=as_low(spread_matrix().T),
    )


def dot_nn(left, right):
    return jnp.dot(left, right, preferred_element_type=F32)


def dot_nt(left, right):
    return lax.dot_general(left, right, (((1,), (1,)), ((), ())), preferred_element_type=F32)


def dot_tn(left, right):
    return lax.dot_general(left, right, (((0,), (0,)), ((), ())), preferred_element_type=F32)


def at(start, size):
    return pl.ds(pl.multiple_of(start, 16), size)


def whole(shape):
    zeros = (0,) * len(shape)
    return pl.BlockSpec(shape, lambda *_: zeros)


def per_micro(shape):
    zeros = (0,) * len(shape)
    return pl.BlockSpec((1,) + shape, lambda m: (m,) + zeros)


def params(steps):
    return pltpu.CompilerParams(
        dimension_semantics=("arbitrary",) * steps, vmem_limit_bytes=VMEM_LIMIT
    )


def normalised(rows):
    center = rows - jnp.mean(rows, axis=-1, keepdims=True)
    spread = jnp.mean(center * center, axis=-1, keepdims=True)
    rate = lax.rsqrt(spread + LN_EPS)
    return center * rate, rate


def norm_back(grad, unit, rate):
    mean_grad = jnp.mean(grad, axis=-1, keepdims=True)
    mean_dot = jnp.mean(grad * unit, axis=-1, keepdims=True)
    return rate * (grad - mean_grad - unit * mean_dot)


def fold_rows(value):
    return jnp.sum(value.reshape(-1, 8, value.shape[-1]), axis=0)


def project_kernel(
    tok_ref, gain_ref, off_ref, w_ref, low_ref, high_ref, q_ref, q3_ref, kv_ref, left_ref, right_ref
):
    for chunk in range(ROWS // 256):
        rows = pl.ds(256 * chunk, 256)
        unit, _ = normalised(tok_ref[0, rows, :])
        normed = (unit * gain_ref[...] + off_ref[...]).astype(BF16)
        query = dot_nn(normed, w_ref[0]).astype(BF16)
        q_ref[0, rows, :] = query
        q3_ref[0, pl.ds(32 * chunk, 32), :] = dot_nn(low_ref[192:224, :], query).astype(BF16)
        for part in range(2):
            lanes = pl.ds(512 * part, 512)
            value = dot_nn(normed, w_ref[1 + part]).astype(BF16)
            kv_ref[0, rows, lanes] = value
            cells = dot_nn(low_ref[...], value).astype(BF16)
            start = 0
            for level in range(1, 5):
                count = 256 >> level
                kv_ref[0, pl.ds(OFF[level] + count * chunk, count), lanes] = cells[
                    start : start + count
                ]
                start += count
    for part in range(2):
        lanes = pl.ds(512 * part, 512)
        kv_ref[0, pl.ds(OFF[5], 64), lanes] = dot_nn(
            high_ref[...], kv_ref[0, pl.ds(0, ROWS), lanes]
        ).astype(BF16)
    for level in range(LEVELS - 1):
        edge = pl.ds(HALO * level, HALO)
        left_ref[0, edge, :] = kv_ref[0, pl.ds(OFF[level], HALO), :]
        right_ref[0, edge, :] = kv_ref[0, pl.ds(OFF[level] + CELLS[level] - HALO, HALO), :]
    left_ref[0, pl.ds(EDGE, 16), :] = kv_ref[0, pl.ds(OFF[7], 16), :]
    right_ref[0, pl.ds(EDGE, 16), :] = kv_ref[0, pl.ds(OFF[7], 16), :]


def project(tokens, gain, offset, weight, const):
    micro = tokens.shape[0]
    width = tokens.shape[2]
    shape = jax.ShapeDtypeStruct
    return pl.pallas_call(
        project_kernel,
        grid=(micro,),
        in_specs=[
            per_micro((ROWS, width)),
            whole((1, width)),
            whole((1, width)),
            whole((3, width, width)),
            whole((240, 256)),
            whole((64, ROWS)),
        ],
        out_specs=[
            per_micro((ROWS, width)),
            per_micro((ROWS // 8, width)),
            per_micro((2 * ROWS, 2 * width)),
            per_micro((EDGES, 2 * width)),
            per_micro((EDGES, 2 * width)),
        ],
        out_shape=[
            shape((micro, ROWS, width), BF16),
            shape((micro, ROWS // 8, width), BF16),
            shape((micro, 2 * ROWS, 2 * width), BF16),
            shape((micro, EDGES, 2 * width), BF16),
            shape((micro, EDGES, 2 * width), BF16),
        ],
        compiler_params=params(1),
        name="project",
    )(tokens, gain, offset, weight, const["means_low"], const["means_high"])


def fine_windows(tile):
    return [
        (POFF[0] + 64 * tile, 96),
        (POFF[1] + 32 * tile, 64),
        (POFF[2] + 16 * tile, 16),
        (POFF[2] + 16 * tile + 32, 16),
    ]


def coarse_windows(tile):
    return [
        (POFF[3] + 64 * tile, 96),
        (POFF[4] + 32 * tile, 64),
        (POFF[5] + 16 * tile, 16),
        (POFF[5] + 16 * tile + 32, 16),
        (POFF[6], 16),
        (POFF[6] + 32, 16),
        (POFF[7], 32),
    ]


FINE_LEVELS = [96, 64, 32]
COARSE_LEVELS = [96, 64, 32, 32, 32]


def gather_rows(ref, windows, lanes):
    return jnp.concatenate([ref[0, at(start, size), lanes] for start, size in windows], axis=0)


def tile_bias(kid_ref, qid_ref, row, windows, levels, bias):
    keys = jnp.concatenate([kid_ref[0, at(start, size), :] for start, size in windows], axis=0)
    keys = jnp.concatenate([keys, keys], axis=1)
    out = []
    start = 0
    for index, count in enumerate(levels):
        part = slice(start, start + count)
        owner = qid_ref[0, pl.ds(row + index, 1), :]
        out.append(jnp.where(keys[part] == owner, bias[part], NEG))
        start += count
    return jnp.concatenate(out, axis=0)


def head_stack(value, mask):
    return jnp.concatenate([value] * QUAD, axis=0) * mask


def head_pick(stacked):
    lane = lax.broadcasted_iota(jnp.int32, (TILE, QL), 1) // HEAD_DIM
    out = stacked[0:TILE]
    for head in range(1, QUAD):
        out = jnp.where(lane == head, stacked[TILE * head : TILE * (head + 1)], out)
    return out


def tile_scores(keys, queries, mask, levels):
    out = []
    start = 0
    for index, count in enumerate(levels):
        stacked = head_stack(queries[TILE * index : TILE * (index + 1)], mask)
        out.append(dot_nt(keys[start : start + count], stacked))
        start += count
    return jnp.concatenate(out, axis=0)


def three_terms(row):
    high = row.astype(BF16)
    rest = row - high.astype(F32)
    middle = rest.astype(BF16)
    low = (rest - middle.astype(F32)).astype(BF16)
    return high, middle, low


def own_cell(tile):
    cell = lax.broadcasted_iota(jnp.int32, (16, QL), 0)
    token = lax.broadcasted_iota(jnp.int32, (16, QL), 1) % TILE
    return cell == 8 * (tile % 2) + token // 8


def attend_kernel(
    q_ref,
    q3_ref,
    kv_ref,
    left_ref,
    right_ref,
    top_ref,
    kid_ref,
    qidf_ref,
    qidc_ref,
    fine_ref,
    coarse_ref,
    means_ref,
    mask_ref,
    spread_ref,
    mixed_ref,
    kvp_ref,
    lse_ref,
    lsec_ref,
    lsex_ref,
    oc_ref,
):
    for level in range(LEVELS - 1):
        base = POFF[level]
        count = CELLS[level]
        edge = pl.ds(HALO * level, HALO)
        kvp_ref[0, pl.ds(base, HALO), :] = left_ref[0, edge, :]
        kvp_ref[0, pl.ds(base + HALO, count), :] = kv_ref[0, pl.ds(OFF[level], count), :]
        kvp_ref[0, pl.ds(base + HALO + count, HALO), :] = right_ref[0, edge, :]
    kvp_ref[0, pl.ds(POFF[7], 4 * PIECE7), :] = top_ref[0]
    mask = mask_ref[...]

    def coarse_tile(tile, carry):
        windows = coarse_windows(tile)
        bias = tile_bias(kid_ref, qidc_ref, 8 * tile, windows, COARSE_LEVELS, coarse_ref[tile])
        rows = at(TILE * tile, TILE)
        for quad in range(2):
            lanes = pl.ds(QL * quad, QL)
            vlanes = pl.ds(512 + QL * quad, QL)
            queries = dot_nn(means_ref[...], q3_ref[0, rows, lanes]).astype(BF16)
            keys = gather_rows(kvp_ref, windows, lanes)
            scores = tile_scores(keys, queries, mask, COARSE_LEVELS) + bias
            top = jnp.max(scores, axis=0, keepdims=True)
            share = jnp.exp(scores - top)
            total = jnp.sum(share, axis=0, keepdims=True)
            lse = top + jnp.log(total)
            lsec_ref[0, pl.ds(2 * tile + quad, 1), :] = lse
            share = (share * (1.0 / total)).astype(BF16)
            values = gather_rows(kvp_ref, windows, vlanes)
            oc_ref[0, rows, lanes] = head_pick(dot_tn(share, values)).astype(BF16)
            high, middle, low = three_terms(lse)
            terms = jnp.concatenate([high, middle, low, low, low, low, low, low], axis=0)
            terms = dot_nn(terms, spread_ref[...])
            lsex_ref[0, pl.ds(2 * tile + quad, 1), :] = terms[0:1] + terms[1:2] + terms[2:3]
        return carry

    lax.fori_loop(0, COARSE_TILES, coarse_tile, 0, unroll=2)

    def fine_tile(tile, carry):
        windows = fine_windows(tile)
        bias = tile_bias(kid_ref, qidf_ref, 8 * tile, windows, FINE_LEVELS, fine_ref[...])
        rows = at(TILE * tile, TILE)
        own = own_cell(tile)
        for quad in range(2):
            lanes = pl.ds(QL * quad, QL)
            vlanes = pl.ds(512 + QL * quad, QL)
            queries = dot_nn(means_ref[0 : FINE * TILE, :], q_ref[0, rows, lanes]).astype(BF16)
            keys = gather_rows(kvp_ref, windows, lanes)
            scores = tile_scores(keys, queries, mask, FINE_LEVELS) + bias
            far = lsex_ref[
                0, pl.ds(2 * (tile // 8) + quad, 1), pl.ds(pl.multiple_of(QL * (tile % 8), QL), QL)
            ]
            top = jnp.maximum(jnp.max(scores, axis=0, keepdims=True), far)
            share = jnp.exp(scores - top)
            far_share = jnp.exp(far - top)
            total = jnp.sum(share, axis=0, keepdims=True) + far_share
            lse_ref[0, pl.ds(2 * tile + quad, 1), :] = top + jnp.log(total)
            inverse = 1.0 / total
            share = jnp.concatenate(
                [share * inverse, jnp.where(own, far_share * inverse, 0.0)], axis=0
            ).astype(BF16)
            values = jnp.concatenate(
                [
                    gather_rows(kvp_ref, windows, vlanes),
                    oc_ref[0, at(16 * (tile // 2), 16), lanes],
                ],
                axis=0,
            )
            mixed_ref[0, rows, lanes] = head_pick(dot_tn(share, values)).astype(BF16)
        return carry

    lax.fori_loop(0, FINE_TILES, fine_tile, 0, unroll=4)


def attend(q, q3, kv, left, right, top, ids, const):
    micro, _, width = q.shape
    shape = jax.ShapeDtypeStruct
    return pl.pallas_call(
        attend_kernel,
        grid=(micro,),
        in_specs=[
            per_micro((ROWS, width)),
            per_micro((ROWS // 8, width)),
            per_micro((2 * ROWS, 2 * width)),
            per_micro((EDGE, 2 * width)),
            per_micro((EDGE, 2 * width)),
            per_micro((4 * PIECE7, 2 * width)),
            per_micro((PADDED, 128)),
            per_micro((8 * FINE_TILES, QL)),
            per_micro((8 * COARSE_TILES, QL)),
            whole((FINE_KEYS, QL)),
            whole((COARSE_TILES, COARSE_KEYS, QL)),
            whole((5 * TILE, TILE)),
            whole((QL, QL)),
            whole((QL, 8 * QL)),
        ],
        out_specs=[
            per_micro((ROWS, width)),
            per_micro((PADDED, 2 * width)),
            per_micro((2 * FINE_TILES, QL)),
            per_micro((2 * COARSE_TILES, QL)),
            per_micro((2 * COARSE_TILES, 8 * QL)),
            per_micro((ROWS // 8, width)),
        ],
        out_shape=[
            shape((micro, ROWS, width), BF16),
            shape((micro, PADDED, 2 * width), BF16),
            shape((micro, 2 * FINE_TILES, QL), F32),
            shape((micro, 2 * COARSE_TILES, QL), F32),
            shape((micro, 2 * COARSE_TILES, 8 * QL), F32),
            shape((micro, ROWS // 8, width), BF16),
        ],
        compiler_params=params(1),
        name="attend",
    )(
        q,
        q3,
        kv,
        left,
        right,
        top,
        ids["key"],
        ids["fine"],
        ids["coarse"],
        const["fine"],
        const["coarse"],
        const["query_means"],
        const["head_mask"],
        const["spread"],
    )


def add_rows(ref, windows, lanes, value):
    start = 0
    for base, count in windows:
        rows = at(base, count)
        ref[rows, lanes] = ref[rows, lanes] + value[start : start + count]
        start += count


def mean_scores(grads, means_ref, levels):
    out = [grads[0 : levels[0]]]
    start = levels[0]
    for index, count in enumerate(levels[1:]):
        out.append(dot_nn(grads[start : start + count], means_ref[index]).astype(BF16))
        start += count
    return jnp.concatenate(out, axis=0)


def attend_back_kernel(
    piece_ref,
    q_ref,
    q3_ref,
    kvp_ref,
    lse_ref,
    lsec_ref,
    lsex_ref,
    oc_ref,
    dout_ref,
    kid_ref,
    qidf_ref,
    qidc_ref,
    fine_ref,
    coarse_ref,
    means_ref,
    grad_means_ref,
    mask_ref,
    spread_t_ref,
    dq_ref,
    dq3_ref,
    dkv_ref,
    left_ref,
    right_ref,
    top_ref,
    acc_ref,
    dcell_ref,
    delta_ref,
):
    acc_ref[...] = jnp.zeros(acc_ref.shape, F32)
    dcell_ref[...] = jnp.zeros(dcell_ref.shape, F32)
    mask = mask_ref[...]

    def fine_tile(tile, carry):
        windows = fine_windows(tile)
        bias = tile_bias(kid_ref, qidf_ref, 8 * tile, windows, FINE_LEVELS, fine_ref[...])
        rows = at(TILE * tile, TILE)
        own = own_cell(tile)
        cells = at(16 * (tile // 2), 16)
        for quad in range(2):
            lanes = pl.ds(QL * quad, QL)
            vlanes = pl.ds(512 + QL * quad, QL)
            query = q_ref[0, rows, lanes]
            queries = dot_nn(means_ref[0 : FINE * TILE, :], query).astype(BF16)
            keys = gather_rows(kvp_ref, windows, lanes)
            lse = lse_ref[0, pl.ds(2 * tile + quad, 1), :]
            wide = pl.ds(pl.multiple_of(QL * (tile % 8), QL), QL)
            coarse_row = pl.ds(2 * (tile // 8) + quad, 1)
            far_share = jnp.exp(lsex_ref[0, coarse_row, wide] - lse)
            share = jnp.exp(tile_scores(keys, queries, mask, FINE_LEVELS) + bias - lse)
            share = jnp.concatenate([share, jnp.where(own, far_share, 0.0)], axis=0)
            values = jnp.concatenate(
                [gather_rows(kvp_ref, windows, vlanes), oc_ref[0, cells, lanes]], axis=0
            )
            dout = head_stack(dout_ref[0, rows, lanes], mask)
            weighted = share * dot_nt(values, dout)
            delta = jnp.sum(weighted, axis=0, keepdims=True)
            delta_ref[coarse_row, wide] = far_share * delta
            grads = (weighted[0:FINE_KEYS] - share[0:FINE_KEYS] * delta).astype(BF16)
            dvalues = dot_nn(share.astype(BF16), dout)
            add_rows(acc_ref, windows, vlanes, dvalues)
            dcell_ref[cells, lanes] = dcell_ref[cells, lanes] + dvalues[FINE_KEYS:]
            grads = mean_scores(grads, grad_means_ref, FINE_LEVELS)
            add_rows(acc_ref, windows, lanes, dot_nn(grads, head_stack(query, mask)))
            dq_ref[0, rows, lanes] = (head_pick(dot_tn(grads, keys)) * 0.125).astype(BF16)
        return carry

    lax.fori_loop(0, FINE_TILES, fine_tile, 0, unroll=4)

    def coarse_tile(tile, carry):
        windows = coarse_windows(tile)
        bias = tile_bias(kid_ref, qidc_ref, 8 * tile, windows, COARSE_LEVELS, coarse_ref[tile])
        rows = at(TILE * tile, TILE)
        for quad in range(2):
            lanes = pl.ds(QL * quad, QL)
            vlanes = pl.ds(512 + QL * quad, QL)
            row = pl.ds(2 * tile + quad, 1)
            query = q3_ref[0, rows, lanes]
            queries = dot_nn(means_ref[...], query).astype(BF16)
            keys = gather_rows(kvp_ref, windows, lanes)
            lse = lsec_ref[0, row, :]
            share = jnp.exp(tile_scores(keys, queries, mask, COARSE_LEVELS) + bias - lse)
            high, middle, low = three_terms(delta_ref[row, :])
            terms = jnp.concatenate([high, middle, low, low, low, low, low, low], axis=0)
            terms = dot_nn(terms, spread_t_ref[...])
            delta = terms[0:1] + terms[1:2] + terms[2:3]
            values = gather_rows(kvp_ref, windows, vlanes)
            dout = head_stack(dcell_ref[rows, lanes].astype(BF16), mask)
            grads = (share * (dot_nt(values, dout) - delta)).astype(BF16)
            add_rows(acc_ref, windows, vlanes, dot_nn(share.astype(BF16), dout))
            grads = mean_scores(grads, grad_means_ref, COARSE_LEVELS)
            add_rows(acc_ref, windows, lanes, dot_nn(grads, head_stack(query, mask)))
            dq3_ref[0, rows, lanes] = (head_pick(dot_tn(grads, keys)) * 0.125).astype(BF16)
        return carry

    lax.fori_loop(0, COARSE_TILES, coarse_tile, 0, unroll=2)

    scale = jnp.where(lax.broadcasted_iota(jnp.int32, (1, acc_ref.shape[1]), 1) < 512, 0.125, 1.0)

    def low(start, count):
        return (acc_ref[pl.ds(start, count), :] * scale).astype(BF16)

    for level in range(LEVELS - 1):
        base = POFF[level]
        count = CELLS[level]
        edge = pl.ds(HALO * level, HALO)
        left_ref[0, edge, :] = low(base, HALO)
        dkv_ref[0, pl.ds(OFF[level], count), :] = low(base + HALO, count)
        right_ref[0, edge, :] = low(base + HALO + count, HALO)
    dkv_ref[0, pl.ds(OFF[7], 16), :] = jnp.zeros((16, acc_ref.shape[1]), BF16)
    piece = piece_ref[0]
    blank = jnp.zeros((PIECE7, acc_ref.shape[1]), F32)

    def high(index):
        rows = pl.ds(pl.multiple_of(POFF[7] + PIECE7 * index, PIECE7), PIECE7)
        return jnp.concatenate([acc_ref[rows, :] * scale, blank], axis=0).astype(BF16)

    ends = high(3 - piece)
    left_ref[0, pl.ds(EDGE, 16), :] = ends
    right_ref[0, pl.ds(EDGE, 16), :] = ends
    top_ref[0] = high((piece + 2) % 4)


def attend_back(piece, q, q3, kvp, stats, dout, ids, const):
    micro, _, width = q.shape
    lse, lsec, lsex, oc = stats
    shape = jax.ShapeDtypeStruct
    return pl.pallas_call(
        attend_back_kernel,
        grid=(micro,),
        in_specs=[
            pl.BlockSpec(memory_space=pltpu.SMEM),
            per_micro((ROWS, width)),
            per_micro((ROWS // 8, width)),
            per_micro((PADDED, 2 * width)),
            per_micro((2 * FINE_TILES, QL)),
            per_micro((2 * COARSE_TILES, QL)),
            per_micro((2 * COARSE_TILES, 8 * QL)),
            per_micro((ROWS // 8, width)),
            per_micro((ROWS, width)),
            per_micro((PADDED, 128)),
            per_micro((8 * FINE_TILES, QL)),
            per_micro((8 * COARSE_TILES, QL)),
            whole((FINE_KEYS, QL)),
            whole((COARSE_TILES, COARSE_KEYS, QL)),
            whole((5 * TILE, TILE)),
            whole((4, QL, QL)),
            whole((QL, QL)),
            whole((8 * QL, QL)),
        ],
        out_specs=[
            per_micro((ROWS, width)),
            per_micro((ROWS // 8, width)),
            per_micro((2 * ROWS, 2 * width)),
            per_micro((EDGES, 2 * width)),
            per_micro((EDGES, 2 * width)),
            per_micro((16, 2 * width)),
        ],
        out_shape=[
            shape((micro, ROWS, width), BF16),
            shape((micro, ROWS // 8, width), BF16),
            shape((micro, 2 * ROWS, 2 * width), BF16),
            shape((micro, EDGES, 2 * width), BF16),
            shape((micro, EDGES, 2 * width), BF16),
            shape((micro, 16, 2 * width), BF16),
        ],
        scratch_shapes=[
            pltpu.VMEM((PADDED, 2 * width), F32),
            pltpu.VMEM((ROWS // 8, width), F32),
            pltpu.VMEM((2 * COARSE_TILES, 8 * QL), F32),
        ],
        compiler_params=params(1),
        name="attend_back",
    )(
        piece.reshape(1),
        q,
        q3,
        kvp,
        lse,
        lsec,
        lsex,
        oc,
        dout,
        ids["key"],
        ids["fine"],
        ids["coarse"],
        const["fine"],
        const["coarse"],
        const["query_means"],
        const["grad_means"],
        const["head_mask"],
        const["spread_t"],
    )


MID_ROWS = 512
FF_CHUNK = 512
ROOT = math.sqrt(2.0 / math.pi)


def middle_kernel(
    tok_ref,
    cot_ref,
    mixed_ref,
    gain_ref,
    off_ref,
    wo_ref,
    wi_ref,
    bi_ref,
    wd_ref,
    bd_ref,
    out_ref,
    dmid_ref,
    dmix_ref,
    gwo_ref,
    gwi_ref,
    gwd_ref,
    gbi_ref,
    gsmall_ref,
    acc_o,
    acc_i,
    acc_d,
):
    step = pl.program_id(0)

    @pl.when(step == 0)
    def _():
        acc_o[...] = jnp.zeros(acc_o.shape, F32)
        acc_i[...] = jnp.zeros(acc_i.shape, F32)
        acc_d[...] = jnp.zeros(acc_d.shape, F32)
        gbi_ref[...] = jnp.zeros(gbi_ref.shape, F32)
        gsmall_ref[...] = jnp.zeros(gsmall_ref.shape, F32)

    cot = cot_ref[...]
    top = cot.astype(BF16)
    mixed = mixed_ref[...]
    middle = tok_ref[...] + dot_nn(mixed, wo_ref[...])
    unit, rate = normalised(middle)
    second = (unit * gain_ref[...] + off_ref[...]).astype(BF16)
    gsmall_ref[0:8, :] = gsmall_ref[0:8, :] + fold_rows(top.astype(F32))
    result = middle + bd_ref[...]
    back = jnp.zeros(cot.shape, F32)
    for part in range(wi_ref.shape[0]):
        cols = pl.ds(FF_CHUNK * part, FF_CHUNK)
        wi = wi_ref[part]
        wd = wd_ref[part]
        pre = dot_nn(second, wi) + bi_ref[:, cols]
        square = pre * pre
        tanh = jnp.tanh(ROOT * pre * (1.0 + 0.044715 * square))
        half = 0.5 * (1.0 + tanh)
        activ = (pre * half).astype(BF16)
        slope = half + (0.5 * ROOT) * pre * (1.0 - tanh * tanh) * (1.0 + 3 * 0.044715 * square)
        result = result + dot_nn(activ, wd)
        grad = dot_nt(top, wd) * slope
        grad_low = grad.astype(BF16)
        gbi_ref[:, cols] = gbi_ref[:, cols] + fold_rows(grad_low.astype(F32))
        back = back + dot_nt(grad_low, wi)
        acc_d[part] = acc_d[part] + dot_tn(activ, top)
        acc_i[part] = acc_i[part] + dot_tn(second, grad_low)
    out_ref[...] = result
    gsmall_ref[8:16, :] = gsmall_ref[8:16, :] + fold_rows(back * unit)
    gsmall_ref[16:24, :] = gsmall_ref[16:24, :] + fold_rows(back)
    dmid = cot + norm_back(back * gain_ref[...], unit, rate)
    dmid_ref[...] = dmid
    branch = dmid.astype(BF16)
    dmix_ref[...] = dot_nt(branch, wo_ref[...]).astype(BF16)
    acc_o[...] = acc_o[...] + dot_tn(mixed, branch)

    @pl.when(step == pl.num_programs(0) - 1)
    def _():
        gwo_ref[...] = acc_o[...].astype(BF16)
        gwi_ref[...] = acc_i[...].astype(BF16)
        gwd_ref[...] = acc_d[...].astype(BF16)


def middle_part(tokens, cot, mixed, gain, offset, wo, wi, bi, wd, bd):
    rows, width = tokens.shape
    parts = wi.shape[0]
    hidden = parts * FF_CHUNK
    shape = jax.ShapeDtypeStruct
    tiled = pl.BlockSpec((MID_ROWS, width), lambda r: (r, 0))
    return pl.pallas_call(
        middle_kernel,
        grid=(rows // MID_ROWS,),
        in_specs=[
            tiled,
            tiled,
            tiled,
            whole((1, width)),
            whole((1, width)),
            whole((width, width)),
            whole((parts, width, FF_CHUNK)),
            whole((1, hidden)),
            whole((parts, FF_CHUNK, width)),
            whole((1, width)),
        ],
        out_specs=[
            tiled,
            tiled,
            tiled,
            whole((width, width)),
            whole((parts, width, FF_CHUNK)),
            whole((parts, FF_CHUNK, width)),
            whole((8, hidden)),
            whole((24, width)),
        ],
        out_shape=[
            shape((rows, width), F32),
            shape((rows, width), F32),
            shape((rows, width), BF16),
            shape((width, width), BF16),
            shape((parts, width, FF_CHUNK), BF16),
            shape((parts, FF_CHUNK, width), BF16),
            shape((8, hidden), F32),
            shape((24, width), F32),
        ],
        scratch_shapes=[
            pltpu.VMEM((width, width), F32),
            pltpu.VMEM((parts, width, FF_CHUNK), F32),
            pltpu.VMEM((parts, FF_CHUNK, width), F32),
        ],
        compiler_params=params(1),
        name="middle",
    )(tokens, cot, mixed, gain, offset, wo, wi, bi, wd, bd)


def finish_kernel(
    tok_ref,
    dmid_ref,
    dq_ref,
    dq3_ref,
    dkv_ref,
    left_ref,
    right_ref,
    top_ref,
    gain_ref,
    off_ref,
    w_ref,
    low_ref,
    high_ref,
    grad_ref,
    gw_ref,
    gsmall_ref,
    cells_ref,
    acc_ref,
):
    step = pl.program_id(0)

    @pl.when(step == 0)
    def _():
        acc_ref[...] = jnp.zeros(acc_ref.shape, F32)
        gsmall_ref[...] = jnp.zeros(gsmall_ref.shape, F32)

    cells_ref[...] = dkv_ref[0]

    def add(start, value):
        rows = pl.ds(start, HALO)
        cells_ref[rows, :] = (cells_ref[rows, :].astype(F32) + value.astype(F32)).astype(BF16)

    for level in range(LEVELS - 1):
        edge = pl.ds(HALO * level, HALO)
        add(OFF[level], left_ref[0, edge, :])
        add(OFF[level] + CELLS[level] - HALO, right_ref[0, edge, :])
    add(OFF[7], top_ref[0])

    for chunk in range(ROWS // 256):
        rows = pl.ds(256 * chunk, 256)
        unit, rate = normalised(tok_ref[0, rows, :])
        normed = (unit * gain_ref[...] + off_ref[...]).astype(BF16)
        cells = jnp.concatenate(
            [
                cells_ref[pl.ds(OFF[level] + (256 >> level) * chunk, 256 >> level), :]
                for level in range(1, 5)
            ],
            axis=0,
        )
        dkv = (
            cells_ref[rows, :].astype(F32)
            + dot_nn(low_ref[...], cells)
            + dot_nn(high_ref[rows, :], cells_ref[pl.ds(OFF[5], 64), :])
        ).astype(BF16)
        dq = (
            dq_ref[0, rows, :].astype(F32)
            + dot_nn(low_ref[:, 192:224], dq3_ref[0, pl.ds(32 * chunk, 32), :])
        ).astype(BF16)
        parts = [dq, dkv[:, 0:512], dkv[:, 512:1024]]
        back = jnp.zeros(unit.shape, F32)
        for index in range(3):
            back = back + dot_nt(parts[index], w_ref[index])
            acc_ref[index] = acc_ref[index] + dot_tn(normed, parts[index])
        gsmall_ref[0:8, :] = gsmall_ref[0:8, :] + fold_rows(back * unit)
        gsmall_ref[8:16, :] = gsmall_ref[8:16, :] + fold_rows(back)
        grad_ref[0, rows, :] = dmid_ref[0, rows, :] + norm_back(back * gain_ref[...], unit, rate)

    @pl.when(step == pl.num_programs(0) - 1)
    def _():
        gw_ref[...] = acc_ref[...].astype(BF16)


def finish(tokens, dmid, dq, dq3, dkv, left, right, top, gain, offset, weight, const):
    micro, _, width = tokens.shape
    shape = jax.ShapeDtypeStruct
    return pl.pallas_call(
        finish_kernel,
        grid=(micro,),
        in_specs=[
            per_micro((ROWS, width)),
            per_micro((ROWS, width)),
            per_micro((ROWS, width)),
            per_micro((ROWS // 8, width)),
            per_micro((2 * ROWS, 2 * width)),
            per_micro((EDGE, 2 * width)),
            per_micro((EDGE, 2 * width)),
            per_micro((16, 2 * width)),
            whole((1, width)),
            whole((1, width)),
            whole((3, width, width)),
            whole((256, 240)),
            whole((ROWS, 64)),
        ],
        out_specs=[
            per_micro((ROWS, width)),
            whole((3, width, width)),
            whole((16, width)),
        ],
        out_shape=[
            shape((micro, ROWS, width), F32),
            shape((3, width, width), BF16),
            shape((16, width), F32),
        ],
        scratch_shapes=[
            pltpu.VMEM((2 * ROWS, 2 * width), BF16),
            pltpu.VMEM((3, width, width), F32),
        ],
        compiler_params=params(1),
        name="finish",
    )(
        tokens,
        dmid,
        dq,
        dq3,
        dkv,
        left,
        right,
        top,
        gain,
        offset,
        weight,
        const["means_low_t"],
        const["means_high_t"],
    )


def cell_documents(segments, piece):
    micro, length = segments.shape
    keys = []
    fine = []
    coarse = []
    for level in range(LEVELS):
        cell = 1 << level
        grouped = segments.reshape(micro, length // cell, cell)
        lowest = grouped[:, :, 0]
        highest = grouped[:, :, cell - 1]
        same = lowest == highest
        key = jnp.where(same, lowest, -2)
        query = jnp.where(same, lowest, -1)
        own = lax.dynamic_slice_in_dim(query, piece * CELLS[level], CELLS[level], axis=1)
        if level < LEVELS - 1:
            padded = jnp.pad(key, ((0, 0), (HALO, HALO)), constant_values=-3)
            keys.append(
                lax.dynamic_slice_in_dim(
                    padded, piece * CELLS[level], CELLS[level] + 2 * HALO, axis=1
                )
            )
        else:
            owner = jnp.arange(key.shape[1]) // PIECE7
            counted = (jnp.abs(owner // 2 - piece // 2) == 1) & (jnp.abs(owner - piece) >= 2)
            keys.append(jnp.where(counted[None], key, -3))
        if level < FINE:
            fine.append(jnp.repeat(own, cell, axis=1).reshape(micro, FINE_TILES, 1, TILE))
        else:
            coarse.append(jnp.repeat(own, cell // 8, axis=1).reshape(micro, COARSE_TILES, 1, TILE))

    def rows(parts):
        value = jnp.concatenate(parts, axis=2)
        value = jnp.pad(value, ((0, 0), (0, 0), (0, 8 - len(parts)), (0, 0)))
        return jnp.tile(value, (1, 1, 1, QUAD)).reshape(micro, -1, QL)

    key = jnp.concatenate(keys, axis=1)
    return dict(
        key=jnp.broadcast_to(key[:, :, None], key.shape + (128,)),
        fine=rows(fine),
        coarse=rows(coarse),
    )


def same_core(chips):
    return [[2 * chip + core for chip in range(chips)] for core in range(2)]


def core_swap(value, chips):
    pairs = [(place, place ^ 1) for place in range(2 * chips)]
    return lax.ppermute(value, "dp", pairs)


def chip_exchange(value, chips):
    return lax.all_to_all(value, "dp", 0, 0, axis_index_groups=same_core(chips), tiled=True)


def gather(value, core, chips):
    mine = chip_exchange(jnp.broadcast_to(value[None], (chips,) + value.shape), chips)
    other = core_swap(mine, chips)
    first = jnp.where(core == 0, mine, other)
    second = jnp.where(core == 0, other, mine)
    return jnp.stack([first, second], axis=1).reshape((2 * chips,) + value.shape)


def reduce_shards(value, core, chips, swap):
    value = value.reshape((chips, 2) + value.shape[1:])
    pick = lambda index: lax.dynamic_index_in_dim(value, index, axis=1, keepdims=False)
    add = lambda left, right: left.astype(F32) + right.astype(F32)
    pair = add(pick(core), core_swap(pick(1 - core), chips)).astype(BF16)
    total = jnp.sum(chip_exchange(pair, chips).astype(F32), axis=0).astype(BF16)
    total = add(total, swap(total, 1)).astype(BF16)
    return add(total, swap(total, 3))


def body(
    tokens,
    segment_ids,
    norm_gains,
    norm_biases,
    qkv_weight,
    out_weight,
    in_weight,
    in_bias,
    down_weight,
    down_bias,
    cotangent,
):
    micro, _, row_count, width = tokens.shape
    pieces = lax.axis_size("sp")
    piece = lax.axis_index("sp")
    assert row_count == ROWS and pieces == 4
    const = constants()
    tokens = tokens[:, 0]
    cotangent = cotangent[:, 0]

    dp = lax.axis_size("dp")
    place = lax.axis_index("dp")
    core = place % 2
    chips = dp // 2
    shard = width // dp
    hidden = in_weight.shape[1]
    parts = hidden // FF_CHUNK

    small = [norm_gains.reshape(-1), norm_biases.reshape(-1), in_bias, down_bias]
    sizes = [value.size for value in small]
    small = jnp.concatenate(small)
    lines = -(-small.size // width)
    small = jnp.pad(small, (0, lines * width - small.size)).reshape(lines, width)
    first = gather(jnp.concatenate([qkv_weight.reshape(3 * shard, width), small]), core, chips)
    second = gather(
        jnp.concatenate(
            [
                out_weight,
                in_weight.reshape(shard, parts, FF_CHUNK).swapaxes(0, 1).reshape(-1, width),
                down_weight,
            ]
        ),
        core,
        chips,
    )
    wqkv = first[:, : 3 * shard].reshape(dp, 3, shard, width).swapaxes(0, 1)
    wqkv = wqkv.reshape(3, width, width)
    small = first[:, 3 * shard :].reshape(dp, lines * width)[:, : sum(sizes)].astype(F32)
    gains, offsets, bi, bd = jnp.split(small, np.cumsum(sizes)[:-1].tolist(), axis=1)
    gains = gains.reshape(dp, 2, shard).swapaxes(0, 1).reshape(2, width)
    offsets = offsets.reshape(dp, 2, shard).swapaxes(0, 1).reshape(2, width)
    wo = second[:, :shard].reshape(width, width)
    wi = second[:, shard : shard * (1 + parts)].reshape(dp, parts, shard, width)
    wi = wi.swapaxes(0, 1).reshape(parts, width, FF_CHUNK)
    wd = second[:, shard * (1 + parts) :].reshape(parts, FF_CHUNK, width)

    ids = cell_documents(segment_ids[:, 0], piece)

    swap = lambda value, bits: lax.ppermute(value, "sp", [(p, p ^ bits) for p in range(pieces)])
    even = piece % 2 == 0

    q, q3, kv, to_left, to_right = project(tokens, gains[0:1], offsets[0:1], wqkv, const)
    near = swap(jnp.where(even, to_right, to_left), 1)
    far = swap(jnp.where(even, to_left, to_right), 3)
    from_left = jnp.where(even, far, near)[:, :EDGE]
    from_right = jnp.where(even, near, far)[:, :EDGE]
    across = swap(kv[:, OFF[7] : OFF[7] + PIECE7], 2)
    owner = jnp.arange(pieces)[None, :, None, None]
    tops = jnp.where(
        owner == piece ^ 2,
        across[:, None],
        jnp.where(owner == piece ^ 3, far[:, None, EDGE : EDGE + PIECE7], jnp.zeros((), BF16)),
    ).reshape(micro, pieces * PIECE7, 2 * width)

    mixed, kvp, *stats = attend(q, q3, kv, from_left, from_right, tops, ids, const)

    flat = lambda value: value.reshape(micro * ROWS, width)
    outputs, dmid, dmix, gwo, gwi, gwd, gbi, gtwo = middle_part(
        flat(tokens),
        flat(cotangent),
        flat(mixed),
        gains[1:2],
        offsets[1:2],
        wo,
        wi,
        bi.reshape(1, hidden),
        wd,
        bd.reshape(1, width),
    )
    split = lambda value: value.reshape(micro, ROWS, width)

    dq, dq3, dkv, dleft, dright, dtop = attend_back(
        piece, q, q3, kvp, stats, split(dmix), ids, const
    )
    near = swap(jnp.where(even, dright, dleft), 1)
    far = swap(jnp.where(even, dleft, dright), 3)
    dfrom_left = jnp.where(even, far, near)[:, :EDGE]
    dfrom_right = jnp.where(even, near, far)[:, :EDGE]
    dtop_own = swap(dtop, 2).astype(F32) + far[:, EDGE:].astype(F32)
    dtop_own = dtop_own.astype(BF16)

    rest = reduce_shards(
        jnp.concatenate(
            [
                gwo.reshape(dp, shard, width),
                gwi.reshape(parts, dp, shard, width).swapaxes(0, 1).reshape(dp, parts * shard, width),
                gwd.reshape(dp, parts * shard, width),
            ],
            axis=1,
        ),
        core,
        chips,
        swap,
    )

    input_grad, gwqkv, gone = finish(
        tokens,
        split(dmid),
        dq,
        dq3,
        dkv,
        dfrom_left,
        dfrom_right,
        dtop_own,
        gains[0:1],
        offsets[0:1],
        wqkv,
        const,
    )

    fold = lambda value: jnp.sum(value.reshape(-1, 8, value.shape[1]), axis=1)
    one, two, bias = fold(gone), fold(gtwo), fold(gbi)
    small = jnp.concatenate([one[0:1], two[1:2], one[1:2], two[2:3], two[0:1], bias.reshape(-1, width)])
    small = jnp.pad(small, ((0, 16 - small.shape[0]), (0, 0))).astype(BF16)
    total = reduce_shards(
        jnp.concatenate(
            [
                gwqkv.reshape(3, dp, shard, width).swapaxes(0, 1).reshape(dp, 3 * shard, width),
                jnp.broadcast_to(small[None], (dp,) + small.shape),
            ],
            axis=1,
        ),
        core,
        chips,
        swap,
    )
    small = total[3 * shard :]
    own = lambda value, size: lax.dynamic_slice_in_dim(value, place * size, size, axis=-1)
    gin = rest[shard : shard * (1 + parts)].reshape(parts, shard, FF_CHUNK).swapaxes(0, 1)

    return (
        outputs.reshape(micro, 1, ROWS, width),
        input_grad[:, None],
        own(small[0:2], shard),
        own(small[2:4], shard),
        total[: 3 * shard].reshape(3, shard, width),
        rest[:shard],
        gin.reshape(shard, hidden),
        own(small[5 : 5 + parts].reshape(hidden), hidden // dp),
        rest[shard * (1 + parts) :],
        own(small[4], shard),
    )


def solution(mesh):
    in_specs = (
        P(None, "dp", "sp", None),
        P(None, "dp", None),
        P(None, "dp"),
        P(None, "dp"),
        P(None, "dp", None),
        P("dp", None),
        P("dp", None),
        P("dp"),
        P("dp", None),
        P("dp"),
        P(None, "dp", "sp", None),
    )
    out_specs = (
        P(None, "dp", "sp", None),
        P(None, "dp", "sp", None),
        P(None, "dp"),
        P(None, "dp"),
        P(None, "dp", None),
        P("dp", None),
        P("dp", None),
        P("dp"),
        P("dp", None),
        P("dp"),
    )
    return jax.shard_map(body, mesh=mesh, in_specs=in_specs, out_specs=out_specs, check_vma=False)
```

```python
import math

import jax
import jax.numpy as jnp
import numpy as np
from jax import lax
from jax.experimental import pallas as pl
from jax.experimental.pallas import tpu as pltpu
from jax.sharding import PartitionSpec as P

HEADS = 8
HEAD_DIM = 64
BLOCK = 16
LEVELS = 8
HALO = 16
TILE = 64
QUAD = 4
QL = QUAD * HEAD_DIM
NEG = -1e30
FINE = 3
ROWS = 1024
EDGE = 112
EDGES = 128
GROUP = 8
GROUP_BACK = 4
F32 = jnp.float32
BF16 = jnp.bfloat16

CELLS = [ROWS >> level for level in range(LEVELS)]
OFF = [2 * ROWS - (2 * ROWS >> level) for level in range(LEVELS)]
POFF = []
_at = 0
for _level in range(LEVELS - 1):
    POFF.append(_at)
    _at += CELLS[_level] + 2 * HALO
POFF.append(_at)
PIECE7 = CELLS[LEVELS - 1]
PADDED = _at + 4 * PIECE7
FINE_TILES = ROWS // TILE
COARSE_TILES = ROWS // 8 // TILE
FINE_KEYS = 192
COARSE_KEYS = 256
LN_EPS = 1e-05
VMEM_LIMIT = 62 * 1024 * 1024


def _counts(level, query, key):
    query = query[None, :]
    key = key[:, None]
    near = np.abs(query // 16 - key // 16)
    if level == 0:
        return near <= 1
    return (near == 1) & (np.abs(query // 8 - key // 8) >= 2)


def _bias(parts):
    rows = []
    for level, allowed in parts:
        rows.append(np.where(allowed, np.float32(level * math.log(2.0)), np.float32(NEG)))
    block = np.concatenate(rows, axis=0).astype(np.float32)
    return np.tile(block, (1, QUAD))


def _two_blocks():
    return np.concatenate([np.arange(16) - 16, np.arange(16) + 16])


def fine_bias():
    token = np.arange(TILE)
    return _bias(
        [
            (0, _counts(0, token, np.arange(96) - 16)),
            (1, _counts(1, token // 2, np.arange(64) - 16)),
            (2, _counts(2, token // 4, _two_blocks())),
        ]
    )


def coarse_bias():
    cell = np.arange(TILE)
    out = []
    for tile in range(COARSE_TILES):
        out.append(
            _bias(
                [
                    (3, _counts(3, cell, np.arange(96) - 16)),
                    (4, _counts(4, cell // 2, np.arange(64) - 16)),
                    (5, _counts(5, cell // 4, _two_blocks())),
                    (6, _counts(6, 8 * tile + cell // 8, _two_blocks())),
                    (7, np.ones((4 * PIECE7, TILE), bool)),
                ]
            )
        )
    return np.stack(out)


STEP = [0, 1, 2, 0, 1, 2, 3, 4]


def mean_rows(cell, count):
    return (np.arange(count)[None, :] // cell == np.arange(count // cell)[:, None]).astype(
        np.float32
    ) / cell


def spread_matrix():
    out = np.zeros((QUAD, TILE, 8, QUAD, TILE), np.float32)
    for part in range(8):
        for token in range(TILE):
            for head in range(QUAD):
                out[head, 8 * part + token // 8, part, head, token] = 1.0
    return out.reshape(QL, 8 * QL)


def constants():
    head_mask = np.kron(np.eye(QUAD), np.ones((TILE, HEAD_DIM)))
    low = [mean_rows(1 << level, 256) for level in range(1, 5)]
    high = [mean_rows(1 << level, ROWS) for level in range(5, 8)] + [np.zeros((8, ROWS))]
    key_low = [rows * 0.5 ** STEP[level] for level, rows in zip(range(1, 5), low)]
    key_high = [rows * 0.5**step for step, rows in zip(STEP[5:] + [0], high)]
    as_low = lambda value: jnp.asarray(value.astype(np.float32)).astype(BF16)
    low, high = np.concatenate(low), np.concatenate(high)
    return dict(
        fine=jnp.asarray(fine_bias()),
        coarse=jnp.asarray(coarse_bias()),
        head_mask=as_low(head_mask),
        low=as_low(np.stack([np.concatenate(key_low), low])),
        high=as_low(np.stack([np.concatenate(key_high), high])),
        low_t=as_low(low.T),
        high_t=as_low(high.T),
        spread=as_low(spread_matrix()),
        spread_t=as_low(spread_matrix().T),
    )


def dot_nn(left, right):
    return jnp.dot(left, right, preferred_element_type=F32)


def dot_nt(left, right):
    return lax.dot_general(left, right, (((1,), (1,)), ((), ())), preferred_element_type=F32)


def dot_tn(left, right):
    return lax.dot_general(left, right, (((0,), (0,)), ((), ())), preferred_element_type=F32)


def at(start, size):
    return pl.ds(pl.multiple_of(start, 16), size)


def whole(shape):
    zeros = (0,) * len(shape)
    return pl.BlockSpec(shape, lambda *_: zeros)


def one_of(shape, micro):
    zeros = (0,) * len(shape)
    return pl.BlockSpec((1,) + shape, lambda *_: (micro,) + zeros)


def each_of(shape):
    zeros = (0,) * len(shape)
    return pl.BlockSpec((1,) + shape, lambda step: (step,) + zeros)


SCALAR = pl.BlockSpec(memory_space=pltpu.SMEM)
KEPT = pl.BlockSpec(memory_space=pl.ANY)


def timing(micros):
    return pl.CostEstimate(
        flops=int(micros * 4e8), bytes_accessed=int(micros * 3e6), transcendentals=0
    )


def params():
    return pltpu.CompilerParams(
        dimension_semantics=("arbitrary",), vmem_limit_bytes=VMEM_LIMIT
    )


def normalised(rows):
    center = rows - jnp.mean(rows, axis=-1, keepdims=True)
    spread = jnp.mean(center * center, axis=-1, keepdims=True)
    rate = lax.rsqrt(spread + LN_EPS)
    return center * rate, rate


def norm_back(grad, unit, rate):
    mean_grad = jnp.mean(grad, axis=-1, keepdims=True)
    mean_dot = jnp.mean(grad * unit, axis=-1, keepdims=True)
    return rate * (grad - mean_grad - unit * mean_dot)


def fold_rows(value):
    return jnp.sum(value.reshape(-1, 8, value.shape[-1]), axis=0)


def take_weight(target, index, mine, other, core, start):
    chips, shard = mine.shape[0], target.shape[2]
    for chip in range(chips):
        target[index, 2 * chip + core] = mine[chip, pl.ds(start, shard), :]
        target[index, 2 * chip + 1 - core] = other[chip, pl.ds(start, shard), :]


def weight_of(ref, index):
    return ref[index].reshape(ref.shape[1] * ref.shape[2], ref.shape[3])


def project_kernel(
    where_ref,
    tok_ref,
    vec_ref,
    mine_ref,
    other_ref,
    low_ref,
    high_ref,
    q_ref,
    q3_ref,
    kv_ref,
    near_ref,
    far_ref,
    top_ref,
    w_ref,
    norm_ref,
):
    piece, core = where_ref[0], where_ref[1]
    shard = w_ref.shape[2]
    for index in range(3):
        take_weight(w_ref, index, mine_ref, other_ref, core, shard * index)
    for chunk in range(ROWS // 256):
        rows = pl.ds(256 * chunk, 256)
        unit, _ = normalised(tok_ref[0, rows, :])
        norm_ref[rows, :] = (unit * vec_ref[0:1] + vec_ref[2:3]).astype(BF16)
    for half in range(2):
        rows = pl.ds(512 * half, 512)
        for index in range(3):
            value = dot_nn(norm_ref[rows, :], weight_of(w_ref, index)).astype(BF16)
            if index == 0:
                q_ref[rows, :] = value
            else:
                kv_ref[rows, pl.ds(512 * (index - 1), 512)] = value
    for chunk in range(ROWS // 256):
        rows = pl.ds(256 * chunk, 256)
        q3_ref[pl.ds(32 * chunk, 32), :] = dot_nn(low_ref[1, 192:224, :], q_ref[rows, :]).astype(
            BF16
        )
        for part in range(2):
            lanes = pl.ds(512 * part, 512)
            cells = dot_nn(low_ref[part], kv_ref[rows, lanes]).astype(BF16)
            start = 0
            for level in range(1, 5):
                count = 256 >> level
                kv_ref[pl.ds(OFF[level] + count * chunk, count), lanes] = cells[
                    start : start + count
                ]
                start += count
    for part in range(2):
        lanes = pl.ds(512 * part, 512)
        kv_ref[pl.ds(OFF[5], 64), lanes] = dot_nn(high_ref[part], kv_ref[pl.ds(0, ROWS), lanes]).astype(
            BF16
        )

    def edges(left_ref, right_ref):
        for level in range(LEVELS - 1):
            edge = pl.ds(HALO * level, HALO)
            left_ref[edge, :] = kv_ref[pl.ds(OFF[level], HALO), :]
            right_ref[edge, :] = kv_ref[pl.ds(OFF[level] + CELLS[level] - HALO, HALO), :]

    pl.when(piece % 2 == 0)(lambda: edges(far_ref, near_ref))
    pl.when(piece % 2 == 1)(lambda: edges(near_ref, far_ref))
    high = kv_ref[pl.ds(OFF[7], 16), :]
    near_ref[pl.ds(EDGE, 16), :] = high
    far_ref[pl.ds(EDGE, 16), :] = high
    top_ref[...] = high


def project(micro, where, tokens, vec, mine, other, const):
    width = tokens.shape[2]
    shape = jax.ShapeDtypeStruct
    shard = width // (2 * mine.shape[0])
    outs = [
        shape((ROWS, width), BF16),
        shape((ROWS // 8, width), BF16),
        shape((2 * ROWS, 2 * width), BF16),
        shape((EDGES, 2 * width), BF16),
        shape((EDGES, 2 * width), BF16),
        shape((16, 2 * width), BF16),
    ]
    return pl.pallas_call(
        project_kernel,
        grid=(1,),
        in_specs=[
            SCALAR,
            one_of((ROWS, width), micro),
            whole(vec.shape),
            whole(mine.shape),
            whole(other.shape),
            whole((2, 240, 256)),
            whole((2, 64, ROWS)),
        ],
        out_specs=[whole(out.shape) for out in outs],
        out_shape=outs,
        scratch_shapes=[
            pltpu.VMEM((3, width // shard, shard, width), BF16),
            pltpu.VMEM((ROWS, width), BF16),
        ],
        compiler_params=params(),
        cost_estimate=timing(6),
        name="project",
    )(where, tokens, vec, mine, other, const["low"], const["high"])


def fine_windows(tile):
    return [
        (POFF[0] + 64 * tile, 96),
        (POFF[1] + 32 * tile, 64),
        (POFF[2] + 16 * tile, 16),
        (POFF[2] + 16 * tile + 32, 16),
    ]


def coarse_windows(tile):
    return [
        (POFF[3] + 64 * tile, 96),
        (POFF[4] + 32 * tile, 64),
        (POFF[5] + 16 * tile, 16),
        (POFF[5] + 16 * tile + 32, 16),
        (POFF[6], 16),
        (POFF[6] + 32, 16),
        (POFF[7], 32),
    ]


FINE_LEVELS = [96, 64, 32]
COARSE_LEVELS = [96, 64, 32, 32, 32]


def gather_rows(ref, windows, lanes):
    return jnp.concatenate([ref[at(start, size), lanes] for start, size in windows], axis=0)


def tile_bias(kid_ref, qid_ref, row, windows, levels, bias):
    keys = jnp.concatenate([kid_ref[0, at(start, size), :] for start, size in windows], axis=0)
    keys = jnp.concatenate([keys, keys], axis=1)
    out = []
    start = 0
    for index, count in enumerate(levels):
        part = slice(start, start + count)
        owner = qid_ref[0, pl.ds(row + index, 1), :]
        out.append(jnp.where(keys[part] == owner, bias[part], NEG))
        start += count
    return jnp.concatenate(out, axis=0)


def lane_sums(value, steps):
    halves = []
    for half in range(2):
        part = value[:, 128 * half : 128 * (half + 1)]
        lane = lax.broadcasted_iota(jnp.int32, part.shape, 1)
        for step in range(steps):
            size = 1 << step
            first = (lane & size) == 0
            part = part + jnp.where(
                first, pltpu.roll(part, 128 - size, 1), pltpu.roll(part, size, 1)
            )
        halves.append(part)
    return jnp.concatenate(halves, axis=1)


def level_sums(value, levels):
    out = [value[0 : levels[0]]]
    start = levels[0]
    for index, count in enumerate(levels[1:]):
        out.append(lane_sums(value[start : start + count], index + 1))
        start += count
    return jnp.concatenate(out, axis=0)


def head_stack(value, mask):
    return jnp.concatenate([value] * QUAD, axis=0) * mask


def head_pick(stacked):
    lane = lax.broadcasted_iota(jnp.int32, (TILE, QL), 1) // HEAD_DIM
    out = stacked[0:TILE]
    for head in range(1, QUAD):
        out = jnp.where(lane == head, stacked[TILE * head : TILE * (head + 1)], out)
    return out


def three_terms(row):
    high = row.astype(BF16)
    rest = row - high.astype(F32)
    middle = rest.astype(BF16)
    low = (rest - middle.astype(F32)).astype(BF16)
    return high, middle, low


def own_cell(tile):
    cell = lax.broadcasted_iota(jnp.int32, (16, QL), 0)
    token = lax.broadcasted_iota(jnp.int32, (16, QL), 1) % TILE
    return cell == 8 * (tile % 2) + token // 8


def attend_kernel(
    where_ref,
    q_ref,
    q3_ref,
    kv_ref,
    near_ref,
    far_ref,
    across_ref,
    kid_ref,
    qidf_ref,
    qidc_ref,
    fine_ref,
    coarse_ref,
    mask_ref,
    spread_ref,
    mixed_ref,
    kvp_ref,
    lse_ref,
    lsec_ref,
    lsex_ref,
    oc_ref,
):
    piece = where_ref[0]

    def edges(left_ref, right_ref):
        for level in range(LEVELS - 1):
            base = POFF[level]
            edge = pl.ds(HALO * level, HALO)
            kvp_ref[pl.ds(base, HALO), :] = left_ref[edge, :]
            kvp_ref[pl.ds(base + HALO + CELLS[level], HALO), :] = right_ref[edge, :]

    pl.when(piece % 2 == 0)(lambda: edges(far_ref, near_ref))
    pl.when(piece % 2 == 1)(lambda: edges(near_ref, far_ref))
    for level in range(LEVELS - 1):
        count = CELLS[level]
        kvp_ref[pl.ds(POFF[level] + HALO, count), :] = kv_ref[pl.ds(OFF[level], count), :]
    across = across_ref[...].astype(F32)[0:PIECE7]
    ends = far_ref[pl.ds(EDGE, 16), :].astype(F32)[0:PIECE7]
    tops = []
    for owner in range(4):
        top = jnp.where(owner == (piece + 2) % 4, across, jnp.where(owner == 3 - piece, ends, 0.0))
        tops.append(top)
    kvp_ref[pl.ds(POFF[7], 4 * PIECE7), :] = jnp.concatenate(tops, axis=0).astype(BF16)
    mask = mask_ref[...]
    scaled = mask * jnp.asarray(0.125, BF16)

    units = [(tile, quad) for tile in range(COARSE_TILES) for quad in range(2)]
    biases = [
        tile_bias(kid_ref, qidc_ref, 8 * tile, coarse_windows(tile), COARSE_LEVELS, coarse_ref[tile])
        for tile in range(COARSE_TILES)
    ]
    scores = []
    for tile, quad in units:
        lanes = pl.ds(QL * quad, QL)
        query = head_stack(q3_ref[pl.ds(TILE * tile, TILE), lanes], scaled)
        scores.append(dot_nt(gather_rows(kvp_ref, coarse_windows(tile), lanes), query))
    shares = []
    terms = []
    for index, (tile, quad) in enumerate(units):
        score = level_sums(scores[index], COARSE_LEVELS) + biases[index // 2]
        top = jnp.max(score, axis=0, keepdims=True)
        share = jnp.exp(score - top)
        total = jnp.sum(share, axis=0, keepdims=True)
        lse = top + jnp.log(total)
        lsec_ref[pl.ds(index, 1), :] = lse
        terms.extend(three_terms(lse))
        shares.append((share * (1.0 / total)).astype(BF16))
    results = []
    for (tile, quad), share in zip(units, shares):
        values = gather_rows(kvp_ref, coarse_windows(tile), pl.ds(512 + QL * quad, QL))
        results.append(dot_tn(share, values))
    terms.extend([terms[-1]] * 4)
    terms = dot_nn(jnp.concatenate(terms, axis=0), spread_ref[...])
    for index, (tile, quad) in enumerate(units):
        oc_ref[pl.ds(TILE * tile, TILE), pl.ds(QL * quad, QL)] = head_pick(results[index]).astype(
            BF16
        )
        part = terms[3 * index : 3 * index + 3]
        lsex_ref[pl.ds(index, 1), :] = part[0:1] + part[1:2] + part[2:3]

    def fine_group(group, carry):
        tiles = [GROUP * group + index for index in range(GROUP)]
        units = [(tile, quad) for tile in tiles for quad in range(2)]
        biases = [
            tile_bias(kid_ref, qidf_ref, 8 * tile, fine_windows(tile), FINE_LEVELS, fine_ref[...])
            for tile in tiles
        ]
        scores = []
        for tile, quad in units:
            lanes = pl.ds(QL * quad, QL)
            query = head_stack(q_ref[at(TILE * tile, TILE), lanes], scaled)
            scores.append(dot_nt(gather_rows(kvp_ref, fine_windows(tile), lanes), query))
        shares = []
        for index, (tile, quad) in enumerate(units):
            score = level_sums(scores[index], FINE_LEVELS) + biases[index // 2]
            far = lsex_ref[
                pl.ds(2 * (tile // 8) + quad, 1), pl.ds(pl.multiple_of(QL * (tile % 8), QL), QL)
            ]
            top = jnp.maximum(jnp.max(score, axis=0, keepdims=True), far)
            share = jnp.exp(score - top)
            far_share = jnp.exp(far - top)
            total = jnp.sum(share, axis=0, keepdims=True) + far_share
            lse_ref[pl.ds(2 * tile + quad, 1), :] = top + jnp.log(total)
            inverse = 1.0 / total
            shares.append(
                jnp.concatenate(
                    [share * inverse, jnp.where(own_cell(tile), far_share * inverse, 0.0)], axis=0
                ).astype(BF16)
            )
        results = []
        for (tile, quad), share in zip(units, shares):
            values = jnp.concatenate(
                [
                    gather_rows(kvp_ref, fine_windows(tile), pl.ds(512 + QL * quad, QL)),
                    oc_ref[at(16 * (tile // 2), 16), pl.ds(QL * quad, QL)],
                ],
                axis=0,
            )
            results.append(dot_tn(share, values))
        for (tile, quad), result in zip(units, results):
            mixed_ref[0, at(TILE * tile, TILE), pl.ds(QL * quad, QL)] = head_pick(result).astype(
                BF16
            )
        return carry

    lax.fori_loop(0, FINE_TILES // GROUP, fine_group, 0)


def stat_shapes(width):
    shape = jax.ShapeDtypeStruct
    return [
        shape((PADDED, 2 * width), BF16),
        shape((2 * FINE_TILES, QL), F32),
        shape((2 * COARSE_TILES, QL), F32),
        shape((2 * COARSE_TILES, 8 * QL), F32),
        shape((ROWS // 8, width), BF16),
    ]


def id_specs(micro):
    return [
        one_of((PADDED, 128), micro),
        one_of((8 * FINE_TILES, QL), micro),
        one_of((8 * COARSE_TILES, QL), micro),
        whole((FINE_KEYS, QL)),
        whole((COARSE_TILES, COARSE_KEYS, QL)),
        whole((QL, QL)),
    ]


def id_args(ids, const):
    return [ids["key"], ids["fine"], ids["coarse"], const["fine"], const["coarse"], const["head_mask"]]


def attend(micro, where, cells, received, kept, ids, const):
    q, q3, kv = cells
    width = q.shape[1]
    outs = stat_shapes(width)
    ins = [where, q, q3, kv, *received, *id_args(ids, const), const["spread"]]
    specs = [SCALAR]
    specs += [whole(value.shape) for value in (q, q3, kv) + tuple(received)]
    specs += id_specs(micro) + [whole((QL, 8 * QL))]
    aliases = {}
    if kept is not None:
        aliases = {len(ins): 0}
        ins.append(kept)
        specs.append(KEPT)
    count = len(specs)
    given = 14
    return pl.pallas_call(
        lambda *refs: attend_kernel(*refs[:given], *refs[count:]),
        grid=(1,),
        in_specs=specs,
        out_specs=[one_of((ROWS, width), micro)] + [whole(out.shape) for out in outs],
        out_shape=[jax.ShapeDtypeStruct((ids["key"].shape[0], ROWS, width), BF16)] + outs,
        input_output_aliases=aliases,
        compiler_params=params(),
        cost_estimate=timing(11),
        name="attend",
    )(*ins)


def add_rows(ref, windows, lanes, value):
    start = 0
    for base, count in windows:
        rows = at(base, count)
        ref[rows, lanes] = ref[rows, lanes] + value[start : start + count]
        start += count


def attend_back_kernel(
    where_ref,
    q_ref,
    q3_ref,
    kvp_ref,
    lse_ref,
    lsec_ref,
    lsex_ref,
    oc_ref,
    dout_ref,
    kid_ref,
    qidf_ref,
    qidc_ref,
    fine_ref,
    coarse_ref,
    mask_ref,
    spread_t_ref,
    dq_ref,
    dq3_ref,
    dkv_ref,
    near_ref,
    far_ref,
    top_ref,
    acc_ref,
    dcell_ref,
    delta_ref,
):
    acc_ref[...] = jnp.zeros(acc_ref.shape, F32)
    dcell_ref[...] = jnp.zeros(dcell_ref.shape, F32)
    mask = mask_ref[...]
    scaled = mask * jnp.asarray(0.125, BF16)

    def fine_group(group, carry):
        tiles = [GROUP_BACK * group + index for index in range(GROUP_BACK)]
        units = [(tile, quad) for tile in tiles for quad in range(2)]
        biases = [
            tile_bias(kid_ref, qidf_ref, 8 * tile, fine_windows(tile), FINE_LEVELS, fine_ref[...])
            for tile in tiles
        ]
        at_unit = lambda unit: (at(TILE * unit[0], TILE), pl.ds(QL * unit[1], QL))
        queries = [head_stack(q_ref[at_unit(unit)], scaled) for unit in units]
        douts = [head_stack(dout_ref[(0,) + at_unit(unit)], mask) for unit in units]
        scores = []
        steers = []
        for index, (tile, quad) in enumerate(units):
            keys = gather_rows(kvp_ref, fine_windows(tile), pl.ds(QL * quad, QL))
            scores.append(dot_nt(keys, queries[index]))
            values = jnp.concatenate(
                [
                    gather_rows(kvp_ref, fine_windows(tile), pl.ds(512 + QL * quad, QL)),
                    oc_ref[at(16 * (tile // 2), 16), pl.ds(QL * quad, QL)],
                ],
                axis=0,
            )
            steers.append(dot_nt(values, douts[index]))
        shares = []
        grads = []
        for index, (tile, quad) in enumerate(units):
            lse = lse_ref[pl.ds(2 * tile + quad, 1), :]
            wide = pl.ds(pl.multiple_of(QL * (tile % 8), QL), QL)
            coarse_row = pl.ds(2 * (tile // 8) + quad, 1)
            far_share = jnp.exp(lsex_ref[coarse_row, wide] - lse)
            share = jnp.exp(level_sums(scores[index], FINE_LEVELS) + biases[index // 2] - lse)
            share = jnp.concatenate([share, jnp.where(own_cell(tile), far_share, 0.0)], axis=0)
            weighted = share * steers[index]
            delta = jnp.sum(weighted, axis=0, keepdims=True)
            delta_ref[coarse_row, wide] = far_share * delta
            grad = weighted[0:FINE_KEYS] - share[0:FINE_KEYS] * delta
            grads.append(level_sums(grad, FINE_LEVELS).astype(BF16))
            shares.append(share.astype(BF16))
        dvalues = [dot_nn(share, dout) for share, dout in zip(shares, douts)]
        dkeys = [dot_nn(grad, query) for grad, query in zip(grads, queries)]
        dqueries = []
        for (tile, quad), grad in zip(units, grads):
            keys = gather_rows(kvp_ref, fine_windows(tile), pl.ds(QL * quad, QL))
            dqueries.append(dot_tn(grad, keys))
        for index, (tile, quad) in enumerate(units):
            lanes = pl.ds(QL * quad, QL)
            cells = at(16 * (tile // 2), 16)
            windows = fine_windows(tile)
            add_rows(acc_ref, windows, pl.ds(512 + QL * quad, QL), dvalues[index])
            dcell_ref[cells, lanes] = dcell_ref[cells, lanes] + dvalues[index][FINE_KEYS:]
            add_rows(acc_ref, windows, lanes, dkeys[index])
            dq_ref[at_unit((tile, quad))] = (head_pick(dqueries[index]) * 0.125).astype(BF16)
        return carry

    lax.fori_loop(0, FINE_TILES // GROUP_BACK, fine_group, 0)

    units = [(tile, quad) for tile in range(COARSE_TILES) for quad in range(2)]
    biases = [
        tile_bias(kid_ref, qidc_ref, 8 * tile, coarse_windows(tile), COARSE_LEVELS, coarse_ref[tile])
        for tile in range(COARSE_TILES)
    ]
    at_unit = lambda unit: (pl.ds(TILE * unit[0], TILE), pl.ds(QL * unit[1], QL))
    queries = [head_stack(q3_ref[at_unit(unit)], scaled) for unit in units]
    douts = [head_stack(dcell_ref[at_unit(unit)].astype(BF16), mask) for unit in units]
    terms = []
    for index in range(len(units)):
        terms.extend(three_terms(delta_ref[pl.ds(index, 1), :]))
    terms.extend([terms[-1]] * 4)
    terms = dot_nn(jnp.concatenate(terms, axis=0), spread_t_ref[...])
    steers = []
    scores = []
    for (tile, quad), dout, query in zip(units, douts, queries):
        values = gather_rows(kvp_ref, coarse_windows(tile), pl.ds(512 + QL * quad, QL))
        steers.append(dot_nt(values, dout))
        keys = gather_rows(kvp_ref, coarse_windows(tile), pl.ds(QL * quad, QL))
        scores.append(dot_nt(keys, query))
    shares = []
    grads = []
    for index, (tile, quad) in enumerate(units):
        score = level_sums(scores[index], COARSE_LEVELS) + biases[index // 2]
        share = jnp.exp(score - lsec_ref[pl.ds(index, 1), :])
        part = terms[3 * index : 3 * index + 3]
        delta = part[0:1] + part[1:2] + part[2:3]
        grads.append(level_sums(share * (steers[index] - delta), COARSE_LEVELS).astype(BF16))
        shares.append(share.astype(BF16))
    dvalues = [dot_nn(share, dout) for share, dout in zip(shares, douts)]
    dkeys = [dot_nn(grad, query) for grad, query in zip(grads, queries)]
    dqueries = []
    for (tile, quad), grad in zip(units, grads):
        keys = gather_rows(kvp_ref, coarse_windows(tile), pl.ds(QL * quad, QL))
        dqueries.append(dot_tn(grad, keys))
    for index, (tile, quad) in enumerate(units):
        windows = coarse_windows(tile)
        add_rows(acc_ref, windows, pl.ds(512 + QL * quad, QL), dvalues[index])
        add_rows(acc_ref, windows, pl.ds(QL * quad, QL), dkeys[index])
        dq3_ref[at_unit((tile, quad))] = (head_pick(dqueries[index]) * 0.125).astype(BF16)

    key_lane = lax.broadcasted_iota(jnp.int32, (1, acc_ref.shape[1]), 1) < 512

    def scale(level):
        return jnp.where(key_lane, 0.5 ** STEP[level], 1.0)

    def low(level, start, count):
        return (acc_ref[pl.ds(start, count), :] * scale(level)).astype(BF16)

    def edges(left_ref, right_ref):
        for level in range(LEVELS - 1):
            base = POFF[level]
            edge = pl.ds(HALO * level, HALO)
            left_ref[edge, :] = low(level, base, HALO)
            right_ref[edge, :] = low(level, base + HALO + CELLS[level], HALO)

    piece = where_ref[0]
    pl.when(piece % 2 == 0)(lambda: edges(far_ref, near_ref))
    pl.when(piece % 2 == 1)(lambda: edges(near_ref, far_ref))
    for level in range(LEVELS - 1):
        dkv_ref[pl.ds(OFF[level], CELLS[level]), :] = low(level, POFF[level] + HALO, CELLS[level])
    dkv_ref[pl.ds(OFF[7], 16), :] = jnp.zeros((16, acc_ref.shape[1]), BF16)
    blank = jnp.zeros((PIECE7, acc_ref.shape[1]), F32)

    def high(index):
        rows = pl.ds(pl.multiple_of(POFF[7] + PIECE7 * index, PIECE7), PIECE7)
        return jnp.concatenate([acc_ref[rows, :] * scale(7), blank], axis=0).astype(BF16)

    near_ref[pl.ds(EDGE, 16), :] = jnp.zeros((16, acc_ref.shape[1]), BF16)
    far_ref[pl.ds(EDGE, 16), :] = high(3 - piece)
    top_ref[...] = high((piece + 2) % 4)


def attend_back(micro, where, q, q3, stats, dout, ids, const):
    width = q.shape[1]
    shape = jax.ShapeDtypeStruct
    outs = [
        shape((ROWS, width), BF16),
        shape((ROWS // 8, width), BF16),
        shape((2 * ROWS, 2 * width), BF16),
        shape((EDGES, 2 * width), BF16),
        shape((EDGES, 2 * width), BF16),
        shape((16, 2 * width), BF16),
    ]
    return pl.pallas_call(
        attend_back_kernel,
        grid=(1,),
        in_specs=[SCALAR]
        + [whole(value.shape) for value in (q, q3, *stats)]
        + [one_of((ROWS, width), micro)]
        + id_specs(micro)
        + [whole((8 * QL, QL))],
        out_specs=[whole(out.shape) for out in outs],
        out_shape=outs,
        scratch_shapes=[
            pltpu.VMEM((PADDED, 2 * width), F32),
            pltpu.VMEM((ROWS // 8, width), F32),
            pltpu.VMEM((2 * COARSE_TILES, 8 * QL), F32),
        ],
        compiler_params=params(),
        cost_estimate=timing(17),
        name="attend_back",
    )(where, q, q3, *stats, dout, *id_args(ids, const), const["spread_t"])


MID_ROWS = 512
FF_CHUNK = 512
ROOT = math.sqrt(2.0 / math.pi)


def share_out(send_ref, keep_ref, core, start, piece_of):
    for chip in range(send_ref.shape[0]):
        keep = piece_of(2 * chip + core)
        keep_ref[chip, pl.ds(start, keep.shape[0]), :] = keep
        send_ref[chip, pl.ds(start, keep.shape[0]), :] = piece_of(2 * chip + 1 - core)


def row_piece(ref, shard):
    def piece_of(index):
        return ref[pl.ds(pl.multiple_of(shard * index, shard), shard), :].astype(BF16)

    return piece_of


def middle_kernel(
    where_ref,
    tok_ref,
    cot_ref,
    mixed_ref,
    vec_ref,
    mine_ref,
    other_ref,
    out_ref,
    dmid_ref,
    dmix_ref,
    send_ref,
    keep_ref,
    wo_ref,
    wi_ref,
    wd_ref,
    acc_o,
    acc_i,
    acc_d,
    acc_b,
    acc_s,
    activ_ref,
    grad_ref,
):
    step = pl.program_id(0)
    core = where_ref[1]
    parts = wi_ref.shape[0]
    shard = wo_ref.shape[2]

    @pl.when(step == 0)
    def _():
        acc_o[...] = jnp.zeros(acc_o.shape, F32)
        acc_i[...] = jnp.zeros(acc_i.shape, F32)
        acc_d[...] = jnp.zeros(acc_d.shape, F32)
        acc_b[...] = jnp.zeros(acc_b.shape, F32)
        acc_s[...] = jnp.zeros(acc_s.shape, F32)
        take_weight(wo_ref, 0, mine_ref, other_ref, core, 0)
        for part in range(parts):
            take_weight(wi_ref, part, mine_ref, other_ref, core, shard * (1 + part))
        take_weight(wd_ref, 0, mine_ref, other_ref, core, shard * (1 + parts))

    wo = weight_of(wo_ref, 0)
    pieces = FF_CHUNK // wd_ref.shape[2]
    wi = [weight_of(wi_ref, part) for part in range(parts)]
    wd = [
        wd_ref[0, pieces * part : pieces * (part + 1)].reshape(FF_CHUNK, wo.shape[1])
        for part in range(parts)
    ]
    cot = cot_ref[...]
    top = cot.astype(BF16)
    mixed = mixed_ref[...]
    middle = tok_ref[...] + dot_nn(mixed, wo)
    unit, rate = normalised(middle)
    second = (unit * vec_ref[1:2] + vec_ref[3:4]).astype(BF16)
    result = middle + vec_ref[4:5]
    back = jnp.zeros(cot.shape, F32)
    pres = {}

    def first(part):
        pres[part] = (dot_nn(second, wi[part]) + vec_ref[5 + part : 6 + part], dot_nt(top, wd[part]))

    first(0)
    for part in range(parts):
        if part + 1 < parts:
            first(part + 1)
        pre, grad = pres.pop(part)
        square = pre * pre
        tanh = jnp.tanh(pre * (ROOT + (ROOT * 0.044715) * square))
        half = 0.5 + 0.5 * tanh
        activ = (pre * half).astype(BF16)
        slope = half + (pre * (0.5 - 0.5 * (tanh * tanh))) * (
            ROOT + (ROOT * 3 * 0.044715) * square
        )
        grad = (grad * slope).astype(BF16)
        cols = pl.ds(FF_CHUNK * part, FF_CHUNK)
        activ_ref[:, cols] = activ
        grad_ref[:, cols] = grad
        acc_b[:, cols] = acc_b[:, cols] + fold_rows(grad.astype(F32))
        result = result + dot_nn(activ, wd[part])
        back = back + dot_nt(grad, wi[part])
    out_ref[...] = result
    acc_d[...] = acc_d[...] + dot_tn(activ_ref[...], top)
    for part in range(parts):
        acc_i[part] = acc_i[part] + dot_tn(second, grad_ref[:, pl.ds(FF_CHUNK * part, FF_CHUNK)])
    dmid = cot + norm_back(back * vec_ref[1:2], unit, rate)
    dmid_ref[...] = dmid
    branch = dmid.astype(BF16)
    dmix_ref[...] = dot_nt(branch, wo).astype(BF16)
    acc_o[...] = acc_o[...] + dot_tn(mixed, branch)
    acc_s[0:8, :] = acc_s[0:8, :] + fold_rows(top.astype(F32))
    acc_s[8:16, :] = acc_s[8:16, :] + fold_rows(back * unit)
    acc_s[16:24, :] = acc_s[16:24, :] + fold_rows(back)

    @pl.when(step == pl.num_programs(0) - 1)
    def _():
        share_out(send_ref, keep_ref, core, 0, row_piece(acc_o, shard))
        for part in range(parts):
            share_out(
                send_ref, keep_ref, core, shard * (1 + part), row_piece(acc_i.at[part], shard)
            )
        share_out(send_ref, keep_ref, core, shard * (1 + parts), row_piece(acc_d, shard * parts))
        total = lambda value: jnp.sum(value, axis=0, keepdims=True)
        lines = [total(acc_s[8 * index : 8 * index + 8, :]) for index in range(3)]
        for part in range(parts):
            lines.append(total(acc_b[:, pl.ds(FF_CHUNK * part, FF_CHUNK)]))
        lines.append(jnp.zeros((16 - len(lines), lines[0].shape[1]), F32))
        lines = jnp.concatenate(lines, axis=0).astype(BF16)
        share_out(send_ref, keep_ref, core, shard * (1 + 2 * parts), lambda index: lines)


def middle_part(where, tokens, cot, mixed, vec, mine, other):
    rows, width = tokens.shape
    chips, lines, _ = mine.shape
    shard = width // (2 * chips)
    parts = (lines // shard - 1) // 2
    hidden = parts * FF_CHUNK
    shape = jax.ShapeDtypeStruct
    tiled = pl.BlockSpec((MID_ROWS, width), lambda r: (r, 0))
    shared = shape((chips, lines + 16, width), BF16)
    single = lambda dims: pl.BlockSpec(
        dims, lambda *_: (0,) * len(dims), pipeline_mode=pl.Buffered(1)
    )
    return pl.pallas_call(
        middle_kernel,
        grid=(rows // MID_ROWS,),
        in_specs=[SCALAR, tiled, tiled, tiled, whole(vec.shape), single(mine.shape), single(mine.shape)],
        out_specs=[tiled, tiled, tiled, single(shared.shape), single(shared.shape)],
        out_shape=[
            shape((rows, width), F32),
            shape((rows, width), F32),
            shape((rows, width), BF16),
            shared,
            shared,
        ],
        scratch_shapes=[
            pltpu.VMEM((1, 2 * chips, shard, width), BF16),
            pltpu.VMEM((parts, 2 * chips, shard, FF_CHUNK), BF16),
            pltpu.VMEM((1, 2 * chips, shard * parts, width), BF16),
            pltpu.VMEM((width, width), F32),
            pltpu.VMEM((parts, width, FF_CHUNK), F32),
            pltpu.VMEM((hidden, width), F32),
            pltpu.VMEM((8, hidden), F32),
            pltpu.VMEM((24, width), F32),
            pltpu.VMEM((MID_ROWS, hidden), BF16),
            pltpu.VMEM((MID_ROWS, hidden), BF16),
        ],
        compiler_params=params(),
        cost_estimate=timing(40),
        name="middle",
    )(where, tokens, cot, mixed, vec, mine, other)


def collect_kernel(
    where_ref,
    tok_ref,
    dq_ref,
    dq3_ref,
    dkv_ref,
    near_ref,
    far_ref,
    across_ref,
    vec_ref,
    low_ref,
    high_ref,
    *refs,
    first,
):
    if first:
        dp_ref, gw_ref, cells_ref, norm_ref = refs
    else:
        held_ref, kept_ref, dp_ref, send_ref, keep_ref, cells_ref, norm_ref, gw_ref = refs
    piece, core = where_ref[0], where_ref[1]
    cells_ref[...] = dkv_ref[...]

    def add(start, value):
        rows = pl.ds(start, HALO)
        cells_ref[rows, :] = (cells_ref[rows, :].astype(F32) + value.astype(F32)).astype(BF16)

    def edges(left_ref, right_ref):
        for level in range(LEVELS - 1):
            edge = pl.ds(HALO * level, HALO)

            @pl.when(piece > 0)
            def _():
                add(OFF[level], left_ref[edge, :])

            @pl.when(piece < 3)
            def _():
                add(OFF[level] + CELLS[level] - HALO, right_ref[edge, :])

    pl.when(piece % 2 == 0)(lambda: edges(far_ref, near_ref))
    pl.when(piece % 2 == 1)(lambda: edges(near_ref, far_ref))
    add(OFF[7], across_ref[...].astype(F32) + far_ref[pl.ds(EDGE, 16), :].astype(F32))

    for chunk in range(ROWS // 256):
        rows = pl.ds(256 * chunk, 256)
        unit, _ = normalised(tok_ref[0, rows, :])
        norm_ref[rows, :] = (unit * vec_ref[0:1] + vec_ref[2:3]).astype(BF16)
        cells = jnp.concatenate(
            [
                cells_ref[pl.ds(OFF[level] + (256 >> level) * chunk, 256 >> level), :]
                for level in range(1, 5)
            ],
            axis=0,
        )
        dkv = (
            cells_ref[rows, :].astype(F32)
            + dot_nn(low_ref[...], cells)
            + dot_nn(high_ref[rows, :], cells_ref[pl.ds(OFF[5], 64), :])
        ).astype(BF16)
        dq = (
            dq_ref[rows, :].astype(F32)
            + dot_nn(low_ref[:, 192:224], dq3_ref[pl.ds(32 * chunk, 32), :])
        ).astype(BF16)
        dp_ref[0, rows, pl.ds(0, 512)] = dq
        dp_ref[0, rows, pl.ds(512, 1024)] = dkv
    for index in range(3):
        grad = dot_tn(norm_ref[...], dp_ref[0, :, pl.ds(512 * index, 512)])
        gw_ref[index] = grad if first else held_ref[index] + grad
    if not first:
        shard = send_ref.shape[1] // 3
        for index in range(3):
            share_out(send_ref, keep_ref, core, shard * index, row_piece(gw_ref.at[index], shard))


def collect(micro, where, tokens, grads, received, vec, kept, held, dp, const):
    width = tokens.shape[2]
    shape = jax.ShapeDtypeStruct
    first = held is None
    ins = list(grads) + list(received) + [vec, const["low_t"], const["high_t"]]
    specs = [SCALAR, one_of((ROWS, width), micro)] + [whole(value.shape) for value in ins]
    outs = [shape((tokens.shape[0], ROWS, 3 * width), BF16)]
    scratch = [pltpu.VMEM((2 * ROWS, 2 * width), BF16), pltpu.VMEM((ROWS, width), BF16)]
    aliases = {}
    if first:
        outs.append(shape((3, width, width), F32))
    else:
        ins += [held, kept]
        specs += [whole(held.shape), KEPT]
        aliases = {12: 0}
        outs += [shape((dp // 2, 3 * width // dp, width), BF16)] * 2
        scratch.append(pltpu.VMEM((3, width, width), F32))
    return pl.pallas_call(
        lambda *refs: collect_kernel(*refs, first=first),
        grid=(1,),
        in_specs=specs,
        out_specs=[one_of((ROWS, 3 * width), micro)] + [whole(out.shape) for out in outs[1:]],
        out_shape=outs,
        scratch_shapes=scratch,
        input_output_aliases=aliases,
        compiler_params=params(),
        cost_estimate=timing(7),
        name="collect",
    )(where, tokens, *ins)


def finish_kernel(
    where_ref, tok_ref, dmid_ref, dp_ref, vec_ref, mine_ref, other_ref, grad_ref, small_ref, w_ref, acc_ref
):
    step = pl.program_id(0)
    core = where_ref[1]

    @pl.when(step == 0)
    def _():
        acc_ref[...] = jnp.zeros(acc_ref.shape, F32)
        for index in range(3):
            take_weight(w_ref, index, mine_ref, other_ref, core, w_ref.shape[2] * index)

    for half in range(2):
        rows = pl.ds(512 * half, 512)
        back = dot_nt(dp_ref[0, rows, pl.ds(0, 512)], weight_of(w_ref, 0))
        for index in range(1, 3):
            back = back + dot_nt(dp_ref[0, rows, pl.ds(512 * index, 512)], weight_of(w_ref, index))
        unit, rate = normalised(tok_ref[0, rows, :])
        acc_ref[0:8, :] = acc_ref[0:8, :] + fold_rows(back * unit)
        acc_ref[8:16, :] = acc_ref[8:16, :] + fold_rows(back)
        grad_ref[0, rows, :] = dmid_ref[0, rows, :] + norm_back(back * vec_ref[0:1], unit, rate)

    @pl.when(step == pl.num_programs(0) - 1)
    def _():
        total = lambda value: jnp.sum(value, axis=0, keepdims=True)
        blank = jnp.zeros((14, acc_ref.shape[1]), F32)
        lines = jnp.concatenate([total(acc_ref[0:8, :]), total(acc_ref[8:16, :]), blank], axis=0)
        small_ref[...] = jnp.broadcast_to(lines[None], small_ref.shape).astype(BF16)


def finish(where, tokens, dmid, dproj, vec, mine, other):
    micro, _, width = tokens.shape
    shape = jax.ShapeDtypeStruct
    dp = 2 * mine.shape[0]
    small = shape((dp, 16, width), BF16)
    return pl.pallas_call(
        finish_kernel,
        grid=(micro,),
        in_specs=[
            SCALAR,
            each_of((ROWS, width)),
            each_of((ROWS, width)),
            each_of((ROWS, 3 * width)),
            whole(vec.shape),
            whole(mine.shape),
            whole(other.shape),
        ],
        out_specs=[each_of((ROWS, width)), whole(small.shape)],
        out_shape=[shape((micro, ROWS, width), F32), small],
        scratch_shapes=[
            pltpu.VMEM((3, dp, width // dp, width), BF16),
            pltpu.VMEM((16, width), F32),
        ],
        compiler_params=params(),
        cost_estimate=timing(9),
        name="finish",
    )(where, tokens, dmid, dproj, vec, mine, other)


def cell_documents(segments, piece):
    micro, length = segments.shape
    keys = []
    fine = []
    coarse = []
    for level in range(LEVELS):
        cell = 1 << level
        grouped = segments.reshape(micro, length // cell, cell)
        lowest = grouped[:, :, 0]
        highest = grouped[:, :, cell - 1]
        same = lowest == highest
        key = jnp.where(same, lowest, -2)
        query = jnp.where(same, lowest, -1)
        own = lax.dynamic_slice_in_dim(query, piece * CELLS[level], CELLS[level], axis=1)
        if level < LEVELS - 1:
            padded = jnp.pad(key, ((0, 0), (HALO, HALO)), constant_values=-3)
            keys.append(
                lax.dynamic_slice_in_dim(
                    padded, piece * CELLS[level], CELLS[level] + 2 * HALO, axis=1
                )
            )
        else:
            owner = jnp.arange(key.shape[1]) // PIECE7
            counted = (jnp.abs(owner // 2 - piece // 2) == 1) & (jnp.abs(owner - piece) >= 2)
            keys.append(jnp.where(counted[None], key, -3))
        if level < FINE:
            fine.append(jnp.repeat(own, cell, axis=1).reshape(micro, FINE_TILES, 1, TILE))
        else:
            coarse.append(jnp.repeat(own, cell // 8, axis=1).reshape(micro, COARSE_TILES, 1, TILE))

    def rows(parts):
        value = jnp.concatenate(parts, axis=2)
        value = jnp.pad(value, ((0, 0), (0, 0), (0, 8 - len(parts)), (0, 0)))
        return jnp.tile(value, (1, 1, 1, QUAD)).reshape(micro, -1, QL)

    key = jnp.concatenate(keys, axis=1)
    return dict(
        key=jnp.broadcast_to(key[:, :, None], key.shape + (128,)),
        fine=rows(fine),
        coarse=rows(coarse),
    )


def same_core(chips):
    return [[2 * chip + core for chip in range(chips)] for core in range(2)]


def core_swap(value, chips):
    pairs = [(place, place ^ 1) for place in range(2 * chips)]
    return lax.ppermute(value, "dp", pairs)


def chip_exchange(value, chips):
    return lax.all_to_all(value, "dp", 0, 0, axis_index_groups=same_core(chips), tiled=True)


def after(value, *done):
    return lax.optimization_barrier((value,) + done)[0]


def add(left, right):
    return left.astype(F32) + right.astype(F32)


def body(
    tokens,
    segment_ids,
    norm_gains,
    norm_biases,
    qkv_weight,
    out_weight,
    in_weight,
    in_bias,
    down_weight,
    down_bias,
    cotangent,
):
    micro, _, row_count, width = tokens.shape
    pieces = lax.axis_size("sp")
    piece = lax.axis_index("sp")
    assert row_count == ROWS and pieces == 4 and micro == 2
    const = constants()
    tokens = tokens[:, 0]
    cotangent = cotangent[:, 0]
    dp = lax.axis_size("dp")
    place = lax.axis_index("dp")
    chips = dp // 2
    shard = width // dp
    hidden = in_weight.shape[1]
    parts = hidden // FF_CHUNK
    where = jnp.stack([piece, place % 2]).astype(jnp.int32)
    swap = lambda value, bits: lax.ppermute(value, "sp", [(p, p ^ bits) for p in range(pieces)])
    spread = lambda value: chip_exchange(
        jnp.broadcast_to(value[None], (chips,) + value.shape), chips
    )

    small = jnp.concatenate([norm_gains.reshape(-1), norm_biases.reshape(-1), down_bias, in_bias])
    count = small.size
    lines = -(-count // width)
    small = jnp.pad(small, (0, lines * width - count)).reshape(lines, width)
    mine = spread(jnp.concatenate([qkv_weight.reshape(3 * shard, width), small]))
    other = core_swap(mine, chips)
    ids = cell_documents(segment_ids[:, 0], piece)
    rest = jnp.concatenate(
        [
            out_weight,
            in_weight.reshape(shard, parts, FF_CHUNK).swapaxes(0, 1).reshape(-1, width),
            down_weight,
        ]
    )
    rest_mine = spread(after(rest, mine))
    first = (place % 2) == 0
    both = [value[:, 3 * shard :].reshape(chips, -1)[:, :count] for value in (mine, other)]
    both = jnp.stack(
        [jnp.where(first, both[0], both[1]), jnp.where(first, both[1], both[0])], axis=1
    ).reshape(dp, count)
    vec = jnp.concatenate(
        [
            both[:, : 5 * shard].reshape(dp, 5, shard).swapaxes(0, 1).reshape(5, width),
            both[:, 5 * shard :].reshape(parts, width),
            jnp.zeros((16 - 5 - parts, width), BF16),
        ]
    ).astype(F32)

    cells, received = [], []
    for m in range(2):
        q, q3, kv, near, far, top = project(m, where, tokens, vec, mine, other, const)
        cells.append((q, q3, kv))
        received.append((swap(near, 1), swap(far, 3), swap(top, 2)))
    rest_mine = after(rest_mine, cells[1][0])
    rest_other = core_swap(rest_mine, chips)
    mixed = None
    stats = []
    for m in range(2):
        mixed, *stat = attend(m, where, cells[m], received[m], mixed, ids, const)
        stats.append(stat)

    flat = lambda value: value.reshape(micro * ROWS, width)
    split = lambda value: value.reshape(micro, ROWS, width)
    outputs, dmid, dmix, send, keep = middle_part(
        where, flat(tokens), flat(cotangent), flat(mixed), vec, rest_mine, rest_other
    )

    grads, back = [], []

    def attention_back(m):
        dq, dq3, dkv, near, far, top = attend_back(
            m, where, cells[m][0], cells[m][1], stats[m], split(dmix), ids, const
        )
        grads.append((dq, dq3, dkv))
        back.append((swap(near, 1), swap(far, 3), swap(top, 2)))

    come = core_swap(send, chips)
    attention_back(0)
    pair = add(keep, after(come, grads[0][0])).astype(BF16)
    come = chip_exchange(pair, chips)
    attention_back(1)
    total = jnp.sum(after(come, grads[1][0]).astype(F32), axis=0).astype(BF16)
    come = swap(total, 1)
    dproj, held = collect(0, where, tokens, grads[0], back[0], vec, None, None, dp, const)
    total = add(total, after(come, held)).astype(BF16)
    come = swap(total, 3)
    dproj, send, keep = collect(1, where, tokens, grads[1], back[1], vec, dproj, held, dp, const)
    rest = add(total, after(come, send))

    come = core_swap(send, chips)
    pair = add(keep, come).astype(BF16)
    come = chip_exchange(pair, chips)
    input_grad, small = finish(where, tokens, split(dmid), dproj, vec, mine, other)
    small = jnp.sum(lax.all_to_all(small, "dp", 0, 0, tiled=True).astype(F32), axis=0)
    total = jnp.sum(come.astype(F32), axis=0)
    total = jnp.concatenate([total, small]).astype(BF16)
    total = add(total, swap(total, 1)).astype(BF16)
    total = add(total, swap(total, 3))

    own = lambda value, size: lax.dynamic_slice_in_dim(value, place * size, size, axis=-1)
    small_two = rest[shard * (1 + 2 * parts) :]
    small_one = total[3 * shard :]
    gin = rest[shard : shard * (1 + parts)].reshape(parts, shard, FF_CHUNK).swapaxes(0, 1)
    return (
        outputs.reshape(micro, 1, ROWS, width),
        input_grad[:, None],
        own(jnp.stack([small_one[0], small_two[1]]), shard),
        own(jnp.stack([small_one[1], small_two[2]]), shard),
        total[: 3 * shard].reshape(3, shard, width),
        rest[:shard],
        gin.reshape(shard, hidden),
        own(small_two[3 : 3 + parts].reshape(hidden), hidden // dp),
        rest[shard * (1 + parts) : shard * (1 + 2 * parts)],
        own(small_two[0], shard),
    )


def solution(mesh):
    in_specs = (
        P(None, "dp", "sp", None),
        P(None, "dp", None),
        P(None, "dp"),
        P(None, "dp"),
        P(None, "dp", None),
        P("dp", None),
        P("dp", None),
        P("dp"),
        P("dp", None),
        P("dp"),
        P(None, "dp", "sp", None),
    )
    out_specs = (
        P(None, "dp", "sp", None),
        P(None, "dp", "sp", None),
        P(None, "dp"),
        P(None, "dp"),
        P(None, "dp", None),
        P("dp", None),
        P("dp", None),
        P("dp"),
        P("dp", None),
        P("dp"),
    )
    return jax.shard_map(body, mesh=mesh, in_specs=in_specs, out_specs=out_specs, check_vma=False)
```

```python
import math

import jax
import jax.numpy as jnp
import numpy as np
from jax import lax
from jax.experimental import pallas as pl
from jax.experimental.pallas import tpu as pltpu
from jax.sharding import PartitionSpec as P

HEADS = 8
HEAD_DIM = 64
BLOCK = 16
LEVELS = 8
HALO = 16
TILE = 64
QUAD = 4
QL = QUAD * HEAD_DIM
NEG = -1e30
FINE = 3
ROWS = 1024
EDGE = 112
EDGES = 128
VEC = 16
GROUP = 8
GROUP_BACK = 4
F32 = jnp.float32
BF16 = jnp.bfloat16

CELLS = [ROWS >> level for level in range(LEVELS)]
OFF = [2 * ROWS - (2 * ROWS >> level) for level in range(LEVELS)]
POFF = []
_at = 0
for _level in range(LEVELS - 1):
    POFF.append(_at)
    _at += CELLS[_level] + 2 * HALO
POFF.append(_at)
PIECE7 = CELLS[LEVELS - 1]
PADDED = _at + 4 * PIECE7
FINE_TILES = ROWS // TILE
COARSE_TILES = ROWS // 8 // TILE
FINE_KEYS = 192
COARSE_KEYS = 256
LN_EPS = 1e-05
VMEM_LIMIT = 62 * 1024 * 1024


def _counts(level, query, key):
    query = query[None, :]
    key = key[:, None]
    near = np.abs(query // 16 - key // 16)
    if level == 0:
        return near <= 1
    return (near == 1) & (np.abs(query // 8 - key // 8) >= 2)


def _bias(parts):
    rows = []
    for level, allowed in parts:
        rows.append(np.where(allowed, np.float32(level * math.log(2.0)), np.float32(NEG)))
    block = np.concatenate(rows, axis=0).astype(np.float32)
    return np.tile(block, (1, QUAD))


def _two_blocks():
    return np.concatenate([np.arange(16) - 16, np.arange(16) + 16])


def fine_bias():
    token = np.arange(TILE)
    return _bias(
        [
            (0, _counts(0, token, np.arange(96) - 16)),
            (1, _counts(1, token // 2, np.arange(64) - 16)),
            (2, _counts(2, token // 4, _two_blocks())),
        ]
    )


def coarse_bias():
    cell = np.arange(TILE)
    out = []
    for tile in range(COARSE_TILES):
        out.append(
            _bias(
                [
                    (3, _counts(3, cell, np.arange(96) - 16)),
                    (4, _counts(4, cell // 2, np.arange(64) - 16)),
                    (5, _counts(5, cell // 4, _two_blocks())),
                    (6, _counts(6, 8 * tile + cell // 8, _two_blocks())),
                    (7, np.ones((4 * PIECE7, TILE), bool)),
                ]
            )
        )
    return np.stack(out)


STEP = [0, 1, 2, 0, 1, 2, 3, 4]


def mean_rows(cell, count):
    return (np.arange(count)[None, :] // cell == np.arange(count // cell)[:, None]).astype(
        np.float32
    ) / cell


def spread_matrix():
    out = np.zeros((QUAD, TILE, 8, QUAD, TILE), np.float32)
    for part in range(8):
        for token in range(TILE):
            for head in range(QUAD):
                out[head, 8 * part + token // 8, part, head, token] = 1.0
    return out.reshape(QL, 8 * QL)


def constants():
    head_mask = np.kron(np.eye(QUAD), np.ones((TILE, HEAD_DIM)))
    low = [mean_rows(1 << level, 256) for level in range(1, 5)]
    high = [mean_rows(1 << level, ROWS) for level in range(5, 8)] + [np.zeros((8, ROWS))]
    key_low = [rows * 0.5 ** STEP[level] for level, rows in zip(range(1, 5), low)]
    key_high = [rows * 0.5**step for step, rows in zip(STEP[5:] + [0], high)]
    as_low = lambda value: jnp.asarray(value.astype(np.float32)).astype(BF16)
    low, high = np.concatenate(low), np.concatenate(high)
    return dict(
        fine=jnp.asarray(fine_bias()),
        coarse=jnp.asarray(coarse_bias()),
        head_mask=as_low(head_mask),
        low=as_low(np.stack([np.concatenate(key_low), low])),
        high=as_low(np.stack([np.concatenate(key_high), high])),
        low_t=as_low(low.T),
        high_t=as_low(high.T),
        spread=as_low(spread_matrix()),
        spread_t=as_low(spread_matrix().T),
    )


def dot_nn(left, right):
    return jnp.dot(left, right, preferred_element_type=F32)


def dot_nt(left, right):
    return lax.dot_general(left, right, (((1,), (1,)), ((), ())), preferred_element_type=F32)


def dot_tn(left, right):
    return lax.dot_general(left, right, (((0,), (0,)), ((), ())), preferred_element_type=F32)


def at(start, size):
    return pl.ds(pl.multiple_of(start, 16), size)


def whole(shape):
    zeros = (0,) * len(shape)
    return pl.BlockSpec(shape, lambda *_: zeros)


def one_of(shape, micro):
    zeros = (0,) * len(shape)
    return pl.BlockSpec((1,) + shape, lambda *_: (micro,) + zeros)


def each_of(shape):
    zeros = (0,) * len(shape)
    return pl.BlockSpec((1,) + shape, lambda step: (step,) + zeros)


SCALAR = pl.BlockSpec(memory_space=pltpu.SMEM)
KEPT = pl.BlockSpec(memory_space=pl.ANY)


def timing(micros):
    return pl.CostEstimate(
        flops=int(micros * 4e8), bytes_accessed=int(micros * 3e6), transcendentals=0
    )


def params():
    return pltpu.CompilerParams(
        dimension_semantics=("arbitrary",), vmem_limit_bytes=VMEM_LIMIT
    )


def normalised(rows):
    center = rows - jnp.mean(rows, axis=-1, keepdims=True)
    spread = jnp.mean(center * center, axis=-1, keepdims=True)
    rate = lax.rsqrt(spread + LN_EPS)
    return center * rate, rate


def norm_back(grad, unit, rate):
    mean_grad = jnp.mean(grad, axis=-1, keepdims=True)
    mean_dot = jnp.mean(grad * unit, axis=-1, keepdims=True)
    return rate * (grad - mean_grad - unit * mean_dot)


def fold_rows(value):
    return jnp.sum(value.reshape(-1, 8, value.shape[-1]), axis=0)


def take_weight(target, index, mine, other, core, start):
    chips, shard = mine.shape[0], target.shape[2]
    for chip in range(chips):
        target[index, 2 * chip + core] = mine[chip, pl.ds(start, shard), :]
        target[index, 2 * chip + 1 - core] = other[chip, pl.ds(start, shard), :]


def weight_of(ref, index):
    return ref[index].reshape(ref.shape[1] * ref.shape[2], ref.shape[3])


def project_kernel(
    where_ref,
    tok_ref,
    mine_ref,
    other_ref,
    low_ref,
    high_ref,
    q_ref,
    q3_ref,
    kv_ref,
    near_ref,
    far_ref,
    top_ref,
    vec_ref,
    w_ref,
    norm_ref,
):
    piece, core = where_ref[0], where_ref[1]
    shard = w_ref.shape[2]
    for index in range(3):
        take_weight(w_ref, index, mine_ref, other_ref, core, shard * index)
    vec = jnp.zeros(vec_ref.shape, F32)
    for chip in range(mine_ref.shape[0]):
        for ref in (mine_ref, other_ref):
            vec = vec + ref[chip, pl.ds(3 * shard, VEC), :].astype(F32)
    vec_ref[...] = vec
    for chunk in range(ROWS // 256):
        rows = pl.ds(256 * chunk, 256)
        unit, _ = normalised(tok_ref[0, rows, :])
        norm_ref[rows, :] = (unit * vec[0:1] + vec[2:3]).astype(BF16)
    for half in range(2):
        rows = pl.ds(512 * half, 512)
        for index in range(3):
            value = dot_nn(norm_ref[rows, :], weight_of(w_ref, index)).astype(BF16)
            if index == 0:
                q_ref[rows, :] = value
            else:
                kv_ref[rows, pl.ds(512 * (index - 1), 512)] = value
    for chunk in range(ROWS // 256):
        rows = pl.ds(256 * chunk, 256)
        q3_ref[pl.ds(32 * chunk, 32), :] = dot_nn(low_ref[1, 192:224, :], q_ref[rows, :]).astype(
            BF16
        )
        for part in range(2):
            lanes = pl.ds(512 * part, 512)
            cells = dot_nn(low_ref[part], kv_ref[rows, lanes]).astype(BF16)
            start = 0
            for level in range(1, 5):
                count = 256 >> level
                kv_ref[pl.ds(OFF[level] + count * chunk, count), lanes] = cells[
                    start : start + count
                ]
                start += count
    for part in range(2):
        lanes = pl.ds(512 * part, 512)
        kv_ref[pl.ds(OFF[5], 64), lanes] = dot_nn(high_ref[part], kv_ref[pl.ds(0, ROWS), lanes]).astype(
            BF16
        )

    def edges(left_ref, right_ref):
        for level in range(LEVELS - 1):
            edge = pl.ds(HALO * level, HALO)
            left_ref[edge, :] = kv_ref[pl.ds(OFF[level], HALO), :]
            right_ref[edge, :] = kv_ref[pl.ds(OFF[level] + CELLS[level] - HALO, HALO), :]

    pl.when(piece % 2 == 0)(lambda: edges(far_ref, near_ref))
    pl.when(piece % 2 == 1)(lambda: edges(near_ref, far_ref))
    high = kv_ref[pl.ds(OFF[7], 16), :]
    near_ref[pl.ds(EDGE, 16), :] = high
    far_ref[pl.ds(EDGE, 16), :] = high
    top_ref[...] = high


def project(micro, where, tokens, mine, other, const):
    width = tokens.shape[2]
    shape = jax.ShapeDtypeStruct
    shard = width // (2 * mine.shape[0])
    outs = [
        shape((ROWS, width), BF16),
        shape((ROWS // 8, width), BF16),
        shape((2 * ROWS, 2 * width), BF16),
        shape((EDGES, 2 * width), BF16),
        shape((EDGES, 2 * width), BF16),
        shape((16, 2 * width), BF16),
        shape((VEC, width), F32),
    ]
    return pl.pallas_call(
        project_kernel,
        grid=(1,),
        in_specs=[
            SCALAR,
            one_of((ROWS, width), micro),
            whole(mine.shape),
            whole(other.shape),
            whole((2, 240, 256)),
            whole((2, 64, ROWS)),
        ],
        out_specs=[whole(out.shape) for out in outs],
        out_shape=outs,
        scratch_shapes=[
            pltpu.VMEM((3, width // shard, shard, width), BF16),
            pltpu.VMEM((ROWS, width), BF16),
        ],
        compiler_params=params(),
        cost_estimate=timing(6),
        name="project",
    )(where, tokens, mine, other, const["low"], const["high"])


def fine_windows(tile):
    return [
        (POFF[0] + 64 * tile, 96),
        (POFF[1] + 32 * tile, 64),
        (POFF[2] + 16 * tile, 16),
        (POFF[2] + 16 * tile + 32, 16),
    ]


def coarse_windows(tile):
    return [
        (POFF[3] + 64 * tile, 96),
        (POFF[4] + 32 * tile, 64),
        (POFF[5] + 16 * tile, 16),
        (POFF[5] + 16 * tile + 32, 16),
        (POFF[6], 16),
        (POFF[6] + 32, 16),
        (POFF[7], 32),
    ]


FINE_LEVELS = [96, 64, 32]
COARSE_LEVELS = [96, 64, 32, 32, 32]


def gather_rows(ref, windows, lanes):
    return jnp.concatenate([ref[at(start, size), lanes] for start, size in windows], axis=0)


def tile_bias(kid_ref, qid_ref, row, windows, levels, bias):
    keys = jnp.concatenate([kid_ref[0, at(start, size), :] for start, size in windows], axis=0)
    keys = jnp.concatenate([keys, keys], axis=1)
    out = []
    start = 0
    for index, count in enumerate(levels):
        part = slice(start, start + count)
        owner = qid_ref[0, pl.ds(row + index, 1), :]
        out.append(jnp.where(keys[part] == owner, bias[part], NEG))
        start += count
    return jnp.concatenate(out, axis=0)


def lane_sums(value, steps):
    halves = []
    for half in range(2):
        part = value[:, 128 * half : 128 * (half + 1)]
        lane = lax.broadcasted_iota(jnp.int32, part.shape, 1)
        for step in range(steps):
            size = 1 << step
            first = (lane & size) == 0
            part = part + jnp.where(
                first, pltpu.roll(part, 128 - size, 1), pltpu.roll(part, size, 1)
            )
        halves.append(part)
    return jnp.concatenate(halves, axis=1)


def level_sums(value, levels):
    out = [value[0 : levels[0]]]
    start = levels[0]
    for index, count in enumerate(levels[1:]):
        out.append(lane_sums(value[start : start + count], index + 1))
        start += count
    return jnp.concatenate(out, axis=0)


def head_stack(value, mask):
    return jnp.concatenate([value] * QUAD, axis=0) * mask


def head_pick(stacked):
    lane = lax.broadcasted_iota(jnp.int32, (TILE, QL), 1) // HEAD_DIM
    out = stacked[0:TILE]
    for head in range(1, QUAD):
        out = jnp.where(lane == head, stacked[TILE * head : TILE * (head + 1)], out)
    return out


def three_terms(row):
    high = row.astype(BF16)
    rest = row - high.astype(F32)
    middle = rest.astype(BF16)
    low = (rest - middle.astype(F32)).astype(BF16)
    return high, middle, low


def own_cell(tile):
    cell = lax.broadcasted_iota(jnp.int32, (16, QL), 0)
    token = lax.broadcasted_iota(jnp.int32, (16, QL), 1) % TILE
    return cell == 8 * (tile % 2) + token // 8


def attend_kernel(
    where_ref,
    q_ref,
    q3_ref,
    kv_ref,
    near_ref,
    far_ref,
    across_ref,
    kid_ref,
    qidf_ref,
    qidc_ref,
    fine_ref,
    coarse_ref,
    mask_ref,
    spread_ref,
    mixed_ref,
    kvp_ref,
    lse_ref,
    lsec_ref,
    lsex_ref,
    oc_ref,
):
    piece = where_ref[0]

    def edges(left_ref, right_ref):
        for level in range(LEVELS - 1):
            base = POFF[level]
            edge = pl.ds(HALO * level, HALO)
            kvp_ref[pl.ds(base, HALO), :] = left_ref[edge, :]
            kvp_ref[pl.ds(base + HALO + CELLS[level], HALO), :] = right_ref[edge, :]

    pl.when(piece % 2 == 0)(lambda: edges(far_ref, near_ref))
    pl.when(piece % 2 == 1)(lambda: edges(near_ref, far_ref))
    for level in range(LEVELS - 1):
        count = CELLS[level]
        kvp_ref[pl.ds(POFF[level] + HALO, count), :] = kv_ref[pl.ds(OFF[level], count), :]
    across = across_ref[...].astype(F32)[0:PIECE7]
    ends = far_ref[pl.ds(EDGE, 16), :].astype(F32)[0:PIECE7]
    tops = []
    for owner in range(4):
        top = jnp.where(owner == (piece + 2) % 4, across, jnp.where(owner == 3 - piece, ends, 0.0))
        tops.append(top)
    kvp_ref[pl.ds(POFF[7], 4 * PIECE7), :] = jnp.concatenate(tops, axis=0).astype(BF16)
    mask = mask_ref[...]
    scaled = mask * jnp.asarray(0.125, BF16)

    units = [(tile, quad) for tile in range(COARSE_TILES) for quad in range(2)]
    biases = [
        tile_bias(kid_ref, qidc_ref, 8 * tile, coarse_windows(tile), COARSE_LEVELS, coarse_ref[tile])
        for tile in range(COARSE_TILES)
    ]
    scores = []
    for tile, quad in units:
        lanes = pl.ds(QL * quad, QL)
        query = head_stack(q3_ref[pl.ds(TILE * tile, TILE), lanes], scaled)
        scores.append(dot_nt(gather_rows(kvp_ref, coarse_windows(tile), lanes), query))
    shares = []
    terms = []
    for index, (tile, quad) in enumerate(units):
        score = level_sums(scores[index], COARSE_LEVELS) + biases[index // 2]
        top = jnp.max(score, axis=0, keepdims=True)
        share = jnp.exp(score - top)
        total = jnp.sum(share, axis=0, keepdims=True)
        lse = top + jnp.log(total)
        lsec_ref[pl.ds(index, 1), :] = lse
        terms.extend(three_terms(lse))
        shares.append((share * (1.0 / total)).astype(BF16))
    results = []
    for (tile, quad), share in zip(units, shares):
        values = gather_rows(kvp_ref, coarse_windows(tile), pl.ds(512 + QL * quad, QL))
        results.append(dot_tn(share, values))
    terms.extend([terms[-1]] * 4)
    terms = dot_nn(jnp.concatenate(terms, axis=0), spread_ref[...])
    for index, (tile, quad) in enumerate(units):
        oc_ref[pl.ds(TILE * tile, TILE), pl.ds(QL * quad, QL)] = head_pick(results[index]).astype(
            BF16
        )
        part = terms[3 * index : 3 * index + 3]
        lsex_ref[pl.ds(index, 1), :] = part[0:1] + part[1:2] + part[2:3]

    def fine_group(group, carry):
        tiles = [GROUP * group + index for index in range(GROUP)]
        units = [(tile, quad) for tile in tiles for quad in range(2)]
        biases = [
            tile_bias(kid_ref, qidf_ref, 8 * tile, fine_windows(tile), FINE_LEVELS, fine_ref[...])
            for tile in tiles
        ]
        scores = []
        for tile, quad in units:
            lanes = pl.ds(QL * quad, QL)
            query = head_stack(q_ref[at(TILE * tile, TILE), lanes], scaled)
            scores.append(dot_nt(gather_rows(kvp_ref, fine_windows(tile), lanes), query))
        shares = []
        for index, (tile, quad) in enumerate(units):
            score = level_sums(scores[index], FINE_LEVELS) + biases[index // 2]
            far = lsex_ref[
                pl.ds(2 * (tile // 8) + quad, 1), pl.ds(pl.multiple_of(QL * (tile % 8), QL), QL)
            ]
            top = jnp.maximum(jnp.max(score, axis=0, keepdims=True), far)
            share = jnp.exp(score - top)
            far_share = jnp.exp(far - top)
            total = jnp.sum(share, axis=0, keepdims=True) + far_share
            lse_ref[pl.ds(2 * tile + quad, 1), :] = top + jnp.log(total)
            inverse = 1.0 / total
            shares.append(
                jnp.concatenate(
                    [share * inverse, jnp.where(own_cell(tile), far_share * inverse, 0.0)], axis=0
                ).astype(BF16)
            )
        results = []
        for (tile, quad), share in zip(units, shares):
            values = jnp.concatenate(
                [
                    gather_rows(kvp_ref, fine_windows(tile), pl.ds(512 + QL * quad, QL)),
                    oc_ref[at(16 * (tile // 2), 16), pl.ds(QL * quad, QL)],
                ],
                axis=0,
            )
            results.append(dot_tn(share, values))
        for (tile, quad), result in zip(units, results):
            mixed_ref[0, at(TILE * tile, TILE), pl.ds(QL * quad, QL)] = head_pick(result).astype(
                BF16
            )
        return carry

    lax.fori_loop(0, FINE_TILES // GROUP, fine_group, 0)


def stat_shapes(width):
    shape = jax.ShapeDtypeStruct
    return [
        shape((PADDED, 2 * width), BF16),
        shape((2 * FINE_TILES, QL), F32),
        shape((2 * COARSE_TILES, QL), F32),
        shape((2 * COARSE_TILES, 8 * QL), F32),
        shape((ROWS // 8, width), BF16),
    ]


def id_specs(micro):
    return [
        one_of((PADDED, 128), micro),
        one_of((8 * FINE_TILES, QL), micro),
        one_of((8 * COARSE_TILES, QL), micro),
        whole((FINE_KEYS, QL)),
        whole((COARSE_TILES, COARSE_KEYS, QL)),
        whole((QL, QL)),
    ]


def id_args(ids, const):
    return [ids["key"], ids["fine"], ids["coarse"], const["fine"], const["coarse"], const["head_mask"]]


def attend(micro, where, cells, received, kept, ids, const):
    q, q3, kv = cells
    width = q.shape[1]
    outs = stat_shapes(width)
    ins = [where, q, q3, kv, *received, *id_args(ids, const), const["spread"]]
    specs = [SCALAR]
    specs += [whole(value.shape) for value in (q, q3, kv) + tuple(received)]
    specs += id_specs(micro) + [whole((QL, 8 * QL))]
    aliases = {}
    if kept is not None:
        aliases = {len(ins): 0}
        ins.append(kept)
        specs.append(KEPT)
    count = len(specs)
    given = 14
    return pl.pallas_call(
        lambda *refs: attend_kernel(*refs[:given], *refs[count:]),
        grid=(1,),
        in_specs=specs,
        out_specs=[one_of((ROWS, width), micro)] + [whole(out.shape) for out in outs],
        out_shape=[jax.ShapeDtypeStruct((ids["key"].shape[0], ROWS, width), BF16)] + outs,
        input_output_aliases=aliases,
        compiler_params=params(),
        cost_estimate=timing(11),
        name="attend",
    )(*ins)


def add_rows(ref, windows, lanes, value):
    start = 0
    for base, count in windows:
        rows = at(base, count)
        ref[rows, lanes] = ref[rows, lanes] + value[start : start + count]
        start += count


def attend_back_kernel(
    where_ref,
    q_ref,
    q3_ref,
    kvp_ref,
    lse_ref,
    lsec_ref,
    lsex_ref,
    oc_ref,
    dout_ref,
    kid_ref,
    qidf_ref,
    qidc_ref,
    fine_ref,
    coarse_ref,
    mask_ref,
    spread_t_ref,
    dq_ref,
    dq3_ref,
    dkv_ref,
    near_ref,
    far_ref,
    top_ref,
    acc_ref,
    dcell_ref,
    delta_ref,
):
    acc_ref[...] = jnp.zeros(acc_ref.shape, F32)
    dcell_ref[...] = jnp.zeros(dcell_ref.shape, F32)
    mask = mask_ref[...]
    scaled = mask * jnp.asarray(0.125, BF16)

    def fine_group(group, carry):
        tiles = [GROUP_BACK * group + index for index in range(GROUP_BACK)]
        units = [(tile, quad) for tile in tiles for quad in range(2)]
        biases = [
            tile_bias(kid_ref, qidf_ref, 8 * tile, fine_windows(tile), FINE_LEVELS, fine_ref[...])
            for tile in tiles
        ]
        at_unit = lambda unit: (at(TILE * unit[0], TILE), pl.ds(QL * unit[1], QL))
        queries = [head_stack(q_ref[at_unit(unit)], scaled) for unit in units]
        douts = [head_stack(dout_ref[(0,) + at_unit(unit)], mask) for unit in units]
        scores = []
        steers = []
        for index, (tile, quad) in enumerate(units):
            keys = gather_rows(kvp_ref, fine_windows(tile), pl.ds(QL * quad, QL))
            scores.append(dot_nt(keys, queries[index]))
            values = jnp.concatenate(
                [
                    gather_rows(kvp_ref, fine_windows(tile), pl.ds(512 + QL * quad, QL)),
                    oc_ref[at(16 * (tile // 2), 16), pl.ds(QL * quad, QL)],
                ],
                axis=0,
            )
            steers.append(dot_nt(values, douts[index]))
        shares = []
        grads = []
        for index, (tile, quad) in enumerate(units):
            lse = lse_ref[pl.ds(2 * tile + quad, 1), :]
            wide = pl.ds(pl.multiple_of(QL * (tile % 8), QL), QL)
            coarse_row = pl.ds(2 * (tile // 8) + quad, 1)
            far_share = jnp.exp(lsex_ref[coarse_row, wide] - lse)
            share = jnp.exp(level_sums(scores[index], FINE_LEVELS) + biases[index // 2] - lse)
            share = jnp.concatenate([share, jnp.where(own_cell(tile), far_share, 0.0)], axis=0)
            weighted = share * steers[index]
            delta = jnp.sum(weighted, axis=0, keepdims=True)
            delta_ref[coarse_row, wide] = far_share * delta
            grad = weighted[0:FINE_KEYS] - share[0:FINE_KEYS] * delta
            grads.append(level_sums(grad, FINE_LEVELS).astype(BF16))
            shares.append(share.astype(BF16))
        dvalues = [dot_nn(share, dout) for share, dout in zip(shares, douts)]
        dkeys = [dot_nn(grad, query) for grad, query in zip(grads, queries)]
        dqueries = []
        for (tile, quad), grad in zip(units, grads):
            keys = gather_rows(kvp_ref, fine_windows(tile), pl.ds(QL * quad, QL))
            dqueries.append(dot_tn(grad, keys))
        for index, (tile, quad) in enumerate(units):
            lanes = pl.ds(QL * quad, QL)
            cells = at(16 * (tile // 2), 16)
            windows = fine_windows(tile)
            add_rows(acc_ref, windows, pl.ds(512 + QL * quad, QL), dvalues[index])
            dcell_ref[cells, lanes] = dcell_ref[cells, lanes] + dvalues[index][FINE_KEYS:]
            add_rows(acc_ref, windows, lanes, dkeys[index])
            dq_ref[at_unit((tile, quad))] = (head_pick(dqueries[index]) * 0.125).astype(BF16)
        return carry

    lax.fori_loop(0, FINE_TILES // GROUP_BACK, fine_group, 0)

    units = [(tile, quad) for tile in range(COARSE_TILES) for quad in range(2)]
    biases = [
        tile_bias(kid_ref, qidc_ref, 8 * tile, coarse_windows(tile), COARSE_LEVELS, coarse_ref[tile])
        for tile in range(COARSE_TILES)
    ]
    at_unit = lambda unit: (pl.ds(TILE * unit[0], TILE), pl.ds(QL * unit[1], QL))
    queries = [head_stack(q3_ref[at_unit(unit)], scaled) for unit in units]
    douts = [head_stack(dcell_ref[at_unit(unit)].astype(BF16), mask) for unit in units]
    terms = []
    for index in range(len(units)):
        terms.extend(three_terms(delta_ref[pl.ds(index, 1), :]))
    terms.extend([terms[-1]] * 4)
    terms = dot_nn(jnp.concatenate(terms, axis=0), spread_t_ref[...])
    steers = []
    scores = []
    for (tile, quad), dout, query in zip(units, douts, queries):
        values = gather_rows(kvp_ref, coarse_windows(tile), pl.ds(512 + QL * quad, QL))
        steers.append(dot_nt(values, dout))
        keys = gather_rows(kvp_ref, coarse_windows(tile), pl.ds(QL * quad, QL))
        scores.append(dot_nt(keys, query))
    shares = []
    grads = []
    for index, (tile, quad) in enumerate(units):
        score = level_sums(scores[index], COARSE_LEVELS) + biases[index // 2]
        share = jnp.exp(score - lsec_ref[pl.ds(index, 1), :])
        part = terms[3 * index : 3 * index + 3]
        delta = part[0:1] + part[1:2] + part[2:3]
        grads.append(level_sums(share * (steers[index] - delta), COARSE_LEVELS).astype(BF16))
        shares.append(share.astype(BF16))
    dvalues = [dot_nn(share, dout) for share, dout in zip(shares, douts)]
    dkeys = [dot_nn(grad, query) for grad, query in zip(grads, queries)]
    dqueries = []
    for (tile, quad), grad in zip(units, grads):
        keys = gather_rows(kvp_ref, coarse_windows(tile), pl.ds(QL * quad, QL))
        dqueries.append(dot_tn(grad, keys))
    for index, (tile, quad) in enumerate(units):
        windows = coarse_windows(tile)
        add_rows(acc_ref, windows, pl.ds(512 + QL * quad, QL), dvalues[index])
        add_rows(acc_ref, windows, pl.ds(QL * quad, QL), dkeys[index])
        dq3_ref[at_unit((tile, quad))] = (head_pick(dqueries[index]) * 0.125).astype(BF16)

    key_lane = lax.broadcasted_iota(jnp.int32, (1, acc_ref.shape[1]), 1) < 512

    def scale(level):
        return jnp.where(key_lane, 0.5 ** STEP[level], 1.0)

    def low(level, start, count):
        return (acc_ref[pl.ds(start, count), :] * scale(level)).astype(BF16)

    def edges(left_ref, right_ref):
        for level in range(LEVELS - 1):
            base = POFF[level]
            edge = pl.ds(HALO * level, HALO)
            left_ref[edge, :] = low(level, base, HALO)
            right_ref[edge, :] = low(level, base + HALO + CELLS[level], HALO)

    piece = where_ref[0]
    pl.when(piece % 2 == 0)(lambda: edges(far_ref, near_ref))
    pl.when(piece % 2 == 1)(lambda: edges(near_ref, far_ref))
    for level in range(LEVELS - 1):
        dkv_ref[pl.ds(OFF[level], CELLS[level]), :] = low(level, POFF[level] + HALO, CELLS[level])
    dkv_ref[pl.ds(OFF[7], 16), :] = jnp.zeros((16, acc_ref.shape[1]), BF16)
    blank = jnp.zeros((PIECE7, acc_ref.shape[1]), F32)

    def high(index):
        rows = pl.ds(pl.multiple_of(POFF[7] + PIECE7 * index, PIECE7), PIECE7)
        return jnp.concatenate([acc_ref[rows, :] * scale(7), blank], axis=0).astype(BF16)

    near_ref[pl.ds(EDGE, 16), :] = jnp.zeros((16, acc_ref.shape[1]), BF16)
    far_ref[pl.ds(EDGE, 16), :] = high(3 - piece)
    top_ref[...] = high((piece + 2) % 4)


def attend_back(micro, where, q, q3, stats, dout, ids, const):
    width = q.shape[1]
    shape = jax.ShapeDtypeStruct
    outs = [
        shape((ROWS, width), BF16),
        shape((ROWS // 8, width), BF16),
        shape((2 * ROWS, 2 * width), BF16),
        shape((EDGES, 2 * width), BF16),
        shape((EDGES, 2 * width), BF16),
        shape((16, 2 * width), BF16),
    ]
    return pl.pallas_call(
        attend_back_kernel,
        grid=(1,),
        in_specs=[SCALAR]
        + [whole(value.shape) for value in (q, q3, *stats)]
        + [one_of((ROWS, width), micro)]
        + id_specs(micro)
        + [whole((8 * QL, QL))],
        out_specs=[whole(out.shape) for out in outs],
        out_shape=outs,
        scratch_shapes=[
            pltpu.VMEM((PADDED, 2 * width), F32),
            pltpu.VMEM((ROWS // 8, width), F32),
            pltpu.VMEM((2 * COARSE_TILES, 8 * QL), F32),
        ],
        compiler_params=params(),
        cost_estimate=timing(17),
        name="attend_back",
    )(where, q, q3, *stats, dout, *id_args(ids, const), const["spread_t"])


MID_ROWS = 512
FF_CHUNK = 512
ROOT = math.sqrt(2.0 / math.pi)


def share_out(send_ref, keep_ref, core, start, piece_of):
    for chip in range(send_ref.shape[0]):
        keep = piece_of(2 * chip + core)
        keep_ref[chip, pl.ds(start, keep.shape[0]), :] = keep
        send_ref[chip, pl.ds(start, keep.shape[0]), :] = piece_of(2 * chip + 1 - core)


def row_piece(ref, shard):
    def piece_of(index):
        return ref[pl.ds(pl.multiple_of(shard * index, shard), shard), :].astype(BF16)

    return piece_of


def middle_kernel(
    where_ref,
    tok_ref,
    cot_ref,
    mixed_ref,
    vec_ref,
    mine_ref,
    other_ref,
    out_ref,
    dmid_ref,
    dmix_ref,
    send_ref,
    keep_ref,
    wo_ref,
    wi_ref,
    wd_ref,
    acc_o,
    acc_i,
    acc_d,
    acc_b,
    acc_s,
    activ_ref,
    grad_ref,
):
    step = pl.program_id(0)
    core = where_ref[1]
    parts = wi_ref.shape[0]
    shard = wo_ref.shape[2]

    @pl.when(step == 0)
    def _():
        acc_o[...] = jnp.zeros(acc_o.shape, F32)
        acc_i[...] = jnp.zeros(acc_i.shape, F32)
        acc_d[...] = jnp.zeros(acc_d.shape, F32)
        acc_b[...] = jnp.zeros(acc_b.shape, F32)
        acc_s[...] = jnp.zeros(acc_s.shape, F32)
        take_weight(wo_ref, 0, mine_ref, other_ref, core, 0)
        for part in range(parts):
            take_weight(wi_ref, part, mine_ref, other_ref, core, shard * (1 + part))
        take_weight(wd_ref, 0, mine_ref, other_ref, core, shard * (1 + parts))

    wo = weight_of(wo_ref, 0)
    pieces = FF_CHUNK // wd_ref.shape[2]
    wi = [weight_of(wi_ref, part) for part in range(parts)]
    wd = [
        wd_ref[0, pieces * part : pieces * (part + 1)].reshape(FF_CHUNK, wo.shape[1])
        for part in range(parts)
    ]
    cot = cot_ref[...]
    top = cot.astype(BF16)
    mixed = mixed_ref[...]
    middle = tok_ref[...] + dot_nn(mixed, wo)
    unit, rate = normalised(middle)
    second = (unit * vec_ref[1:2] + vec_ref[3:4]).astype(BF16)
    result = middle + vec_ref[4:5]
    back = jnp.zeros(cot.shape, F32)
    pres = {}

    def first(part):
        pres[part] = (dot_nn(second, wi[part]) + vec_ref[5 + part : 6 + part], dot_nt(top, wd[part]))

    first(0)
    for part in range(parts):
        if part + 1 < parts:
            first(part + 1)
        pre, grad = pres.pop(part)
        square = pre * pre
        tanh = jnp.tanh(pre * (ROOT + (ROOT * 0.044715) * square))
        half = 0.5 + 0.5 * tanh
        activ = (pre * half).astype(BF16)
        slope = half + (pre * (0.5 - 0.5 * (tanh * tanh))) * (
            ROOT + (ROOT * 3 * 0.044715) * square
        )
        grad = (grad * slope).astype(BF16)
        cols = pl.ds(FF_CHUNK * part, FF_CHUNK)
        activ_ref[:, cols] = activ
        grad_ref[:, cols] = grad
        acc_b[:, cols] = acc_b[:, cols] + fold_rows(grad.astype(F32))
        result = result + dot_nn(activ, wd[part])
        back = back + dot_nt(grad, wi[part])
    out_ref[...] = result
    acc_d[...] = acc_d[...] + dot_tn(activ_ref[...], top)
    for part in range(parts):
        acc_i[part] = acc_i[part] + dot_tn(second, grad_ref[:, pl.ds(FF_CHUNK * part, FF_CHUNK)])
    dmid = cot + norm_back(back * vec_ref[1:2], unit, rate)
    dmid_ref[...] = dmid
    branch = dmid.astype(BF16)
    dmix_ref[...] = dot_nt(branch, wo).astype(BF16)
    acc_o[...] = acc_o[...] + dot_tn(mixed, branch)
    acc_s[0:8, :] = acc_s[0:8, :] + fold_rows(top.astype(F32))
    acc_s[8:16, :] = acc_s[8:16, :] + fold_rows(back * unit)
    acc_s[16:24, :] = acc_s[16:24, :] + fold_rows(back)

    @pl.when(step == pl.num_programs(0) - 1)
    def _():
        share_out(send_ref, keep_ref, core, 0, row_piece(acc_o, shard))
        for part in range(parts):
            share_out(
                send_ref, keep_ref, core, shard * (1 + part), row_piece(acc_i.at[part], shard)
            )
        share_out(send_ref, keep_ref, core, shard * (1 + parts), row_piece(acc_d, shard * parts))
        total = lambda value: jnp.sum(value, axis=0, keepdims=True)
        lines = [total(acc_s[8 * index : 8 * index + 8, :]) for index in range(3)]
        for part in range(parts):
            lines.append(total(acc_b[:, pl.ds(FF_CHUNK * part, FF_CHUNK)]))
        lines.append(jnp.zeros((16 - len(lines), lines[0].shape[1]), F32))
        lines = jnp.concatenate(lines, axis=0).astype(BF16)
        share_out(send_ref, keep_ref, core, shard * (1 + 2 * parts), lambda index: lines)


def middle_part(where, tokens, cot, mixed, vec, mine, other):
    rows, width = tokens.shape
    chips, lines, _ = mine.shape
    shard = width // (2 * chips)
    parts = (lines // shard - 1) // 2
    hidden = parts * FF_CHUNK
    shape = jax.ShapeDtypeStruct
    tiled = pl.BlockSpec((MID_ROWS, width), lambda r: (r, 0))
    shared = shape((chips, lines + 16, width), BF16)
    single = lambda dims: pl.BlockSpec(
        dims, lambda *_: (0,) * len(dims), pipeline_mode=pl.Buffered(1)
    )
    return pl.pallas_call(
        middle_kernel,
        grid=(rows // MID_ROWS,),
        in_specs=[SCALAR, tiled, tiled, tiled, whole(vec.shape), single(mine.shape), single(mine.shape)],
        out_specs=[tiled, tiled, tiled, single(shared.shape), single(shared.shape)],
        out_shape=[
            shape((rows, width), F32),
            shape((rows, width), F32),
            shape((rows, width), BF16),
            shared,
            shared,
        ],
        scratch_shapes=[
            pltpu.VMEM((1, 2 * chips, shard, width), BF16),
            pltpu.VMEM((parts, 2 * chips, shard, FF_CHUNK), BF16),
            pltpu.VMEM((1, 2 * chips, shard * parts, width), BF16),
            pltpu.VMEM((width, width), F32),
            pltpu.VMEM((parts, width, FF_CHUNK), F32),
            pltpu.VMEM((hidden, width), F32),
            pltpu.VMEM((8, hidden), F32),
            pltpu.VMEM((24, width), F32),
            pltpu.VMEM((MID_ROWS, hidden), BF16),
            pltpu.VMEM((MID_ROWS, hidden), BF16),
        ],
        compiler_params=params(),
        cost_estimate=timing(40),
        name="middle",
    )(where, tokens, cot, mixed, vec, mine, other)


def collect_kernel(
    where_ref, tok_ref, dq_ref, dq3_ref, dkv_ref, near_ref, far_ref, across_ref, low_ref, high_ref, *refs, first
):
    if first:
        dp_ref, gw_ref, sum_ref, cells_ref, norm_ref = refs
    else:
        held_ref, held_sum_ref, vec_ref, mine_ref, other_ref = refs[:5]
        dp_ref, send_ref, keep_ref, cells_ref, norm_ref, gw_ref, w_ref = refs[6:]
    piece, core = where_ref[0], where_ref[1]
    cells_ref[...] = dkv_ref[...]

    def add(start, value):
        rows = pl.ds(start, HALO)
        cells_ref[rows, :] = (cells_ref[rows, :].astype(F32) + value.astype(F32)).astype(BF16)

    def edges(left_ref, right_ref):
        for level in range(LEVELS - 1):
            edge = pl.ds(HALO * level, HALO)

            @pl.when(piece > 0)
            def _():
                add(OFF[level], left_ref[edge, :])

            @pl.when(piece < 3)
            def _():
                add(OFF[level] + CELLS[level] - HALO, right_ref[edge, :])

    pl.when(piece % 2 == 0)(lambda: edges(far_ref, near_ref))
    pl.when(piece % 2 == 1)(lambda: edges(near_ref, far_ref))
    add(OFF[7], across_ref[...].astype(F32) + far_ref[pl.ds(EDGE, 16), :].astype(F32))

    sums = [jnp.zeros((8, 512), F32), jnp.zeros((8, 1024), F32)]
    for chunk in range(ROWS // 256):
        rows = pl.ds(256 * chunk, 256)
        norm_ref[rows, :] = normalised(tok_ref[0, rows, :])[0].astype(BF16)
        cells = jnp.concatenate(
            [
                cells_ref[pl.ds(OFF[level] + (256 >> level) * chunk, 256 >> level), :]
                for level in range(1, 5)
            ],
            axis=0,
        )
        dkv = (
            cells_ref[rows, :].astype(F32)
            + dot_nn(low_ref[...], cells)
            + dot_nn(high_ref[rows, :], cells_ref[pl.ds(OFF[5], 64), :])
        ).astype(BF16)
        dq = (
            dq_ref[rows, :].astype(F32)
            + dot_nn(low_ref[:, 192:224], dq3_ref[pl.ds(32 * chunk, 32), :])
        ).astype(BF16)
        dp_ref[0, rows, pl.ds(0, 512)] = dq
        dp_ref[0, rows, pl.ds(512, 1024)] = dkv
        sums = [old + fold_rows(new.astype(F32)) for old, new in zip(sums, (dq, dkv))]
    sums = jnp.concatenate(sums, axis=1)
    if first:
        sum_ref[...] = sums
    else:
        sums = jnp.sum(sums + held_sum_ref[...], axis=0, keepdims=True)
        row = lax.broadcasted_iota(jnp.int32, (VEC, 512), 0)
        lines = vec_ref[...].astype(BF16)
        gain = dot_tn(lines, jnp.where(row == 0, 1.0, 0.0).astype(BF16))
        offset = dot_tn(lines, jnp.where(row == 2, 1.0, 0.0).astype(BF16))
        ones = jnp.ones((8, 512), BF16)
        grad_gain = jnp.zeros((8, 512), F32)
        grad_offset = jnp.zeros((8, 512), F32)
        for index in range(3):
            take_weight(w_ref, index, mine_ref, other_ref, core, w_ref.shape[2] * index)
    for index in range(3):
        grad = dot_tn(norm_ref[...], dp_ref[0, :, pl.ds(512 * index, 512)])
        if first:
            gw_ref[index] = grad
        else:
            grad = grad + held_ref[index]
            total = sums[:, 512 * index : 512 * (index + 1)]
            gw_ref[index] = gain * grad + offset * total
            weight = weight_of(w_ref, index)
            high, middle, _ = three_terms(weight.astype(F32) * grad)
            grad_gain = grad_gain + dot_nt(ones, high) + dot_nt(ones, middle)
            high, middle, low = three_terms(total)
            terms = jnp.concatenate([high, middle, low] + [jnp.zeros_like(low)] * 5, axis=0)
            grad_offset = grad_offset + dot_nt(terms, weight)
    if not first:
        shard = w_ref.shape[2]
        for index in range(3):
            share_out(send_ref, keep_ref, core, shard * index, row_piece(gw_ref.at[index], shard))
        grad_offset = jnp.sum(grad_offset, axis=0, keepdims=True)
        blank = jnp.zeros((VEC - 2, 512), F32)
        lines = jnp.concatenate([grad_gain[0:1], grad_offset, blank], axis=0).astype(BF16)
        share_out(send_ref, keep_ref, core, 3 * shard, lambda index: lines)


def collect(micro, where, tokens, grads, received, const, held=None):
    width = tokens.shape[2]
    shape = jax.ShapeDtypeStruct
    first = held is None
    ins = list(grads) + list(received) + [const["low_t"], const["high_t"]]
    outs = [shape((tokens.shape[0], ROWS, 3 * width), BF16)]
    scratch = [pltpu.VMEM((2 * ROWS, 2 * width), BF16), pltpu.VMEM((ROWS, width), BF16)]
    kept = []
    aliases = {}
    if first:
        outs += [shape((3, width, width), F32), shape((8, 3 * width), F32)]
    else:
        ins += held[1:]
        kept = [held[0]]
        mine = held[-1]
        chips, lines, _ = mine.shape
        shard = width // (2 * chips)
        aliases = {2 + len(ins): 0}
        outs += [shape((chips, lines, width), BF16)] * 2
        scratch.append(pltpu.VMEM((3, width, width), F32))
        scratch.append(pltpu.VMEM((3, 2 * chips, shard, width), BF16))
    specs = [SCALAR, one_of((ROWS, width), micro)] + [whole(value.shape) for value in ins]
    return pl.pallas_call(
        lambda *refs: collect_kernel(*refs, first=first),
        grid=(1,),
        in_specs=specs + [KEPT] * len(kept),
        out_specs=[one_of((ROWS, 3 * width), micro)] + [whole(out.shape) for out in outs[1:]],
        out_shape=outs,
        scratch_shapes=scratch,
        input_output_aliases=aliases,
        compiler_params=params(),
        cost_estimate=timing(8),
        name="collect",
    )(where, tokens, *ins, *kept)


def finish_kernel(where_ref, tok_ref, dmid_ref, dp_ref, vec_ref, mine_ref, other_ref, *refs):
    grad_ref, w_ref = refs[-2:]
    core = where_ref[1]
    for index in range(3):
        take_weight(w_ref, index, mine_ref, other_ref, core, w_ref.shape[2] * index)
    for half in range(2):
        rows = pl.ds(512 * half, 512)
        back = dot_nt(dp_ref[0, rows, pl.ds(0, 512)], weight_of(w_ref, 0))
        for index in range(1, 3):
            back = back + dot_nt(dp_ref[0, rows, pl.ds(512 * index, 512)], weight_of(w_ref, index))
        unit, rate = normalised(tok_ref[0, rows, :])
        grad_ref[0, rows, :] = dmid_ref[0, rows, :] + norm_back(back * vec_ref[0:1], unit, rate)


def finish(micro, where, tokens, dmid, dproj, vec, mine, other, kept):
    width = tokens.shape[2]
    dp = 2 * mine.shape[0]
    ins = [where, tokens, dmid, dproj, vec, mine, other] + ([] if kept is None else [kept])
    return pl.pallas_call(
        finish_kernel,
        grid=(1,),
        in_specs=[
            SCALAR,
            one_of((ROWS, width), micro),
            one_of((ROWS, width), micro),
            one_of((ROWS, 3 * width), micro),
            whole(vec.shape),
            whole(mine.shape),
            whole(other.shape),
        ]
        + [KEPT] * (len(ins) - 7),
        out_specs=one_of((ROWS, width), micro),
        out_shape=jax.ShapeDtypeStruct(tokens.shape, F32),
        scratch_shapes=[pltpu.VMEM((3, dp, width // dp, width), BF16)],
        input_output_aliases={} if kept is None else {7: 0},
        compiler_params=params(),
        cost_estimate=timing(6),
        name="finish",
    )(*ins)


def cell_documents(segments, piece):
    micro, length = segments.shape
    keys = []
    fine = []
    coarse = []
    for level in range(LEVELS):
        cell = 1 << level
        grouped = segments.reshape(micro, length // cell, cell)
        lowest = grouped[:, :, 0]
        highest = grouped[:, :, cell - 1]
        same = lowest == highest
        key = jnp.where(same, lowest, -2)
        query = jnp.where(same, lowest, -1)
        own = lax.dynamic_slice_in_dim(query, piece * CELLS[level], CELLS[level], axis=1)
        if level < LEVELS - 1:
            padded = jnp.pad(key, ((0, 0), (HALO, HALO)), constant_values=-3)
            keys.append(
                lax.dynamic_slice_in_dim(
                    padded, piece * CELLS[level], CELLS[level] + 2 * HALO, axis=1
                )
            )
        else:
            owner = jnp.arange(key.shape[1]) // PIECE7
            counted = (jnp.abs(owner // 2 - piece // 2) == 1) & (jnp.abs(owner - piece) >= 2)
            keys.append(jnp.where(counted[None], key, -3))
        if level < FINE:
            fine.append(jnp.repeat(own, cell, axis=1).reshape(micro, FINE_TILES, 1, TILE))
        else:
            coarse.append(jnp.repeat(own, cell // 8, axis=1).reshape(micro, COARSE_TILES, 1, TILE))

    def rows(parts):
        value = jnp.concatenate(parts, axis=2)
        value = jnp.pad(value, ((0, 0), (0, 0), (0, 8 - len(parts)), (0, 0)))
        return jnp.tile(value, (1, 1, 1, QUAD)).reshape(micro, -1, QL)

    key = jnp.concatenate(keys, axis=1)
    return dict(
        key=jnp.broadcast_to(key[:, :, None], key.shape + (128,)),
        fine=rows(fine),
        coarse=rows(coarse),
    )


def same_core(chips):
    return [[2 * chip + core for chip in range(chips)] for core in range(2)]


def core_swap(value, chips):
    pairs = [(place, place ^ 1) for place in range(2 * chips)]
    return lax.ppermute(value, "dp", pairs)


def chip_exchange(value, chips):
    return lax.all_to_all(value, "dp", 0, 0, axis_index_groups=same_core(chips), tiled=True)


def after(value, *done):
    return lax.optimization_barrier((value,) + done)[0]


def add(left, right):
    return left.astype(F32) + right.astype(F32)


def body(
    tokens,
    segment_ids,
    norm_gains,
    norm_biases,
    qkv_weight,
    out_weight,
    in_weight,
    in_bias,
    down_weight,
    down_bias,
    cotangent,
):
    micro, _, row_count, width = tokens.shape
    pieces = lax.axis_size("sp")
    piece = lax.axis_index("sp")
    assert row_count == ROWS and pieces == 4 and micro == 2
    const = constants()
    tokens = tokens[:, 0]
    cotangent = cotangent[:, 0]
    dp = lax.axis_size("dp")
    place = lax.axis_index("dp")
    chips = dp // 2
    shard = width // dp
    hidden = in_weight.shape[1]
    parts = hidden // FF_CHUNK
    where = jnp.stack([piece, place % 2]).astype(jnp.int32)
    swap = lambda value, bits: lax.ppermute(value, "sp", [(p, p ^ bits) for p in range(pieces)])
    spread = lambda value: chip_exchange(
        jnp.broadcast_to(value[None], (chips,) + value.shape), chips
    )

    def placed(value, start):
        lines = jnp.zeros((value.shape[0], start * value.shape[1]), BF16)
        return lax.dynamic_update_slice(lines, value, (0, place * value.shape[1])).reshape(-1, width)

    small = placed(jnp.concatenate([norm_gains, norm_biases, down_bias[None]]), dp)
    small = jnp.concatenate([small, placed(in_bias[None], dp)])
    small = jnp.pad(small, ((0, VEC - small.shape[0]), (0, 0)))
    mine = spread(jnp.concatenate([qkv_weight.reshape(3 * shard, width), small]))
    ids = cell_documents(segment_ids[:, 0], piece)
    other = core_swap(mine, chips)
    rest = jnp.concatenate(
        [
            out_weight,
            in_weight.reshape(shard, parts, FF_CHUNK).swapaxes(0, 1).reshape(-1, width),
            down_weight,
        ]
    )
    rest_mine = spread(after(rest, other))

    cells, received = [], []
    for m in range(2):
        q, q3, kv, near, far, top, vec = project(m, where, tokens, mine, other, const)
        cells.append((q, q3, kv))
        received.append((swap(near, 1), swap(far, 3), swap(top, 2)))
    mixed, *stat = attend(0, where, cells[0], received[0], None, ids, const)
    stats = [stat]
    rest_mine = after(rest_mine, stat[1])
    rest_other = core_swap(rest_mine, chips)
    mixed, *stat = attend(1, after(where, rest_mine), cells[1], received[1], mixed, ids, const)
    stats.append(stat)

    flat = lambda value: value.reshape(micro * ROWS, width)
    split = lambda value: value.reshape(micro, ROWS, width)
    outputs, dmid, dmix, send, keep = middle_part(
        where, flat(tokens), flat(cotangent), flat(mixed), vec, rest_mine, rest_other
    )

    grads, back = [], []

    def attention_back(m, where):
        dq, dq3, dkv, near, far, top = attend_back(
            m, where, cells[m][0], cells[m][1], stats[m], split(dmix), ids, const
        )
        grads.append((dq, dq3, dkv))
        back.append((swap(near, 1), swap(far, 3), swap(top, 2)))

    come = core_swap(send, chips)
    attention_back(0, where)
    pair = add(keep, after(come, grads[0][1])).astype(BF16)
    come = chip_exchange(pair, chips)
    attention_back(1, after(where, pair))
    dproj, held, sums = collect(0, where, tokens, grads[0], back[0], const)
    total = jnp.sum(after(come, sums).astype(F32), axis=0).astype(BF16)
    come = swap(total, 1)
    dproj, send, keep = collect(
        1, after(where, total), tokens, grads[1], back[1], const, [dproj, held, sums, vec, mine, other]
    )
    qkv_come = core_swap(send, chips)
    total = add(total, after(come, send)).astype(BF16)
    come = swap(total, 3)
    input_grad = finish(0, after(where, total), tokens, split(dmid), dproj, vec, mine, other, None)
    pair = add(keep, after(qkv_come, input_grad)).astype(BF16)
    qkv_come = chip_exchange(pair, chips)
    input_grad = finish(
        1, after(where, pair), tokens, split(dmid), dproj, vec, mine, other, input_grad
    )
    rest = add(total, after(come, input_grad))
    total = jnp.sum(qkv_come.astype(F32), axis=0).astype(BF16)
    total = add(total, swap(total, 1)).astype(BF16)
    total = add(total, swap(total, 3))

    own = lambda value, size: lax.dynamic_slice_in_dim(value, place * size, size, axis=-1)
    small_two = rest[shard * (1 + 2 * parts) :]
    small_one = total[3 * shard :]
    gin = rest[shard : shard * (1 + parts)].reshape(parts, shard, FF_CHUNK).swapaxes(0, 1)
    return (
        outputs.reshape(micro, 1, ROWS, width),
        input_grad[:, None],
        own(jnp.stack([small_one[0], small_two[1]]), shard),
        own(jnp.stack([small_one[1], small_two[2]]), shard),
        total[: 3 * shard].reshape(3, shard, width),
        rest[:shard],
        gin.reshape(shard, hidden),
        own(small_two[3 : 3 + parts].reshape(hidden), hidden // dp),
        rest[shard * (1 + parts) : shard * (1 + 2 * parts)],
        own(small_two[0], shard),
    )


def solution(mesh):
    in_specs = (
        P(None, "dp", "sp", None),
        P(None, "dp", None),
        P(None, "dp"),
        P(None, "dp"),
        P(None, "dp", None),
        P("dp", None),
        P("dp", None),
        P("dp"),
        P("dp", None),
        P("dp"),
        P(None, "dp", "sp", None),
    )
    out_specs = (
        P(None, "dp", "sp", None),
        P(None, "dp", "sp", None),
        P(None, "dp"),
        P(None, "dp"),
        P(None, "dp", None),
        P("dp", None),
        P("dp", None),
        P("dp"),
        P("dp", None),
        P("dp"),
    )
    return jax.shard_map(body, mesh=mesh, in_specs=in_specs, out_specs=out_specs, check_vma=False)
```

```python
import math

import jax
import jax.numpy as jnp
import numpy as np
from jax import lax
from jax.experimental import pallas as pl
from jax.experimental.pallas import tpu as pltpu
from jax.sharding import PartitionSpec as P

HEADS = 8
HEAD_DIM = 64
BLOCK = 16
LEVELS = 8
HALO = 16
TILE = 64
QUAD = 4
QL = QUAD * HEAD_DIM
NEG = -1e30
FINE = 3
ROWS = 1024
EDGE = 112
VEC = 16
GROUP = 8
GROUP_BACK = 4
F32 = jnp.float32
BF16 = jnp.bfloat16

CELLS = [ROWS >> level for level in range(LEVELS)]
OFF = [2 * ROWS - (2 * ROWS >> level) for level in range(LEVELS)]
POFF = []
_at = 0
for _level in range(LEVELS - 1):
    POFF.append(_at)
    _at += CELLS[_level] + 2 * HALO
POFF.append(_at)
PIECE7 = CELLS[LEVELS - 1]
PADDED = _at + 4 * PIECE7
FINE_TILES = ROWS // TILE
COARSE_TILES = ROWS // 8 // TILE
FINE_KEYS = 192
COARSE_KEYS = 256
LN_EPS = 1e-05
VMEM_LIMIT = 62 * 1024 * 1024


def _counts(level, query, key):
    query = query[None, :]
    key = key[:, None]
    near = np.abs(query // 16 - key // 16)
    if level == 0:
        return near <= 1
    return (near == 1) & (np.abs(query // 8 - key // 8) >= 2)


def _bias(parts):
    rows = []
    for level, allowed in parts:
        rows.append(np.where(allowed, np.float32(level * math.log(2.0)), np.float32(NEG)))
    block = np.concatenate(rows, axis=0).astype(np.float32)
    return np.tile(block, (1, QUAD))


def _two_blocks():
    return np.concatenate([np.arange(16) - 16, np.arange(16) + 16])


def fine_bias():
    token = np.arange(TILE)
    return _bias(
        [
            (0, _counts(0, token, np.arange(96) - 16)),
            (1, _counts(1, token // 2, np.arange(64) - 16)),
            (2, _counts(2, token // 4, _two_blocks())),
        ]
    )


def coarse_bias():
    cell = np.arange(TILE)
    out = []
    for tile in range(COARSE_TILES):
        out.append(
            _bias(
                [
                    (3, _counts(3, cell, np.arange(96) - 16)),
                    (4, _counts(4, cell // 2, np.arange(64) - 16)),
                    (5, _counts(5, cell // 4, _two_blocks())),
                    (6, _counts(6, 8 * tile + cell // 8, _two_blocks())),
                    (7, np.ones((4 * PIECE7, TILE), bool)),
                ]
            )
        )
    return np.stack(out)


STEP = [0, 1, 2, 0, 1, 2, 3, 4]


def mean_rows(cell, count):
    return (np.arange(count)[None, :] // cell == np.arange(count // cell)[:, None]).astype(
        np.float32
    ) / cell


def spread_matrix():
    out = np.zeros((QUAD, TILE, 8, QUAD, TILE), np.float32)
    for part in range(8):
        for token in range(TILE):
            for head in range(QUAD):
                out[head, 8 * part + token // 8, part, head, token] = 1.0
    return out.reshape(QL, 8 * QL)


def constants():
    head_mask = np.kron(np.eye(QUAD), np.ones((TILE, HEAD_DIM)))
    low = [mean_rows(1 << level, 256) for level in range(1, 5)]
    high = [mean_rows(1 << level, ROWS) for level in range(5, 8)] + [np.zeros((8, ROWS))]
    key_low = [rows * 0.5 ** STEP[level] for level, rows in zip(range(1, 5), low)]
    key_high = [rows * 0.5**step for step, rows in zip(STEP[5:] + [0], high)]
    as_low = lambda value: jnp.asarray(value.astype(np.float32)).astype(BF16)
    low, high = np.concatenate(low), np.concatenate(high)
    return dict(
        fine=jnp.asarray(fine_bias()),
        coarse=jnp.asarray(coarse_bias()),
        head_mask=as_low(head_mask),
        low=as_low(np.stack([np.concatenate(key_low), low])),
        high=as_low(np.stack([np.concatenate(key_high), high])),
        low_t=as_low(low.T),
        high_t=as_low(high.T),
        spread=as_low(spread_matrix()),
        spread_t=as_low(spread_matrix().T),
    )


def dot_nn(left, right):
    return jnp.dot(left, right, preferred_element_type=F32)


def dot_nt(left, right):
    return lax.dot_general(left, right, (((1,), (1,)), ((), ())), preferred_element_type=F32)


def dot_tn(left, right):
    return lax.dot_general(left, right, (((0,), (0,)), ((), ())), preferred_element_type=F32)


def at(start, size):
    return pl.ds(pl.multiple_of(start, 16), size)


def whole(shape):
    zeros = (0,) * len(shape)
    return pl.BlockSpec(shape, lambda *_: zeros)


def one_of(shape, micro):
    zeros = (0,) * len(shape)
    return pl.BlockSpec((1,) + shape, lambda *_: (micro,) + zeros)


def each_of(shape):
    zeros = (0,) * len(shape)
    return pl.BlockSpec((1,) + shape, lambda step: (step,) + zeros)


SCALAR = pl.BlockSpec(memory_space=pltpu.SMEM)
KEPT = pl.BlockSpec(memory_space=pl.ANY)


def timing(micros):
    return pl.CostEstimate(
        flops=int(micros * 4e8), bytes_accessed=int(micros * 3e6), transcendentals=0
    )


def params():
    return pltpu.CompilerParams(
        dimension_semantics=("arbitrary",), vmem_limit_bytes=VMEM_LIMIT
    )


def normalised(rows):
    center = rows - jnp.mean(rows, axis=-1, keepdims=True)
    spread = jnp.mean(center * center, axis=-1, keepdims=True)
    rate = lax.rsqrt(spread + LN_EPS)
    return center * rate, rate


def norm_back(grad, unit, rate):
    mean_grad = jnp.mean(grad, axis=-1, keepdims=True)
    mean_dot = jnp.mean(grad * unit, axis=-1, keepdims=True)
    return rate * (grad - mean_grad - unit * mean_dot)


def fold_rows(value):
    return jnp.sum(value.reshape(-1, 8, value.shape[-1]), axis=0)


def take_weight(target, index, mine, other, core, start):
    chips, shard = mine.shape[0], target.shape[2]
    for chip in range(chips):
        target[index, 2 * chip + core] = mine[chip, pl.ds(start, shard), :]
        target[index, 2 * chip + 1 - core] = other[chip, pl.ds(start, shard), :]


def weight_of(ref, index):
    return ref[index].reshape(ref.shape[1] * ref.shape[2], ref.shape[3])


def project_kernel(
    where_ref,
    tok_ref,
    mine_ref,
    other_ref,
    low_ref,
    high_ref,
    q_ref,
    q3_ref,
    kv_ref,
    near_ref,
    far_ref,
    top_ref,
    vec_ref,
    w_ref,
    norm_ref,
):
    piece, core = where_ref[0], where_ref[1]
    shard = w_ref.shape[2]

    @pl.when(pl.program_id(0) == 0)
    def _():
        for index in range(3):
            take_weight(w_ref, index, mine_ref, other_ref, core, shard * index)
        vec = jnp.zeros(vec_ref.shape, F32)
        for chip in range(mine_ref.shape[0]):
            for ref in (mine_ref, other_ref):
                vec = vec + ref[chip, pl.ds(3 * shard, VEC), :].astype(F32)
        vec_ref[...] = vec

    for chunk in range(ROWS // 256):
        rows = pl.ds(256 * chunk, 256)
        unit, _ = normalised(tok_ref[0, rows, :])
        norm_ref[rows, :] = (unit * vec_ref[0:1] + vec_ref[2:3]).astype(BF16)
    for half in range(2):
        rows = pl.ds(512 * half, 512)
        for index in range(3):
            value = dot_nn(norm_ref[rows, :], weight_of(w_ref, index)).astype(BF16)
            if index == 0:
                q_ref[0, rows, :] = value
            else:
                kv_ref[0, rows, pl.ds(512 * (index - 1), 512)] = value
    for chunk in range(ROWS // 256):
        rows = pl.ds(256 * chunk, 256)
        q3_ref[0, pl.ds(32 * chunk, 32), :] = dot_nn(
            low_ref[1, 192:224, :], q_ref[0, rows, :]
        ).astype(BF16)
        for part in range(2):
            lanes = pl.ds(512 * part, 512)
            cells = dot_nn(low_ref[part], kv_ref[0, rows, lanes]).astype(BF16)
            start = 0
            for level in range(1, 5):
                count = 256 >> level
                kv_ref[0, pl.ds(OFF[level] + count * chunk, count), lanes] = cells[
                    start : start + count
                ]
                start += count
    for part in range(2):
        lanes = pl.ds(512 * part, 512)
        kv_ref[0, pl.ds(OFF[5], 64), lanes] = dot_nn(
            high_ref[part], kv_ref[0, pl.ds(0, ROWS), lanes]
        ).astype(BF16)

    def edges(left_ref, right_ref):
        for level in range(LEVELS - 1):
            edge = pl.ds(HALO * level, HALO)
            left_ref[0, edge, :] = kv_ref[0, pl.ds(OFF[level], HALO), :]
            right_ref[0, edge, :] = kv_ref[0, pl.ds(OFF[level] + CELLS[level] - HALO, HALO), :]

    pl.when(piece % 2 == 0)(lambda: edges(far_ref, near_ref))
    pl.when(piece % 2 == 1)(lambda: edges(near_ref, far_ref))
    top_ref[0] = kv_ref[0, pl.ds(OFF[7], 16), :]


def cell_shapes(width):
    return [(ROWS, width), (ROWS // 8, width), (2 * ROWS, 2 * width)]


def edge_shapes(width):
    return [(EDGE, 2 * width), (EDGE, 2 * width), (16, 2 * width)]


def project(where, tokens, mine, other, const):
    micro, _, width = tokens.shape
    shape = jax.ShapeDtypeStruct
    shard = width // (2 * mine.shape[0])
    outs = cell_shapes(width) + edge_shapes(width)
    return pl.pallas_call(
        project_kernel,
        grid=(micro,),
        in_specs=[
            SCALAR,
            each_of((ROWS, width)),
            whole(mine.shape),
            whole(other.shape),
            whole((2, 240, 256)),
            whole((2, 64, ROWS)),
        ],
        out_specs=[each_of(out) for out in outs] + [whole((VEC, width))],
        out_shape=[shape((micro,) + out, BF16) for out in outs] + [shape((VEC, width), F32)],
        scratch_shapes=[
            pltpu.VMEM((3, width // shard, shard, width), BF16),
            pltpu.VMEM((ROWS, width), BF16),
        ],
        compiler_params=params(),
        cost_estimate=timing(13),
        name="project",
    )(where, tokens, mine, other, const["low"], const["high"])


def fine_windows(tile):
    return [
        (POFF[0] + 64 * tile, 96),
        (POFF[1] + 32 * tile, 64),
        (POFF[2] + 16 * tile, 16),
        (POFF[2] + 16 * tile + 32, 16),
    ]


def coarse_windows(tile):
    return [
        (POFF[3] + 64 * tile, 96),
        (POFF[4] + 32 * tile, 64),
        (POFF[5] + 16 * tile, 16),
        (POFF[5] + 16 * tile + 32, 16),
        (POFF[6], 16),
        (POFF[6] + 32, 16),
        (POFF[7], 32),
    ]


FINE_LEVELS = [96, 64, 32]
COARSE_LEVELS = [96, 64, 32, 32, 32]


def gather_rows(ref, windows, lanes):
    return jnp.concatenate([ref[0, at(start, size), lanes] for start, size in windows], axis=0)


def tile_bias(kid_ref, qid_ref, row, windows, levels, bias):
    keys = jnp.concatenate([kid_ref[0, at(start, size), :] for start, size in windows], axis=0)
    keys = jnp.concatenate([keys, keys], axis=1)
    out = []
    start = 0
    for index, count in enumerate(levels):
        part = slice(start, start + count)
        owner = qid_ref[0, pl.ds(row + index, 1), :]
        out.append(jnp.where(keys[part] == owner, bias[part], NEG))
        start += count
    return jnp.concatenate(out, axis=0)


def lane_sums(value, steps):
    halves = []
    for half in range(2):
        part = value[:, 128 * half : 128 * (half + 1)]
        lane = lax.broadcasted_iota(jnp.int32, part.shape, 1)
        for step in range(steps):
            size = 1 << step
            first = (lane & size) == 0
            part = part + jnp.where(
                first, pltpu.roll(part, 128 - size, 1), pltpu.roll(part, size, 1)
            )
        halves.append(part)
    return jnp.concatenate(halves, axis=1)


def level_sums(value, levels):
    out = [value[0 : levels[0]]]
    start = levels[0]
    for index, count in enumerate(levels[1:]):
        out.append(lane_sums(value[start : start + count], index + 1))
        start += count
    return jnp.concatenate(out, axis=0)


def head_stack(value, mask):
    return jnp.concatenate([value] * QUAD, axis=0) * mask


def head_pick(stacked):
    lane = lax.broadcasted_iota(jnp.int32, (TILE, QL), 1) // HEAD_DIM
    out = stacked[0:TILE]
    for head in range(1, QUAD):
        out = jnp.where(lane == head, stacked[TILE * head : TILE * (head + 1)], out)
    return out


def three_terms(row):
    high = row.astype(BF16)
    rest = row - high.astype(F32)
    middle = rest.astype(BF16)
    low = (rest - middle.astype(F32)).astype(BF16)
    return high, middle, low


def own_cell(tile):
    cell = lax.broadcasted_iota(jnp.int32, (16, QL), 0)
    token = lax.broadcasted_iota(jnp.int32, (16, QL), 1) % TILE
    return cell == 8 * (tile % 2) + token // 8


def attend_kernel(
    where_ref,
    q_ref,
    q3_ref,
    kv_ref,
    near_ref,
    far_ref,
    across_ref,
    ends_ref,
    kid_ref,
    qidf_ref,
    qidc_ref,
    fine_ref,
    coarse_ref,
    mask_ref,
    spread_ref,
    mixed_ref,
    kvp_ref,
    lse_ref,
    lsec_ref,
    lsex_ref,
    oc_ref,
):
    piece = where_ref[0]

    def edges(left_ref, right_ref):
        for level in range(LEVELS - 1):
            base = POFF[level]
            edge = pl.ds(HALO * level, HALO)
            kvp_ref[0, pl.ds(base, HALO), :] = left_ref[0, edge, :]
            kvp_ref[0, pl.ds(base + HALO + CELLS[level], HALO), :] = right_ref[0, edge, :]

    pl.when(piece % 2 == 0)(lambda: edges(far_ref, near_ref))
    pl.when(piece % 2 == 1)(lambda: edges(near_ref, far_ref))
    for level in range(LEVELS - 1):
        count = CELLS[level]
        kvp_ref[0, pl.ds(POFF[level] + HALO, count), :] = kv_ref[0, pl.ds(OFF[level], count), :]
    across = across_ref[0].astype(F32)[0:PIECE7]
    ends = ends_ref[0].astype(F32)[0:PIECE7]
    tops = []
    for owner in range(4):
        top = jnp.where(owner == (piece + 2) % 4, across, jnp.where(owner == 3 - piece, ends, 0.0))
        tops.append(top)
    kvp_ref[0, pl.ds(POFF[7], 4 * PIECE7), :] = jnp.concatenate(tops, axis=0).astype(BF16)
    mask = mask_ref[...]
    scaled = mask * jnp.asarray(0.125, BF16)

    units = [(tile, quad) for tile in range(COARSE_TILES) for quad in range(2)]
    biases = [
        tile_bias(kid_ref, qidc_ref, 8 * tile, coarse_windows(tile), COARSE_LEVELS, coarse_ref[tile])
        for tile in range(COARSE_TILES)
    ]
    scores = []
    for tile, quad in units:
        lanes = pl.ds(QL * quad, QL)
        query = head_stack(q3_ref[0, pl.ds(TILE * tile, TILE), lanes], scaled)
        scores.append(dot_nt(gather_rows(kvp_ref, coarse_windows(tile), lanes), query))
    shares = []
    terms = []
    for index, (tile, quad) in enumerate(units):
        score = level_sums(scores[index], COARSE_LEVELS) + biases[index // 2]
        top = jnp.max(score, axis=0, keepdims=True)
        share = jnp.exp(score - top)
        total = jnp.sum(share, axis=0, keepdims=True)
        lse = top + jnp.log(total)
        lsec_ref[0, pl.ds(index, 1), :] = lse
        terms.extend(three_terms(lse))
        shares.append((share * (1.0 / total)).astype(BF16))
    results = []
    for (tile, quad), share in zip(units, shares):
        values = gather_rows(kvp_ref, coarse_windows(tile), pl.ds(512 + QL * quad, QL))
        results.append(dot_tn(share, values))
    terms.extend([terms[-1]] * 4)
    terms = dot_nn(jnp.concatenate(terms, axis=0), spread_ref[...])
    for index, (tile, quad) in enumerate(units):
        oc_ref[0, pl.ds(TILE * tile, TILE), pl.ds(QL * quad, QL)] = head_pick(
            results[index]
        ).astype(BF16)
        part = terms[3 * index : 3 * index + 3]
        lsex_ref[0, pl.ds(index, 1), :] = part[0:1] + part[1:2] + part[2:3]

    def fine_group(group, carry):
        tiles = [GROUP * group + index for index in range(GROUP)]
        units = [(tile, quad) for tile in tiles for quad in range(2)]
        biases = [
            tile_bias(kid_ref, qidf_ref, 8 * tile, fine_windows(tile), FINE_LEVELS, fine_ref[...])
            for tile in tiles
        ]
        scores = []
        for tile, quad in units:
            lanes = pl.ds(QL * quad, QL)
            query = head_stack(q_ref[0, at(TILE * tile, TILE), lanes], scaled)
            scores.append(dot_nt(gather_rows(kvp_ref, fine_windows(tile), lanes), query))
        shares = []
        for index, (tile, quad) in enumerate(units):
            score = level_sums(scores[index], FINE_LEVELS) + biases[index // 2]
            far = lsex_ref[
                0, pl.ds(2 * (tile // 8) + quad, 1), pl.ds(pl.multiple_of(QL * (tile % 8), QL), QL)
            ]
            top = jnp.maximum(jnp.max(score, axis=0, keepdims=True), far)
            share = jnp.exp(score - top)
            far_share = jnp.exp(far - top)
            total = jnp.sum(share, axis=0, keepdims=True) + far_share
            lse_ref[0, pl.ds(2 * tile + quad, 1), :] = top + jnp.log(total)
            inverse = 1.0 / total
            shares.append(
                jnp.concatenate(
                    [share * inverse, jnp.where(own_cell(tile), far_share * inverse, 0.0)], axis=0
                ).astype(BF16)
            )
        results = []
        for (tile, quad), share in zip(units, shares):
            values = jnp.concatenate(
                [
                    gather_rows(kvp_ref, fine_windows(tile), pl.ds(512 + QL * quad, QL)),
                    oc_ref[0, at(16 * (tile // 2), 16), pl.ds(QL * quad, QL)],
                ],
                axis=0,
            )
            results.append(dot_tn(share, values))
        for (tile, quad), result in zip(units, results):
            mixed_ref[0, at(TILE * tile, TILE), pl.ds(QL * quad, QL)] = head_pick(result).astype(
                BF16
            )
        return carry

    lax.fori_loop(0, FINE_TILES // GROUP, fine_group, 0)


def stat_shapes(width):
    return [
        ((PADDED, 2 * width), BF16),
        ((2 * FINE_TILES, QL), F32),
        ((2 * COARSE_TILES, QL), F32),
        ((2 * COARSE_TILES, 8 * QL), F32),
        ((ROWS // 8, width), BF16),
    ]


def id_specs(spec):
    return [
        spec((PADDED, 128)),
        spec((8 * FINE_TILES, QL)),
        spec((8 * COARSE_TILES, QL)),
        whole((FINE_KEYS, QL)),
        whole((COARSE_TILES, COARSE_KEYS, QL)),
        whole((QL, QL)),
    ]


def id_args(ids, const):
    return [ids["key"], ids["fine"], ids["coarse"], const["fine"], const["coarse"], const["head_mask"]]


def attend(where, cells, received, ids, const):
    micro, _, width = cells[0].shape
    outs = [((ROWS, width), BF16)] + stat_shapes(width)
    ins = list(cells) + list(received)
    return pl.pallas_call(
        attend_kernel,
        grid=(micro,),
        in_specs=[SCALAR]
        + [each_of(value.shape[1:]) for value in ins]
        + id_specs(each_of)
        + [whole((QL, 8 * QL))],
        out_specs=[each_of(dims) for dims, _ in outs],
        out_shape=[jax.ShapeDtypeStruct((micro,) + dims, kind) for dims, kind in outs],
        compiler_params=params(),
        cost_estimate=timing(23),
        name="attend",
    )(where, *ins, *id_args(ids, const), const["spread"])


def add_rows(ref, windows, lanes, value):
    start = 0
    for base, count in windows:
        rows = at(base, count)
        ref[rows, lanes] = ref[rows, lanes] + value[start : start + count]
        start += count


def attend_back_kernel(
    where_ref,
    q_ref,
    q3_ref,
    kvp_ref,
    lse_ref,
    lsec_ref,
    lsex_ref,
    oc_ref,
    dout_ref,
    kid_ref,
    qidf_ref,
    qidc_ref,
    fine_ref,
    coarse_ref,
    mask_ref,
    spread_t_ref,
    dq_ref,
    dq3_ref,
    dkv_ref,
    near_ref,
    far_ref,
    across_ref,
    ends_ref,
    acc_ref,
    dcell_ref,
    delta_ref,
):
    acc_ref[...] = jnp.zeros(acc_ref.shape, F32)
    dcell_ref[...] = jnp.zeros(dcell_ref.shape, F32)
    mask = mask_ref[...]
    scaled = mask * jnp.asarray(0.125, BF16)

    def fine_group(group, carry):
        tiles = [GROUP_BACK * group + index for index in range(GROUP_BACK)]
        units = [(tile, quad) for tile in tiles for quad in range(2)]
        biases = [
            tile_bias(kid_ref, qidf_ref, 8 * tile, fine_windows(tile), FINE_LEVELS, fine_ref[...])
            for tile in tiles
        ]
        at_unit = lambda unit: (at(TILE * unit[0], TILE), pl.ds(QL * unit[1], QL))
        queries = [head_stack(q_ref[(0,) + at_unit(unit)], scaled) for unit in units]
        douts = [head_stack(dout_ref[(0,) + at_unit(unit)], mask) for unit in units]
        scores = []
        steers = []
        for index, (tile, quad) in enumerate(units):
            keys = gather_rows(kvp_ref, fine_windows(tile), pl.ds(QL * quad, QL))
            scores.append(dot_nt(keys, queries[index]))
            values = jnp.concatenate(
                [
                    gather_rows(kvp_ref, fine_windows(tile), pl.ds(512 + QL * quad, QL)),
                    oc_ref[0, at(16 * (tile // 2), 16), pl.ds(QL * quad, QL)],
                ],
                axis=0,
            )
            steers.append(dot_nt(values, douts[index]))
        shares = []
        grads = []
        for index, (tile, quad) in enumerate(units):
            lse = lse_ref[0, pl.ds(2 * tile + quad, 1), :]
            wide = pl.ds(pl.multiple_of(QL * (tile % 8), QL), QL)
            coarse_row = pl.ds(2 * (tile // 8) + quad, 1)
            far_share = jnp.exp(lsex_ref[0, coarse_row, wide] - lse)
            share = jnp.exp(level_sums(scores[index], FINE_LEVELS) + biases[index // 2] - lse)
            share = jnp.concatenate([share, jnp.where(own_cell(tile), far_share, 0.0)], axis=0)
            weighted = share * steers[index]
            delta = jnp.sum(weighted, axis=0, keepdims=True)
            delta_ref[coarse_row, wide] = far_share * delta
            grad = weighted[0:FINE_KEYS] - share[0:FINE_KEYS] * delta
            grads.append(level_sums(grad, FINE_LEVELS).astype(BF16))
            shares.append(share.astype(BF16))
        dvalues = [dot_nn(share, dout) for share, dout in zip(shares, douts)]
        dkeys = [dot_nn(grad, query) for grad, query in zip(grads, queries)]
        dqueries = []
        for (tile, quad), grad in zip(units, grads):
            keys = gather_rows(kvp_ref, fine_windows(tile), pl.ds(QL * quad, QL))
            dqueries.append(dot_tn(grad, keys))
        for index, (tile, quad) in enumerate(units):
            lanes = pl.ds(QL * quad, QL)
            cells = at(16 * (tile // 2), 16)
            windows = fine_windows(tile)
            add_rows(acc_ref, windows, pl.ds(512 + QL * quad, QL), dvalues[index])
            dcell_ref[cells, lanes] = dcell_ref[cells, lanes] + dvalues[index][FINE_KEYS:]
            add_rows(acc_ref, windows, lanes, dkeys[index])
            dq_ref[at_unit((tile, quad))] = (head_pick(dqueries[index]) * 0.125).astype(BF16)
        return carry

    lax.fori_loop(0, FINE_TILES // GROUP_BACK, fine_group, 0)

    units = [(tile, quad) for tile in range(COARSE_TILES) for quad in range(2)]
    biases = [
        tile_bias(kid_ref, qidc_ref, 8 * tile, coarse_windows(tile), COARSE_LEVELS, coarse_ref[tile])
        for tile in range(COARSE_TILES)
    ]
    at_unit = lambda unit: (pl.ds(TILE * unit[0], TILE), pl.ds(QL * unit[1], QL))
    queries = [head_stack(q3_ref[(0,) + at_unit(unit)], scaled) for unit in units]
    douts = [head_stack(dcell_ref[at_unit(unit)].astype(BF16), mask) for unit in units]
    terms = []
    for index in range(len(units)):
        terms.extend(three_terms(delta_ref[pl.ds(index, 1), :]))
    terms.extend([terms[-1]] * 4)
    terms = dot_nn(jnp.concatenate(terms, axis=0), spread_t_ref[...])
    steers = []
    scores = []
    for (tile, quad), dout, query in zip(units, douts, queries):
        values = gather_rows(kvp_ref, coarse_windows(tile), pl.ds(512 + QL * quad, QL))
        steers.append(dot_nt(values, dout))
        keys = gather_rows(kvp_ref, coarse_windows(tile), pl.ds(QL * quad, QL))
        scores.append(dot_nt(keys, query))
    shares = []
    grads = []
    for index, (tile, quad) in enumerate(units):
        score = level_sums(scores[index], COARSE_LEVELS) + biases[index // 2]
        share = jnp.exp(score - lsec_ref[0, pl.ds(index, 1), :])
        part = terms[3 * index : 3 * index + 3]
        delta = part[0:1] + part[1:2] + part[2:3]
        grads.append(level_sums(share * (steers[index] - delta), COARSE_LEVELS).astype(BF16))
        shares.append(share.astype(BF16))
    dvalues = [dot_nn(share, dout) for share, dout in zip(shares, douts)]
    dkeys = [dot_nn(grad, query) for grad, query in zip(grads, queries)]
    dqueries = []
    for (tile, quad), grad in zip(units, grads):
        keys = gather_rows(kvp_ref, coarse_windows(tile), pl.ds(QL * quad, QL))
        dqueries.append(dot_tn(grad, keys))
    for index, (tile, quad) in enumerate(units):
        windows = coarse_windows(tile)
        add_rows(acc_ref, windows, pl.ds(512 + QL * quad, QL), dvalues[index])
        add_rows(acc_ref, windows, pl.ds(QL * quad, QL), dkeys[index])
        dq3_ref[at_unit((tile, quad))] = (head_pick(dqueries[index]) * 0.125).astype(BF16)

    key_lane = lax.broadcasted_iota(jnp.int32, (1, acc_ref.shape[1]), 1) < 512

    def scale(level):
        return jnp.where(key_lane, 0.5 ** STEP[level], 1.0)

    def low(level, start, count):
        return (acc_ref[pl.ds(start, count), :] * scale(level)).astype(BF16)

    def edges(left_ref, right_ref):
        for level in range(LEVELS - 1):
            base = POFF[level]
            edge = pl.ds(HALO * level, HALO)
            left_ref[edge, :] = low(level, base, HALO)
            right_ref[edge, :] = low(level, base + HALO + CELLS[level], HALO)

    piece = where_ref[0]
    pl.when(piece % 2 == 0)(lambda: edges(far_ref, near_ref))
    pl.when(piece % 2 == 1)(lambda: edges(near_ref, far_ref))
    for level in range(LEVELS - 1):
        dkv_ref[pl.ds(OFF[level], CELLS[level]), :] = low(level, POFF[level] + HALO, CELLS[level])
    dkv_ref[pl.ds(OFF[7], 16), :] = jnp.zeros((16, acc_ref.shape[1]), BF16)
    blank = jnp.zeros((PIECE7, acc_ref.shape[1]), F32)

    def high(index):
        rows = pl.ds(pl.multiple_of(POFF[7] + PIECE7 * index, PIECE7), PIECE7)
        return jnp.concatenate([acc_ref[rows, :] * scale(7), blank], axis=0).astype(BF16)

    ends_ref[...] = high(3 - piece)
    across_ref[...] = high((piece + 2) % 4)


def attend_back(micro, where, cells, stats, dout, ids, const):
    width = dout.shape[2]
    shape = jax.ShapeDtypeStruct
    outs = cell_shapes(width) + edge_shapes(width) + edge_shapes(width)[2:]
    one = lambda dims: one_of(dims, micro)
    ins = list(cells[:2]) + list(stats) + [dout]
    return pl.pallas_call(
        attend_back_kernel,
        grid=(1,),
        in_specs=[SCALAR]
        + [one(value.shape[1:]) for value in ins]
        + id_specs(one)
        + [whole((8 * QL, QL))],
        out_specs=[whole(out) for out in outs],
        out_shape=[shape(out, BF16) for out in outs],
        scratch_shapes=[
            pltpu.VMEM((PADDED, 2 * width), F32),
            pltpu.VMEM((ROWS // 8, width), F32),
            pltpu.VMEM((2 * COARSE_TILES, 8 * QL), F32),
        ],
        compiler_params=params(),
        cost_estimate=timing(20),
        name="attend_back",
    )(where, *ins, *id_args(ids, const), const["spread_t"])


MID_ROWS = 512
FF_CHUNK = 512
ROOT = math.sqrt(2.0 / math.pi)


def share_out(send_ref, keep_ref, core, start, piece_of):
    for chip in range(send_ref.shape[0]):
        keep = piece_of(2 * chip + core)
        keep_ref[chip, pl.ds(start, keep.shape[0]), :] = keep
        send_ref[chip, pl.ds(start, keep.shape[0]), :] = piece_of(2 * chip + 1 - core)


def row_piece(ref, shard):
    def piece_of(index):
        return ref[pl.ds(pl.multiple_of(shard * index, shard), shard), :].astype(BF16)

    return piece_of


def middle_kernel(
    where_ref,
    tok_ref,
    cot_ref,
    mixed_ref,
    vec_ref,
    mine_ref,
    other_ref,
    out_ref,
    dmid_ref,
    dmix_ref,
    send_ref,
    keep_ref,
    wo_ref,
    wi_ref,
    wd_ref,
    acc_o,
    acc_i,
    acc_d,
    acc_b,
    acc_s,
    activ_ref,
    grad_ref,
):
    step = pl.program_id(0)
    core = where_ref[1]
    parts = wi_ref.shape[0]
    shard = wo_ref.shape[2]

    @pl.when(step == 0)
    def _():
        acc_o[...] = jnp.zeros(acc_o.shape, F32)
        acc_i[...] = jnp.zeros(acc_i.shape, F32)
        acc_d[...] = jnp.zeros(acc_d.shape, F32)
        acc_b[...] = jnp.zeros(acc_b.shape, F32)
        acc_s[...] = jnp.zeros(acc_s.shape, F32)
        take_weight(wo_ref, 0, mine_ref, other_ref, core, 0)
        for part in range(parts):
            take_weight(wi_ref, part, mine_ref, other_ref, core, shard * (1 + part))
        take_weight(wd_ref, 0, mine_ref, other_ref, core, shard * (1 + parts))

    wo = weight_of(wo_ref, 0)
    pieces = FF_CHUNK // wd_ref.shape[2]
    wi = [weight_of(wi_ref, part) for part in range(parts)]
    wd = [
        wd_ref[0, pieces * part : pieces * (part + 1)].reshape(FF_CHUNK, wo.shape[1])
        for part in range(parts)
    ]
    cot = cot_ref[...]
    top = cot.astype(BF16)
    mixed = mixed_ref[...]
    middle = tok_ref[...] + dot_nn(mixed, wo)
    unit, rate = normalised(middle)
    second = (unit * vec_ref[1:2] + vec_ref[3:4]).astype(BF16)
    result = middle + vec_ref[4:5]
    back = jnp.zeros(cot.shape, F32)
    pres = {}

    def first(part):
        pres[part] = (dot_nn(second, wi[part]) + vec_ref[5 + part : 6 + part], dot_nt(top, wd[part]))

    first(0)
    for part in range(parts):
        if part + 1 < parts:
            first(part + 1)
        pre, grad = pres.pop(part)
        square = pre * pre
        tanh = jnp.tanh(pre * (ROOT + (ROOT * 0.044715) * square))
        half = 0.5 + 0.5 * tanh
        activ = (pre * half).astype(BF16)
        slope = half + (pre * (0.5 - 0.5 * (tanh * tanh))) * (
            ROOT + (ROOT * 3 * 0.044715) * square
        )
        grad = (grad * slope).astype(BF16)
        cols = pl.ds(FF_CHUNK * part, FF_CHUNK)
        activ_ref[:, cols] = activ
        grad_ref[:, cols] = grad
        acc_b[:, cols] = acc_b[:, cols] + fold_rows(grad.astype(F32))
        result = result + dot_nn(activ, wd[part])
        back = back + dot_nt(grad, wi[part])
    out_ref[...] = result
    acc_d[...] = acc_d[...] + dot_tn(activ_ref[...], top)
    for part in range(parts):
        acc_i[part] = acc_i[part] + dot_tn(second, grad_ref[:, pl.ds(FF_CHUNK * part, FF_CHUNK)])
    dmid = cot + norm_back(back * vec_ref[1:2], unit, rate)
    dmid_ref[...] = dmid
    branch = dmid.astype(BF16)
    dmix_ref[...] = dot_nt(branch, wo).astype(BF16)
    acc_o[...] = acc_o[...] + dot_tn(mixed, branch)
    acc_s[0:8, :] = acc_s[0:8, :] + fold_rows(top.astype(F32))
    acc_s[8:16, :] = acc_s[8:16, :] + fold_rows(back * unit)
    acc_s[16:24, :] = acc_s[16:24, :] + fold_rows(back)

    @pl.when(step == pl.num_programs(0) - 1)
    def _():
        share_out(send_ref, keep_ref, core, 0, row_piece(acc_o, shard))
        for part in range(parts):
            share_out(
                send_ref, keep_ref, core, shard * (1 + part), row_piece(acc_i.at[part], shard)
            )
        share_out(send_ref, keep_ref, core, shard * (1 + parts), row_piece(acc_d, shard * parts))
        total = lambda value: jnp.sum(value, axis=0, keepdims=True)
        lines = [total(acc_s[8 * index : 8 * index + 8, :]) for index in range(3)]
        for part in range(parts):
            lines.append(total(acc_b[:, pl.ds(FF_CHUNK * part, FF_CHUNK)]))
        lines.append(jnp.zeros((16 - len(lines), lines[0].shape[1]), F32))
        lines = jnp.concatenate(lines, axis=0).astype(BF16)
        share_out(send_ref, keep_ref, core, shard * (1 + 2 * parts), lambda index: lines)


def middle_part(where, tokens, cot, mixed, vec, mine, other):
    rows, width = tokens.shape
    chips, lines, _ = mine.shape
    shard = width // (2 * chips)
    parts = (lines // shard - 1) // 2
    hidden = parts * FF_CHUNK
    shape = jax.ShapeDtypeStruct
    tiled = pl.BlockSpec((MID_ROWS, width), lambda r: (r, 0))
    shared = shape((chips, lines + 16, width), BF16)
    single = lambda dims: pl.BlockSpec(
        dims, lambda *_: (0,) * len(dims), pipeline_mode=pl.Buffered(1)
    )
    return pl.pallas_call(
        middle_kernel,
        grid=(rows // MID_ROWS,),
        in_specs=[SCALAR, tiled, tiled, tiled, whole(vec.shape), single(mine.shape), single(mine.shape)],
        out_specs=[tiled, tiled, tiled, single(shared.shape), single(shared.shape)],
        out_shape=[
            shape((rows, width), F32),
            shape((rows, width), F32),
            shape((rows, width), BF16),
            shared,
            shared,
        ],
        scratch_shapes=[
            pltpu.VMEM((1, 2 * chips, shard, width), BF16),
            pltpu.VMEM((parts, 2 * chips, shard, FF_CHUNK), BF16),
            pltpu.VMEM((1, 2 * chips, shard * parts, width), BF16),
            pltpu.VMEM((width, width), F32),
            pltpu.VMEM((parts, width, FF_CHUNK), F32),
            pltpu.VMEM((hidden, width), F32),
            pltpu.VMEM((8, hidden), F32),
            pltpu.VMEM((24, width), F32),
            pltpu.VMEM((MID_ROWS, hidden), BF16),
            pltpu.VMEM((MID_ROWS, hidden), BF16),
        ],
        compiler_params=params(),
        cost_estimate=timing(40),
        name="middle",
    )(where, tokens, cot, mixed, vec, mine, other)


def collect_kernel(
    where_ref, tok_ref, dq_ref, dq3_ref, dkv_ref, near_ref, far_ref, across_ref, ends_ref, low_ref, high_ref, *refs, first
):
    if first:
        dp_ref, gw_ref, sum_ref, cells_ref, norm_ref = refs
    else:
        held_ref, held_sum_ref, vec_ref, mine_ref, other_ref = refs[:5]
        dp_ref, send_ref, keep_ref, cells_ref, norm_ref, gw_ref, w_ref = refs[6:]
    piece, core = where_ref[0], where_ref[1]
    cells_ref[...] = dkv_ref[...]

    def add(start, value):
        rows = pl.ds(start, HALO)
        cells_ref[rows, :] = (cells_ref[rows, :].astype(F32) + value.astype(F32)).astype(BF16)

    def edges(left_ref, right_ref):
        for level in range(LEVELS - 1):
            edge = pl.ds(HALO * level, HALO)

            @pl.when(piece > 0)
            def _():
                add(OFF[level], left_ref[edge, :])

            @pl.when(piece < 3)
            def _():
                add(OFF[level] + CELLS[level] - HALO, right_ref[edge, :])

    pl.when(piece % 2 == 0)(lambda: edges(far_ref, near_ref))
    pl.when(piece % 2 == 1)(lambda: edges(near_ref, far_ref))
    add(OFF[7], across_ref[...].astype(F32) + ends_ref[...].astype(F32))

    sums = [jnp.zeros((8, 512), F32), jnp.zeros((8, 1024), F32)]
    for chunk in range(ROWS // 256):
        rows = pl.ds(256 * chunk, 256)
        norm_ref[rows, :] = normalised(tok_ref[0, rows, :])[0].astype(BF16)
        cells = jnp.concatenate(
            [
                cells_ref[pl.ds(OFF[level] + (256 >> level) * chunk, 256 >> level), :]
                for level in range(1, 5)
            ],
            axis=0,
        )
        dkv = (
            cells_ref[rows, :].astype(F32)
            + dot_nn(low_ref[...], cells)
            + dot_nn(high_ref[rows, :], cells_ref[pl.ds(OFF[5], 64), :])
        ).astype(BF16)
        dq = (
            dq_ref[rows, :].astype(F32)
            + dot_nn(low_ref[:, 192:224], dq3_ref[pl.ds(32 * chunk, 32), :])
        ).astype(BF16)
        dp_ref[0, rows, pl.ds(0, 512)] = dq
        dp_ref[0, rows, pl.ds(512, 1024)] = dkv
        sums = [old + fold_rows(new.astype(F32)) for old, new in zip(sums, (dq, dkv))]
    sums = jnp.concatenate(sums, axis=1)
    if first:
        sum_ref[...] = sums
    else:
        sums = jnp.sum(sums + held_sum_ref[...], axis=0, keepdims=True)
        row = lax.broadcasted_iota(jnp.int32, (VEC, 512), 0)
        lines = vec_ref[...].astype(BF16)
        gain = dot_tn(lines, jnp.where(row == 0, 1.0, 0.0).astype(BF16))
        offset = dot_tn(lines, jnp.where(row == 2, 1.0, 0.0).astype(BF16))
        ones = jnp.ones((8, 512), BF16)
        grad_gain = jnp.zeros((8, 512), F32)
        grad_offset = jnp.zeros((8, 512), F32)
        for index in range(3):
            take_weight(w_ref, index, mine_ref, other_ref, core, w_ref.shape[2] * index)
    for index in range(3):
        grad = dot_tn(norm_ref[...], dp_ref[0, :, pl.ds(512 * index, 512)])
        if first:
            gw_ref[index] = grad
        else:
            grad = grad + held_ref[index]
            total = sums[:, 512 * index : 512 * (index + 1)]
            gw_ref[index] = gain * grad + offset * total
            weight = weight_of(w_ref, index)
            high, middle, _ = three_terms(weight.astype(F32) * grad)
            grad_gain = grad_gain + dot_nt(ones, high) + dot_nt(ones, middle)
            high, middle, low = three_terms(total)
            terms = jnp.concatenate([high, middle, low] + [jnp.zeros_like(low)] * 5, axis=0)
            grad_offset = grad_offset + dot_nt(terms, weight)
    if not first:
        shard = w_ref.shape[2]
        for index in range(3):
            share_out(send_ref, keep_ref, core, shard * index, row_piece(gw_ref.at[index], shard))
        grad_offset = jnp.sum(grad_offset, axis=0, keepdims=True)
        blank = jnp.zeros((VEC - 2, 512), F32)
        lines = jnp.concatenate([grad_gain[0:1], grad_offset, blank], axis=0).astype(BF16)
        share_out(send_ref, keep_ref, core, 3 * shard, lambda index: lines)


def collect(micro, where, tokens, grads, received, const, held=None):
    width = tokens.shape[2]
    shape = jax.ShapeDtypeStruct
    first = held is None
    ins = list(grads) + list(received) + [const["low_t"], const["high_t"]]
    outs = [shape((tokens.shape[0], ROWS, 3 * width), BF16)]
    scratch = [pltpu.VMEM((2 * ROWS, 2 * width), BF16), pltpu.VMEM((ROWS, width), BF16)]
    kept = []
    aliases = {}
    if first:
        outs += [shape((3, width, width), F32), shape((8, 3 * width), F32)]
    else:
        ins += held[1:]
        kept = [held[0]]
        mine = held[-1]
        chips, lines, _ = mine.shape
        shard = width // (2 * chips)
        aliases = {2 + len(ins): 0}
        outs += [shape((chips, lines, width), BF16)] * 2
        scratch.append(pltpu.VMEM((3, width, width), F32))
        scratch.append(pltpu.VMEM((3, 2 * chips, shard, width), BF16))
    specs = [SCALAR, one_of((ROWS, width), micro)] + [whole(value.shape) for value in ins]
    return pl.pallas_call(
        lambda *refs: collect_kernel(*refs, first=first),
        grid=(1,),
        in_specs=specs + [KEPT] * len(kept),
        out_specs=[one_of((ROWS, 3 * width), micro)] + [whole(out.shape) for out in outs[1:]],
        out_shape=outs,
        scratch_shapes=scratch,
        input_output_aliases=aliases,
        compiler_params=params(),
        cost_estimate=timing(8),
        name="collect",
    )(where, tokens, *ins, *kept)


FIN_ROWS = 256


def finish_kernel(where_ref, tok_ref, dmid_ref, dp_ref, vec_ref, mine_ref, other_ref, *refs):
    grad_ref, w_ref = refs[-2:]
    core = where_ref[1]

    @pl.when(pl.program_id(0) == 0)
    def _():
        for index in range(3):
            take_weight(w_ref, index, mine_ref, other_ref, core, w_ref.shape[2] * index)

    back = dot_nt(dp_ref[0, :, pl.ds(0, 512)], weight_of(w_ref, 0))
    for index in range(1, 3):
        back = back + dot_nt(dp_ref[0, :, pl.ds(512 * index, 512)], weight_of(w_ref, index))
    unit, rate = normalised(tok_ref[0])
    grad_ref[0] = dmid_ref[0] + norm_back(back * vec_ref[0:1], unit, rate)


def finish(micro, where, tokens, dmid, dproj, vec, mine, other, kept):
    width = tokens.shape[2]
    dp = 2 * mine.shape[0]
    ins = [where, tokens, dmid, dproj, vec, mine, other] + ([] if kept is None else [kept])
    chunk = lambda lanes: pl.BlockSpec((1, FIN_ROWS, lanes), lambda r: (micro, r, 0))
    return pl.pallas_call(
        finish_kernel,
        grid=(ROWS // FIN_ROWS,),
        in_specs=[
            SCALAR,
            chunk(width),
            chunk(width),
            chunk(3 * width),
            whole(vec.shape),
            whole(mine.shape),
            whole(other.shape),
        ]
        + [KEPT] * (len(ins) - 7),
        out_specs=chunk(width),
        out_shape=jax.ShapeDtypeStruct(tokens.shape, F32),
        scratch_shapes=[pltpu.VMEM((3, dp, width // dp, width), BF16)],
        input_output_aliases={} if kept is None else {7: 0},
        compiler_params=params(),
        cost_estimate=timing(6),
        name="finish",
    )(*ins)


def cell_documents(segments, piece):
    micro, length = segments.shape
    keys = []
    fine = []
    coarse = []
    for level in range(LEVELS):
        cell = 1 << level
        grouped = segments.reshape(micro, length // cell, cell)
        lowest = grouped[:, :, 0]
        highest = grouped[:, :, cell - 1]
        same = lowest == highest
        key = jnp.where(same, lowest, -2)
        query = jnp.where(same, lowest, -1)
        own = lax.dynamic_slice_in_dim(query, piece * CELLS[level], CELLS[level], axis=1)
        if level < LEVELS - 1:
            padded = jnp.pad(key, ((0, 0), (HALO, HALO)), constant_values=-3)
            keys.append(
                lax.dynamic_slice_in_dim(
                    padded, piece * CELLS[level], CELLS[level] + 2 * HALO, axis=1
                )
            )
        else:
            owner = jnp.arange(key.shape[1]) // PIECE7
            counted = (jnp.abs(owner // 2 - piece // 2) == 1) & (jnp.abs(owner - piece) >= 2)
            keys.append(jnp.where(counted[None], key, -3))
        if level < FINE:
            fine.append(jnp.repeat(own, cell, axis=1).reshape(micro, FINE_TILES, 1, TILE))
        else:
            coarse.append(jnp.repeat(own, cell // 8, axis=1).reshape(micro, COARSE_TILES, 1, TILE))

    def rows(parts):
        value = jnp.concatenate(parts, axis=2)
        value = jnp.pad(value, ((0, 0), (0, 0), (0, 8 - len(parts)), (0, 0)))
        return jnp.tile(value, (1, 1, 1, QUAD)).reshape(micro, -1, QL)

    key = jnp.concatenate(keys, axis=1)
    return dict(
        key=jnp.broadcast_to(key[:, :, None], key.shape + (128,)),
        fine=rows(fine),
        coarse=rows(coarse),
    )


def same_core(chips):
    return [[2 * chip + core for chip in range(chips)] for core in range(2)]


def core_swap(value, chips):
    pairs = [(place, place ^ 1) for place in range(2 * chips)]
    return lax.ppermute(value, "dp", pairs)


def chip_exchange(value, chips):
    return lax.all_to_all(value, "dp", 0, 0, axis_index_groups=same_core(chips), tiled=True)


def after(value, *done):
    return lax.optimization_barrier((value,) + done)[0]


def add(left, right):
    return left.astype(F32) + right.astype(F32)


def body(
    tokens,
    segment_ids,
    norm_gains,
    norm_biases,
    qkv_weight,
    out_weight,
    in_weight,
    in_bias,
    down_weight,
    down_bias,
    cotangent,
):
    micro, _, row_count, width = tokens.shape
    pieces = lax.axis_size("sp")
    piece = lax.axis_index("sp")
    assert row_count == ROWS and pieces == 4 and micro == 2
    const = constants()
    tokens = tokens[:, 0]
    cotangent = cotangent[:, 0]
    dp = lax.axis_size("dp")
    place = lax.axis_index("dp")
    chips = dp // 2
    shard = width // dp
    hidden = in_weight.shape[1]
    parts = hidden // FF_CHUNK
    where = jnp.stack([piece, place % 2]).astype(jnp.int32)
    swap = lambda value, bits: lax.ppermute(value, "sp", [(p, p ^ bits) for p in range(pieces)])
    spread = lambda value: chip_exchange(
        jnp.broadcast_to(value[None], (chips,) + value.shape), chips
    )

    def placed(value, start):
        lines = jnp.zeros((value.shape[0], start * value.shape[1]), BF16)
        return lax.dynamic_update_slice(lines, value, (0, place * value.shape[1])).reshape(-1, width)

    small = placed(jnp.concatenate([norm_gains, norm_biases, down_bias[None]]), dp)
    small = jnp.concatenate([small, placed(in_bias[None], dp)])
    small = jnp.pad(small, ((0, VEC - small.shape[0]), (0, 0)))
    mine = spread(jnp.concatenate([qkv_weight.reshape(3 * shard, width), small]))
    ids = cell_documents(segment_ids[:, 0], piece)
    other = core_swap(mine, chips)
    rest = jnp.concatenate(
        [
            out_weight,
            in_weight.reshape(shard, parts, FF_CHUNK).swapaxes(0, 1).reshape(-1, width),
            down_weight,
        ]
    )
    def halo(near, far, across, ends):
        middle = lax.ppermute(far, "sp", [(1, 2), (2, 1)])
        return swap(near, 1), middle, swap(across, 2), lax.ppermute(ends, "sp", [(0, 3), (3, 0)])

    q, q3, kv, near, far, top, vec = project(where, tokens, mine, other, const)
    cells = (q, q3, kv)
    received = halo(near, far, top, top)
    rest_mine = spread(after(rest, received[3]))
    mixed, *stats = attend(where, cells, received, ids, const)
    rest_mine = after(rest_mine, stats[1])
    rest_other = core_swap(rest_mine, chips)

    flat = lambda value: value.reshape(micro * ROWS, width)
    split = lambda value: value.reshape(micro, ROWS, width)
    outputs, dmid, dmix, send, keep = middle_part(
        where, flat(tokens), flat(cotangent), flat(mixed), vec, rest_mine, rest_other
    )

    grads, back = [], []

    def attention_back(m, where):
        dq, dq3, dkv, *edges = attend_back(m, where, cells, stats, split(dmix), ids, const)
        grads.append((dq, dq3, dkv))
        back.append(halo(*edges))

    come = core_swap(send, chips)
    attention_back(0, where)
    pair = add(keep, after(come, grads[0][1])).astype(BF16)
    come = chip_exchange(pair, chips)
    attention_back(1, after(where, pair))
    dproj, held, sums = collect(0, after(where, grads[1][1]), tokens, grads[0], back[0], const)

    odd = piece % 2 == 1
    total = jnp.sum(after(come, sums).astype(F32), axis=0)
    left, right = total[:, : width // 2], total[:, width // 2 :]
    half = jnp.where(odd, right, left).astype(BF16)
    come = swap(jnp.where(odd, left, right).astype(BF16), 1)
    dproj, send, keep = collect(
        1, after(where, half), tokens, grads[1], back[1], const, [dproj, held, sums, vec, mine, other]
    )
    qkv_come = core_swap(send, chips)
    half = add(half, after(come, send)).astype(BF16)
    come = swap(half, 2)
    input_grad = finish(0, after(where, half), tokens, split(dmid), dproj, vec, mine, other, None)
    pair = add(keep, after(qkv_come, input_grad)).astype(BF16)
    qkv_come = chip_exchange(pair, chips)
    input_grad = finish(
        1, after(where, pair), tokens, split(dmid), dproj, vec, mine, other, input_grad
    )
    half = add(half, after(come, input_grad)).astype(BF16)
    come = swap(half, 1)
    total = jnp.sum(after(qkv_come, half).astype(F32), axis=0).astype(BF16)
    qkv_come = swap(total, 1)
    come = after(come, total)
    rest = jnp.where(
        odd, jnp.concatenate([come, half], axis=1), jnp.concatenate([half, come], axis=1)
    ).astype(F32)
    total = add(total, qkv_come).astype(BF16)
    total = add(total, swap(total, 2))

    own = lambda value, size: lax.dynamic_slice_in_dim(value, place * size, size, axis=-1)
    small_two = rest[shard * (1 + 2 * parts) :]
    small_one = total[3 * shard :]
    gin = rest[shard : shard * (1 + parts)].reshape(parts, shard, FF_CHUNK).swapaxes(0, 1)
    return (
        outputs.reshape(micro, 1, ROWS, width),
        input_grad[:, None],
        own(jnp.stack([small_one[0], small_two[1]]), shard),
        own(jnp.stack([small_one[1], small_two[2]]), shard),
        total[: 3 * shard].reshape(3, shard, width),
        rest[:shard],
        gin.reshape(shard, hidden),
        own(small_two[3 : 3 + parts].reshape(hidden), hidden // dp),
        rest[shard * (1 + parts) : shard * (1 + 2 * parts)],
        own(small_two[0], shard),
    )


def solution(mesh):
    in_specs = (
        P(None, "dp", "sp", None),
        P(None, "dp", None),
        P(None, "dp"),
        P(None, "dp"),
        P(None, "dp", None),
        P("dp", None),
        P("dp", None),
        P("dp"),
        P("dp", None),
        P("dp"),
        P(None, "dp", "sp", None),
    )
    out_specs = (
        P(None, "dp", "sp", None),
        P(None, "dp", "sp", None),
        P(None, "dp"),
        P(None, "dp"),
        P(None, "dp", None),
        P("dp", None),
        P("dp", None),
        P("dp"),
        P("dp", None),
        P("dp"),
    )
    return jax.shard_map(body, mesh=mesh, in_specs=in_specs, out_specs=out_specs, check_vma=False)
```

```python
import math

import jax
import jax.numpy as jnp
import numpy as np
from jax import lax
from jax.experimental import pallas as pl
from jax.experimental.pallas import tpu as pltpu
from jax.sharding import PartitionSpec as P

HEADS = 8
HEAD_DIM = 64
BLOCK = 16
LEVELS = 8
HALO = 16
TILE = 64
QUAD = 4
QL = QUAD * HEAD_DIM
NEG = -1e30
FINE = 3
ROWS = 1024
EDGE = 112
VEC = 16
GROUP = 8
GROUP_BACK = 4
F32 = jnp.float32
BF16 = jnp.bfloat16

CELLS = [ROWS >> level for level in range(LEVELS)]
OFF = [2 * ROWS - (2 * ROWS >> level) for level in range(LEVELS)]
POFF = []
_at = 0
for _level in range(LEVELS - 1):
    POFF.append(_at)
    _at += CELLS[_level] + 2 * HALO
POFF.append(_at)
PIECE7 = CELLS[LEVELS - 1]
PADDED = _at + 4 * PIECE7
FINE_TILES = ROWS // TILE
COARSE_TILES = ROWS // 8 // TILE
FINE_KEYS = 192
COARSE_KEYS = 256
LN_EPS = 1e-05
VMEM_LIMIT = 62 * 1024 * 1024


def _counts(level, query, key):
    query = query[None, :]
    key = key[:, None]
    near = np.abs(query // 16 - key // 16)
    if level == 0:
        return near <= 1
    return (near == 1) & (np.abs(query // 8 - key // 8) >= 2)


def _bias(parts):
    rows = []
    for level, allowed in parts:
        rows.append(np.where(allowed, np.float32(level * math.log(2.0)), np.float32(NEG)))
    block = np.concatenate(rows, axis=0).astype(np.float32)
    return np.tile(block, (1, QUAD))


def _two_blocks():
    return np.concatenate([np.arange(16) - 16, np.arange(16) + 16])


def fine_bias():
    token = np.arange(TILE)
    return _bias(
        [
            (0, _counts(0, token, np.arange(96) - 16)),
            (1, _counts(1, token // 2, np.arange(64) - 16)),
            (2, _counts(2, token // 4, _two_blocks())),
        ]
    )


def coarse_bias():
    cell = np.arange(TILE)
    out = []
    for tile in range(COARSE_TILES):
        out.append(
            _bias(
                [
                    (3, _counts(3, cell, np.arange(96) - 16)),
                    (4, _counts(4, cell // 2, np.arange(64) - 16)),
                    (5, _counts(5, cell // 4, _two_blocks())),
                    (6, _counts(6, 8 * tile + cell // 8, _two_blocks())),
                    (7, np.ones((4 * PIECE7, TILE), bool)),
                ]
            )
        )
    return np.stack(out)


STEP = [0, 1, 2, 0, 1, 2, 3, 4]


def mean_rows(cell, count):
    return (np.arange(count)[None, :] // cell == np.arange(count // cell)[:, None]).astype(
        np.float32
    ) / cell


def spread_matrix():
    out = np.zeros((QUAD, TILE, 8, QUAD, TILE), np.float32)
    for part in range(8):
        for token in range(TILE):
            for head in range(QUAD):
                out[head, 8 * part + token // 8, part, head, token] = 1.0
    return out.reshape(QL, 8 * QL)


def constants():
    head_mask = np.kron(np.eye(QUAD), np.ones((TILE, HEAD_DIM)))
    low = [mean_rows(1 << level, 256) for level in range(1, 5)]
    high = [mean_rows(1 << level, ROWS) for level in range(5, 8)] + [np.zeros((8, ROWS))]
    key_low = [rows * 0.5 ** STEP[level] for level, rows in zip(range(1, 5), low)]
    key_high = [rows * 0.5**step for step, rows in zip(STEP[5:] + [0], high)]
    as_low = lambda value: jnp.asarray(value.astype(np.float32)).astype(BF16)
    low, high = np.concatenate(low), np.concatenate(high)
    return dict(
        fine=jnp.asarray(fine_bias()),
        coarse=jnp.asarray(coarse_bias()),
        head_mask=as_low(head_mask),
        low=as_low(np.stack([np.concatenate(key_low), low])),
        high=as_low(np.stack([np.concatenate(key_high), high])),
        low_t=as_low(low.T),
        high_t=as_low(high.T),
        spread=as_low(spread_matrix()),
        spread_t=as_low(spread_matrix().T),
    )


def dot_nn(left, right):
    return jnp.dot(left, right, preferred_element_type=F32)


def dot_nt(left, right):
    return lax.dot_general(left, right, (((1,), (1,)), ((), ())), preferred_element_type=F32)


def dot_tn(left, right):
    return lax.dot_general(left, right, (((0,), (0,)), ((), ())), preferred_element_type=F32)


def at(start, size):
    return pl.ds(pl.multiple_of(start, 16), size)


def whole(shape):
    zeros = (0,) * len(shape)
    return pl.BlockSpec(shape, lambda *_: zeros)


def one_of(shape, micro):
    zeros = (0,) * len(shape)
    return pl.BlockSpec((1,) + shape, lambda *_: (micro,) + zeros)


def each_of(shape):
    zeros = (0,) * len(shape)
    return pl.BlockSpec((1,) + shape, lambda step: (step,) + zeros)


SCALAR = pl.BlockSpec(memory_space=pltpu.SMEM)
KEPT = pl.BlockSpec(memory_space=pl.ANY)


def timing(micros):
    return pl.CostEstimate(
        flops=int(micros * 4e8), bytes_accessed=int(micros * 3e6), transcendentals=0
    )


def params():
    return pltpu.CompilerParams(
        dimension_semantics=("arbitrary",), vmem_limit_bytes=VMEM_LIMIT
    )


def normalised(rows):
    center = rows - jnp.mean(rows, axis=-1, keepdims=True)
    spread = jnp.mean(center * center, axis=-1, keepdims=True)
    rate = lax.rsqrt(spread + LN_EPS)
    return center * rate, rate


def norm_back(grad, unit, rate):
    mean_grad = jnp.mean(grad, axis=-1, keepdims=True)
    mean_dot = jnp.mean(grad * unit, axis=-1, keepdims=True)
    return rate * (grad - mean_grad - unit * mean_dot)


def fold_rows(value):
    return jnp.sum(value.reshape(-1, 8, value.shape[-1]), axis=0)


def take_weight(target, index, mine, other, core, start):
    chips, shard = mine.shape[0], target.shape[2]
    for chip in range(chips):
        target[index, 2 * chip + core] = mine[chip, pl.ds(start, shard), :]
        target[index, 2 * chip + 1 - core] = other[chip, pl.ds(start, shard), :]


def weight_of(ref, index):
    return ref[index].reshape(ref.shape[1] * ref.shape[2], ref.shape[3])


def project_kernel(
    where_ref,
    tok_ref,
    mine_ref,
    other_ref,
    low_ref,
    high_ref,
    q_ref,
    q3_ref,
    kv_ref,
    near_ref,
    far_ref,
    top_ref,
    vec_ref,
    w_ref,
    norm_ref,
):
    piece, core = where_ref[0], where_ref[1]
    shard = w_ref.shape[2]

    @pl.when(pl.program_id(0) == 0)
    def _():
        for index in range(3):
            take_weight(w_ref, index, mine_ref, other_ref, core, shard * index)
        vec = jnp.zeros(vec_ref.shape, F32)
        for chip in range(mine_ref.shape[0]):
            for ref in (mine_ref, other_ref):
                vec = vec + ref[chip, pl.ds(3 * shard, VEC), :].astype(F32)
        vec_ref[...] = vec

    for chunk in range(ROWS // 256):
        rows = pl.ds(256 * chunk, 256)
        unit, _ = normalised(tok_ref[0, rows, :])
        norm_ref[rows, :] = (unit * vec_ref[0:1] + vec_ref[2:3]).astype(BF16)
    for half in range(2):
        rows = pl.ds(512 * half, 512)
        for index in range(3):
            value = dot_nn(norm_ref[rows, :], weight_of(w_ref, index)).astype(BF16)
            if index == 0:
                q_ref[0, rows, :] = value
            else:
                kv_ref[0, rows, pl.ds(512 * (index - 1), 512)] = value
    for chunk in range(ROWS // 256):
        rows = pl.ds(256 * chunk, 256)
        q3_ref[0, pl.ds(32 * chunk, 32), :] = dot_nn(
            low_ref[1, 192:224, :], q_ref[0, rows, :]
        ).astype(BF16)
        for part in range(2):
            lanes = pl.ds(512 * part, 512)
            cells = dot_nn(low_ref[part], kv_ref[0, rows, lanes]).astype(BF16)
            start = 0
            for level in range(1, 5):
                count = 256 >> level
                kv_ref[0, pl.ds(OFF[level] + count * chunk, count), lanes] = cells[
                    start : start + count
                ]
                start += count
    for part in range(2):
        lanes = pl.ds(512 * part, 512)
        kv_ref[0, pl.ds(OFF[5], 64), lanes] = dot_nn(
            high_ref[part], kv_ref[0, pl.ds(0, ROWS), lanes]
        ).astype(BF16)

    def edges(left_ref, right_ref):
        for level in range(LEVELS - 1):
            edge = pl.ds(HALO * level, HALO)
            left_ref[0, edge, :] = kv_ref[0, pl.ds(OFF[level], HALO), :]
            right_ref[0, edge, :] = kv_ref[0, pl.ds(OFF[level] + CELLS[level] - HALO, HALO), :]

    pl.when(piece % 2 == 0)(lambda: edges(far_ref, near_ref))
    pl.when(piece % 2 == 1)(lambda: edges(near_ref, far_ref))
    top_ref[0] = kv_ref[0, pl.ds(OFF[7], 16), :]


def cell_shapes(width):
    return [(ROWS, width), (ROWS // 8, width), (2 * ROWS, 2 * width)]


def edge_shapes(width):
    return [(EDGE, 2 * width), (EDGE, 2 * width), (16, 2 * width)]


def project(where, tokens, mine, other, const):
    micro, _, width = tokens.shape
    shape = jax.ShapeDtypeStruct
    shard = width // (2 * mine.shape[0])
    outs = cell_shapes(width) + edge_shapes(width)
    return pl.pallas_call(
        project_kernel,
        grid=(micro,),
        in_specs=[
            SCALAR,
            each_of((ROWS, width)),
            whole(mine.shape),
            whole(other.shape),
            whole((2, 240, 256)),
            whole((2, 64, ROWS)),
        ],
        out_specs=[each_of(out) for out in outs] + [whole((VEC, width))],
        out_shape=[shape((micro,) + out, BF16) for out in outs] + [shape((VEC, width), F32)],
        scratch_shapes=[
            pltpu.VMEM((3, width // shard, shard, width), BF16),
            pltpu.VMEM((ROWS, width), BF16),
        ],
        compiler_params=params(),
        cost_estimate=timing(13),
        name="project",
    )(where, tokens, mine, other, const["low"], const["high"])


def fine_windows(tile):
    return [
        (POFF[0] + 64 * tile, 96),
        (POFF[1] + 32 * tile, 64),
        (POFF[2] + 16 * tile, 16),
        (POFF[2] + 16 * tile + 32, 16),
    ]


def coarse_windows(tile):
    return [
        (POFF[3] + 64 * tile, 96),
        (POFF[4] + 32 * tile, 64),
        (POFF[5] + 16 * tile, 16),
        (POFF[5] + 16 * tile + 32, 16),
        (POFF[6], 16),
        (POFF[6] + 32, 16),
        (POFF[7], 32),
    ]


FINE_LEVELS = [96, 64, 32]
COARSE_LEVELS = [96, 64, 32, 32, 32]


def gather_rows(ref, windows, lanes):
    return jnp.concatenate([ref[0, at(start, size), lanes] for start, size in windows], axis=0)


def tile_bias(kid_ref, qid_ref, tile, tiles, windows, levels, bias):
    keys = jnp.concatenate([kid_ref[0, at(start, size), :] for start, size in windows], axis=0)
    keys = keys.astype(F32)
    keys = jnp.concatenate([keys, keys], axis=1)
    out = []
    start = 0
    for index, count in enumerate(levels):
        part = slice(start, start + count)
        owner = qid_ref[0, pl.ds(tiles * index + tile, 1), :]
        out.append(jnp.where(keys[part] == owner, bias[part], NEG))
        start += count
    return jnp.concatenate(out, axis=0)


def lane_sums(value, steps):
    halves = []
    for half in range(2):
        part = value[:, 128 * half : 128 * (half + 1)]
        lane = lax.broadcasted_iota(jnp.int32, part.shape, 1)
        for step in range(steps):
            size = 1 << step
            first = (lane & size) == 0
            part = part + jnp.where(
                first, pltpu.roll(part, 128 - size, 1), pltpu.roll(part, size, 1)
            )
        halves.append(part)
    return jnp.concatenate(halves, axis=1)


def level_sums(value, levels):
    out = [value[0 : levels[0]]]
    start = levels[0]
    for index, count in enumerate(levels[1:]):
        out.append(lane_sums(value[start : start + count], index + 1))
        start += count
    return jnp.concatenate(out, axis=0)


def head_stack(value, mask):
    return jnp.concatenate([value] * QUAD, axis=0) * mask


def head_pick(stacked):
    lane = lax.broadcasted_iota(jnp.int32, (TILE, QL), 1) // HEAD_DIM
    out = stacked[0:TILE]
    for head in range(1, QUAD):
        out = jnp.where(lane == head, stacked[TILE * head : TILE * (head + 1)], out)
    return out


def three_terms(row):
    high = row.astype(BF16)
    rest = row - high.astype(F32)
    middle = rest.astype(BF16)
    low = (rest - middle.astype(F32)).astype(BF16)
    return high, middle, low


def own_cell(tile):
    cell = lax.broadcasted_iota(jnp.int32, (16, QL), 0)
    token = lax.broadcasted_iota(jnp.int32, (16, QL), 1) % TILE
    return cell == 8 * (tile % 2) + token // 8


def attend_kernel(
    where_ref,
    q_ref,
    q3_ref,
    kv_ref,
    near_ref,
    far_ref,
    across_ref,
    ends_ref,
    kid_ref,
    qidf_ref,
    qidc_ref,
    fine_ref,
    coarse_ref,
    mask_ref,
    spread_ref,
    mixed_ref,
    kvp_ref,
    lse_ref,
    lsec_ref,
    lsex_ref,
    oc_ref,
):
    piece = where_ref[0]

    def edges(left_ref, right_ref):
        for level in range(LEVELS - 1):
            base = POFF[level]
            edge = pl.ds(HALO * level, HALO)
            kvp_ref[0, pl.ds(base, HALO), :] = left_ref[0, edge, :]
            kvp_ref[0, pl.ds(base + HALO + CELLS[level], HALO), :] = right_ref[0, edge, :]

    pl.when(piece % 2 == 0)(lambda: edges(far_ref, near_ref))
    pl.when(piece % 2 == 1)(lambda: edges(near_ref, far_ref))
    for level in range(LEVELS - 1):
        count = CELLS[level]
        kvp_ref[0, pl.ds(POFF[level] + HALO, count), :] = kv_ref[0, pl.ds(OFF[level], count), :]
    across = across_ref[0].astype(F32)[0:PIECE7]
    ends = ends_ref[0].astype(F32)[0:PIECE7]
    tops = []
    for owner in range(4):
        top = jnp.where(owner == (piece + 2) % 4, across, jnp.where(owner == 3 - piece, ends, 0.0))
        tops.append(top)
    kvp_ref[0, pl.ds(POFF[7], 4 * PIECE7), :] = jnp.concatenate(tops, axis=0).astype(BF16)
    mask = mask_ref[...]
    scaled = mask * jnp.asarray(0.125, BF16)

    units = [(tile, quad) for tile in range(COARSE_TILES) for quad in range(2)]
    biases = [
        tile_bias(kid_ref, qidc_ref, tile, 8, coarse_windows(tile), COARSE_LEVELS, coarse_ref[tile])
        for tile in range(COARSE_TILES)
    ]
    scores = []
    for tile, quad in units:
        lanes = pl.ds(QL * quad, QL)
        query = head_stack(q3_ref[0, pl.ds(TILE * tile, TILE), lanes], scaled)
        scores.append(dot_nt(gather_rows(kvp_ref, coarse_windows(tile), lanes), query))
    shares = []
    terms = []
    for index, (tile, quad) in enumerate(units):
        score = level_sums(scores[index], COARSE_LEVELS) + biases[index // 2]
        top = jnp.max(score, axis=0, keepdims=True)
        share = jnp.exp(score - top)
        total = jnp.sum(share, axis=0, keepdims=True)
        lse = top + jnp.log(total)
        lsec_ref[0, pl.ds(index, 1), :] = lse
        terms.extend(three_terms(lse))
        shares.append((share * (1.0 / total)).astype(BF16))
    results = []
    for (tile, quad), share in zip(units, shares):
        values = gather_rows(kvp_ref, coarse_windows(tile), pl.ds(512 + QL * quad, QL))
        results.append(dot_tn(share, values))
    terms.extend([terms[-1]] * 4)
    terms = dot_nn(jnp.concatenate(terms, axis=0), spread_ref[...])
    for index, (tile, quad) in enumerate(units):
        oc_ref[0, pl.ds(TILE * tile, TILE), pl.ds(QL * quad, QL)] = head_pick(
            results[index]
        ).astype(BF16)
        part = terms[3 * index : 3 * index + 3]
        lsex_ref[0, pl.ds(index, 1), :] = part[0:1] + part[1:2] + part[2:3]

    def fine_group(group, carry):
        tiles = [GROUP * group + index for index in range(GROUP)]
        units = [(tile, quad) for tile in tiles for quad in range(2)]
        biases = [
            tile_bias(kid_ref, qidf_ref, tile, FINE_TILES, fine_windows(tile), FINE_LEVELS, fine_ref[...])
            for tile in tiles
        ]
        scores = []
        for tile, quad in units:
            lanes = pl.ds(QL * quad, QL)
            query = head_stack(q_ref[0, at(TILE * tile, TILE), lanes], scaled)
            scores.append(dot_nt(gather_rows(kvp_ref, fine_windows(tile), lanes), query))
        shares = []
        for index, (tile, quad) in enumerate(units):
            score = level_sums(scores[index], FINE_LEVELS) + biases[index // 2]
            far = lsex_ref[
                0, pl.ds(2 * (tile // 8) + quad, 1), pl.ds(pl.multiple_of(QL * (tile % 8), QL), QL)
            ]
            top = jnp.maximum(jnp.max(score, axis=0, keepdims=True), far)
            share = jnp.exp(score - top)
            far_share = jnp.exp(far - top)
            total = jnp.sum(share, axis=0, keepdims=True) + far_share
            lse_ref[0, pl.ds(2 * tile + quad, 1), :] = top + jnp.log(total)
            inverse = 1.0 / total
            shares.append(
                jnp.concatenate(
                    [share * inverse, jnp.where(own_cell(tile), far_share * inverse, 0.0)], axis=0
                ).astype(BF16)
            )
        results = []
        for (tile, quad), share in zip(units, shares):
            values = jnp.concatenate(
                [
                    gather_rows(kvp_ref, fine_windows(tile), pl.ds(512 + QL * quad, QL)),
                    oc_ref[0, at(16 * (tile // 2), 16), pl.ds(QL * quad, QL)],
                ],
                axis=0,
            )
            results.append(dot_tn(share, values))
        for (tile, quad), result in zip(units, results):
            mixed_ref[0, at(TILE * tile, TILE), pl.ds(QL * quad, QL)] = head_pick(result).astype(
                BF16
            )
        return carry

    lax.fori_loop(0, FINE_TILES // GROUP, fine_group, 0)


def stat_shapes(width):
    return [
        ((PADDED, 2 * width), BF16),
        ((2 * FINE_TILES, QL), F32),
        ((2 * COARSE_TILES, QL), F32),
        ((2 * COARSE_TILES, 8 * QL), F32),
        ((ROWS // 8, width), BF16),
    ]


def id_specs(spec):
    return [
        spec((PADDED, 128)),
        spec((FINE * FINE_TILES, QL)),
        spec((8 * (LEVELS - FINE), QL)),
        whole((FINE_KEYS, QL)),
        whole((COARSE_TILES, COARSE_KEYS, QL)),
        whole((QL, QL)),
    ]


def id_args(ids, const):
    return [ids["key"], ids["fine"], ids["coarse"], const["fine"], const["coarse"], const["head_mask"]]


def attend(where, cells, received, ids, const):
    micro, _, width = cells[0].shape
    outs = [((ROWS, width), BF16)] + stat_shapes(width)
    ins = list(cells) + list(received)
    return pl.pallas_call(
        attend_kernel,
        grid=(micro,),
        in_specs=[SCALAR]
        + [each_of(value.shape[1:]) for value in ins]
        + id_specs(each_of)
        + [whole((QL, 8 * QL))],
        out_specs=[each_of(dims) for dims, _ in outs],
        out_shape=[jax.ShapeDtypeStruct((micro,) + dims, kind) for dims, kind in outs],
        compiler_params=params(),
        cost_estimate=timing(23),
        name="attend",
    )(where, *ins, *id_args(ids, const), const["spread"])


def add_rows(ref, windows, lanes, value):
    start = 0
    for base, count in windows:
        rows = at(base, count)
        ref[rows, lanes] = ref[rows, lanes] + value[start : start + count]
        start += count


def attend_back_kernel(
    where_ref,
    q_ref,
    q3_ref,
    kvp_ref,
    lse_ref,
    lsec_ref,
    lsex_ref,
    oc_ref,
    dout_ref,
    kid_ref,
    qidf_ref,
    qidc_ref,
    fine_ref,
    coarse_ref,
    mask_ref,
    spread_t_ref,
    dq_ref,
    dq3_ref,
    dkv_ref,
    near_ref,
    far_ref,
    across_ref,
    ends_ref,
    acc_ref,
    dcell_ref,
    delta_ref,
):
    acc_ref[...] = jnp.zeros(acc_ref.shape, F32)
    dcell_ref[...] = jnp.zeros(dcell_ref.shape, F32)
    mask = mask_ref[...]
    scaled = mask * jnp.asarray(0.125, BF16)

    def fine_group(group, carry):
        tiles = [GROUP_BACK * group + index for index in range(GROUP_BACK)]
        units = [(tile, quad) for tile in tiles for quad in range(2)]
        biases = [
            tile_bias(kid_ref, qidf_ref, tile, FINE_TILES, fine_windows(tile), FINE_LEVELS, fine_ref[...])
            for tile in tiles
        ]
        at_unit = lambda unit: (at(TILE * unit[0], TILE), pl.ds(QL * unit[1], QL))
        queries = [head_stack(q_ref[(0,) + at_unit(unit)], scaled) for unit in units]
        douts = [head_stack(dout_ref[(0,) + at_unit(unit)], mask) for unit in units]
        scores = []
        steers = []
        for index, (tile, quad) in enumerate(units):
            keys = gather_rows(kvp_ref, fine_windows(tile), pl.ds(QL * quad, QL))
            scores.append(dot_nt(keys, queries[index]))
            values = jnp.concatenate(
                [
                    gather_rows(kvp_ref, fine_windows(tile), pl.ds(512 + QL * quad, QL)),
                    oc_ref[0, at(16 * (tile // 2), 16), pl.ds(QL * quad, QL)],
                ],
                axis=0,
            )
            steers.append(dot_nt(values, douts[index]))
        shares = []
        grads = []
        for index, (tile, quad) in enumerate(units):
            lse = lse_ref[0, pl.ds(2 * tile + quad, 1), :]
            wide = pl.ds(pl.multiple_of(QL * (tile % 8), QL), QL)
            coarse_row = pl.ds(2 * (tile // 8) + quad, 1)
            far_share = jnp.exp(lsex_ref[0, coarse_row, wide] - lse)
            share = jnp.exp(level_sums(scores[index], FINE_LEVELS) + biases[index // 2] - lse)
            share = jnp.concatenate([share, jnp.where(own_cell(tile), far_share, 0.0)], axis=0)
            weighted = share * steers[index]
            delta = jnp.sum(weighted, axis=0, keepdims=True)
            delta_ref[coarse_row, wide] = far_share * delta
            grad = weighted[0:FINE_KEYS] - share[0:FINE_KEYS] * delta
            grads.append(level_sums(grad, FINE_LEVELS).astype(BF16))
            shares.append(share.astype(BF16))
        dvalues = [dot_nn(share, dout) for share, dout in zip(shares, douts)]
        dkeys = [dot_nn(grad, query) for grad, query in zip(grads, queries)]
        dqueries = []
        for (tile, quad), grad in zip(units, grads):
            keys = gather_rows(kvp_ref, fine_windows(tile), pl.ds(QL * quad, QL))
            dqueries.append(dot_tn(grad, keys))
        for index, (tile, quad) in enumerate(units):
            lanes = pl.ds(QL * quad, QL)
            cells = at(16 * (tile // 2), 16)
            windows = fine_windows(tile)
            add_rows(acc_ref, windows, pl.ds(512 + QL * quad, QL), dvalues[index])
            dcell_ref[cells, lanes] = dcell_ref[cells, lanes] + dvalues[index][FINE_KEYS:]
            add_rows(acc_ref, windows, lanes, dkeys[index])
            dq_ref[at_unit((tile, quad))] = (head_pick(dqueries[index]) * 0.125).astype(BF16)
        return carry

    lax.fori_loop(0, FINE_TILES // GROUP_BACK, fine_group, 0)

    units = [(tile, quad) for tile in range(COARSE_TILES) for quad in range(2)]
    biases = [
        tile_bias(kid_ref, qidc_ref, tile, 8, coarse_windows(tile), COARSE_LEVELS, coarse_ref[tile])
        for tile in range(COARSE_TILES)
    ]
    at_unit = lambda unit: (pl.ds(TILE * unit[0], TILE), pl.ds(QL * unit[1], QL))
    queries = [head_stack(q3_ref[(0,) + at_unit(unit)], scaled) for unit in units]
    douts = [head_stack(dcell_ref[at_unit(unit)].astype(BF16), mask) for unit in units]
    terms = []
    for index in range(len(units)):
        terms.extend(three_terms(delta_ref[pl.ds(index, 1), :]))
    terms.extend([terms[-1]] * 4)
    terms = dot_nn(jnp.concatenate(terms, axis=0), spread_t_ref[...])
    steers = []
    scores = []
    for (tile, quad), dout, query in zip(units, douts, queries):
        values = gather_rows(kvp_ref, coarse_windows(tile), pl.ds(512 + QL * quad, QL))
        steers.append(dot_nt(values, dout))
        keys = gather_rows(kvp_ref, coarse_windows(tile), pl.ds(QL * quad, QL))
        scores.append(dot_nt(keys, query))
    shares = []
    grads = []
    for index, (tile, quad) in enumerate(units):
        score = level_sums(scores[index], COARSE_LEVELS) + biases[index // 2]
        share = jnp.exp(score - lsec_ref[0, pl.ds(index, 1), :])
        part = terms[3 * index : 3 * index + 3]
        delta = part[0:1] + part[1:2] + part[2:3]
        grads.append(level_sums(share * (steers[index] - delta), COARSE_LEVELS).astype(BF16))
        shares.append(share.astype(BF16))
    dvalues = [dot_nn(share, dout) for share, dout in zip(shares, douts)]
    dkeys = [dot_nn(grad, query) for grad, query in zip(grads, queries)]
    dqueries = []
    for (tile, quad), grad in zip(units, grads):
        keys = gather_rows(kvp_ref, coarse_windows(tile), pl.ds(QL * quad, QL))
        dqueries.append(dot_tn(grad, keys))
    for index, (tile, quad) in enumerate(units):
        windows = coarse_windows(tile)
        add_rows(acc_ref, windows, pl.ds(512 + QL * quad, QL), dvalues[index])
        add_rows(acc_ref, windows, pl.ds(QL * quad, QL), dkeys[index])
        dq3_ref[at_unit((tile, quad))] = (head_pick(dqueries[index]) * 0.125).astype(BF16)

    key_lane = lax.broadcasted_iota(jnp.int32, (1, acc_ref.shape[1]), 1) < 512

    def scale(level):
        return jnp.where(key_lane, 0.5 ** STEP[level], 1.0)

    def low(level, start, count):
        return (acc_ref[pl.ds(start, count), :] * scale(level)).astype(BF16)

    def edges(left_ref, right_ref):
        for level in range(LEVELS - 1):
            base = POFF[level]
            edge = pl.ds(HALO * level, HALO)
            left_ref[edge, :] = low(level, base, HALO)
            right_ref[edge, :] = low(level, base + HALO + CELLS[level], HALO)

    piece = where_ref[0]
    pl.when(piece % 2 == 0)(lambda: edges(far_ref, near_ref))
    pl.when(piece % 2 == 1)(lambda: edges(near_ref, far_ref))
    for level in range(LEVELS - 1):
        dkv_ref[pl.ds(OFF[level], CELLS[level]), :] = low(level, POFF[level] + HALO, CELLS[level])
    dkv_ref[pl.ds(OFF[7], 16), :] = jnp.zeros((16, acc_ref.shape[1]), BF16)
    blank = jnp.zeros((PIECE7, acc_ref.shape[1]), F32)

    def high(index):
        rows = pl.ds(pl.multiple_of(POFF[7] + PIECE7 * index, PIECE7), PIECE7)
        return jnp.concatenate([acc_ref[rows, :] * scale(7), blank], axis=0).astype(BF16)

    ends_ref[...] = high(3 - piece)
    across_ref[...] = high((piece + 2) % 4)


def attend_back(micro, where, cells, stats, dout, ids, const):
    width = dout.shape[2]
    shape = jax.ShapeDtypeStruct
    outs = cell_shapes(width) + edge_shapes(width) + edge_shapes(width)[2:]
    one = lambda dims: one_of(dims, micro)
    ins = list(cells[:2]) + list(stats) + [dout]
    return pl.pallas_call(
        attend_back_kernel,
        grid=(1,),
        in_specs=[SCALAR]
        + [one(value.shape[1:]) for value in ins]
        + id_specs(one)
        + [whole((8 * QL, QL))],
        out_specs=[whole(out) for out in outs],
        out_shape=[shape(out, BF16) for out in outs],
        scratch_shapes=[
            pltpu.VMEM((PADDED, 2 * width), F32),
            pltpu.VMEM((ROWS // 8, width), F32),
            pltpu.VMEM((2 * COARSE_TILES, 8 * QL), F32),
        ],
        compiler_params=params(),
        cost_estimate=timing(20),
        name="attend_back",
    )(where, *ins, *id_args(ids, const), const["spread_t"])


MID_ROWS = 512
FF_CHUNK = 512
ROOT = math.sqrt(2.0 / math.pi)


def share_out(send_ref, keep_ref, core, start, piece_of):
    for chip in range(send_ref.shape[0]):
        keep = piece_of(2 * chip + core)
        keep_ref[chip, pl.ds(start, keep.shape[0]), :] = keep
        send_ref[chip, pl.ds(start, keep.shape[0]), :] = piece_of(2 * chip + 1 - core)


def row_piece(ref, shard):
    def piece_of(index):
        return ref[pl.ds(pl.multiple_of(shard * index, shard), shard), :].astype(BF16)

    return piece_of


def middle_kernel(
    where_ref,
    tok_ref,
    cot_ref,
    mixed_ref,
    vec_ref,
    mine_ref,
    other_ref,
    out_ref,
    dmid_ref,
    dmix_ref,
    send_ref,
    keep_ref,
    wo_ref,
    wi_ref,
    wd_ref,
    acc_o,
    acc_i,
    acc_d,
    acc_b,
    acc_s,
    activ_ref,
    grad_ref,
):
    step = pl.program_id(0)
    core = where_ref[1]
    parts = wi_ref.shape[0]
    shard = wo_ref.shape[2]

    @pl.when(step == 0)
    def _():
        acc_o[...] = jnp.zeros(acc_o.shape, F32)
        acc_i[...] = jnp.zeros(acc_i.shape, F32)
        acc_d[...] = jnp.zeros(acc_d.shape, F32)
        acc_b[...] = jnp.zeros(acc_b.shape, F32)
        acc_s[...] = jnp.zeros(acc_s.shape, F32)
        take_weight(wo_ref, 0, mine_ref, other_ref, core, 0)
        for part in range(parts):
            take_weight(wi_ref, part, mine_ref, other_ref, core, shard * (1 + part))
        take_weight(wd_ref, 0, mine_ref, other_ref, core, shard * (1 + parts))

    wo = weight_of(wo_ref, 0)
    pieces = FF_CHUNK // wd_ref.shape[2]
    wi = [weight_of(wi_ref, part) for part in range(parts)]
    wd = [
        wd_ref[0, pieces * part : pieces * (part + 1)].reshape(FF_CHUNK, wo.shape[1])
        for part in range(parts)
    ]
    cot = cot_ref[...]
    top = cot.astype(BF16)
    mixed = mixed_ref[...]
    middle = tok_ref[...] + dot_nn(mixed, wo)
    unit, rate = normalised(middle)
    second = (unit * vec_ref[1:2] + vec_ref[3:4]).astype(BF16)
    result = middle + vec_ref[4:5]
    back = jnp.zeros(cot.shape, F32)
    pres = {}

    def first(part):
        pres[part] = (dot_nn(second, wi[part]) + vec_ref[5 + part : 6 + part], dot_nt(top, wd[part]))

    first(0)
    for part in range(parts):
        if part + 1 < parts:
            first(part + 1)
        pre, grad = pres.pop(part)
        square = pre * pre
        tanh = jnp.tanh(pre * (ROOT + (ROOT * 0.044715) * square))
        half = 0.5 + 0.5 * tanh
        activ = (pre * half).astype(BF16)
        slope = half + (pre * (0.5 - 0.5 * (tanh * tanh))) * (
            ROOT + (ROOT * 3 * 0.044715) * square
        )
        grad = (grad * slope).astype(BF16)
        cols = pl.ds(FF_CHUNK * part, FF_CHUNK)
        activ_ref[:, cols] = activ
        grad_ref[:, cols] = grad
        acc_b[:, cols] = acc_b[:, cols] + fold_rows(grad.astype(F32))
        result = result + dot_nn(activ, wd[part])
        back = back + dot_nt(grad, wi[part])
    out_ref[...] = result
    acc_d[...] = acc_d[...] + dot_tn(activ_ref[...], top)
    for part in range(parts):
        acc_i[part] = acc_i[part] + dot_tn(second, grad_ref[:, pl.ds(FF_CHUNK * part, FF_CHUNK)])
    dmid = cot + norm_back(back * vec_ref[1:2], unit, rate)
    dmid_ref[...] = dmid
    branch = dmid.astype(BF16)
    dmix_ref[...] = dot_nt(branch, wo).astype(BF16)
    acc_o[...] = acc_o[...] + dot_tn(mixed, branch)
    acc_s[0:8, :] = acc_s[0:8, :] + fold_rows(top.astype(F32))
    acc_s[8:16, :] = acc_s[8:16, :] + fold_rows(back * unit)
    acc_s[16:24, :] = acc_s[16:24, :] + fold_rows(back)

    @pl.when(step == pl.num_programs(0) - 1)
    def _():
        share_out(send_ref, keep_ref, core, 0, row_piece(acc_o, shard))
        for part in range(parts):
            share_out(
                send_ref, keep_ref, core, shard * (1 + part), row_piece(acc_i.at[part], shard)
            )
        share_out(send_ref, keep_ref, core, shard * (1 + parts), row_piece(acc_d, shard * parts))
        total = lambda value: jnp.sum(value, axis=0, keepdims=True)
        lines = [total(acc_s[8 * index : 8 * index + 8, :]) for index in range(3)]
        for part in range(parts):
            lines.append(total(acc_b[:, pl.ds(FF_CHUNK * part, FF_CHUNK)]))
        lines.append(jnp.zeros((16 - len(lines), lines[0].shape[1]), F32))
        lines = jnp.concatenate(lines, axis=0).astype(BF16)
        share_out(send_ref, keep_ref, core, shard * (1 + 2 * parts), lambda index: lines)


def middle_part(where, tokens, cot, mixed, vec, mine, other):
    rows, width = tokens.shape
    chips, lines, _ = mine.shape
    shard = width // (2 * chips)
    parts = (lines // shard - 1) // 2
    hidden = parts * FF_CHUNK
    shape = jax.ShapeDtypeStruct
    tiled = pl.BlockSpec((MID_ROWS, width), lambda r: (r, 0))
    shared = shape((chips, lines + 16, width), BF16)
    single = lambda dims: pl.BlockSpec(
        dims, lambda *_: (0,) * len(dims), pipeline_mode=pl.Buffered(1)
    )
    return pl.pallas_call(
        middle_kernel,
        grid=(rows // MID_ROWS,),
        in_specs=[SCALAR, tiled, tiled, tiled, whole(vec.shape), single(mine.shape), single(mine.shape)],
        out_specs=[tiled, tiled, tiled, single(shared.shape), single(shared.shape)],
        out_shape=[
            shape((rows, width), F32),
            shape((rows, width), F32),
            shape((rows, width), BF16),
            shared,
            shared,
        ],
        scratch_shapes=[
            pltpu.VMEM((1, 2 * chips, shard, width), BF16),
            pltpu.VMEM((parts, 2 * chips, shard, FF_CHUNK), BF16),
            pltpu.VMEM((1, 2 * chips, shard * parts, width), BF16),
            pltpu.VMEM((width, width), F32),
            pltpu.VMEM((parts, width, FF_CHUNK), F32),
            pltpu.VMEM((hidden, width), F32),
            pltpu.VMEM((8, hidden), F32),
            pltpu.VMEM((24, width), F32),
            pltpu.VMEM((MID_ROWS, hidden), BF16),
            pltpu.VMEM((MID_ROWS, hidden), BF16),
        ],
        compiler_params=params(),
        cost_estimate=timing(40),
        name="middle",
    )(where, tokens, cot, mixed, vec, mine, other)


def collect_kernel(
    where_ref, tok_ref, dq_ref, dq3_ref, dkv_ref, near_ref, far_ref, across_ref, ends_ref, low_ref, high_ref, *refs, first
):
    if first:
        dp_ref, gw_ref, sum_ref, cells_ref, norm_ref = refs
    else:
        held_ref, held_sum_ref, vec_ref, mine_ref, other_ref = refs[:5]
        dp_ref, send_ref, keep_ref, cells_ref, norm_ref, gw_ref, w_ref = refs[6:]
    piece, core = where_ref[0], where_ref[1]
    cells_ref[...] = dkv_ref[...]

    def add(start, value):
        rows = pl.ds(start, HALO)
        cells_ref[rows, :] = (cells_ref[rows, :].astype(F32) + value.astype(F32)).astype(BF16)

    def edges(left_ref, right_ref):
        for level in range(LEVELS - 1):
            edge = pl.ds(HALO * level, HALO)

            @pl.when(piece > 0)
            def _():
                add(OFF[level], left_ref[edge, :])

            @pl.when(piece < 3)
            def _():
                add(OFF[level] + CELLS[level] - HALO, right_ref[edge, :])

    pl.when(piece % 2 == 0)(lambda: edges(far_ref, near_ref))
    pl.when(piece % 2 == 1)(lambda: edges(near_ref, far_ref))
    add(OFF[7], across_ref[...].astype(F32) + ends_ref[...].astype(F32))

    sums = [jnp.zeros((8, 512), F32), jnp.zeros((8, 1024), F32)]
    for chunk in range(ROWS // 256):
        rows = pl.ds(256 * chunk, 256)
        norm_ref[rows, :] = normalised(tok_ref[0, rows, :])[0].astype(BF16)
        cells = jnp.concatenate(
            [
                cells_ref[pl.ds(OFF[level] + (256 >> level) * chunk, 256 >> level), :]
                for level in range(1, 5)
            ],
            axis=0,
        )
        dkv = (
            cells_ref[rows, :].astype(F32)
            + dot_nn(low_ref[...], cells)
            + dot_nn(high_ref[rows, :], cells_ref[pl.ds(OFF[5], 64), :])
        ).astype(BF16)
        dq = (
            dq_ref[rows, :].astype(F32)
            + dot_nn(low_ref[:, 192:224], dq3_ref[pl.ds(32 * chunk, 32), :])
        ).astype(BF16)
        dp_ref[0, rows, pl.ds(0, 512)] = dq
        dp_ref[0, rows, pl.ds(512, 1024)] = dkv
        sums = [old + fold_rows(new.astype(F32)) for old, new in zip(sums, (dq, dkv))]
    sums = jnp.concatenate(sums, axis=1)
    if first:
        sum_ref[...] = sums
    else:
        sums = jnp.sum(sums + held_sum_ref[...], axis=0, keepdims=True)
        row = lax.broadcasted_iota(jnp.int32, (VEC, 512), 0)
        lines = vec_ref[...].astype(BF16)
        gain = dot_tn(lines, jnp.where(row == 0, 1.0, 0.0).astype(BF16))
        offset = dot_tn(lines, jnp.where(row == 2, 1.0, 0.0).astype(BF16))
        ones = jnp.ones((8, 512), BF16)
        grad_gain = jnp.zeros((8, 512), F32)
        grad_offset = jnp.zeros((8, 512), F32)
        for index in range(3):
            take_weight(w_ref, index, mine_ref, other_ref, core, w_ref.shape[2] * index)
    for index in range(3):
        grad = dot_tn(norm_ref[...], dp_ref[0, :, pl.ds(512 * index, 512)])
        if first:
            gw_ref[index] = grad
        else:
            grad = grad + held_ref[index]
            total = sums[:, 512 * index : 512 * (index + 1)]
            gw_ref[index] = gain * grad + offset * total
            weight = weight_of(w_ref, index)
            high, middle, _ = three_terms(weight.astype(F32) * grad)
            grad_gain = grad_gain + dot_nt(ones, high) + dot_nt(ones, middle)
            high, middle, low = three_terms(total)
            terms = jnp.concatenate([high, middle, low] + [jnp.zeros_like(low)] * 5, axis=0)
            grad_offset = grad_offset + dot_nt(terms, weight)
    if not first:
        shard = w_ref.shape[2]
        for index in range(3):
            share_out(send_ref, keep_ref, core, shard * index, row_piece(gw_ref.at[index], shard))
        grad_offset = jnp.sum(grad_offset, axis=0, keepdims=True)
        blank = jnp.zeros((VEC - 2, 512), F32)
        lines = jnp.concatenate([grad_gain[0:1], grad_offset, blank], axis=0).astype(BF16)
        share_out(send_ref, keep_ref, core, 3 * shard, lambda index: lines)


def collect(micro, where, tokens, grads, received, const, held=None):
    width = tokens.shape[2]
    shape = jax.ShapeDtypeStruct
    first = held is None
    ins = list(grads) + list(received) + [const["low_t"], const["high_t"]]
    outs = [shape((tokens.shape[0], ROWS, 3 * width), BF16)]
    scratch = [pltpu.VMEM((2 * ROWS, 2 * width), BF16), pltpu.VMEM((ROWS, width), BF16)]
    kept = []
    aliases = {}
    if first:
        outs += [shape((3, width, width), F32), shape((8, 3 * width), F32)]
    else:
        ins += held[1:]
        kept = [held[0]]
        mine = held[-1]
        chips, lines, _ = mine.shape
        shard = width // (2 * chips)
        aliases = {2 + len(ins): 0}
        outs += [shape((chips, lines, width), BF16)] * 2
        scratch.append(pltpu.VMEM((3, width, width), F32))
        scratch.append(pltpu.VMEM((3, 2 * chips, shard, width), BF16))
    specs = [SCALAR, one_of((ROWS, width), micro)] + [whole(value.shape) for value in ins]
    return pl.pallas_call(
        lambda *refs: collect_kernel(*refs, first=first),
        grid=(1,),
        in_specs=specs + [KEPT] * len(kept),
        out_specs=[one_of((ROWS, 3 * width), micro)] + [whole(out.shape) for out in outs[1:]],
        out_shape=outs,
        scratch_shapes=scratch,
        input_output_aliases=aliases,
        compiler_params=params(),
        cost_estimate=timing(8),
        name="collect",
    )(where, tokens, *ins, *kept)


FIN_ROWS = 256


def finish_kernel(where_ref, tok_ref, dmid_ref, dp_ref, vec_ref, mine_ref, other_ref, *refs):
    grad_ref, w_ref = refs[-2:]
    core = where_ref[1]

    @pl.when(pl.program_id(0) == 0)
    def _():
        for index in range(3):
            take_weight(w_ref, index, mine_ref, other_ref, core, w_ref.shape[2] * index)

    back = dot_nt(dp_ref[0, :, pl.ds(0, 512)], weight_of(w_ref, 0))
    for index in range(1, 3):
        back = back + dot_nt(dp_ref[0, :, pl.ds(512 * index, 512)], weight_of(w_ref, index))
    unit, rate = normalised(tok_ref[0])
    grad_ref[0] = dmid_ref[0] + norm_back(back * vec_ref[0:1], unit, rate)


def finish(micro, where, tokens, dmid, dproj, vec, mine, other, kept):
    width = tokens.shape[2]
    dp = 2 * mine.shape[0]
    ins = [where, tokens, dmid, dproj, vec, mine, other] + ([] if kept is None else [kept])
    chunk = lambda lanes: pl.BlockSpec((1, FIN_ROWS, lanes), lambda r: (micro, r, 0))
    return pl.pallas_call(
        finish_kernel,
        grid=(ROWS // FIN_ROWS,),
        in_specs=[
            SCALAR,
            chunk(width),
            chunk(width),
            chunk(3 * width),
            whole(vec.shape),
            whole(mine.shape),
            whole(other.shape),
        ]
        + [KEPT] * (len(ins) - 7),
        out_specs=chunk(width),
        out_shape=jax.ShapeDtypeStruct(tokens.shape, F32),
        scratch_shapes=[pltpu.VMEM((3, dp, width // dp, width), BF16)],
        input_output_aliases={} if kept is None else {7: 0},
        compiler_params=params(),
        cost_estimate=timing(6),
        name="finish",
    )(*ins)


def twice(chunk):
    lane = lax.broadcasted_iota(jnp.int32, chunk.shape, 1)
    other = pltpu.roll(chunk, 64, 1)
    halves = jnp.where(lane < 64, chunk, other), jnp.where(lane < 64, other, chunk)
    return [jnp.concatenate([half, half], axis=1)[0:1] for half in halves]


def lane_pairs(value, size, merge):
    halves = []
    for half in range(2):
        part = value[:, 128 * half : 128 * (half + 1)]
        lane = lax.broadcasted_iota(jnp.int32, part.shape, 1)
        first = (lane & size) == 0
        pair = jnp.where(first, pltpu.roll(part, 128 - size, 1), pltpu.roll(part, size, 1))
        halves.append(merge(part, pair))
    return jnp.concatenate(halves, axis=1)


def documents_kernel(where_ref, seg_ref, own_ref, kid_ref, qidf_ref, qidc_ref, row_ref):
    piece = where_ref[0]
    length = seg_ref.shape[2]
    margin = (row_ref.shape[0] - length) // 2
    ones = jnp.ones((16, 128), BF16)

    def only_first(row):
        index = lax.broadcasted_iota(jnp.int32, (16, row.shape[1]), 0)
        return jnp.where(index == 0, row.astype(F32), 0.0).astype(BF16)

    outside = jnp.full((margin, 128), -3.0, F32)
    row_ref[pl.ds(0, margin), :] = outside
    row_ref[pl.ds(margin + length, margin), :] = outside
    row_ref[pl.ds(margin, length), :] = dot_tn(only_first(seg_ref[0]), ones)
    for level in range(LEVELS):
        cell = 1 << level
        if level < LEVELS - 1:
            start = ROWS * piece + margin - HALO * cell
            count = CELLS[level] + 2 * HALO
        else:
            start = margin
            count = 4 * PIECE7
        if level == 0:
            key = row_ref[at(start, count), :]
        else:
            lowest = row_ref[pl.ds(start, count, stride=cell), :]
            highest = row_ref[pl.ds(start + cell - 1, count, stride=cell), :]
            key = jnp.where(lowest == highest, lowest, -2.0)
        if level == LEVELS - 1:
            owner = lax.broadcasted_iota(jnp.int32, key.shape, 0) // PIECE7
            counted = (jnp.abs(owner // 2 - piece // 2) == 1) & (jnp.abs(owner - piece) >= 2)
            key = jnp.where(counted, key, -3.0)
        kid_ref[0, pl.ds(POFF[level], count), :] = key.astype(BF16)

    own = own_ref[0].astype(F32)
    rows = []
    for chunk in range(ROWS // 128):
        rows += twice(jnp.broadcast_to(own[:, 128 * chunk : 128 * (chunk + 1)], (8, 128)))
    low = high = jnp.concatenate(rows, axis=0)
    for level in range(FINE):
        if level > 0:
            low = lane_pairs(low, 1 << (level - 1), jnp.minimum)
            high = lane_pairs(high, 1 << (level - 1), jnp.maximum)
        qidf_ref[0, pl.ds(FINE_TILES * level, FINE_TILES), :] = jnp.where(low == high, low, -1.0)

    token = lax.broadcasted_iota(jnp.int32, (ROWS, ROWS // 8), 0)
    cells = lax.broadcasted_iota(jnp.int32, (ROWS, ROWS // 8), 1)
    ends = []
    for step in (0, 7):
        pick = jnp.where(token == 8 * cells + step, 1.0, 0.0).astype(BF16)
        value = dot_nn(only_first(own), pick)[0:1]
        rows = twice(jnp.broadcast_to(value, (8, 128)))
        ends.append(jnp.concatenate(rows + [rows[1]] * 6, axis=0))
    low, high = ends
    for index in range(LEVELS - FINE):
        if index > 0:
            low = lane_pairs(low, 1 << (index - 1), jnp.minimum)
            high = lane_pairs(high, 1 << (index - 1), jnp.maximum)
        qidc_ref[0, pl.ds(8 * index, 8), :] = jnp.where(low == high, low, -1.0)


def cell_documents(where, segments, piece):
    micro, _, length = segments.shape
    shape = jax.ShapeDtypeStruct
    own = lax.dynamic_slice_in_dim(segments, piece * ROWS, ROWS, axis=2)
    outs = [((PADDED, 128), BF16), ((FINE * FINE_TILES, QL), F32), ((8 * (LEVELS - FINE), QL), F32)]
    key, fine, coarse = pl.pallas_call(
        documents_kernel,
        grid=(micro,),
        in_specs=[SCALAR, each_of((1, length)), each_of((1, ROWS))],
        out_specs=[each_of(dims) for dims, _ in outs],
        out_shape=[shape((micro,) + dims, kind) for dims, kind in outs],
        scratch_shapes=[pltpu.VMEM((length + 2 * ROWS, 128), F32)],
        compiler_params=params(),
        cost_estimate=timing(5),
        name="documents",
    )(where, segments, own)
    return dict(key=key, fine=fine, coarse=coarse)


def same_core(chips):
    return [[2 * chip + core for chip in range(chips)] for core in range(2)]


def core_swap(value, chips):
    pairs = [(place, place ^ 1) for place in range(2 * chips)]
    return lax.ppermute(value, "dp", pairs)


def chip_exchange(value, chips):
    return lax.all_to_all(value, "dp", 0, 0, axis_index_groups=same_core(chips), tiled=True)


def after(value, *done):
    return lax.optimization_barrier((value,) + done)[0]


def add(left, right):
    return left.astype(F32) + right.astype(F32)


def body(
    tokens,
    segment_ids,
    norm_gains,
    norm_biases,
    qkv_weight,
    out_weight,
    in_weight,
    in_bias,
    down_weight,
    down_bias,
    cotangent,
):
    micro, _, row_count, width = tokens.shape
    pieces = lax.axis_size("sp")
    piece = lax.axis_index("sp")
    assert row_count == ROWS and pieces == 4 and micro == 2
    const = constants()
    tokens = tokens[:, 0]
    cotangent = cotangent[:, 0]
    dp = lax.axis_size("dp")
    place = lax.axis_index("dp")
    chips = dp // 2
    shard = width // dp
    hidden = in_weight.shape[1]
    parts = hidden // FF_CHUNK
    where = jnp.stack([piece, place % 2]).astype(jnp.int32)
    swap = lambda value, bits: lax.ppermute(value, "sp", [(p, p ^ bits) for p in range(pieces)])
    spread = lambda value: chip_exchange(
        jnp.broadcast_to(value[None], (chips,) + value.shape), chips
    )

    def placed(value, start):
        lines = jnp.zeros((value.shape[0], start * value.shape[1]), BF16)
        return lax.dynamic_update_slice(lines, value, (0, place * value.shape[1])).reshape(-1, width)

    small = placed(jnp.concatenate([norm_gains, norm_biases, down_bias[None]]), dp)
    small = jnp.concatenate([small, placed(in_bias[None], dp)])
    small = jnp.pad(small, ((0, VEC - small.shape[0]), (0, 0)))
    mine = spread(jnp.concatenate([qkv_weight.reshape(3 * shard, width), small]))
    ids = cell_documents(where, segment_ids, piece)
    where, mine = lax.optimization_barrier((after(where, ids["coarse"]), mine))
    other = core_swap(mine, chips)
    rest = jnp.concatenate(
        [
            out_weight,
            in_weight.reshape(shard, parts, FF_CHUNK).swapaxes(0, 1).reshape(-1, width),
            down_weight,
        ]
    )
    rest_mine = spread(after(rest, other))

    def halo(near, far, across, ends):
        middle = lax.ppermute(far, "sp", [(1, 2), (2, 1)])
        return swap(near, 1), middle, swap(across, 2), lax.ppermute(ends, "sp", [(0, 3), (3, 0)])

    q, q3, kv, near, far, top, vec = project(where, tokens, mine, other, const)
    cells = (q, q3, kv)
    received = halo(near, far, top, top)
    rest_mine = after(rest_mine, *received)
    rest_other = core_swap(rest_mine, chips)
    mixed, *stats = attend(after(where, rest_mine), cells, received, ids, const)
    rest_other = after(rest_other, mixed)

    flat = lambda value: value.reshape(micro * ROWS, width)
    split = lambda value: value.reshape(micro, ROWS, width)
    outputs, dmid, dmix, send, keep = middle_part(
        where, flat(tokens), flat(cotangent), flat(mixed), vec, rest_mine, rest_other
    )

    grads, back = [], []

    def attention_back(m, where):
        dq, dq3, dkv, *edges = attend_back(m, where, cells, stats, split(dmix), ids, const)
        grads.append((dq, dq3, dkv))
        back.append(halo(*edges))

    come = core_swap(send, chips)
    attention_back(0, where)
    pair = add(keep, after(come, grads[0][1])).astype(BF16)
    come = chip_exchange(pair, chips)
    attention_back(1, after(where, pair))
    dproj, held, sums = collect(0, after(where, grads[1][1]), tokens, grads[0], back[0], const)

    odd = piece % 2 == 1
    total = jnp.sum(after(come, sums).astype(F32), axis=0).astype(BF16)
    come = swap(total, 1)
    dproj, send, keep = collect(
        1, after(where, total), tokens, grads[1], back[1], const, [dproj, held, sums, vec, mine, other]
    )
    qkv_come = core_swap(send, chips)
    total = add(total, after(come, send)).astype(BF16)
    half = jnp.where(odd, total[:, width // 2 :], total[:, : width // 2])
    come = swap(half, 2)
    input_grad = finish(0, after(where, half), tokens, split(dmid), dproj, vec, mine, other, None)
    pair = add(keep, after(qkv_come, input_grad)).astype(BF16)
    qkv_come = chip_exchange(pair, chips)
    input_grad = finish(
        1, after(where, pair), tokens, split(dmid), dproj, vec, mine, other, input_grad
    )
    half = add(half, after(come, input_grad)).astype(BF16)
    come = swap(half, 1)
    total = jnp.sum(after(qkv_come, half).astype(F32), axis=0).astype(BF16)
    qkv_come = swap(total, 1)
    come = after(come, total)
    rest = jnp.where(
        odd, jnp.concatenate([come, half], axis=1), jnp.concatenate([half, come], axis=1)
    ).astype(F32)
    total = add(total, qkv_come).astype(BF16)
    total = add(total, swap(total, 2))

    own = lambda value, size: lax.dynamic_slice_in_dim(value, place * size, size, axis=-1)
    small_two = rest[shard * (1 + 2 * parts) :]
    small_one = total[3 * shard :]
    gin = rest[shard : shard * (1 + parts)].reshape(parts, shard, FF_CHUNK).swapaxes(0, 1)
    return (
        outputs.reshape(micro, 1, ROWS, width),
        input_grad[:, None],
        own(jnp.stack([small_one[0], small_two[1]]), shard),
        own(jnp.stack([small_one[1], small_two[2]]), shard),
        total[: 3 * shard].reshape(3, shard, width),
        rest[:shard],
        gin.reshape(shard, hidden),
        own(small_two[3 : 3 + parts].reshape(hidden), hidden // dp),
        rest[shard * (1 + parts) : shard * (1 + 2 * parts)],
        own(small_two[0], shard),
    )


def solution(mesh):
    in_specs = (
        P(None, "dp", "sp", None),
        P(None, "dp", None),
        P(None, "dp"),
        P(None, "dp"),
        P(None, "dp", None),
        P("dp", None),
        P("dp", None),
        P("dp"),
        P("dp", None),
        P("dp"),
        P(None, "dp", "sp", None),
    )
    out_specs = (
        P(None, "dp", "sp", None),
        P(None, "dp", "sp", None),
        P(None, "dp"),
        P(None, "dp"),
        P(None, "dp", None),
        P("dp", None),
        P("dp", None),
        P("dp"),
        P("dp", None),
        P("dp"),
    )
    return jax.shard_map(body, mesh=mesh, in_specs=in_specs, out_specs=out_specs, check_vma=False)
```

```python
import math

import jax
import jax.numpy as jnp
import numpy as np
from jax import lax
from jax.experimental import pallas as pl
from jax.experimental.pallas import tpu as pltpu
from jax.sharding import PartitionSpec as P

HEADS = 8
HEAD_DIM = 64
BLOCK = 16
LEVELS = 8
HALO = 16
TILE = 64
QUAD = 4
QL = QUAD * HEAD_DIM
NEG = -1e30
FINE = 3
ROWS = 1024
EDGE = 112
VEC = 16
GROUP = 8
GROUP_BACK = 4
F32 = jnp.float32
BF16 = jnp.bfloat16

CELLS = [ROWS >> level for level in range(LEVELS)]
OFF = [2 * ROWS - (2 * ROWS >> level) for level in range(LEVELS)]
POFF = []
_at = 0
for _level in range(LEVELS - 1):
    POFF.append(_at)
    _at += CELLS[_level] + 2 * HALO
POFF.append(_at)
PIECE7 = CELLS[LEVELS - 1]
PADDED = _at + 4 * PIECE7
FINE_TILES = ROWS // TILE
COARSE_TILES = ROWS // 8 // TILE
FINE_KEYS = 192
COARSE_KEYS = 256
LN_EPS = 1e-05
VMEM_LIMIT = 62 * 1024 * 1024


def _counts(level, query, key):
    query = query[None, :]
    key = key[:, None]
    near = np.abs(query // 16 - key // 16)
    if level == 0:
        return near <= 1
    return (near == 1) & (np.abs(query // 8 - key // 8) >= 2)


def _bias(parts):
    rows = []
    for level, allowed in parts:
        rows.append(np.where(allowed, np.float32(level * math.log(2.0)), np.float32(NEG)))
    block = np.concatenate(rows, axis=0).astype(np.float32)
    return np.tile(block, (1, QUAD))


def _two_blocks():
    return np.concatenate([np.arange(16) - 16, np.arange(16) + 16])


def fine_bias():
    token = np.arange(TILE)
    return _bias(
        [
            (0, _counts(0, token, np.arange(96) - 16)),
            (1, _counts(1, token // 2, np.arange(64) - 16)),
            (2, _counts(2, token // 4, _two_blocks())),
        ]
    )


def coarse_bias():
    cell = np.arange(TILE)
    out = []
    for tile in range(COARSE_TILES):
        out.append(
            _bias(
                [
                    (3, _counts(3, cell, np.arange(96) - 16)),
                    (4, _counts(4, cell // 2, np.arange(64) - 16)),
                    (5, _counts(5, cell // 4, _two_blocks())),
                    (6, _counts(6, 8 * tile + cell // 8, _two_blocks())),
                    (7, np.ones((4 * PIECE7, TILE), bool)),
                ]
            )
        )
    return np.stack(out)


STEP = [0, 1, 2, 0, 1, 2, 3, 4]


def mean_rows(cell, count):
    return (np.arange(count)[None, :] // cell == np.arange(count // cell)[:, None]).astype(
        np.float32
    ) / cell


def spread_matrix():
    out = np.zeros((QUAD, TILE, QUAD, TILE), np.float32)
    for token in range(TILE):
        for head in range(QUAD):
            out[head, token // 8, head, token] = 1.0
    return out.reshape(QL, QL)


def constants():
    head_mask = np.kron(np.eye(QUAD), np.ones((TILE, HEAD_DIM)))
    low = [mean_rows(1 << level, 256) for level in range(1, 5)]
    high = [mean_rows(1 << level, ROWS) for level in range(5, 8)] + [np.zeros((8, ROWS))]
    key_low = [rows * 0.5 ** STEP[level] for level, rows in zip(range(1, 5), low)]
    key_high = [rows * 0.5**step for step, rows in zip(STEP[5:] + [0], high)]
    as_low = lambda value: jnp.asarray(value.astype(np.float32)).astype(BF16)
    low, high = np.concatenate(low), np.concatenate(high)
    return dict(
        fine=jnp.asarray(fine_bias()),
        coarse=jnp.asarray(coarse_bias()),
        head_mask=as_low(head_mask),
        low=as_low(np.stack([np.concatenate(key_low), low])),
        high=as_low(np.stack([np.concatenate(key_high), high])),
        low_t=as_low(low.T),
        high_t=as_low(high.T),
        spread=as_low(spread_matrix()),
        spread_t=as_low(spread_matrix().T),
    )


def dot_nn(left, right):
    return jnp.dot(left, right, preferred_element_type=F32)


def dot_nt(left, right):
    return lax.dot_general(left, right, (((1,), (1,)), ((), ())), preferred_element_type=F32)


def dot_tn(left, right):
    return lax.dot_general(left, right, (((0,), (0,)), ((), ())), preferred_element_type=F32)


def at(start, size):
    return pl.ds(pl.multiple_of(start, 16), size)


def whole(shape):
    zeros = (0,) * len(shape)
    return pl.BlockSpec(shape, lambda *_: zeros)


def one_of(shape, micro):
    zeros = (0,) * len(shape)
    return pl.BlockSpec((1,) + shape, lambda *_: (micro,) + zeros)


def each_of(shape):
    zeros = (0,) * len(shape)
    return pl.BlockSpec((1,) + shape, lambda step: (step,) + zeros)


SCALAR = pl.BlockSpec(memory_space=pltpu.SMEM)
KEPT = pl.BlockSpec(memory_space=pl.ANY)


def timing(micros):
    return pl.CostEstimate(
        flops=int(micros * 4e8), bytes_accessed=int(micros * 3e6), transcendentals=0
    )


def params():
    return pltpu.CompilerParams(
        dimension_semantics=("arbitrary",), vmem_limit_bytes=VMEM_LIMIT
    )


def normalised(rows):
    center = rows - jnp.mean(rows, axis=-1, keepdims=True)
    spread = jnp.mean(center * center, axis=-1, keepdims=True)
    rate = lax.rsqrt(spread + LN_EPS)
    return center * rate, rate


def norm_back(grad, unit, rate):
    mean_grad = jnp.mean(grad, axis=-1, keepdims=True)
    mean_dot = jnp.mean(grad * unit, axis=-1, keepdims=True)
    return rate * (grad - mean_grad - unit * mean_dot)


def fold_rows(value):
    return jnp.sum(value.reshape(-1, 8, value.shape[-1]), axis=0)


def take_weight(target, index, mine, other, core, start):
    chips, shard = mine.shape[0], target.shape[2]
    for chip in range(chips):
        target[index, 2 * chip + core] = mine[chip, pl.ds(start, shard), :]
        target[index, 2 * chip + 1 - core] = other[chip, pl.ds(start, shard), :]


def weight_of(ref, index):
    return ref[index].reshape(ref.shape[1] * ref.shape[2], ref.shape[3])


def project_kernel(
    where_ref,
    tok_ref,
    mine_ref,
    other_ref,
    low_ref,
    high_ref,
    q_ref,
    q3_ref,
    kv_ref,
    near_ref,
    far_ref,
    top_ref,
    vec_ref,
    w_ref,
    norm_ref,
):
    piece, core = where_ref[0], where_ref[1]
    shard = w_ref.shape[2]

    @pl.when(pl.program_id(0) == 0)
    def _():
        for index in range(3):
            take_weight(w_ref, index, mine_ref, other_ref, core, shard * index)
        vec = jnp.zeros(vec_ref.shape, F32)
        for chip in range(mine_ref.shape[0]):
            for ref in (mine_ref, other_ref):
                vec = vec + ref[chip, pl.ds(3 * shard, VEC), :].astype(F32)
        vec_ref[...] = vec

    for chunk in range(ROWS // 256):
        rows = pl.ds(256 * chunk, 256)
        unit, _ = normalised(tok_ref[0, rows, :])
        norm_ref[rows, :] = (unit * vec_ref[0:1] + vec_ref[2:3]).astype(BF16)
    for half in range(2):
        rows = pl.ds(512 * half, 512)
        for index in range(3):
            value = dot_nn(norm_ref[rows, :], weight_of(w_ref, index)).astype(BF16)
            if index == 0:
                q_ref[0, rows, :] = value
            else:
                kv_ref[0, rows, pl.ds(512 * (index - 1), 512)] = value
    for chunk in range(ROWS // 256):
        rows = pl.ds(256 * chunk, 256)
        q3_ref[0, pl.ds(32 * chunk, 32), :] = dot_nn(
            low_ref[1, 192:224, :], q_ref[0, rows, :]
        ).astype(BF16)
        for part in range(2):
            lanes = pl.ds(512 * part, 512)
            cells = dot_nn(low_ref[part], kv_ref[0, rows, lanes]).astype(BF16)
            start = 0
            for level in range(1, 5):
                count = 256 >> level
                kv_ref[0, pl.ds(OFF[level] + count * chunk, count), lanes] = cells[
                    start : start + count
                ]
                start += count
    for part in range(2):
        lanes = pl.ds(512 * part, 512)
        kv_ref[0, pl.ds(OFF[5], 64), lanes] = dot_nn(
            high_ref[part], kv_ref[0, pl.ds(0, ROWS), lanes]
        ).astype(BF16)

    def edges(left_ref, right_ref):
        for level in range(LEVELS - 1):
            edge = pl.ds(HALO * level, HALO)
            left_ref[0, edge, :] = kv_ref[0, pl.ds(OFF[level], HALO), :]
            right_ref[0, edge, :] = kv_ref[0, pl.ds(OFF[level] + CELLS[level] - HALO, HALO), :]

    pl.when(piece % 2 == 0)(lambda: edges(far_ref, near_ref))
    pl.when(piece % 2 == 1)(lambda: edges(near_ref, far_ref))
    top_ref[0] = kv_ref[0, pl.ds(OFF[7], 16), :]


def cell_shapes(width):
    return [(ROWS, width), (ROWS // 8, width), (2 * ROWS, 2 * width)]


def edge_shapes(width):
    return [(EDGE, 2 * width), (EDGE, 2 * width), (16, 2 * width)]


def project(where, tokens, mine, other, const):
    micro, _, width = tokens.shape
    shape = jax.ShapeDtypeStruct
    shard = width // (2 * mine.shape[0])
    outs = cell_shapes(width) + edge_shapes(width)
    return pl.pallas_call(
        project_kernel,
        grid=(micro,),
        in_specs=[
            SCALAR,
            each_of((ROWS, width)),
            whole(mine.shape),
            whole(other.shape),
            whole((2, 240, 256)),
            whole((2, 64, ROWS)),
        ],
        out_specs=[each_of(out) for out in outs] + [whole((VEC, width))],
        out_shape=[shape((micro,) + out, BF16) for out in outs] + [shape((VEC, width), F32)],
        scratch_shapes=[
            pltpu.VMEM((3, width // shard, shard, width), BF16),
            pltpu.VMEM((ROWS, width), BF16),
        ],
        compiler_params=params(),
        cost_estimate=timing(13),
        name="project",
    )(where, tokens, mine, other, const["low"], const["high"])


def fine_windows(tile):
    return [
        (POFF[0] + 64 * tile, 96),
        (POFF[1] + 32 * tile, 64),
        (POFF[2] + 16 * tile, 16),
        (POFF[2] + 16 * tile + 32, 16),
    ]


def coarse_windows(tile):
    return [
        (POFF[3] + 64 * tile, 96),
        (POFF[4] + 32 * tile, 64),
        (POFF[5] + 16 * tile, 16),
        (POFF[5] + 16 * tile + 32, 16),
        (POFF[6], 16),
        (POFF[6] + 32, 16),
        (POFF[7], 32),
    ]


FINE_LEVELS = [96, 64, 32]
COARSE_LEVELS = [96, 64, 32, 32, 32]


def gather_rows(ref, windows, lanes):
    return jnp.concatenate([ref[at(start, size), lanes] for start, size in windows], axis=0)


def tile_bias(kid_ref, qid_ref, tile, tiles, windows, levels, bias):
    keys = jnp.concatenate([kid_ref[0, at(start, size), :] for start, size in windows], axis=0)
    keys = keys.astype(F32)
    keys = jnp.concatenate([keys, keys], axis=1)
    out = []
    start = 0
    for index, count in enumerate(levels):
        part = slice(start, start + count)
        owner = qid_ref[0, pl.ds(tiles * index + tile, 1), :]
        out.append(jnp.where(keys[part] == owner, bias[part], NEG))
        start += count
    return jnp.concatenate(out, axis=0)


def lane_sums(value, steps):
    halves = []
    for half in range(2):
        part = value[:, 128 * half : 128 * (half + 1)]
        lane = lax.broadcasted_iota(jnp.int32, part.shape, 1)
        for step in range(steps):
            size = 1 << step
            first = (lane & size) == 0
            part = part + jnp.where(
                first, pltpu.roll(part, 128 - size, 1), pltpu.roll(part, size, 1)
            )
        halves.append(part)
    return jnp.concatenate(halves, axis=1)


def lane_roll(value, shift):
    if shift == 0:
        return value
    halves = [value[:, 128 * half : 128 * (half + 1)] for half in range(2)]
    return jnp.concatenate([pltpu.roll(part, shift % 128, 1) for part in halves], axis=1)


def far_row(tile, quad):
    return pl.ds(8 * (tile % 8) + 2 * (tile // 8) + quad, 1)


def level_sums(value, levels):
    out = [value[0 : levels[0]]]
    start = levels[0]
    for index, count in enumerate(levels[1:]):
        out.append(lane_sums(value[start : start + count], index + 1))
        start += count
    return jnp.concatenate(out, axis=0)


def head_stack(value, mask):
    return jnp.concatenate([value] * QUAD, axis=0) * mask


def head_pick(stacked):
    lane = lax.broadcasted_iota(jnp.int32, (TILE, QL), 1) // HEAD_DIM
    out = stacked[0:TILE]
    for head in range(1, QUAD):
        out = jnp.where(lane == head, stacked[TILE * head : TILE * (head + 1)], out)
    return out


def three_terms(row):
    high = row.astype(BF16)
    rest = row - high.astype(F32)
    middle = rest.astype(BF16)
    low = (rest - middle.astype(F32)).astype(BF16)
    return high, middle, low


def own_cell(tile):
    cell = lax.broadcasted_iota(jnp.int32, (16, QL), 0)
    token = lax.broadcasted_iota(jnp.int32, (16, QL), 1) % TILE
    return cell == 8 * (tile % 2) + token // 8


def lay_out(piece, kv_ref, near_ref, far_ref, across_ref, ends_ref, kvp_ref):
    def edges(left_ref, right_ref):
        for level in range(LEVELS - 1):
            base = POFF[level]
            edge = pl.ds(HALO * level, HALO)
            kvp_ref[pl.ds(base, HALO), :] = left_ref[0, edge, :]
            kvp_ref[pl.ds(base + HALO + CELLS[level], HALO), :] = right_ref[0, edge, :]

    pl.when(piece % 2 == 0)(lambda: edges(far_ref, near_ref))
    pl.when(piece % 2 == 1)(lambda: edges(near_ref, far_ref))
    for level in range(LEVELS - 1):
        count = CELLS[level]
        kvp_ref[pl.ds(POFF[level] + HALO, count), :] = kv_ref[0, pl.ds(OFF[level], count), :]
    across = across_ref[0].astype(F32)[0:PIECE7]
    ends = ends_ref[0].astype(F32)[0:PIECE7]
    tops = []
    for owner in range(4):
        top = jnp.where(owner == (piece + 2) % 4, across, jnp.where(owner == 3 - piece, ends, 0.0))
        tops.append(top)
    kvp_ref[pl.ds(POFF[7], 4 * PIECE7), :] = jnp.concatenate(tops, axis=0).astype(BF16)


def attend_kernel(
    where_ref,
    q_ref,
    q3_ref,
    kv_ref,
    near_ref,
    far_ref,
    across_ref,
    ends_ref,
    kid_ref,
    qidf_ref,
    qidc_ref,
    fine_ref,
    coarse_ref,
    mask_ref,
    spread_ref,
    mixed_ref,
    lse_ref,
    lsec_ref,
    lsex_ref,
    oc_ref,
    kvp_ref,
):
    lay_out(where_ref[0], kv_ref, near_ref, far_ref, across_ref, ends_ref, kvp_ref)
    mask = mask_ref[...]
    scaled = mask * jnp.asarray(0.125, BF16)

    units = [(tile, quad) for tile in range(COARSE_TILES) for quad in range(2)]
    biases = [
        tile_bias(kid_ref, qidc_ref, tile, 8, coarse_windows(tile), COARSE_LEVELS, coarse_ref[tile])
        for tile in range(COARSE_TILES)
    ]
    scores = []
    for tile, quad in units:
        lanes = pl.ds(QL * quad, QL)
        query = head_stack(q3_ref[0, pl.ds(TILE * tile, TILE), lanes], scaled)
        scores.append(dot_nt(gather_rows(kvp_ref, coarse_windows(tile), lanes), query))
    shares = []
    lines = []
    for index, (tile, quad) in enumerate(units):
        score = level_sums(scores[index], COARSE_LEVELS) + biases[index // 2]
        top = jnp.max(score, axis=0, keepdims=True)
        share = jnp.exp(score - top)
        total = jnp.sum(share, axis=0, keepdims=True)
        lse = top + jnp.log(total)
        lsec_ref[0, pl.ds(index, 1), :] = lse
        lines.append(lse)
        shares.append((share * (1.0 / total)).astype(BF16))
    results = []
    for (tile, quad), share in zip(units, shares):
        values = gather_rows(kvp_ref, coarse_windows(tile), pl.ds(512 + QL * quad, QL))
        results.append(dot_tn(share, values))
    lines = three_terms(jnp.concatenate(lines * 2, axis=0))
    lines = jnp.concatenate([line.astype(F32) for line in lines], axis=0)
    terms = [lane_roll(lines, -8 * part) for part in range(8)]
    terms = dot_nn(jnp.concatenate(terms, axis=0).astype(BF16), spread_ref[...])
    for part in range(8):
        rows = [terms[24 * part + 8 * index : 24 * part + 8 * index + 8] for index in range(3)]
        lsex_ref[0, pl.ds(8 * part, 8), :] = rows[0] + rows[1] + rows[2]
    for index, (tile, quad) in enumerate(units):
        oc_ref[0, pl.ds(TILE * tile, TILE), pl.ds(QL * quad, QL)] = head_pick(
            results[index]
        ).astype(BF16)

    def fine_group(group, carry):
        tiles = [GROUP * group + index for index in range(GROUP)]
        units = [(tile, quad) for tile in tiles for quad in range(2)]
        biases = [
            tile_bias(kid_ref, qidf_ref, tile, FINE_TILES, fine_windows(tile), FINE_LEVELS, fine_ref[...])
            for tile in tiles
        ]
        scores = []
        for tile, quad in units:
            lanes = pl.ds(QL * quad, QL)
            query = head_stack(q_ref[0, at(TILE * tile, TILE), lanes], scaled)
            scores.append(dot_nt(gather_rows(kvp_ref, fine_windows(tile), lanes), query))
        shares = []
        for index, (tile, quad) in enumerate(units):
            score = level_sums(scores[index], FINE_LEVELS) + biases[index // 2]
            far = lsex_ref[0, far_row(tile, quad), :]
            top = jnp.maximum(jnp.max(score, axis=0, keepdims=True), far)
            share = jnp.exp(score - top)
            far_share = jnp.exp(far - top)
            total = jnp.sum(share, axis=0, keepdims=True) + far_share
            lse_ref[0, pl.ds(2 * tile + quad, 1), :] = top + jnp.log(total)
            inverse = 1.0 / total
            shares.append(
                jnp.concatenate(
                    [share * inverse, jnp.where(own_cell(tile), far_share * inverse, 0.0)], axis=0
                ).astype(BF16)
            )
        results = []
        for (tile, quad), share in zip(units, shares):
            values = jnp.concatenate(
                [
                    gather_rows(kvp_ref, fine_windows(tile), pl.ds(512 + QL * quad, QL)),
                    oc_ref[0, at(16 * (tile // 2), 16), pl.ds(QL * quad, QL)],
                ],
                axis=0,
            )
            results.append(dot_tn(share, values))
        for (tile, quad), result in zip(units, results):
            mixed_ref[0, at(TILE * tile, TILE), pl.ds(QL * quad, QL)] = head_pick(result).astype(
                BF16
            )
        return carry

    lax.fori_loop(0, FINE_TILES // GROUP, fine_group, 0)


def stat_shapes(width):
    return [
        ((2 * FINE_TILES, QL), F32),
        ((2 * COARSE_TILES, QL), F32),
        ((64, QL), F32),
        ((ROWS // 8, width), BF16),
    ]


def id_specs(spec):
    return [
        spec((PADDED, 128)),
        spec((FINE * FINE_TILES, QL)),
        spec((8 * (LEVELS - FINE), QL)),
        whole((FINE_KEYS, QL)),
        whole((COARSE_TILES, COARSE_KEYS, QL)),
        whole((QL, QL)),
    ]


def id_args(ids, const):
    return [ids["key"], ids["fine"], ids["coarse"], const["fine"], const["coarse"], const["head_mask"]]


def attend(where, cells, received, ids, const):
    micro, _, width = cells[0].shape
    outs = [((ROWS, width), BF16)] + stat_shapes(width)
    ins = list(cells) + list(received)
    return pl.pallas_call(
        attend_kernel,
        grid=(micro,),
        in_specs=[SCALAR]
        + [each_of(value.shape[1:]) for value in ins]
        + id_specs(each_of)
        + [whole((QL, QL))],
        out_specs=[each_of(dims) for dims, _ in outs],
        out_shape=[jax.ShapeDtypeStruct((micro,) + dims, kind) for dims, kind in outs],
        scratch_shapes=[pltpu.VMEM((PADDED, 2 * width), BF16)],
        compiler_params=params(),
        cost_estimate=timing(23),
        name="attend",
    )(where, *ins, *id_args(ids, const), const["spread"])


def add_rows(ref, windows, lanes, value):
    start = 0
    for base, count in windows:
        rows = at(base, count)
        ref[rows, lanes] = ref[rows, lanes] + value[start : start + count]
        start += count


def attend_back_kernel(
    where_ref,
    q_ref,
    q3_ref,
    kv_ref,
    near_in_ref,
    far_in_ref,
    across_in_ref,
    ends_in_ref,
    lse_ref,
    lsec_ref,
    lsex_ref,
    oc_ref,
    dout_ref,
    kid_ref,
    qidf_ref,
    qidc_ref,
    fine_ref,
    coarse_ref,
    mask_ref,
    spread_t_ref,
    dq_ref,
    dq3_ref,
    dkv_ref,
    near_ref,
    far_ref,
    across_ref,
    ends_ref,
    acc_ref,
    dcell_ref,
    delta_ref,
    kvp_ref,
):
    lay_out(where_ref[0], kv_ref, near_in_ref, far_in_ref, across_in_ref, ends_in_ref, kvp_ref)
    delta_ref[...] = jnp.zeros(delta_ref.shape, F32)
    acc_ref[...] = jnp.zeros(acc_ref.shape, F32)
    dcell_ref[...] = jnp.zeros(dcell_ref.shape, F32)
    mask = mask_ref[...]
    scaled = mask * jnp.asarray(0.125, BF16)

    def fine_group(group, carry):
        tiles = [GROUP_BACK * group + index for index in range(GROUP_BACK)]
        units = [(tile, quad) for tile in tiles for quad in range(2)]
        biases = [
            tile_bias(kid_ref, qidf_ref, tile, FINE_TILES, fine_windows(tile), FINE_LEVELS, fine_ref[...])
            for tile in tiles
        ]
        at_unit = lambda unit: (at(TILE * unit[0], TILE), pl.ds(QL * unit[1], QL))
        queries = [head_stack(q_ref[(0,) + at_unit(unit)], scaled) for unit in units]
        douts = [head_stack(dout_ref[(0,) + at_unit(unit)], mask) for unit in units]
        scores = []
        steers = []
        for index, (tile, quad) in enumerate(units):
            keys = gather_rows(kvp_ref, fine_windows(tile), pl.ds(QL * quad, QL))
            scores.append(dot_nt(keys, queries[index]))
            values = jnp.concatenate(
                [
                    gather_rows(kvp_ref, fine_windows(tile), pl.ds(512 + QL * quad, QL)),
                    oc_ref[0, at(16 * (tile // 2), 16), pl.ds(QL * quad, QL)],
                ],
                axis=0,
            )
            steers.append(dot_nt(values, douts[index]))
        shares = []
        grads = []
        for index, (tile, quad) in enumerate(units):
            lse = lse_ref[0, pl.ds(2 * tile + quad, 1), :]
            far_share = jnp.exp(lsex_ref[0, far_row(tile, quad), :] - lse)
            share = jnp.exp(level_sums(scores[index], FINE_LEVELS) + biases[index // 2] - lse)
            share = jnp.concatenate([share, jnp.where(own_cell(tile), far_share, 0.0)], axis=0)
            weighted = share * steers[index]
            delta = jnp.sum(weighted, axis=0, keepdims=True)
            delta_ref[far_row(tile, quad), :] = far_share * delta
            grad = weighted[0:FINE_KEYS] - share[0:FINE_KEYS] * delta
            grads.append(level_sums(grad, FINE_LEVELS).astype(BF16))
            shares.append(share.astype(BF16))
        dvalues = [dot_nn(share, dout) for share, dout in zip(shares, douts)]
        dkeys = [dot_nn(grad, query) for grad, query in zip(grads, queries)]
        dqueries = []
        for (tile, quad), grad in zip(units, grads):
            keys = gather_rows(kvp_ref, fine_windows(tile), pl.ds(QL * quad, QL))
            dqueries.append(dot_tn(grad, keys))
        for index, (tile, quad) in enumerate(units):
            lanes = pl.ds(QL * quad, QL)
            cells = at(16 * (tile // 2), 16)
            windows = fine_windows(tile)
            add_rows(acc_ref, windows, pl.ds(512 + QL * quad, QL), dvalues[index])
            dcell_ref[cells, lanes] = dcell_ref[cells, lanes] + dvalues[index][FINE_KEYS:]
            add_rows(acc_ref, windows, lanes, dkeys[index])
            dq_ref[at_unit((tile, quad))] = (head_pick(dqueries[index]) * 0.125).astype(BF16)
        return carry

    lax.fori_loop(0, FINE_TILES // GROUP_BACK, fine_group, 0)

    units = [(tile, quad) for tile in range(COARSE_TILES) for quad in range(2)]
    biases = [
        tile_bias(kid_ref, qidc_ref, tile, 8, coarse_windows(tile), COARSE_LEVELS, coarse_ref[tile])
        for tile in range(COARSE_TILES)
    ]
    at_unit = lambda unit: (pl.ds(TILE * unit[0], TILE), pl.ds(QL * unit[1], QL))
    queries = [head_stack(q3_ref[(0,) + at_unit(unit)], scaled) for unit in units]
    douts = [head_stack(dcell_ref[at_unit(unit)].astype(BF16), mask) for unit in units]
    terms = dot_nn(jnp.concatenate(three_terms(delta_ref[...]), axis=0), spread_t_ref[...])
    terms = terms[0:64] + terms[64:128] + terms[128:192]
    deltas = lane_roll(terms[0:8], 0)
    for part in range(1, 8):
        deltas = deltas + lane_roll(terms[8 * part : 8 * part + 8], 8 * part)
    steers = []
    scores = []
    for (tile, quad), dout, query in zip(units, douts, queries):
        values = gather_rows(kvp_ref, coarse_windows(tile), pl.ds(512 + QL * quad, QL))
        steers.append(dot_nt(values, dout))
        keys = gather_rows(kvp_ref, coarse_windows(tile), pl.ds(QL * quad, QL))
        scores.append(dot_nt(keys, query))
    shares = []
    grads = []
    for index, (tile, quad) in enumerate(units):
        score = level_sums(scores[index], COARSE_LEVELS) + biases[index // 2]
        share = jnp.exp(score - lsec_ref[0, pl.ds(index, 1), :])
        delta = deltas[index : index + 1]
        grads.append(level_sums(share * (steers[index] - delta), COARSE_LEVELS).astype(BF16))
        shares.append(share.astype(BF16))
    dvalues = [dot_nn(share, dout) for share, dout in zip(shares, douts)]
    dkeys = [dot_nn(grad, query) for grad, query in zip(grads, queries)]
    dqueries = []
    for (tile, quad), grad in zip(units, grads):
        keys = gather_rows(kvp_ref, coarse_windows(tile), pl.ds(QL * quad, QL))
        dqueries.append(dot_tn(grad, keys))
    for index, (tile, quad) in enumerate(units):
        windows = coarse_windows(tile)
        add_rows(acc_ref, windows, pl.ds(512 + QL * quad, QL), dvalues[index])
        add_rows(acc_ref, windows, pl.ds(QL * quad, QL), dkeys[index])
        dq3_ref[at_unit((tile, quad))] = (head_pick(dqueries[index]) * 0.125).astype(BF16)

    key_lane = lax.broadcasted_iota(jnp.int32, (1, acc_ref.shape[1]), 1) < 512

    def scale(level):
        return jnp.where(key_lane, 0.5 ** STEP[level], 1.0)

    def low(level, start, count):
        return (acc_ref[pl.ds(start, count), :] * scale(level)).astype(BF16)

    def edges(left_ref, right_ref):
        for level in range(LEVELS - 1):
            base = POFF[level]
            edge = pl.ds(HALO * level, HALO)
            left_ref[edge, :] = low(level, base, HALO)
            right_ref[edge, :] = low(level, base + HALO + CELLS[level], HALO)

    piece = where_ref[0]
    pl.when(piece % 2 == 0)(lambda: edges(far_ref, near_ref))
    pl.when(piece % 2 == 1)(lambda: edges(near_ref, far_ref))
    for level in range(LEVELS - 1):
        dkv_ref[pl.ds(OFF[level], CELLS[level]), :] = low(level, POFF[level] + HALO, CELLS[level])
    dkv_ref[pl.ds(OFF[7], 16), :] = jnp.zeros((16, acc_ref.shape[1]), BF16)
    blank = jnp.zeros((PIECE7, acc_ref.shape[1]), F32)

    def high(index):
        rows = pl.ds(pl.multiple_of(POFF[7] + PIECE7 * index, PIECE7), PIECE7)
        return jnp.concatenate([acc_ref[rows, :] * scale(7), blank], axis=0).astype(BF16)

    ends_ref[...] = high(3 - piece)
    across_ref[...] = high((piece + 2) % 4)


def attend_back(micro, where, cells, received, stats, dout, ids, const):
    width = dout.shape[2]
    shape = jax.ShapeDtypeStruct
    outs = cell_shapes(width) + edge_shapes(width) + edge_shapes(width)[2:]
    one = lambda dims: one_of(dims, micro)
    ins = list(cells) + list(received) + list(stats) + [dout]
    return pl.pallas_call(
        attend_back_kernel,
        grid=(1,),
        in_specs=[SCALAR]
        + [one(value.shape[1:]) for value in ins]
        + id_specs(one)
        + [whole((QL, QL))],
        out_specs=[whole(out) for out in outs],
        out_shape=[shape(out, BF16) for out in outs],
        scratch_shapes=[
            pltpu.VMEM((PADDED, 2 * width), F32),
            pltpu.VMEM((ROWS // 8, width), F32),
            pltpu.VMEM((64, QL), F32),
            pltpu.VMEM((PADDED, 2 * width), BF16),
        ],
        compiler_params=params(),
        cost_estimate=timing(20),
        name="attend_back",
    )(where, *ins, *id_args(ids, const), const["spread_t"])


MID_ROWS = 512
FF_CHUNK = 512
ROOT = math.sqrt(2.0 / math.pi)


def share_out(send_ref, keep_ref, core, start, piece_of):
    for chip in range(send_ref.shape[0]):
        keep = piece_of(2 * chip + core)
        keep_ref[chip, pl.ds(start, keep.shape[0]), :] = keep
        send_ref[chip, pl.ds(start, keep.shape[0]), :] = piece_of(2 * chip + 1 - core)


def row_piece(ref, shard):
    def piece_of(index):
        return ref[pl.ds(pl.multiple_of(shard * index, shard), shard), :].astype(BF16)

    return piece_of


def middle_kernel(
    where_ref,
    tok_ref,
    cot_ref,
    mixed_ref,
    vec_ref,
    mine_ref,
    other_ref,
    out_ref,
    dmid_ref,
    dmix_ref,
    send_ref,
    keep_ref,
    wo_ref,
    wi_ref,
    wd_ref,
    acc_o,
    acc_i,
    acc_d,
    acc_b,
    acc_s,
    activ_ref,
    grad_ref,
):
    step = pl.program_id(0)
    core = where_ref[1]
    parts = wi_ref.shape[0]
    shard = wo_ref.shape[2]

    @pl.when(step == 0)
    def _():
        acc_o[...] = jnp.zeros(acc_o.shape, F32)
        acc_i[...] = jnp.zeros(acc_i.shape, F32)
        acc_d[...] = jnp.zeros(acc_d.shape, F32)
        acc_b[...] = jnp.zeros(acc_b.shape, F32)
        acc_s[...] = jnp.zeros(acc_s.shape, F32)
        take_weight(wo_ref, 0, mine_ref, other_ref, core, 0)
        for part in range(parts):
            take_weight(wi_ref, part, mine_ref, other_ref, core, shard * (1 + part))
        take_weight(wd_ref, 0, mine_ref, other_ref, core, shard * (1 + parts))

    wo = weight_of(wo_ref, 0)
    pieces = FF_CHUNK // wd_ref.shape[2]
    wi = [weight_of(wi_ref, part) for part in range(parts)]
    wd = [
        wd_ref[0, pieces * part : pieces * (part + 1)].reshape(FF_CHUNK, wo.shape[1])
        for part in range(parts)
    ]
    cot = cot_ref[...]
    top = cot.astype(BF16)
    mixed = mixed_ref[...]
    middle = tok_ref[...] + dot_nn(mixed, wo)
    unit, rate = normalised(middle)
    second = (unit * vec_ref[1:2] + vec_ref[3:4]).astype(BF16)
    result = middle + vec_ref[4:5]
    back = jnp.zeros(cot.shape, F32)
    pres = {}

    def first(part):
        pres[part] = (dot_nn(second, wi[part]) + vec_ref[5 + part : 6 + part], dot_nt(top, wd[part]))

    first(0)
    for part in range(parts):
        if part + 1 < parts:
            first(part + 1)
        pre, grad = pres.pop(part)
        square = pre * pre
        tanh = jnp.tanh(pre * (ROOT + (ROOT * 0.044715) * square))
        half = 0.5 + 0.5 * tanh
        activ = (pre * half).astype(BF16)
        slope = half + (pre * (0.5 - 0.5 * (tanh * tanh))) * (
            ROOT + (ROOT * 3 * 0.044715) * square
        )
        grad = (grad * slope).astype(BF16)
        cols = pl.ds(FF_CHUNK * part, FF_CHUNK)
        activ_ref[:, cols] = activ
        grad_ref[:, cols] = grad
        acc_b[:, cols] = acc_b[:, cols] + fold_rows(grad.astype(F32))
        result = result + dot_nn(activ, wd[part])
        back = back + dot_nt(grad, wi[part])
    out_ref[...] = result
    acc_d[...] = acc_d[...] + dot_tn(activ_ref[...], top)
    for part in range(parts):
        acc_i[part] = acc_i[part] + dot_tn(second, grad_ref[:, pl.ds(FF_CHUNK * part, FF_CHUNK)])
    dmid = cot + norm_back(back * vec_ref[1:2], unit, rate)
    dmid_ref[...] = dmid
    branch = dmid.astype(BF16)
    dmix_ref[...] = dot_nt(branch, wo).astype(BF16)
    acc_o[...] = acc_o[...] + dot_tn(mixed, branch)
    acc_s[0:8, :] = acc_s[0:8, :] + fold_rows(top.astype(F32))
    acc_s[8:16, :] = acc_s[8:16, :] + fold_rows(back * unit)
    acc_s[16:24, :] = acc_s[16:24, :] + fold_rows(back)

    @pl.when(step == pl.num_programs(0) - 1)
    def _():
        share_out(send_ref, keep_ref, core, 0, row_piece(acc_o, shard))
        for part in range(parts):
            share_out(
                send_ref, keep_ref, core, shard * (1 + part), row_piece(acc_i.at[part], shard)
            )
        share_out(send_ref, keep_ref, core, shard * (1 + parts), row_piece(acc_d, shard * parts))
        total = lambda value: jnp.sum(value, axis=0, keepdims=True)
        lines = [total(acc_s[8 * index : 8 * index + 8, :]) for index in range(3)]
        for part in range(parts):
            lines.append(total(acc_b[:, pl.ds(FF_CHUNK * part, FF_CHUNK)]))
        lines.append(jnp.zeros((16 - len(lines), lines[0].shape[1]), F32))
        lines = jnp.concatenate(lines, axis=0).astype(BF16)
        share_out(send_ref, keep_ref, core, shard * (1 + 2 * parts), lambda index: lines)


def middle_part(where, tokens, cot, mixed, vec, mine, other):
    rows, width = tokens.shape
    chips, lines, _ = mine.shape
    shard = width // (2 * chips)
    parts = (lines // shard - 1) // 2
    hidden = parts * FF_CHUNK
    shape = jax.ShapeDtypeStruct
    tiled = pl.BlockSpec((MID_ROWS, width), lambda r: (r, 0))
    shared = shape((chips, lines + 16, width), BF16)
    single = lambda dims: pl.BlockSpec(
        dims, lambda *_: (0,) * len(dims), pipeline_mode=pl.Buffered(1)
    )
    return pl.pallas_call(
        middle_kernel,
        grid=(rows // MID_ROWS,),
        in_specs=[SCALAR, tiled, tiled, tiled, whole(vec.shape), single(mine.shape), single(mine.shape)],
        out_specs=[tiled, tiled, tiled, single(shared.shape), single(shared.shape)],
        out_shape=[
            shape((rows, width), F32),
            shape((rows, width), F32),
            shape((rows, width), BF16),
            shared,
            shared,
        ],
        scratch_shapes=[
            pltpu.VMEM((1, 2 * chips, shard, width), BF16),
            pltpu.VMEM((parts, 2 * chips, shard, FF_CHUNK), BF16),
            pltpu.VMEM((1, 2 * chips, shard * parts, width), BF16),
            pltpu.VMEM((width, width), F32),
            pltpu.VMEM((parts, width, FF_CHUNK), F32),
            pltpu.VMEM((hidden, width), F32),
            pltpu.VMEM((8, hidden), F32),
            pltpu.VMEM((24, width), F32),
            pltpu.VMEM((MID_ROWS, hidden), BF16),
            pltpu.VMEM((MID_ROWS, hidden), BF16),
        ],
        compiler_params=params(),
        cost_estimate=timing(40),
        name="middle",
    )(where, tokens, cot, mixed, vec, mine, other)


def collect_kernel(
    where_ref, tok_ref, dq_ref, dq3_ref, dkv_ref, near_ref, far_ref, across_ref, ends_ref, low_ref, high_ref, *refs, first
):
    if first:
        dp_ref, gw_ref, sum_ref, cells_ref, norm_ref = refs
    else:
        held_ref, held_sum_ref, vec_ref, mine_ref, other_ref = refs[:5]
        dp_ref, send_ref, keep_ref, cells_ref, norm_ref, gw_ref, w_ref = refs[6:]
    piece, core = where_ref[0], where_ref[1]
    cells_ref[...] = dkv_ref[...]

    def add(start, value):
        rows = pl.ds(start, HALO)
        cells_ref[rows, :] = (cells_ref[rows, :].astype(F32) + value.astype(F32)).astype(BF16)

    def edges(left_ref, right_ref):
        for level in range(LEVELS - 1):
            edge = pl.ds(HALO * level, HALO)

            @pl.when(piece > 0)
            def _():
                add(OFF[level], left_ref[edge, :])

            @pl.when(piece < 3)
            def _():
                add(OFF[level] + CELLS[level] - HALO, right_ref[edge, :])

    pl.when(piece % 2 == 0)(lambda: edges(far_ref, near_ref))
    pl.when(piece % 2 == 1)(lambda: edges(near_ref, far_ref))
    add(OFF[7], across_ref[...].astype(F32) + ends_ref[...].astype(F32))

    sums = [jnp.zeros((8, 512), F32), jnp.zeros((8, 1024), F32)]
    for chunk in range(ROWS // 256):
        rows = pl.ds(256 * chunk, 256)
        norm_ref[rows, :] = normalised(tok_ref[0, rows, :])[0].astype(BF16)
        cells = jnp.concatenate(
            [
                cells_ref[pl.ds(OFF[level] + (256 >> level) * chunk, 256 >> level), :]
                for level in range(1, 5)
            ],
            axis=0,
        )
        dkv = (
            cells_ref[rows, :].astype(F32)
            + dot_nn(low_ref[...], cells)
            + dot_nn(high_ref[rows, :], cells_ref[pl.ds(OFF[5], 64), :])
        ).astype(BF16)
        dq = (
            dq_ref[rows, :].astype(F32)
            + dot_nn(low_ref[:, 192:224], dq3_ref[pl.ds(32 * chunk, 32), :])
        ).astype(BF16)
        dp_ref[0, rows, pl.ds(0, 512)] = dq
        dp_ref[0, rows, pl.ds(512, 1024)] = dkv
        sums = [old + fold_rows(new.astype(F32)) for old, new in zip(sums, (dq, dkv))]
    sums = jnp.concatenate(sums, axis=1)
    if first:
        sum_ref[...] = sums
    else:
        sums = jnp.sum(sums + held_sum_ref[...], axis=0, keepdims=True)
        row = lax.broadcasted_iota(jnp.int32, (VEC, 512), 0)
        lines = vec_ref[...].astype(BF16)
        gain = dot_tn(lines, jnp.where(row == 0, 1.0, 0.0).astype(BF16))
        offset = dot_tn(lines, jnp.where(row == 2, 1.0, 0.0).astype(BF16))
        ones = jnp.ones((8, 512), BF16)
        grad_gain = jnp.zeros((8, 512), F32)
        grad_offset = jnp.zeros((8, 512), F32)
        for index in range(3):
            take_weight(w_ref, index, mine_ref, other_ref, core, w_ref.shape[2] * index)
    for index in range(3):
        grad = dot_tn(norm_ref[...], dp_ref[0, :, pl.ds(512 * index, 512)])
        if first:
            gw_ref[index] = grad.astype(BF16)
        else:
            grad = grad + held_ref[index].astype(F32)
            total = sums[:, 512 * index : 512 * (index + 1)]
            gw_ref[index] = gain * grad + offset * total
            weight = weight_of(w_ref, index)
            high, middle, _ = three_terms(weight.astype(F32) * grad)
            grad_gain = grad_gain + dot_nt(ones, high) + dot_nt(ones, middle)
            high, middle, low = three_terms(total)
            terms = jnp.concatenate([high, middle, low] + [jnp.zeros_like(low)] * 5, axis=0)
            grad_offset = grad_offset + dot_nt(terms, weight)
    if not first:
        shard = w_ref.shape[2]
        for index in range(3):
            share_out(send_ref, keep_ref, core, shard * index, row_piece(gw_ref.at[index], shard))
        grad_offset = jnp.sum(grad_offset, axis=0, keepdims=True)
        blank = jnp.zeros((VEC - 2, 512), F32)
        lines = jnp.concatenate([grad_gain[0:1], grad_offset, blank], axis=0).astype(BF16)
        share_out(send_ref, keep_ref, core, 3 * shard, lambda index: lines)


def collect(micro, where, tokens, grads, received, const, held=None):
    width = tokens.shape[2]
    shape = jax.ShapeDtypeStruct
    first = held is None
    ins = list(grads) + list(received) + [const["low_t"], const["high_t"]]
    outs = [shape((tokens.shape[0], ROWS, 3 * width), BF16)]
    scratch = [pltpu.VMEM((2 * ROWS, 2 * width), BF16), pltpu.VMEM((ROWS, width), BF16)]
    kept = []
    aliases = {}
    if first:
        outs += [shape((3, width, width), BF16), shape((8, 3 * width), F32)]
    else:
        ins += held[1:]
        kept = [held[0]]
        mine = held[-1]
        chips, lines, _ = mine.shape
        shard = width // (2 * chips)
        aliases = {2 + len(ins): 0}
        outs += [shape((chips, lines, width), BF16)] * 2
        scratch.append(pltpu.VMEM((3, width, width), F32))
        scratch.append(pltpu.VMEM((3, 2 * chips, shard, width), BF16))
    specs = [SCALAR, one_of((ROWS, width), micro)] + [whole(value.shape) for value in ins]
    return pl.pallas_call(
        lambda *refs: collect_kernel(*refs, first=first),
        grid=(1,),
        in_specs=specs + [KEPT] * len(kept),
        out_specs=[one_of((ROWS, 3 * width), micro)] + [whole(out.shape) for out in outs[1:]],
        out_shape=outs,
        scratch_shapes=scratch,
        input_output_aliases=aliases,
        compiler_params=params(),
        cost_estimate=timing(8),
        name="collect",
    )(where, tokens, *ins, *kept)


FIN_ROWS = 256


def finish_kernel(where_ref, tok_ref, dmid_ref, dp_ref, vec_ref, mine_ref, other_ref, *refs):
    grad_ref, w_ref = refs[-2:]
    core = where_ref[1]

    @pl.when(pl.program_id(0) == 0)
    def _():
        for index in range(3):
            take_weight(w_ref, index, mine_ref, other_ref, core, w_ref.shape[2] * index)

    back = dot_nt(dp_ref[0, :, pl.ds(0, 512)], weight_of(w_ref, 0))
    for index in range(1, 3):
        back = back + dot_nt(dp_ref[0, :, pl.ds(512 * index, 512)], weight_of(w_ref, index))
    unit, rate = normalised(tok_ref[0])
    grad_ref[0] = dmid_ref[0] + norm_back(back * vec_ref[0:1], unit, rate)


def finish(micro, where, tokens, dmid, dproj, vec, mine, other, kept):
    width = tokens.shape[2]
    dp = 2 * mine.shape[0]
    ins = [where, tokens, dmid, dproj, vec, mine, other] + ([] if kept is None else [kept])
    chunk = lambda lanes: pl.BlockSpec((1, FIN_ROWS, lanes), lambda r: (micro, r, 0))
    return pl.pallas_call(
        finish_kernel,
        grid=(ROWS // FIN_ROWS,),
        in_specs=[
            SCALAR,
            chunk(width),
            chunk(width),
            chunk(3 * width),
            whole(vec.shape),
            whole(mine.shape),
            whole(other.shape),
        ]
        + [KEPT] * (len(ins) - 7),
        out_specs=chunk(width),
        out_shape=jax.ShapeDtypeStruct(tokens.shape, F32),
        scratch_shapes=[pltpu.VMEM((3, dp, width // dp, width), BF16)],
        input_output_aliases={} if kept is None else {7: 0},
        compiler_params=params(),
        cost_estimate=timing(6),
        name="finish",
    )(*ins)


def twice(chunk):
    lane = lax.broadcasted_iota(jnp.int32, chunk.shape, 1)
    other = pltpu.roll(chunk, 64, 1)
    halves = jnp.where(lane < 64, chunk, other), jnp.where(lane < 64, other, chunk)
    return [jnp.concatenate([half, half], axis=1)[0:1] for half in halves]


def lane_pairs(value, size, merge):
    halves = []
    for half in range(2):
        part = value[:, 128 * half : 128 * (half + 1)]
        lane = lax.broadcasted_iota(jnp.int32, part.shape, 1)
        first = (lane & size) == 0
        pair = jnp.where(first, pltpu.roll(part, 128 - size, 1), pltpu.roll(part, size, 1))
        halves.append(merge(part, pair))
    return jnp.concatenate(halves, axis=1)


def documents_kernel(where_ref, seg_ref, own_ref, kid_ref, qidf_ref, qidc_ref, row_ref):
    piece = where_ref[0]
    length = seg_ref.shape[2]
    margin = (row_ref.shape[0] - length) // 2
    ones = jnp.ones((16, 128), BF16)

    def only_first(row):
        index = lax.broadcasted_iota(jnp.int32, (16, row.shape[1]), 0)
        return jnp.where(index == 0, row.astype(F32), 0.0).astype(BF16)

    outside = jnp.full((margin, 128), -3.0, F32)
    row_ref[pl.ds(0, margin), :] = outside
    row_ref[pl.ds(margin + length, margin), :] = outside
    row_ref[pl.ds(margin, length), :] = dot_tn(only_first(seg_ref[0]), ones)
    for level in range(LEVELS):
        cell = 1 << level
        if level < LEVELS - 1:
            start = ROWS * piece + margin - HALO * cell
            count = CELLS[level] + 2 * HALO
        else:
            start = margin
            count = 4 * PIECE7
        if level == 0:
            key = row_ref[at(start, count), :]
        else:
            lowest = row_ref[pl.ds(start, count, stride=cell), :]
            highest = row_ref[pl.ds(start + cell - 1, count, stride=cell), :]
            key = jnp.where(lowest == highest, lowest, -2.0)
        if level == LEVELS - 1:
            owner = lax.broadcasted_iota(jnp.int32, key.shape, 0) // PIECE7
            counted = (jnp.abs(owner // 2 - piece // 2) == 1) & (jnp.abs(owner - piece) >= 2)
            key = jnp.where(counted, key, -3.0)
        kid_ref[0, pl.ds(POFF[level], count), :] = key.astype(BF16)

    own = own_ref[0].astype(F32)
    rows = []
    for chunk in range(ROWS // 128):
        rows += twice(jnp.broadcast_to(own[:, 128 * chunk : 128 * (chunk + 1)], (8, 128)))
    low = high = jnp.concatenate(rows, axis=0)
    for level in range(FINE):
        if level > 0:
            low = lane_pairs(low, 1 << (level - 1), jnp.minimum)
            high = lane_pairs(high, 1 << (level - 1), jnp.maximum)
        qidf_ref[0, pl.ds(FINE_TILES * level, FINE_TILES), :] = jnp.where(low == high, low, -1.0)

    token = lax.broadcasted_iota(jnp.int32, (ROWS, ROWS // 8), 0)
    cells = lax.broadcasted_iota(jnp.int32, (ROWS, ROWS // 8), 1)
    ends = []
    for step in (0, 7):
        pick = jnp.where(token == 8 * cells + step, 1.0, 0.0).astype(BF16)
        value = dot_nn(only_first(own), pick)[0:1]
        rows = twice(jnp.broadcast_to(value, (8, 128)))
        ends.append(jnp.concatenate(rows + [rows[1]] * 6, axis=0))
    low, high = ends
    for index in range(LEVELS - FINE):
        if index > 0:
            low = lane_pairs(low, 1 << (index - 1), jnp.minimum)
            high = lane_pairs(high, 1 << (index - 1), jnp.maximum)
        qidc_ref[0, pl.ds(8 * index, 8), :] = jnp.where(low == high, low, -1.0)


def cell_documents(where, segments, piece):
    micro, _, length = segments.shape
    shape = jax.ShapeDtypeStruct
    own = lax.dynamic_slice_in_dim(segments, piece * ROWS, ROWS, axis=2)
    outs = [((PADDED, 128), BF16), ((FINE * FINE_TILES, QL), F32), ((8 * (LEVELS - FINE), QL), F32)]
    key, fine, coarse = pl.pallas_call(
        documents_kernel,
        grid=(micro,),
        in_specs=[SCALAR, each_of((1, length)), each_of((1, ROWS))],
        out_specs=[each_of(dims) for dims, _ in outs],
        out_shape=[shape((micro,) + dims, kind) for dims, kind in outs],
        scratch_shapes=[pltpu.VMEM((length + 2 * ROWS, 128), F32)],
        compiler_params=params(),
        cost_estimate=timing(5),
        name="documents",
    )(where, segments, own)
    return dict(key=key, fine=fine, coarse=coarse)


def same_core(chips):
    return [[2 * chip + core for chip in range(chips)] for core in range(2)]


def core_swap(value, chips):
    pairs = [(place, place ^ 1) for place in range(2 * chips)]
    return lax.ppermute(value, "dp", pairs)


def chip_exchange(value, chips):
    return lax.all_to_all(value, "dp", 0, 0, axis_index_groups=same_core(chips), tiled=True)


def after(value, *done):
    return lax.optimization_barrier((value,) + done)[0]


def add(left, right):
    return left.astype(F32) + right.astype(F32)


def body(
    tokens,
    segment_ids,
    norm_gains,
    norm_biases,
    qkv_weight,
    out_weight,
    in_weight,
    in_bias,
    down_weight,
    down_bias,
    cotangent,
):
    micro, _, row_count, width = tokens.shape
    pieces = lax.axis_size("sp")
    piece = lax.axis_index("sp")
    assert row_count == ROWS and pieces == 4 and micro == 2
    const = constants()
    tokens = tokens[:, 0]
    cotangent = cotangent[:, 0]
    dp = lax.axis_size("dp")
    place = lax.axis_index("dp")
    chips = dp // 2
    shard = width // dp
    hidden = in_weight.shape[1]
    parts = hidden // FF_CHUNK
    where = jnp.stack([piece, place % 2]).astype(jnp.int32)
    swap = lambda value, bits: lax.ppermute(value, "sp", [(p, p ^ bits) for p in range(pieces)])
    spread = lambda value: chip_exchange(
        jnp.broadcast_to(value[None], (chips,) + value.shape), chips
    )

    def placed(value, start):
        lines = jnp.zeros((value.shape[0], start * value.shape[1]), BF16)
        return lax.dynamic_update_slice(lines, value, (0, place * value.shape[1])).reshape(-1, width)

    small = placed(jnp.concatenate([norm_gains, norm_biases, down_bias[None]]), dp)
    small = jnp.concatenate([small, placed(in_bias[None], dp)])
    small = jnp.pad(small, ((0, VEC - small.shape[0]), (0, 0)))
    mine = spread(jnp.concatenate([qkv_weight.reshape(3 * shard, width), small]))
    ids = cell_documents(where, segment_ids, piece)
    where, mine = lax.optimization_barrier((after(where, ids["coarse"]), mine))
    other = core_swap(mine, chips)
    rest = jnp.concatenate(
        [
            out_weight,
            in_weight.reshape(shard, parts, FF_CHUNK).swapaxes(0, 1).reshape(-1, width),
            down_weight,
        ]
    )
    rest_mine = spread(after(rest, other))

    def halo(near, far, across, ends):
        middle = lax.ppermute(far, "sp", [(1, 2), (2, 1)])
        return swap(near, 1), middle, swap(across, 2), lax.ppermute(ends, "sp", [(0, 3), (3, 0)])

    q, q3, kv, near, far, top, vec = project(where, tokens, mine, other, const)
    cells = (q, q3, kv)
    received = halo(near, far, top, top)
    rest_mine = after(rest_mine, *received)
    rest_other = core_swap(rest_mine, chips)
    mixed, *stats = attend(after(where, rest_mine), cells, received, ids, const)
    rest_other = after(rest_other, mixed)

    flat = lambda value: value.reshape(micro * ROWS, width)
    split = lambda value: value.reshape(micro, ROWS, width)
    outputs, dmid, dmix, send, keep = middle_part(
        where, flat(tokens), flat(cotangent), flat(mixed), vec, rest_mine, rest_other
    )

    grads, back = [], []

    def attention_back(m, where):
        dq, dq3, dkv, *edges = attend_back(m, where, cells, received, stats, split(dmix), ids, const)
        grads.append((dq, dq3, dkv))
        back.append(halo(*edges))

    come = core_swap(send, chips)
    attention_back(0, where)
    pair = add(keep, after(come, grads[0][1])).astype(BF16)
    come = chip_exchange(pair, chips)
    attention_back(1, after(where, pair))
    dproj, held, sums = collect(0, after(where, grads[1][1]), tokens, grads[0], back[0], const)

    odd = piece % 2 == 1
    total = jnp.sum(after(come, sums).astype(F32), axis=0).astype(BF16)
    come = swap(after(total, *back[1]), 1)
    dproj, send, keep = collect(
        1, after(where, total), tokens, grads[1], back[1], const, [dproj, held, sums, vec, mine, other]
    )
    qkv_come = core_swap(send, chips)
    total = add(total, after(come, send)).astype(BF16)
    half = jnp.where(odd, total[:, width // 2 :], total[:, : width // 2])
    come = swap(half, 2)
    input_grad = finish(0, after(where, half), tokens, split(dmid), dproj, vec, mine, other, None)
    pair = add(keep, after(qkv_come, input_grad)).astype(BF16)
    qkv_come = chip_exchange(pair, chips)
    half = add(half, after(come, pair)).astype(BF16)
    come = swap(half, 1)
    input_grad = finish(
        1, after(where, half), tokens, split(dmid), dproj, vec, mine, other, input_grad
    )
    total = jnp.sum(after(qkv_come, input_grad).astype(F32), axis=0).astype(BF16)
    qkv_come = swap(total, 1)
    come = after(come, total)
    rest = jnp.where(
        odd, jnp.concatenate([come, half], axis=1), jnp.concatenate([half, come], axis=1)
    ).astype(F32)
    total = add(total, qkv_come).astype(BF16)
    total = add(total, swap(total, 2))

    own = lambda value, size: lax.dynamic_slice_in_dim(value, place * size, size, axis=-1)
    small_two = rest[shard * (1 + 2 * parts) :]
    small_one = total[3 * shard :]
    gin = rest[shard : shard * (1 + parts)].reshape(parts, shard, FF_CHUNK).swapaxes(0, 1)
    return (
        outputs.reshape(micro, 1, ROWS, width),
        input_grad[:, None],
        own(jnp.stack([small_one[0], small_two[1]]), shard),
        own(jnp.stack([small_one[1], small_two[2]]), shard),
        total[: 3 * shard].reshape(3, shard, width),
        rest[:shard],
        gin.reshape(shard, hidden),
        own(small_two[3 : 3 + parts].reshape(hidden), hidden // dp),
        rest[shard * (1 + parts) : shard * (1 + 2 * parts)],
        own(small_two[0], shard),
    )


def solution(mesh):
    in_specs = (
        P(None, "dp", "sp", None),
        P(None, "dp", None),
        P(None, "dp"),
        P(None, "dp"),
        P(None, "dp", None),
        P("dp", None),
        P("dp", None),
        P("dp"),
        P("dp", None),
        P("dp"),
        P(None, "dp", "sp", None),
    )
    out_specs = (
        P(None, "dp", "sp", None),
        P(None, "dp", "sp", None),
        P(None, "dp"),
        P(None, "dp"),
        P(None, "dp", None),
        P("dp", None),
        P("dp", None),
        P("dp"),
        P("dp", None),
        P("dp"),
    )
    return jax.shard_map(body, mesh=mesh, in_specs=in_specs, out_specs=out_specs, check_vma=False)
```

```python
import math

import jax
import jax.numpy as jnp
import numpy as np
from jax import lax
from jax.experimental import pallas as pl
from jax.experimental.pallas import tpu as pltpu
from jax.sharding import PartitionSpec as P

HEADS = 8
HEAD_DIM = 64
BLOCK = 16
LEVELS = 8
HALO = 16
TILE = 64
QUAD = 4
QL = QUAD * HEAD_DIM
NEG = -1e30
FINE = 3
ROWS = 1024
EDGE = 112
VEC = 16
GROUP = 8
GROUP_BACK = 4
F32 = jnp.float32
BF16 = jnp.bfloat16

CELLS = [ROWS >> level for level in range(LEVELS)]
OFF = [2 * ROWS - (2 * ROWS >> level) for level in range(LEVELS)]
POFF = []
_at = 0
for _level in range(LEVELS - 1):
    POFF.append(_at)
    _at += CELLS[_level] + 2 * HALO
POFF.append(_at)
PIECE7 = CELLS[LEVELS - 1]
PADDED = _at + 4 * PIECE7
FINE_TILES = ROWS // TILE
COARSE_TILES = ROWS // 8 // TILE
FINE_KEYS = 192
COARSE_KEYS = 256
LN_EPS = 1e-05
VMEM_LIMIT = 62 * 1024 * 1024


def _counts(level, query, key):
    query = query[None, :]
    key = key[:, None]
    near = np.abs(query // 16 - key // 16)
    if level == 0:
        return near <= 1
    return (near == 1) & (np.abs(query // 8 - key // 8) >= 2)


def _bias(parts):
    rows = []
    for level, allowed in parts:
        rows.append(np.where(allowed, np.float32(level * math.log(2.0)), np.float32(NEG)))
    block = np.concatenate(rows, axis=0).astype(np.float32)
    return np.tile(block, (1, QUAD // 2))


def _two_blocks():
    return np.concatenate([np.arange(16) - 16, np.arange(16) + 16])


def fine_bias():
    token = np.arange(TILE)
    return _bias(
        [
            (0, _counts(0, token, np.arange(96) - 16)),
            (1, _counts(1, token // 2, np.arange(64) - 16)),
            (2, _counts(2, token // 4, _two_blocks())),
        ]
    )


def coarse_bias():
    cell = np.arange(TILE)
    out = []
    for tile in range(COARSE_TILES):
        out.append(
            _bias(
                [
                    (3, _counts(3, cell, np.arange(96) - 16)),
                    (4, _counts(4, cell // 2, np.arange(64) - 16)),
                    (5, _counts(5, cell // 4, _two_blocks())),
                    (6, _counts(6, 8 * tile + cell // 8, _two_blocks())),
                    (7, np.ones((4 * PIECE7, TILE), bool)),
                ]
            )
        )
    return np.stack(out)


STEP = [0, 1, 2, 0, 1, 2, 3, 4]


def mean_rows(cell, count):
    return (np.arange(count)[None, :] // cell == np.arange(count // cell)[:, None]).astype(
        np.float32
    ) / cell


def spread_matrix():
    out = np.zeros((QUAD, TILE, QUAD, TILE), np.float32)
    for token in range(TILE):
        for head in range(QUAD):
            out[head, token // 8, head, token] = 1.0
    return out.reshape(QL, QL)


def constants():
    head_mask = np.kron(np.eye(QUAD), np.ones((TILE, HEAD_DIM)))
    low = [mean_rows(1 << level, 256) for level in range(1, 5)]
    high = [mean_rows(1 << level, ROWS) for level in range(5, 8)] + [np.zeros((8, ROWS))]
    key_low = [rows * 0.5 ** STEP[level] for level, rows in zip(range(1, 5), low)]
    key_high = [rows * 0.5**step for step, rows in zip(STEP[5:] + [0], high)]
    as_low = lambda value: jnp.asarray(value.astype(np.float32)).astype(BF16)
    low, high = np.concatenate(low), np.concatenate(high)
    return dict(
        fine=jnp.asarray(fine_bias()),
        coarse=jnp.asarray(coarse_bias()),
        head_mask=as_low(head_mask),
        low=as_low(np.stack([np.concatenate(key_low), low])),
        high=as_low(np.stack([np.concatenate(key_high), high])),
        low_t=as_low(low.T),
        high_t=as_low(high.T),
        spread=as_low(spread_matrix()),
        spread_t=as_low(spread_matrix().T),
    )


def dot_nn(left, right):
    return jnp.dot(left, right, preferred_element_type=F32)


def dot_nt(left, right):
    return lax.dot_general(left, right, (((1,), (1,)), ((), ())), preferred_element_type=F32)


def dot_tn(left, right):
    return lax.dot_general(left, right, (((0,), (0,)), ((), ())), preferred_element_type=F32)


def at(start, size):
    return pl.ds(pl.multiple_of(start, 16), size)


def whole(shape):
    zeros = (0,) * len(shape)
    return pl.BlockSpec(shape, lambda *_: zeros)


def one_of(shape, micro):
    zeros = (0,) * len(shape)
    return pl.BlockSpec((1,) + shape, lambda *_: (micro,) + zeros)


def each_of(shape):
    zeros = (0,) * len(shape)
    return pl.BlockSpec((1,) + shape, lambda step: (step,) + zeros)


SCALAR = pl.BlockSpec(memory_space=pltpu.SMEM)
KEPT = pl.BlockSpec(memory_space=pl.ANY)


def timing(micros):
    return pl.CostEstimate(
        flops=int(micros * 4e8), bytes_accessed=int(micros * 3e6), transcendentals=0
    )


def params():
    return pltpu.CompilerParams(
        dimension_semantics=("arbitrary",), vmem_limit_bytes=VMEM_LIMIT
    )


def normalised(rows):
    center = rows - jnp.mean(rows, axis=-1, keepdims=True)
    spread = jnp.mean(center * center, axis=-1, keepdims=True)
    rate = lax.rsqrt(spread + LN_EPS)
    return center * rate, rate


def norm_back(grad, unit, rate):
    mean_grad = jnp.mean(grad, axis=-1, keepdims=True)
    mean_dot = jnp.mean(grad * unit, axis=-1, keepdims=True)
    return rate * (grad - mean_grad - unit * mean_dot)


def fold_rows(value):
    return jnp.sum(value.reshape(-1, 8, value.shape[-1]), axis=0)


def take_weight(target, index, mine, other, core, start):
    chips, shard = mine.shape[0], target.shape[2]
    for chip in range(chips):
        target[index, 2 * chip + core] = mine[chip, pl.ds(start, shard), :]
        target[index, 2 * chip + 1 - core] = other[chip, pl.ds(start, shard), :]


def weight_of(ref, index):
    return ref[index].reshape(ref.shape[1] * ref.shape[2], ref.shape[3])


def project_kernel(
    where_ref,
    tok_ref,
    mine_ref,
    other_ref,
    low_ref,
    high_ref,
    q_ref,
    q3_ref,
    kv_ref,
    near_ref,
    far_ref,
    top_ref,
    vec_ref,
    w_ref,
    norm_ref,
):
    piece, core = where_ref[0], where_ref[1]
    shard = w_ref.shape[2]

    @pl.when(pl.program_id(0) == 0)
    def _():
        for index in range(3):
            take_weight(w_ref, index, mine_ref, other_ref, core, shard * index)
        vec = jnp.zeros(vec_ref.shape, F32)
        for chip in range(mine_ref.shape[0]):
            for ref in (mine_ref, other_ref):
                vec = vec + ref[chip, pl.ds(3 * shard, VEC), :].astype(F32)
        vec_ref[...] = vec

    for chunk in range(ROWS // 256):
        rows = pl.ds(256 * chunk, 256)
        unit, _ = normalised(tok_ref[0, rows, :])
        norm_ref[rows, :] = (unit * vec_ref[0:1] + vec_ref[2:3]).astype(BF16)
    for half in range(2):
        rows = pl.ds(512 * half, 512)
        for index in range(3):
            value = dot_nn(norm_ref[rows, :], weight_of(w_ref, index)).astype(BF16)
            if index == 0:
                q_ref[0, rows, :] = value
            else:
                kv_ref[0, rows, pl.ds(512 * (index - 1), 512)] = value
    for chunk in range(ROWS // 256):
        rows = pl.ds(256 * chunk, 256)
        q3_ref[0, pl.ds(32 * chunk, 32), :] = dot_nn(
            low_ref[1, 192:224, :], q_ref[0, rows, :]
        ).astype(BF16)
        for part in range(2):
            lanes = pl.ds(512 * part, 512)
            cells = dot_nn(low_ref[part], kv_ref[0, rows, lanes]).astype(BF16)
            start = 0
            for level in range(1, 5):
                count = 256 >> level
                kv_ref[0, pl.ds(OFF[level] + count * chunk, count), lanes] = cells[
                    start : start + count
                ]
                start += count
    for part in range(2):
        lanes = pl.ds(512 * part, 512)
        kv_ref[0, pl.ds(OFF[5], 64), lanes] = dot_nn(
            high_ref[part], kv_ref[0, pl.ds(0, ROWS), lanes]
        ).astype(BF16)

    def edges(left_ref, right_ref):
        for level in range(LEVELS - 1):
            edge = pl.ds(HALO * level, HALO)
            left_ref[0, edge, :] = kv_ref[0, pl.ds(OFF[level], HALO), :]
            right_ref[0, edge, :] = kv_ref[0, pl.ds(OFF[level] + CELLS[level] - HALO, HALO), :]

    pl.when(piece % 2 == 0)(lambda: edges(far_ref, near_ref))
    pl.when(piece % 2 == 1)(lambda: edges(near_ref, far_ref))
    top_ref[0] = kv_ref[0, pl.ds(OFF[7], 16), :]


def cell_shapes(width):
    return [(ROWS, width), (ROWS // 8, width), (2 * ROWS, 2 * width)]


def edge_shapes(width):
    return [(EDGE, 2 * width), (EDGE, 2 * width), (16, 2 * width)]


def project(where, tokens, mine, other, const):
    micro, _, width = tokens.shape
    shape = jax.ShapeDtypeStruct
    shard = width // (2 * mine.shape[0])
    outs = cell_shapes(width) + edge_shapes(width)
    return pl.pallas_call(
        project_kernel,
        grid=(micro,),
        in_specs=[
            SCALAR,
            each_of((ROWS, width)),
            whole(mine.shape),
            whole(other.shape),
            whole((2, 240, 256)),
            whole((2, 64, ROWS)),
        ],
        out_specs=[each_of(out) for out in outs] + [whole((VEC, width))],
        out_shape=[shape((micro,) + out, BF16) for out in outs] + [shape((VEC, width), F32)],
        scratch_shapes=[
            pltpu.VMEM((3, width // shard, shard, width), BF16),
            pltpu.VMEM((ROWS, width), BF16),
        ],
        compiler_params=params(),
        cost_estimate=timing(13),
        name="project",
    )(where, tokens, mine, other, const["low"], const["high"])


def fine_windows(tile):
    return [
        (POFF[0] + 64 * tile, 96),
        (POFF[1] + 32 * tile, 64),
        (POFF[2] + 16 * tile, 16),
        (POFF[2] + 16 * tile + 32, 16),
    ]


def coarse_windows(tile):
    return [
        (POFF[3] + 64 * tile, 96),
        (POFF[4] + 32 * tile, 64),
        (POFF[5] + 16 * tile, 16),
        (POFF[5] + 16 * tile + 32, 16),
        (POFF[6], 16),
        (POFF[6] + 32, 16),
        (POFF[7], 32),
    ]


FINE_LEVELS = [96, 64, 32]
COARSE_LEVELS = [96, 64, 32, 32, 32]


def gather_rows(ref, windows, lanes):
    return jnp.concatenate([ref[at(start, size), lanes] for start, size in windows], axis=0)


def tile_bias(kid_ref, qid_ref, tile, tiles, windows, levels, bias):
    keys = jnp.concatenate([kid_ref[0, at(start, size), :] for start, size in windows], axis=0)
    keys = keys.astype(F32)
    keys = jnp.concatenate([keys, keys], axis=1)
    bias = jnp.concatenate([bias, bias], axis=1)
    out = []
    start = 0
    for index, count in enumerate(levels):
        part = slice(start, start + count)
        owner = qid_ref[0, pl.ds(tiles * index + tile, 1), :]
        out.append(jnp.where(keys[part] == owner, bias[part], NEG))
        start += count
    return jnp.concatenate(out, axis=0)


def lane_sums(value, steps):
    halves = []
    for half in range(2):
        part = value[:, 128 * half : 128 * (half + 1)]
        lane = lax.broadcasted_iota(jnp.int32, part.shape, 1)
        for step in range(steps):
            size = 1 << step
            first = (lane & size) == 0
            part = part + jnp.where(
                first, pltpu.roll(part, 128 - size, 1), pltpu.roll(part, size, 1)
            )
        halves.append(part)
    return jnp.concatenate(halves, axis=1)


def lane_roll(value, shift):
    if shift == 0:
        return value
    halves = [value[:, 128 * half : 128 * (half + 1)] for half in range(2)]
    return jnp.concatenate([pltpu.roll(part, shift % 128, 1) for part in halves], axis=1)


def far_row(tile, quad):
    return pl.ds(8 * (tile % 8) + 2 * (tile // 8) + quad, 1)


def level_sums(value, levels):
    out = [value[0 : levels[0]]]
    start = levels[0]
    for index, count in enumerate(levels[1:]):
        out.append(lane_sums(value[start : start + count], index + 1))
        start += count
    return jnp.concatenate(out, axis=0)


def head_stack(value, mask):
    return jnp.concatenate([value] * QUAD, axis=0) * mask


def head_pick(stacked):
    lane = lax.broadcasted_iota(jnp.int32, (TILE, QL), 1) // HEAD_DIM
    out = stacked[0:TILE]
    for head in range(1, QUAD):
        out = jnp.where(lane == head, stacked[TILE * head : TILE * (head + 1)], out)
    return out


def three_terms(row):
    high = row.astype(BF16)
    rest = row - high.astype(F32)
    middle = rest.astype(BF16)
    low = (rest - middle.astype(F32)).astype(BF16)
    return high, middle, low


def own_cell(tile):
    cell = lax.broadcasted_iota(jnp.int32, (16, QL), 0)
    token = lax.broadcasted_iota(jnp.int32, (16, QL), 1) % TILE
    return cell == 8 * (tile % 2) + token // 8


def lay_out(piece, kv_ref, near_ref, far_ref, across_ref, ends_ref, kvp_ref):
    def edges(left_ref, right_ref):
        for level in range(LEVELS - 1):
            base = POFF[level]
            edge = pl.ds(HALO * level, HALO)
            kvp_ref[pl.ds(base, HALO), :] = left_ref[0, edge, :]
            kvp_ref[pl.ds(base + HALO + CELLS[level], HALO), :] = right_ref[0, edge, :]

    pl.when(piece % 2 == 0)(lambda: edges(far_ref, near_ref))
    pl.when(piece % 2 == 1)(lambda: edges(near_ref, far_ref))
    for level in range(LEVELS - 1):
        count = CELLS[level]
        kvp_ref[pl.ds(POFF[level] + HALO, count), :] = kv_ref[0, pl.ds(OFF[level], count), :]
    across = across_ref[0].astype(F32)[0:PIECE7]
    ends = ends_ref[0].astype(F32)[0:PIECE7]
    tops = []
    for owner in range(4):
        top = jnp.where(owner == (piece + 2) % 4, across, jnp.where(owner == 3 - piece, ends, 0.0))
        tops.append(top)
    kvp_ref[pl.ds(POFF[7], 4 * PIECE7), :] = jnp.concatenate(tops, axis=0).astype(BF16)


def attend_kernel(
    where_ref,
    q_ref,
    q3_ref,
    kv_ref,
    near_ref,
    far_ref,
    across_ref,
    ends_ref,
    kid_ref,
    qidf_ref,
    qidc_ref,
    fine_ref,
    coarse_ref,
    mask_ref,
    spread_ref,
    mixed_ref,
    lse_ref,
    lsec_ref,
    lsex_ref,
    oc_ref,
    kvp_ref,
):
    lay_out(where_ref[0], kv_ref, near_ref, far_ref, across_ref, ends_ref, kvp_ref)
    mask = mask_ref[...]
    scaled = mask * jnp.asarray(0.125, BF16)

    units = [(tile, quad) for tile in range(COARSE_TILES) for quad in range(2)]
    biases = [
        tile_bias(kid_ref, qidc_ref, tile, 8, coarse_windows(tile), COARSE_LEVELS, coarse_ref[tile])
        for tile in range(COARSE_TILES)
    ]
    scores = []
    for tile, quad in units:
        lanes = pl.ds(QL * quad, QL)
        query = head_stack(q3_ref[0, pl.ds(TILE * tile, TILE), lanes], scaled)
        scores.append(dot_nt(gather_rows(kvp_ref, coarse_windows(tile), lanes), query))
    shares = []
    lines = []
    for index, (tile, quad) in enumerate(units):
        score = level_sums(scores[index], COARSE_LEVELS) + biases[index // 2]
        top = jnp.max(score, axis=0, keepdims=True)
        share = jnp.exp(score - top)
        total = jnp.sum(share, axis=0, keepdims=True)
        lse = top + jnp.log(total)
        lsec_ref[0, pl.ds(index, 1), :] = lse
        lines.append(lse)
        shares.append((share * (1.0 / total)).astype(BF16))
    results = []
    for (tile, quad), share in zip(units, shares):
        values = gather_rows(kvp_ref, coarse_windows(tile), pl.ds(512 + QL * quad, QL))
        results.append(dot_tn(share, values))
    lines = three_terms(jnp.concatenate(lines * 2, axis=0))
    lines = jnp.concatenate([line.astype(F32) for line in lines], axis=0)
    terms = [lane_roll(lines, -8 * part) for part in range(8)]
    terms = dot_nn(jnp.concatenate(terms, axis=0).astype(BF16), spread_ref[...])
    for part in range(8):
        rows = [terms[24 * part + 8 * index : 24 * part + 8 * index + 8] for index in range(3)]
        lsex_ref[0, pl.ds(8 * part, 8), :] = rows[0] + rows[1] + rows[2]
    for index, (tile, quad) in enumerate(units):
        oc_ref[0, pl.ds(TILE * tile, TILE), pl.ds(QL * quad, QL)] = head_pick(
            results[index]
        ).astype(BF16)

    def fine_group(group, carry):
        tiles = [GROUP * group + index for index in range(GROUP)]
        units = [(tile, quad) for tile in tiles for quad in range(2)]
        biases = [
            tile_bias(kid_ref, qidf_ref, tile, FINE_TILES, fine_windows(tile), FINE_LEVELS, fine_ref[...])
            for tile in tiles
        ]
        scores = []
        for tile, quad in units:
            lanes = pl.ds(QL * quad, QL)
            query = head_stack(q_ref[0, at(TILE * tile, TILE), lanes], scaled)
            scores.append(dot_nt(gather_rows(kvp_ref, fine_windows(tile), lanes), query))
        shares = []
        for index, (tile, quad) in enumerate(units):
            score = level_sums(scores[index], FINE_LEVELS) + biases[index // 2]
            far = lsex_ref[0, far_row(tile, quad), :]
            top = jnp.maximum(jnp.max(score, axis=0, keepdims=True), far)
            share = jnp.exp(score - top)
            far_share = jnp.exp(far - top)
            total = jnp.sum(share, axis=0, keepdims=True) + far_share
            lse_ref[0, pl.ds(2 * tile + quad, 1), :] = top + jnp.log(total)
            inverse = 1.0 / total
            shares.append(
                jnp.concatenate(
                    [share * inverse, jnp.where(own_cell(tile), far_share * inverse, 0.0)], axis=0
                ).astype(BF16)
            )
        results = []
        for (tile, quad), share in zip(units, shares):
            values = jnp.concatenate(
                [
                    gather_rows(kvp_ref, fine_windows(tile), pl.ds(512 + QL * quad, QL)),
                    oc_ref[0, at(16 * (tile // 2), 16), pl.ds(QL * quad, QL)],
                ],
                axis=0,
            )
            results.append(dot_tn(share, values))
        for (tile, quad), result in zip(units, results):
            mixed_ref[0, at(TILE * tile, TILE), pl.ds(QL * quad, QL)] = head_pick(result).astype(
                BF16
            )
        return carry

    lax.fori_loop(0, FINE_TILES // GROUP, fine_group, 0)


def stat_shapes(width):
    return [
        ((2 * FINE_TILES, QL), F32),
        ((2 * COARSE_TILES, QL), F32),
        ((64, QL), F32),
        ((ROWS // 8, width), BF16),
    ]


def id_specs(spec):
    return [
        spec((PADDED, 128)),
        spec((FINE * FINE_TILES, QL)),
        spec((8 * (LEVELS - FINE), QL)),
        whole((FINE_KEYS, QL // 2)),
        whole((COARSE_TILES, COARSE_KEYS, QL // 2)),
        whole((QL, QL)),
    ]


def id_args(ids, const):
    return [ids["key"], ids["fine"], ids["coarse"], const["fine"], const["coarse"], const["head_mask"]]


def attend(where, cells, received, ids, const):
    micro, _, width = cells[0].shape
    outs = [((ROWS, width), BF16)] + stat_shapes(width)
    ins = list(cells) + list(received)
    return pl.pallas_call(
        attend_kernel,
        grid=(micro,),
        in_specs=[SCALAR]
        + [each_of(value.shape[1:]) for value in ins]
        + id_specs(each_of)
        + [whole((QL, QL))],
        out_specs=[each_of(dims) for dims, _ in outs],
        out_shape=[jax.ShapeDtypeStruct((micro,) + dims, kind) for dims, kind in outs],
        scratch_shapes=[pltpu.VMEM((PADDED, 2 * width), BF16)],
        compiler_params=params(),
        cost_estimate=timing(23),
        name="attend",
    )(where, *ins, *id_args(ids, const), const["spread"])


def add_rows(ref, windows, lanes, value):
    start = 0
    for base, count in windows:
        rows = at(base, count)
        ref[rows, lanes] = ref[rows, lanes] + value[start : start + count]
        start += count


def attend_back_kernel(
    where_ref,
    q_ref,
    q3_ref,
    kv_ref,
    near_in_ref,
    far_in_ref,
    across_in_ref,
    ends_in_ref,
    lse_ref,
    lsec_ref,
    lsex_ref,
    oc_ref,
    dout_ref,
    kid_ref,
    qidf_ref,
    qidc_ref,
    fine_ref,
    coarse_ref,
    mask_ref,
    spread_t_ref,
    dq_ref,
    dq3_ref,
    dkv_ref,
    near_ref,
    far_ref,
    across_ref,
    ends_ref,
    acc_ref,
    dcell_ref,
    delta_ref,
    kvp_ref,
):
    lay_out(where_ref[0], kv_ref, near_in_ref, far_in_ref, across_in_ref, ends_in_ref, kvp_ref)
    delta_ref[...] = jnp.zeros(delta_ref.shape, F32)
    acc_ref[...] = jnp.zeros(acc_ref.shape, F32)
    dcell_ref[...] = jnp.zeros(dcell_ref.shape, F32)
    mask = mask_ref[...]
    scaled = mask * jnp.asarray(0.125, BF16)

    def fine_group(group, carry):
        tiles = [GROUP_BACK * group + index for index in range(GROUP_BACK)]
        units = [(tile, quad) for tile in tiles for quad in range(2)]
        biases = [
            tile_bias(kid_ref, qidf_ref, tile, FINE_TILES, fine_windows(tile), FINE_LEVELS, fine_ref[...])
            for tile in tiles
        ]
        at_unit = lambda unit: (at(TILE * unit[0], TILE), pl.ds(QL * unit[1], QL))
        queries = [head_stack(q_ref[(0,) + at_unit(unit)], scaled) for unit in units]
        douts = [head_stack(dout_ref[(0,) + at_unit(unit)], mask) for unit in units]
        scores = []
        steers = []
        for index, (tile, quad) in enumerate(units):
            keys = gather_rows(kvp_ref, fine_windows(tile), pl.ds(QL * quad, QL))
            scores.append(dot_nt(keys, queries[index]))
            values = jnp.concatenate(
                [
                    gather_rows(kvp_ref, fine_windows(tile), pl.ds(512 + QL * quad, QL)),
                    oc_ref[0, at(16 * (tile // 2), 16), pl.ds(QL * quad, QL)],
                ],
                axis=0,
            )
            steers.append(dot_nt(values, douts[index]))
        shares = []
        grads = []
        for index, (tile, quad) in enumerate(units):
            lse = lse_ref[0, pl.ds(2 * tile + quad, 1), :]
            far_share = jnp.exp(lsex_ref[0, far_row(tile, quad), :] - lse)
            share = jnp.exp(level_sums(scores[index], FINE_LEVELS) + biases[index // 2] - lse)
            share = jnp.concatenate([share, jnp.where(own_cell(tile), far_share, 0.0)], axis=0)
            weighted = share * steers[index]
            delta = jnp.sum(weighted, axis=0, keepdims=True)
            delta_ref[far_row(tile, quad), :] = far_share * delta
            grad = weighted[0:FINE_KEYS] - share[0:FINE_KEYS] * delta
            grads.append(level_sums(grad, FINE_LEVELS).astype(BF16))
            shares.append(share.astype(BF16))
        dvalues = [dot_nn(share, dout) for share, dout in zip(shares, douts)]
        dkeys = [dot_nn(grad, query) for grad, query in zip(grads, queries)]
        dqueries = []
        for (tile, quad), grad in zip(units, grads):
            keys = gather_rows(kvp_ref, fine_windows(tile), pl.ds(QL * quad, QL))
            dqueries.append(dot_tn(grad, keys))
        for index, (tile, quad) in enumerate(units):
            lanes = pl.ds(QL * quad, QL)
            cells = at(16 * (tile // 2), 16)
            windows = fine_windows(tile)
            add_rows(acc_ref, windows, pl.ds(512 + QL * quad, QL), dvalues[index])
            dcell_ref[cells, lanes] = dcell_ref[cells, lanes] + dvalues[index][FINE_KEYS:]
            add_rows(acc_ref, windows, lanes, dkeys[index])
            dq_ref[(0,) + at_unit((tile, quad))] = (head_pick(dqueries[index]) * 0.125).astype(BF16)
        return carry

    lax.fori_loop(0, FINE_TILES // GROUP_BACK, fine_group, 0)

    units = [(tile, quad) for tile in range(COARSE_TILES) for quad in range(2)]
    biases = [
        tile_bias(kid_ref, qidc_ref, tile, 8, coarse_windows(tile), COARSE_LEVELS, coarse_ref[tile])
        for tile in range(COARSE_TILES)
    ]
    at_unit = lambda unit: (pl.ds(TILE * unit[0], TILE), pl.ds(QL * unit[1], QL))
    queries = [head_stack(q3_ref[(0,) + at_unit(unit)], scaled) for unit in units]
    douts = [head_stack(dcell_ref[at_unit(unit)].astype(BF16), mask) for unit in units]
    terms = dot_nn(jnp.concatenate(three_terms(delta_ref[...]), axis=0), spread_t_ref[...])
    terms = terms[0:64] + terms[64:128] + terms[128:192]
    deltas = lane_roll(terms[0:8], 0)
    for part in range(1, 8):
        deltas = deltas + lane_roll(terms[8 * part : 8 * part + 8], 8 * part)
    steers = []
    scores = []
    for (tile, quad), dout, query in zip(units, douts, queries):
        values = gather_rows(kvp_ref, coarse_windows(tile), pl.ds(512 + QL * quad, QL))
        steers.append(dot_nt(values, dout))
        keys = gather_rows(kvp_ref, coarse_windows(tile), pl.ds(QL * quad, QL))
        scores.append(dot_nt(keys, query))
    shares = []
    grads = []
    for index, (tile, quad) in enumerate(units):
        score = level_sums(scores[index], COARSE_LEVELS) + biases[index // 2]
        share = jnp.exp(score - lsec_ref[0, pl.ds(index, 1), :])
        delta = deltas[index : index + 1]
        grads.append(level_sums(share * (steers[index] - delta), COARSE_LEVELS).astype(BF16))
        shares.append(share.astype(BF16))
    dvalues = [dot_nn(share, dout) for share, dout in zip(shares, douts)]
    dkeys = [dot_nn(grad, query) for grad, query in zip(grads, queries)]
    dqueries = []
    for (tile, quad), grad in zip(units, grads):
        keys = gather_rows(kvp_ref, coarse_windows(tile), pl.ds(QL * quad, QL))
        dqueries.append(dot_tn(grad, keys))
    for index, (tile, quad) in enumerate(units):
        windows = coarse_windows(tile)
        add_rows(acc_ref, windows, pl.ds(512 + QL * quad, QL), dvalues[index])
        add_rows(acc_ref, windows, pl.ds(QL * quad, QL), dkeys[index])
        dq3_ref[(0,) + at_unit((tile, quad))] = (head_pick(dqueries[index]) * 0.125).astype(BF16)

    key_lane = lax.broadcasted_iota(jnp.int32, (1, acc_ref.shape[1]), 1) < 512

    def scale(level):
        return jnp.where(key_lane, 0.5 ** STEP[level], 1.0)

    def low(level, start, count):
        return (acc_ref[pl.ds(start, count), :] * scale(level)).astype(BF16)

    def edges(left_ref, right_ref):
        for level in range(LEVELS - 1):
            base = POFF[level]
            edge = pl.ds(HALO * level, HALO)
            left_ref[0, edge, :] = low(level, base, HALO)
            right_ref[0, edge, :] = low(level, base + HALO + CELLS[level], HALO)

    piece = where_ref[0]
    pl.when(piece % 2 == 0)(lambda: edges(far_ref, near_ref))
    pl.when(piece % 2 == 1)(lambda: edges(near_ref, far_ref))
    for level in range(LEVELS - 1):
        dkv_ref[0, pl.ds(OFF[level], CELLS[level]), :] = low(level, POFF[level] + HALO, CELLS[level])
    dkv_ref[0, pl.ds(OFF[7], 16), :] = jnp.zeros((16, acc_ref.shape[1]), BF16)
    blank = jnp.zeros((PIECE7, acc_ref.shape[1]), F32)

    def high(index):
        rows = pl.ds(pl.multiple_of(POFF[7] + PIECE7 * index, PIECE7), PIECE7)
        return jnp.concatenate([acc_ref[rows, :] * scale(7), blank], axis=0).astype(BF16)

    ends_ref[0] = high(3 - piece)
    across_ref[0] = high((piece + 2) % 4)


def attend_back(where, cells, received, stats, dout, ids, const):
    micro, _, width = dout.shape
    shape = jax.ShapeDtypeStruct
    outs = cell_shapes(width) + edge_shapes(width) + edge_shapes(width)[2:]
    ins = list(cells) + list(received) + list(stats) + [dout]
    return pl.pallas_call(
        attend_back_kernel,
        grid=(micro,),
        in_specs=[SCALAR]
        + [each_of(value.shape[1:]) for value in ins]
        + id_specs(each_of)
        + [whole((QL, QL))],
        out_specs=[each_of(out) for out in outs],
        out_shape=[shape((micro,) + out, BF16) for out in outs],
        scratch_shapes=[
            pltpu.VMEM((PADDED, 2 * width), F32),
            pltpu.VMEM((ROWS // 8, width), F32),
            pltpu.VMEM((64, QL), F32),
            pltpu.VMEM((PADDED, 2 * width), BF16),
        ],
        compiler_params=params(),
        cost_estimate=timing(38),
        name="attend_back",
    )(where, *ins, *id_args(ids, const), const["spread_t"])


MID_ROWS = 512
FF_CHUNK = 512
ROOT = math.sqrt(2.0 / math.pi)


def share_out(send_ref, keep_ref, core, start, piece_of):
    for chip in range(send_ref.shape[0]):
        keep = piece_of(2 * chip + core)
        keep_ref[chip, pl.ds(start, keep.shape[0]), :] = keep
        send_ref[chip, pl.ds(start, keep.shape[0]), :] = piece_of(2 * chip + 1 - core)


def give(send_ref, start, piece_of):
    for index in range(send_ref.shape[0]):
        piece = piece_of(index)
        send_ref[index, pl.ds(start, piece.shape[0]), :] = piece


def row_piece(ref, shard):
    def piece_of(index):
        return ref[pl.ds(pl.multiple_of(shard * index, shard), shard), :].astype(BF16)

    return piece_of


def middle_kernel(
    where_ref,
    tok_ref,
    cot_ref,
    mixed_ref,
    vec_ref,
    mine_ref,
    other_ref,
    out_ref,
    dmid_ref,
    dmix_ref,
    send_ref,
    wo_ref,
    wi_ref,
    wd_ref,
    acc_o,
    acc_i,
    acc_d,
    acc_b,
    acc_s,
    activ_ref,
    grad_ref,
):
    step = pl.program_id(0)
    core = where_ref[1]
    parts = wi_ref.shape[0]
    shard = wo_ref.shape[2]

    @pl.when(step == 0)
    def _():
        acc_o[...] = jnp.zeros(acc_o.shape, F32)
        acc_i[...] = jnp.zeros(acc_i.shape, F32)
        acc_d[...] = jnp.zeros(acc_d.shape, F32)
        acc_b[...] = jnp.zeros(acc_b.shape, F32)
        acc_s[...] = jnp.zeros(acc_s.shape, F32)
        take_weight(wo_ref, 0, mine_ref, other_ref, core, 0)
        for part in range(parts):
            take_weight(wi_ref, part, mine_ref, other_ref, core, shard * (1 + part))
        take_weight(wd_ref, 0, mine_ref, other_ref, core, shard * (1 + parts))

    wo = weight_of(wo_ref, 0)
    pieces = FF_CHUNK // wd_ref.shape[2]
    wi = [weight_of(wi_ref, part) for part in range(parts)]
    wd = [
        wd_ref[0, pieces * part : pieces * (part + 1)].reshape(FF_CHUNK, wo.shape[1])
        for part in range(parts)
    ]
    cot = cot_ref[...]
    top = cot.astype(BF16)
    mixed = mixed_ref[...]
    middle = tok_ref[...] + dot_nn(mixed, wo)
    unit, rate = normalised(middle)
    second = (unit * vec_ref[1:2] + vec_ref[3:4]).astype(BF16)
    result = middle + vec_ref[4:5]
    back = jnp.zeros(cot.shape, F32)
    pres = {}

    def first(part):
        pres[part] = (dot_nn(second, wi[part]) + vec_ref[5 + part : 6 + part], dot_nt(top, wd[part]))

    first(0)
    for part in range(parts):
        if part + 1 < parts:
            first(part + 1)
        pre, grad = pres.pop(part)
        square = pre * pre
        tanh = jnp.tanh(pre * (ROOT + (ROOT * 0.044715) * square))
        half = 0.5 + 0.5 * tanh
        activ = (pre * half).astype(BF16)
        slope = half + (pre * (0.5 - 0.5 * (tanh * tanh))) * (
            ROOT + (ROOT * 3 * 0.044715) * square
        )
        grad = (grad * slope).astype(BF16)
        cols = pl.ds(FF_CHUNK * part, FF_CHUNK)
        activ_ref[:, cols] = activ
        grad_ref[:, cols] = grad
        acc_b[:, cols] = acc_b[:, cols] + fold_rows(grad.astype(F32))
        result = result + dot_nn(activ, wd[part])
        back = back + dot_nt(grad, wi[part])
    out_ref[...] = result
    acc_d[...] = acc_d[...] + dot_tn(activ_ref[...], top)
    for part in range(parts):
        acc_i[part] = acc_i[part] + dot_tn(second, grad_ref[:, pl.ds(FF_CHUNK * part, FF_CHUNK)])
    dmid = cot + norm_back(back * vec_ref[1:2], unit, rate)
    dmid_ref[...] = dmid
    branch = dmid.astype(BF16)
    dmix_ref[...] = dot_nt(branch, wo).astype(BF16)
    acc_o[...] = acc_o[...] + dot_tn(mixed, branch)
    acc_s[0:8, :] = acc_s[0:8, :] + fold_rows(top.astype(F32))
    acc_s[8:16, :] = acc_s[8:16, :] + fold_rows(back * unit)
    acc_s[16:24, :] = acc_s[16:24, :] + fold_rows(back)

    @pl.when(step == pl.num_programs(0) - 1)
    def _():
        give(send_ref, 0, row_piece(acc_o, shard))
        for part in range(parts):
            give(send_ref, shard * (1 + part), row_piece(acc_i.at[part], shard))
        give(send_ref, shard * (1 + parts), row_piece(acc_d, shard * parts))
        total = lambda value: jnp.sum(value, axis=0, keepdims=True)
        lines = [total(acc_s[8 * index : 8 * index + 8, :]) for index in range(3)]
        for part in range(parts):
            lines.append(total(acc_b[:, pl.ds(FF_CHUNK * part, FF_CHUNK)]))
        lines.append(jnp.zeros((16 - len(lines), lines[0].shape[1]), F32))
        lines = jnp.concatenate(lines, axis=0).astype(BF16)
        give(send_ref, shard * (1 + 2 * parts), lambda index: lines)


def middle_part(where, tokens, cot, mixed, vec, mine, other):
    rows, width = tokens.shape
    chips, lines, _ = mine.shape
    shard = width // (2 * chips)
    parts = (lines // shard - 1) // 2
    hidden = parts * FF_CHUNK
    shape = jax.ShapeDtypeStruct
    tiled = pl.BlockSpec((MID_ROWS, width), lambda r: (r, 0))
    shared = shape((2 * chips, lines + 16, width), BF16)
    single = lambda dims: pl.BlockSpec(
        dims, lambda *_: (0,) * len(dims), pipeline_mode=pl.Buffered(1)
    )
    return pl.pallas_call(
        middle_kernel,
        grid=(rows // MID_ROWS,),
        in_specs=[SCALAR, tiled, tiled, tiled, whole(vec.shape), single(mine.shape), single(mine.shape)],
        out_specs=[tiled, tiled, tiled, single(shared.shape)],
        out_shape=[
            shape((rows, width), F32),
            shape((rows, width), F32),
            shape((rows, width), BF16),
            shared,
        ],
        scratch_shapes=[
            pltpu.VMEM((1, 2 * chips, shard, width), BF16),
            pltpu.VMEM((parts, 2 * chips, shard, FF_CHUNK), BF16),
            pltpu.VMEM((1, 2 * chips, shard * parts, width), BF16),
            pltpu.VMEM((width, width), F32),
            pltpu.VMEM((parts, width, FF_CHUNK), F32),
            pltpu.VMEM((hidden, width), F32),
            pltpu.VMEM((8, hidden), F32),
            pltpu.VMEM((24, width), F32),
            pltpu.VMEM((MID_ROWS, hidden), BF16),
            pltpu.VMEM((MID_ROWS, hidden), BF16),
        ],
        compiler_params=params(),
        cost_estimate=timing(40),
        name="middle",
    )(where, tokens, cot, mixed, vec, mine, other)


def collect_kernel(
    where_ref, tok_ref, dq_ref, dq3_ref, dkv_ref, near_ref, far_ref, across_ref, ends_ref, low_ref, high_ref, *refs, first
):
    if first:
        dp_ref, gw_ref, sum_ref, cells_ref, norm_ref = refs
    else:
        held_ref, held_sum_ref, vec_ref, mine_ref, other_ref = refs[:5]
        dp_ref, send_ref, keep_ref, cells_ref, norm_ref, gw_ref, w_ref = refs[6:]
    piece, core = where_ref[0], where_ref[1]
    cells_ref[...] = dkv_ref[0]

    def add(start, value):
        rows = pl.ds(start, HALO)
        cells_ref[rows, :] = (cells_ref[rows, :].astype(F32) + value.astype(F32)).astype(BF16)

    def edges(left_ref, right_ref):
        for level in range(LEVELS - 1):
            edge = pl.ds(HALO * level, HALO)

            @pl.when(piece > 0)
            def _():
                add(OFF[level], left_ref[0, edge, :])

            @pl.when(piece < 3)
            def _():
                add(OFF[level] + CELLS[level] - HALO, right_ref[0, edge, :])

    pl.when(piece % 2 == 0)(lambda: edges(far_ref, near_ref))
    pl.when(piece % 2 == 1)(lambda: edges(near_ref, far_ref))
    add(OFF[7], across_ref[0].astype(F32) + ends_ref[0].astype(F32))

    sums = [jnp.zeros((8, 512), F32), jnp.zeros((8, 1024), F32)]
    for chunk in range(ROWS // 256):
        rows = pl.ds(256 * chunk, 256)
        norm_ref[rows, :] = normalised(tok_ref[0, rows, :])[0].astype(BF16)
        cells = jnp.concatenate(
            [
                cells_ref[pl.ds(OFF[level] + (256 >> level) * chunk, 256 >> level), :]
                for level in range(1, 5)
            ],
            axis=0,
        )
        dkv = (
            cells_ref[rows, :].astype(F32)
            + dot_nn(low_ref[...], cells)
            + dot_nn(high_ref[rows, :], cells_ref[pl.ds(OFF[5], 64), :])
        ).astype(BF16)
        dq = (
            dq_ref[0, rows, :].astype(F32)
            + dot_nn(low_ref[:, 192:224], dq3_ref[0, pl.ds(32 * chunk, 32), :])
        ).astype(BF16)
        dp_ref[0, rows, pl.ds(0, 512)] = dq
        dp_ref[0, rows, pl.ds(512, 1024)] = dkv
        sums = [old + fold_rows(new.astype(F32)) for old, new in zip(sums, (dq, dkv))]
    sums = jnp.concatenate(sums, axis=1)
    if first:
        sum_ref[...] = sums
    else:
        sums = jnp.sum(sums + held_sum_ref[...], axis=0, keepdims=True)
        row = lax.broadcasted_iota(jnp.int32, (VEC, 512), 0)
        lines = vec_ref[...].astype(BF16)
        gain = dot_tn(lines, jnp.where(row == 0, 1.0, 0.0).astype(BF16))
        offset = dot_tn(lines, jnp.where(row == 2, 1.0, 0.0).astype(BF16))
        ones = jnp.ones((8, 512), BF16)
        grad_gain = jnp.zeros((8, 512), F32)
        grad_offset = jnp.zeros((8, 512), F32)
        for index in range(3):
            take_weight(w_ref, index, mine_ref, other_ref, core, w_ref.shape[2] * index)
    for index in range(3):
        grad = dot_tn(norm_ref[...], dp_ref[0, :, pl.ds(512 * index, 512)])
        if first:
            gw_ref[index] = grad.astype(BF16)
        else:
            grad = grad + held_ref[index].astype(F32)
            total = sums[:, 512 * index : 512 * (index + 1)]
            gw_ref[index] = gain * grad + offset * total
            weight = weight_of(w_ref, index)
            high, middle, _ = three_terms(weight.astype(F32) * grad)
            grad_gain = grad_gain + dot_nt(ones, high) + dot_nt(ones, middle)
            high, middle, low = three_terms(total)
            terms = jnp.concatenate([high, middle, low] + [jnp.zeros_like(low)] * 5, axis=0)
            grad_offset = grad_offset + dot_nt(terms, weight)
    if not first:
        shard = w_ref.shape[2]
        for index in range(3):
            share_out(send_ref, keep_ref, core, shard * index, row_piece(gw_ref.at[index], shard))
        grad_offset = jnp.sum(grad_offset, axis=0, keepdims=True)
        blank = jnp.zeros((VEC - 2, 512), F32)
        lines = jnp.concatenate([grad_gain[0:1], grad_offset, blank], axis=0).astype(BF16)
        share_out(send_ref, keep_ref, core, 3 * shard, lambda index: lines)


def collect(micro, where, tokens, grads, received, const, held=None):
    width = tokens.shape[2]
    shape = jax.ShapeDtypeStruct
    first = held is None
    moved = list(grads) + list(received)
    ins = moved + [const["low_t"], const["high_t"]]
    outs = [shape((tokens.shape[0], ROWS, 3 * width), BF16)]
    scratch = [pltpu.VMEM((2 * ROWS, 2 * width), BF16), pltpu.VMEM((ROWS, width), BF16)]
    kept = []
    aliases = {}
    if first:
        outs += [shape((3, width, width), BF16), shape((8, 3 * width), F32)]
    else:
        ins += held[1:]
        kept = [held[0]]
        mine = held[-1]
        chips, lines, _ = mine.shape
        shard = width // (2 * chips)
        aliases = {2 + len(ins): 0}
        outs += [shape((chips, lines, width), BF16)] * 2
        scratch.append(pltpu.VMEM((3, width, width), F32))
        scratch.append(pltpu.VMEM((3, 2 * chips, shard, width), BF16))
    specs = [SCALAR, one_of((ROWS, width), micro)]
    specs += [one_of(value.shape[1:], micro) for value in moved]
    specs += [whole(value.shape) for value in ins[len(moved) :]]
    return pl.pallas_call(
        lambda *refs: collect_kernel(*refs, first=first),
        grid=(1,),
        in_specs=specs + [KEPT] * len(kept),
        out_specs=[one_of((ROWS, 3 * width), micro)] + [whole(out.shape) for out in outs[1:]],
        out_shape=outs,
        scratch_shapes=scratch,
        input_output_aliases=aliases,
        compiler_params=params(),
        cost_estimate=timing(8),
        name="collect",
    )(where, tokens, *ins, *kept)


FIN_ROWS = 256


def finish_kernel(where_ref, tok_ref, dmid_ref, dp_ref, vec_ref, mine_ref, other_ref, *refs):
    grad_ref, w_ref = refs[-2:]
    core = where_ref[1]

    @pl.when(pl.program_id(0) == 0)
    def _():
        for index in range(3):
            take_weight(w_ref, index, mine_ref, other_ref, core, w_ref.shape[2] * index)

    back = dot_nt(dp_ref[0, :, pl.ds(0, 512)], weight_of(w_ref, 0))
    for index in range(1, 3):
        back = back + dot_nt(dp_ref[0, :, pl.ds(512 * index, 512)], weight_of(w_ref, index))
    unit, rate = normalised(tok_ref[0])
    grad_ref[0] = dmid_ref[0] + norm_back(back * vec_ref[0:1], unit, rate)


def finish(micro, where, tokens, dmid, dproj, vec, mine, other, kept):
    width = tokens.shape[2]
    dp = 2 * mine.shape[0]
    ins = [where, tokens, dmid, dproj, vec, mine, other] + ([] if kept is None else [kept])
    chunk = lambda lanes: pl.BlockSpec((1, FIN_ROWS, lanes), lambda r: (micro, r, 0))
    return pl.pallas_call(
        finish_kernel,
        grid=(ROWS // FIN_ROWS,),
        in_specs=[
            SCALAR,
            chunk(width),
            chunk(width),
            chunk(3 * width),
            whole(vec.shape),
            whole(mine.shape),
            whole(other.shape),
        ]
        + [KEPT] * (len(ins) - 7),
        out_specs=chunk(width),
        out_shape=jax.ShapeDtypeStruct(tokens.shape, F32),
        scratch_shapes=[pltpu.VMEM((3, dp, width // dp, width), BF16)],
        input_output_aliases={} if kept is None else {7: 0},
        compiler_params=params(),
        cost_estimate=timing(6),
        name="finish",
    )(*ins)


def twice(chunk):
    lane = lax.broadcasted_iota(jnp.int32, chunk.shape, 1)
    other = pltpu.roll(chunk, 64, 1)
    halves = jnp.where(lane < 64, chunk, other), jnp.where(lane < 64, other, chunk)
    return [jnp.concatenate([half, half], axis=1)[0:1] for half in halves]


def lane_pairs(value, size, merge):
    halves = []
    for half in range(2):
        part = value[:, 128 * half : 128 * (half + 1)]
        lane = lax.broadcasted_iota(jnp.int32, part.shape, 1)
        first = (lane & size) == 0
        pair = jnp.where(first, pltpu.roll(part, 128 - size, 1), pltpu.roll(part, size, 1))
        halves.append(merge(part, pair))
    return jnp.concatenate(halves, axis=1)


def documents_kernel(where_ref, seg_ref, own_ref, kid_ref, qidf_ref, qidc_ref, row_ref):
    piece = where_ref[0]
    length = seg_ref.shape[2]
    margin = (row_ref.shape[0] - length) // 2
    ones = jnp.ones((16, 128), BF16)

    def only_first(row):
        index = lax.broadcasted_iota(jnp.int32, (16, row.shape[1]), 0)
        return jnp.where(index == 0, row.astype(F32), 0.0).astype(BF16)

    outside = jnp.full((margin, 128), -3.0, F32)
    row_ref[pl.ds(0, margin), :] = outside
    row_ref[pl.ds(margin + length, margin), :] = outside
    row_ref[pl.ds(margin, length), :] = dot_tn(only_first(seg_ref[0]), ones)
    for level in range(LEVELS):
        cell = 1 << level
        if level < LEVELS - 1:
            start = ROWS * piece + margin - HALO * cell
            count = CELLS[level] + 2 * HALO
        else:
            start = margin
            count = 4 * PIECE7
        if level == 0:
            key = row_ref[at(start, count), :]
        else:
            lowest = row_ref[pl.ds(start, count, stride=cell), :]
            highest = row_ref[pl.ds(start + cell - 1, count, stride=cell), :]
            key = jnp.where(lowest == highest, lowest, -2.0)
        if level == LEVELS - 1:
            owner = lax.broadcasted_iota(jnp.int32, key.shape, 0) // PIECE7
            counted = (jnp.abs(owner // 2 - piece // 2) == 1) & (jnp.abs(owner - piece) >= 2)
            key = jnp.where(counted, key, -3.0)
        kid_ref[0, pl.ds(POFF[level], count), :] = key.astype(BF16)

    own = own_ref[0].astype(F32)
    rows = []
    for chunk in range(ROWS // 128):
        rows += twice(jnp.broadcast_to(own[:, 128 * chunk : 128 * (chunk + 1)], (8, 128)))
    low = high = jnp.concatenate(rows, axis=0)
    for level in range(FINE):
        if level > 0:
            low = lane_pairs(low, 1 << (level - 1), jnp.minimum)
            high = lane_pairs(high, 1 << (level - 1), jnp.maximum)
        qidf_ref[0, pl.ds(FINE_TILES * level, FINE_TILES), :] = jnp.where(low == high, low, -1.0)

    token = lax.broadcasted_iota(jnp.int32, (ROWS, ROWS // 8), 0)
    cells = lax.broadcasted_iota(jnp.int32, (ROWS, ROWS // 8), 1)
    ends = []
    for step in (0, 7):
        pick = jnp.where(token == 8 * cells + step, 1.0, 0.0).astype(BF16)
        value = dot_nn(only_first(own), pick)[0:1]
        rows = twice(jnp.broadcast_to(value, (8, 128)))
        ends.append(jnp.concatenate(rows + [rows[1]] * 6, axis=0))
    low, high = ends
    for index in range(LEVELS - FINE):
        if index > 0:
            low = lane_pairs(low, 1 << (index - 1), jnp.minimum)
            high = lane_pairs(high, 1 << (index - 1), jnp.maximum)
        qidc_ref[0, pl.ds(8 * index, 8), :] = jnp.where(low == high, low, -1.0)


def cell_documents(where, segments, piece):
    micro, _, length = segments.shape
    shape = jax.ShapeDtypeStruct
    own = lax.dynamic_slice_in_dim(segments, piece * ROWS, ROWS, axis=2)
    outs = [((PADDED, 128), BF16), ((FINE * FINE_TILES, QL), F32), ((8 * (LEVELS - FINE), QL), F32)]
    key, fine, coarse = pl.pallas_call(
        documents_kernel,
        grid=(micro,),
        in_specs=[SCALAR, each_of((1, length)), each_of((1, ROWS))],
        out_specs=[each_of(dims) for dims, _ in outs],
        out_shape=[shape((micro,) + dims, kind) for dims, kind in outs],
        scratch_shapes=[pltpu.VMEM((length + 2 * ROWS, 128), F32)],
        compiler_params=params(),
        cost_estimate=timing(5),
        name="documents",
    )(where, segments, own)
    return dict(key=key, fine=fine, coarse=coarse)


def same_core(chips):
    return [[2 * chip + core for chip in range(chips)] for core in range(2)]


def core_swap(value, chips):
    pairs = [(place, place ^ 1) for place in range(2 * chips)]
    return lax.ppermute(value, "dp", pairs)


def chip_exchange(value, chips):
    return lax.all_to_all(value, "dp", 0, 0, axis_index_groups=same_core(chips), tiled=True)


def after(value, *done):
    return lax.optimization_barrier((value,) + done)[0]


def add(left, right):
    return left.astype(F32) + right.astype(F32)


def body(
    tokens,
    segment_ids,
    norm_gains,
    norm_biases,
    qkv_weight,
    out_weight,
    in_weight,
    in_bias,
    down_weight,
    down_bias,
    cotangent,
):
    micro, _, row_count, width = tokens.shape
    pieces = lax.axis_size("sp")
    piece = lax.axis_index("sp")
    assert row_count == ROWS and pieces == 4 and micro == 2
    const = constants()
    tokens = tokens[:, 0]
    cotangent = cotangent[:, 0]
    dp = lax.axis_size("dp")
    place = lax.axis_index("dp")
    chips = dp // 2
    shard = width // dp
    hidden = in_weight.shape[1]
    parts = hidden // FF_CHUNK
    where = jnp.stack([piece, place % 2]).astype(jnp.int32)
    swap = lambda value, bits: lax.ppermute(value, "sp", [(p, p ^ bits) for p in range(pieces)])
    spread = lambda value: chip_exchange(
        jnp.broadcast_to(value[None], (chips,) + value.shape), chips
    )

    def placed(value, start):
        lines = jnp.zeros((value.shape[0], start * value.shape[1]), BF16)
        return lax.dynamic_update_slice(lines, value, (0, place * value.shape[1])).reshape(-1, width)

    small = placed(jnp.concatenate([norm_gains, norm_biases, down_bias[None]]), dp)
    small = jnp.concatenate([small, placed(in_bias[None], dp)])
    small = jnp.pad(small, ((0, VEC - small.shape[0]), (0, 0)))
    mine = spread(jnp.concatenate([qkv_weight.reshape(3 * shard, width), small]))
    ids = cell_documents(where, segment_ids, piece)
    where, mine = lax.optimization_barrier((after(where, ids["coarse"]), mine))
    other = core_swap(mine, chips)
    rest = jnp.concatenate(
        [
            out_weight,
            in_weight.reshape(shard, parts, FF_CHUNK).swapaxes(0, 1).reshape(-1, width),
            down_weight,
        ]
    )
    rest_mine = spread(after(rest, other))

    def halo(near, far, across, ends):
        middle = lax.ppermute(far, "sp", [(1, 2), (2, 1)])
        return swap(near, 1), middle, swap(across, 2), lax.ppermute(ends, "sp", [(0, 3), (3, 0)])

    q, q3, kv, near, far, top, vec = project(where, tokens, mine, other, const)
    cells = (q, q3, kv)
    received = halo(near, far, top, top)
    rest_mine = after(rest_mine, *received)
    rest_other = core_swap(rest_mine, chips)
    mixed, *stats = attend(after(where, rest_mine), cells, received, ids, const)
    rest_other = after(rest_other, mixed)

    flat = lambda value: value.reshape(micro * ROWS, width)
    split = lambda value: value.reshape(micro, ROWS, width)
    outputs, dmid, dmix, send = middle_part(
        where, flat(tokens), flat(cotangent), flat(mixed), vec, rest_mine, rest_other
    )
    come = lax.all_to_all(send, "dp", 0, 0, tiled=True)
    dq, dq3, dkv, *edges = attend_back(where, cells, received, stats, split(dmix), ids, const)
    grads = (dq, dq3, dkv)
    back = halo(*edges)
    dproj, held, sums = collect(0, where, tokens, grads, back, const)

    odd = piece % 2 == 1
    total = jnp.sum(after(come, sums).astype(F32), axis=0).astype(BF16)
    come = swap(total, 1)
    dproj, send, keep = collect(
        1, after(where, total), tokens, grads, back, const, [dproj, held, sums, vec, mine, other]
    )
    qkv_come = core_swap(send, chips)
    total = add(total, after(come, send)).astype(BF16)
    half = jnp.where(odd, total[:, width // 2 :], total[:, : width // 2])
    come = swap(half, 2)
    input_grad = finish(0, after(where, half), tokens, split(dmid), dproj, vec, mine, other, None)
    pair = add(keep, after(qkv_come, input_grad)).astype(BF16)
    qkv_come = chip_exchange(pair, chips)
    half = add(half, after(come, pair)).astype(BF16)
    come = swap(half, 1)
    input_grad = finish(
        1, after(where, half), tokens, split(dmid), dproj, vec, mine, other, input_grad
    )
    total = jnp.sum(after(qkv_come, input_grad).astype(F32), axis=0).astype(BF16)
    qkv_come = swap(total, 1)
    come = after(come, total)
    rest = jnp.where(
        odd, jnp.concatenate([come, half], axis=1), jnp.concatenate([half, come], axis=1)
    ).astype(F32)
    total = add(total, qkv_come).astype(BF16)
    total = add(total, swap(total, 2))

    own = lambda value, size: lax.dynamic_slice_in_dim(value, place * size, size, axis=-1)
    small_two = rest[shard * (1 + 2 * parts) :]
    small_one = total[3 * shard :]
    gin = rest[shard : shard * (1 + parts)].reshape(parts, shard, FF_CHUNK).swapaxes(0, 1)
    return (
        outputs.reshape(micro, 1, ROWS, width),
        input_grad[:, None],
        own(jnp.stack([small_one[0], small_two[1]]), shard),
        own(jnp.stack([small_one[1], small_two[2]]), shard),
        total[: 3 * shard].reshape(3, shard, width),
        rest[:shard],
        gin.reshape(shard, hidden),
        own(small_two[3 : 3 + parts].reshape(hidden), hidden // dp),
        rest[shard * (1 + parts) : shard * (1 + 2 * parts)],
        own(small_two[0], shard),
    )


def solution(mesh):
    in_specs = (
        P(None, "dp", "sp", None),
        P(None, "dp", None),
        P(None, "dp"),
        P(None, "dp"),
        P(None, "dp", None),
        P("dp", None),
        P("dp", None),
        P("dp"),
        P("dp", None),
        P("dp"),
        P(None, "dp", "sp", None),
    )
    out_specs = (
        P(None, "dp", "sp", None),
        P(None, "dp", "sp", None),
        P(None, "dp"),
        P(None, "dp"),
        P(None, "dp", None),
        P("dp", None),
        P("dp", None),
        P("dp"),
        P("dp", None),
        P("dp"),
    )
    return jax.shard_map(body, mesh=mesh, in_specs=in_specs, out_specs=out_specs, check_vma=False)
```

```python
import math

import jax
import jax.numpy as jnp
import numpy as np
from jax import lax
from jax.experimental import pallas as pl
from jax.experimental.pallas import tpu as pltpu
from jax.sharding import PartitionSpec as P

HEADS = 8
HEAD_DIM = 64
BLOCK = 16
LEVELS = 8
HALO = 16
TILE = 64
QUAD = 4
QL = QUAD * HEAD_DIM
NEG = -1e30
FINE = 3
ROWS = 1024
EDGE = 112
VEC = 16
GROUP = 8
GROUP_BACK = 4
F32 = jnp.float32
BF16 = jnp.bfloat16

CELLS = [ROWS >> level for level in range(LEVELS)]
OFF = [2 * ROWS - (2 * ROWS >> level) for level in range(LEVELS)]
POFF = []
_at = 0
for _level in range(LEVELS - 1):
    POFF.append(_at)
    _at += CELLS[_level] + 2 * HALO
POFF.append(_at)
PIECE7 = CELLS[LEVELS - 1]
PADDED = _at + 4 * PIECE7
FINE_TILES = ROWS // TILE
COARSE_TILES = ROWS // 8 // TILE
FINE_KEYS = 192
COARSE_KEYS = 256
LN_EPS = 1e-05
VMEM_LIMIT = 62 * 1024 * 1024


def _counts(level, query, key):
    query = query[None, :]
    key = key[:, None]
    near = np.abs(query // 16 - key // 16)
    if level == 0:
        return near <= 1
    return (near == 1) & (np.abs(query // 8 - key // 8) >= 2)


def _bias(parts):
    rows = []
    for level, allowed in parts:
        rows.append(np.where(allowed, np.float32(level * math.log(2.0)), np.float32(NEG)))
    block = np.concatenate(rows, axis=0).astype(np.float32)
    return np.tile(block, (1, QUAD // 2))


def _two_blocks():
    return np.concatenate([np.arange(16) - 16, np.arange(16) + 16])


def fine_bias():
    token = np.arange(TILE)
    return _bias(
        [
            (0, _counts(0, token, np.arange(96) - 16)),
            (1, _counts(1, token // 2, np.arange(64) - 16)),
            (2, _counts(2, token // 4, _two_blocks())),
        ]
    )


def coarse_bias():
    cell = np.arange(TILE)
    out = []
    for tile in range(COARSE_TILES):
        out.append(
            _bias(
                [
                    (3, _counts(3, cell, np.arange(96) - 16)),
                    (4, _counts(4, cell // 2, np.arange(64) - 16)),
                    (5, _counts(5, cell // 4, _two_blocks())),
                    (6, _counts(6, 8 * tile + cell // 8, _two_blocks())),
                    (7, np.ones((4 * PIECE7, TILE), bool)),
                ]
            )
        )
    return np.stack(out)


STEP = [0, 1, 2, 0, 1, 2, 3, 4]


def mean_rows(cell, count):
    return (np.arange(count)[None, :] // cell == np.arange(count // cell)[:, None]).astype(
        np.float32
    ) / cell


def spread_matrix():
    out = np.zeros((QUAD, TILE, QUAD, TILE), np.float32)
    for token in range(TILE):
        for head in range(QUAD):
            out[head, token // 8, head, token] = 1.0
    return out.reshape(QL, QL)


def constants():
    head_mask = np.kron(np.eye(QUAD), np.ones((TILE, HEAD_DIM)))
    low = [mean_rows(1 << level, 256) for level in range(1, 5)]
    high = [mean_rows(1 << level, ROWS) for level in range(5, 8)] + [np.zeros((8, ROWS))]
    key_low = [rows * 0.5 ** STEP[level] for level, rows in zip(range(1, 5), low)]
    key_high = [rows * 0.5**step for step, rows in zip(STEP[5:] + [0], high)]
    as_low = lambda value: jnp.asarray(value.astype(np.float32)).astype(BF16)
    low, high = np.concatenate(low), np.concatenate(high)
    return dict(
        fine=jnp.asarray(fine_bias()),
        coarse=jnp.asarray(coarse_bias()),
        head_mask=as_low(head_mask),
        low=as_low(np.stack([np.concatenate(key_low), low])),
        high=as_low(np.stack([np.concatenate(key_high), high])),
        low_t=as_low(low.T),
        high_t=as_low(high.T),
        spread=as_low(spread_matrix()),
        spread_t=as_low(spread_matrix().T),
    )


def dot_nn(left, right):
    return jnp.dot(left, right, preferred_element_type=F32)


def dot_nt(left, right):
    return lax.dot_general(left, right, (((1,), (1,)), ((), ())), preferred_element_type=F32)


def dot_tn(left, right):
    return lax.dot_general(left, right, (((0,), (0,)), ((), ())), preferred_element_type=F32)


def at(start, size):
    return pl.ds(pl.multiple_of(start, 16), size)


def whole(shape):
    zeros = (0,) * len(shape)
    return pl.BlockSpec(shape, lambda *_: zeros)


def one_of(shape, micro):
    zeros = (0,) * len(shape)
    return pl.BlockSpec((1,) + shape, lambda *_: (micro,) + zeros)


def each_of(shape):
    zeros = (0,) * len(shape)
    return pl.BlockSpec((1,) + shape, lambda step: (step,) + zeros)


SCALAR = pl.BlockSpec(memory_space=pltpu.SMEM)
KEPT = pl.BlockSpec(memory_space=pl.ANY)


def timing(micros):
    return pl.CostEstimate(
        flops=int(micros * 4e8), bytes_accessed=int(micros * 3e6), transcendentals=0
    )


def params():
    return pltpu.CompilerParams(
        dimension_semantics=("arbitrary",), vmem_limit_bytes=VMEM_LIMIT
    )


def normalised(rows):
    center = rows - jnp.mean(rows, axis=-1, keepdims=True)
    spread = jnp.mean(center * center, axis=-1, keepdims=True)
    rate = lax.rsqrt(spread + LN_EPS)
    return center * rate, rate


def norm_back(grad, unit, rate):
    mean_grad = jnp.mean(grad, axis=-1, keepdims=True)
    mean_dot = jnp.mean(grad * unit, axis=-1, keepdims=True)
    return rate * (grad - mean_grad - unit * mean_dot)


def fold_rows(value):
    return jnp.sum(value.reshape(-1, 8, value.shape[-1]), axis=0)


def take_weight(target, index, mine, other, core, start):
    chips, shard = mine.shape[0], target.shape[2]
    for chip in range(chips):
        target[index, 2 * chip + core] = mine[chip, pl.ds(start, shard), :]
        target[index, 2 * chip + 1 - core] = other[chip, pl.ds(start, shard), :]


def weight_of(ref, index):
    return ref[index].reshape(ref.shape[1] * ref.shape[2], ref.shape[3])


def project_kernel(
    where_ref,
    tok_ref,
    mine_ref,
    other_ref,
    low_ref,
    high_ref,
    q_ref,
    q3_ref,
    kv_ref,
    near_ref,
    far_ref,
    top_ref,
    vec_ref,
    w_ref,
    norm_ref,
):
    piece, core = where_ref[0], where_ref[1]
    shard = w_ref.shape[2]

    @pl.when(pl.program_id(0) == 0)
    def _():
        for index in range(3):
            take_weight(w_ref, index, mine_ref, other_ref, core, shard * index)
        vec = jnp.zeros(vec_ref.shape, F32)
        for chip in range(mine_ref.shape[0]):
            for ref in (mine_ref, other_ref):
                vec = vec + ref[chip, pl.ds(3 * shard, VEC), :].astype(F32)
        vec_ref[...] = vec

    for chunk in range(ROWS // 256):
        rows = pl.ds(256 * chunk, 256)
        unit, _ = normalised(tok_ref[0, rows, :])
        norm_ref[rows, :] = (unit * vec_ref[0:1] + vec_ref[2:3]).astype(BF16)
    for half in range(2):
        rows = pl.ds(512 * half, 512)
        for index in range(3):
            value = dot_nn(norm_ref[rows, :], weight_of(w_ref, index)).astype(BF16)
            if index == 0:
                q_ref[0, rows, :] = value
            else:
                kv_ref[0, rows, pl.ds(512 * (index - 1), 512)] = value
    for chunk in range(ROWS // 256):
        rows = pl.ds(256 * chunk, 256)
        q3_ref[0, pl.ds(32 * chunk, 32), :] = dot_nn(
            low_ref[1, 192:224, :], q_ref[0, rows, :]
        ).astype(BF16)
        for part in range(2):
            lanes = pl.ds(512 * part, 512)
            cells = dot_nn(low_ref[part], kv_ref[0, rows, lanes]).astype(BF16)
            start = 0
            for level in range(1, 5):
                count = 256 >> level
                kv_ref[0, pl.ds(OFF[level] + count * chunk, count), lanes] = cells[
                    start : start + count
                ]
                start += count
    for part in range(2):
        lanes = pl.ds(512 * part, 512)
        kv_ref[0, pl.ds(OFF[5], 64), lanes] = dot_nn(
            high_ref[part], kv_ref[0, pl.ds(0, ROWS), lanes]
        ).astype(BF16)

    def edges(left_ref, right_ref):
        for level in range(LEVELS - 1):
            edge = pl.ds(HALO * level, HALO)
            left_ref[0, edge, :] = kv_ref[0, pl.ds(OFF[level], HALO), :]
            right_ref[0, edge, :] = kv_ref[0, pl.ds(OFF[level] + CELLS[level] - HALO, HALO), :]

    pl.when(piece % 2 == 0)(lambda: edges(far_ref, near_ref))
    pl.when(piece % 2 == 1)(lambda: edges(near_ref, far_ref))
    top_ref[0] = kv_ref[0, pl.ds(OFF[7], 16), :]


def cell_shapes(width):
    return [(ROWS, width), (ROWS // 8, width), (2 * ROWS, 2 * width)]


def edge_shapes(width):
    return [(EDGE, 2 * width), (EDGE, 2 * width), (16, 2 * width)]


def project(where, tokens, mine, other, const):
    micro, _, width = tokens.shape
    shape = jax.ShapeDtypeStruct
    shard = width // (2 * mine.shape[0])
    outs = cell_shapes(width) + edge_shapes(width)
    return pl.pallas_call(
        project_kernel,
        grid=(micro,),
        in_specs=[
            SCALAR,
            each_of((ROWS, width)),
            whole(mine.shape),
            whole(other.shape),
            whole((2, 240, 256)),
            whole((2, 64, ROWS)),
        ],
        out_specs=[each_of(out) for out in outs] + [whole((VEC, width))],
        out_shape=[shape((micro,) + out, BF16) for out in outs] + [shape((VEC, width), F32)],
        scratch_shapes=[
            pltpu.VMEM((3, width // shard, shard, width), BF16),
            pltpu.VMEM((ROWS, width), BF16),
        ],
        compiler_params=params(),
        cost_estimate=timing(13),
        name="project",
    )(where, tokens, mine, other, const["low"], const["high"])


def fine_windows(tile):
    return [
        (POFF[0] + 64 * tile, 96),
        (POFF[1] + 32 * tile, 64),
        (POFF[2] + 16 * tile, 16),
        (POFF[2] + 16 * tile + 32, 16),
    ]


def coarse_windows(tile):
    return [
        (POFF[3] + 64 * tile, 96),
        (POFF[4] + 32 * tile, 64),
        (POFF[5] + 16 * tile, 16),
        (POFF[5] + 16 * tile + 32, 16),
        (POFF[6], 16),
        (POFF[6] + 32, 16),
        (POFF[7], 32),
    ]


FINE_LEVELS = [96, 64, 32]
COARSE_LEVELS = [96, 64, 32, 32, 32]


def gather_rows(ref, windows, lanes):
    return jnp.concatenate([ref[at(start, size), lanes] for start, size in windows], axis=0)


def tile_bias(kid_ref, qid_ref, tile, tiles, windows, levels, bias):
    keys = jnp.concatenate([kid_ref[0, at(start, size), :] for start, size in windows], axis=0)
    keys = keys.astype(F32)
    keys = jnp.concatenate([keys, keys], axis=1)
    bias = jnp.concatenate([bias, bias], axis=1)
    out = []
    start = 0
    for index, count in enumerate(levels):
        part = slice(start, start + count)
        owner = qid_ref[0, pl.ds(tiles * index + tile, 1), :]
        out.append(jnp.where(keys[part] == owner, bias[part], NEG))
        start += count
    return jnp.concatenate(out, axis=0)


def lane_sums(value, steps):
    halves = []
    for half in range(2):
        part = value[:, 128 * half : 128 * (half + 1)]
        lane = lax.broadcasted_iota(jnp.int32, part.shape, 1)
        for step in range(steps):
            size = 1 << step
            first = (lane & size) == 0
            part = part + jnp.where(
                first, pltpu.roll(part, 128 - size, 1), pltpu.roll(part, size, 1)
            )
        halves.append(part)
    return jnp.concatenate(halves, axis=1)


def lane_roll(value, shift):
    if shift == 0:
        return value
    halves = [value[:, 128 * half : 128 * (half + 1)] for half in range(2)]
    return jnp.concatenate([pltpu.roll(part, shift % 128, 1) for part in halves], axis=1)


def far_row(tile, quad):
    return pl.ds(8 * (tile % 8) + 2 * (tile // 8) + quad, 1)


def level_sums(value, levels):
    out = [value[0 : levels[0]]]
    start = levels[0]
    for index, count in enumerate(levels[1:]):
        out.append(lane_sums(value[start : start + count], index + 1))
        start += count
    return jnp.concatenate(out, axis=0)


def head_stack(value, mask):
    return jnp.concatenate([value] * QUAD, axis=0) * mask


def head_pick(stacked):
    lane = lax.broadcasted_iota(jnp.int32, (TILE, QL), 1) // HEAD_DIM
    out = stacked[0:TILE]
    for head in range(1, QUAD):
        out = jnp.where(lane == head, stacked[TILE * head : TILE * (head + 1)], out)
    return out


def three_terms(row):
    high = row.astype(BF16)
    rest = row - high.astype(F32)
    middle = rest.astype(BF16)
    low = (rest - middle.astype(F32)).astype(BF16)
    return high, middle, low


def own_cell(tile):
    cell = lax.broadcasted_iota(jnp.int32, (16, QL), 0)
    token = lax.broadcasted_iota(jnp.int32, (16, QL), 1) % TILE
    return cell == 8 * (tile % 2) + token // 8


def lay_out(piece, kv_ref, near_ref, far_ref, across_ref, ends_ref, kvp_ref):
    def edges(left_ref, right_ref):
        for level in range(LEVELS - 1):
            base = POFF[level]
            edge = pl.ds(HALO * level, HALO)
            kvp_ref[pl.ds(base, HALO), :] = left_ref[0, edge, :]
            kvp_ref[pl.ds(base + HALO + CELLS[level], HALO), :] = right_ref[0, edge, :]

    pl.when(piece % 2 == 0)(lambda: edges(far_ref, near_ref))
    pl.when(piece % 2 == 1)(lambda: edges(near_ref, far_ref))
    for level in range(LEVELS - 1):
        count = CELLS[level]
        kvp_ref[pl.ds(POFF[level] + HALO, count), :] = kv_ref[0, pl.ds(OFF[level], count), :]
    across = across_ref[0].astype(F32)[0:PIECE7]
    ends = ends_ref[0].astype(F32)[0:PIECE7]
    tops = []
    for owner in range(4):
        top = jnp.where(owner == (piece + 2) % 4, across, jnp.where(owner == 3 - piece, ends, 0.0))
        tops.append(top)
    kvp_ref[pl.ds(POFF[7], 4 * PIECE7), :] = jnp.concatenate(tops, axis=0).astype(BF16)


def attend_kernel(
    where_ref,
    q_ref,
    q3_ref,
    kv_ref,
    near_ref,
    far_ref,
    across_ref,
    ends_ref,
    kid_ref,
    qidf_ref,
    qidc_ref,
    fine_ref,
    coarse_ref,
    mask_ref,
    spread_ref,
    mixed_ref,
    lse_ref,
    lsec_ref,
    lsex_ref,
    oc_ref,
    kvp_ref,
):
    lay_out(where_ref[0], kv_ref, near_ref, far_ref, across_ref, ends_ref, kvp_ref)
    mask = mask_ref[...]
    scaled = mask * jnp.asarray(0.125, BF16)

    units = [(tile, quad) for tile in range(COARSE_TILES) for quad in range(2)]
    biases = [
        tile_bias(kid_ref, qidc_ref, tile, 8, coarse_windows(tile), COARSE_LEVELS, coarse_ref[tile])
        for tile in range(COARSE_TILES)
    ]
    scores = []
    for tile, quad in units:
        lanes = pl.ds(QL * quad, QL)
        query = head_stack(q3_ref[0, pl.ds(TILE * tile, TILE), lanes], scaled)
        scores.append(dot_nt(gather_rows(kvp_ref, coarse_windows(tile), lanes), query))
    shares = []
    lines = []
    for index, (tile, quad) in enumerate(units):
        score = level_sums(scores[index], COARSE_LEVELS) + biases[index // 2]
        top = jnp.max(score, axis=0, keepdims=True)
        share = jnp.exp(score - top)
        total = jnp.sum(share, axis=0, keepdims=True)
        lse = top + jnp.log(total)
        lsec_ref[0, pl.ds(index, 1), :] = lse
        lines.append(lse)
        shares.append((share * (1.0 / total)).astype(BF16))
    results = []
    for (tile, quad), share in zip(units, shares):
        values = gather_rows(kvp_ref, coarse_windows(tile), pl.ds(512 + QL * quad, QL))
        results.append(dot_tn(share, values))
    lines = three_terms(jnp.concatenate(lines * 2, axis=0))
    lines = jnp.concatenate([line.astype(F32) for line in lines], axis=0)
    terms = [lane_roll(lines, -8 * part) for part in range(8)]
    terms = dot_nn(jnp.concatenate(terms, axis=0).astype(BF16), spread_ref[...])
    for part in range(8):
        rows = [terms[24 * part + 8 * index : 24 * part + 8 * index + 8] for index in range(3)]
        lsex_ref[0, pl.ds(8 * part, 8), :] = rows[0] + rows[1] + rows[2]
    for index, (tile, quad) in enumerate(units):
        oc_ref[0, pl.ds(TILE * tile, TILE), pl.ds(QL * quad, QL)] = head_pick(
            results[index]
        ).astype(BF16)

    def fine_group(group, carry):
        tiles = [GROUP * group + index for index in range(GROUP)]
        units = [(tile, quad) for tile in tiles for quad in range(2)]
        biases = [
            tile_bias(kid_ref, qidf_ref, tile, FINE_TILES, fine_windows(tile), FINE_LEVELS, fine_ref[...])
            for tile in tiles
        ]
        scores = []
        for tile, quad in units:
            lanes = pl.ds(QL * quad, QL)
            query = head_stack(q_ref[0, at(TILE * tile, TILE), lanes], scaled)
            scores.append(dot_nt(gather_rows(kvp_ref, fine_windows(tile), lanes), query))
        shares = []
        for index, (tile, quad) in enumerate(units):
            score = level_sums(scores[index], FINE_LEVELS) + biases[index // 2]
            far = lsex_ref[0, far_row(tile, quad), :]
            top = jnp.maximum(jnp.max(score, axis=0, keepdims=True), far)
            share = jnp.exp(score - top)
            far_share = jnp.exp(far - top)
            total = jnp.sum(share, axis=0, keepdims=True) + far_share
            lse_ref[0, pl.ds(2 * tile + quad, 1), :] = top + jnp.log(total)
            inverse = 1.0 / total
            shares.append(
                jnp.concatenate(
                    [share * inverse, jnp.where(own_cell(tile), far_share * inverse, 0.0)], axis=0
                ).astype(BF16)
            )
        results = []
        for (tile, quad), share in zip(units, shares):
            values = jnp.concatenate(
                [
                    gather_rows(kvp_ref, fine_windows(tile), pl.ds(512 + QL * quad, QL)),
                    oc_ref[0, at(16 * (tile // 2), 16), pl.ds(QL * quad, QL)],
                ],
                axis=0,
            )
            results.append(dot_tn(share, values))
        for (tile, quad), result in zip(units, results):
            mixed_ref[0, at(TILE * tile, TILE), pl.ds(QL * quad, QL)] = head_pick(result).astype(
                BF16
            )
        return carry

    lax.fori_loop(0, FINE_TILES // GROUP, fine_group, 0)


def stat_shapes(width):
    return [
        ((2 * FINE_TILES, QL), F32),
        ((2 * COARSE_TILES, QL), F32),
        ((64, QL), F32),
        ((ROWS // 8, width), BF16),
    ]


def id_specs(spec):
    return [
        spec((PADDED, 128)),
        spec((FINE * FINE_TILES, QL)),
        spec((8 * (LEVELS - FINE), QL)),
        whole((FINE_KEYS, QL // 2)),
        whole((COARSE_TILES, COARSE_KEYS, QL // 2)),
        whole((QL, QL)),
    ]


def id_args(ids, const):
    return [ids["key"], ids["fine"], ids["coarse"], const["fine"], const["coarse"], const["head_mask"]]


def attend(where, cells, received, ids, const):
    micro, _, width = cells[0].shape
    outs = [((ROWS, width), BF16)] + stat_shapes(width)
    ins = list(cells) + list(received)
    return pl.pallas_call(
        attend_kernel,
        grid=(micro,),
        in_specs=[SCALAR]
        + [each_of(value.shape[1:]) for value in ins]
        + id_specs(each_of)
        + [whole((QL, QL))],
        out_specs=[each_of(dims) for dims, _ in outs],
        out_shape=[jax.ShapeDtypeStruct((micro,) + dims, kind) for dims, kind in outs],
        scratch_shapes=[pltpu.VMEM((PADDED, 2 * width), BF16)],
        compiler_params=params(),
        cost_estimate=timing(23),
        name="attend",
    )(where, *ins, *id_args(ids, const), const["spread"])


def add_rows(ref, windows, lanes, value):
    start = 0
    for base, count in windows:
        rows = at(base, count)
        ref[rows, lanes] = ref[rows, lanes] + value[start : start + count]
        start += count


def attend_back_kernel(
    where_ref,
    q_ref,
    q3_ref,
    kv_ref,
    near_in_ref,
    far_in_ref,
    across_in_ref,
    ends_in_ref,
    lse_ref,
    lsec_ref,
    lsex_ref,
    oc_ref,
    dout_ref,
    kid_ref,
    qidf_ref,
    qidc_ref,
    fine_ref,
    coarse_ref,
    mask_ref,
    spread_t_ref,
    dq_ref,
    dq3_ref,
    dkv_ref,
    near_ref,
    far_ref,
    across_ref,
    ends_ref,
    acc_ref,
    dcell_ref,
    delta_ref,
    kvp_ref,
):
    lay_out(where_ref[0], kv_ref, near_in_ref, far_in_ref, across_in_ref, ends_in_ref, kvp_ref)
    delta_ref[...] = jnp.zeros(delta_ref.shape, F32)
    acc_ref[...] = jnp.zeros(acc_ref.shape, F32)
    dcell_ref[...] = jnp.zeros(dcell_ref.shape, F32)
    mask = mask_ref[...]
    scaled = mask * jnp.asarray(0.125, BF16)

    def fine_group(group, carry):
        tiles = [GROUP_BACK * group + index for index in range(GROUP_BACK)]
        units = [(tile, quad) for tile in tiles for quad in range(2)]
        biases = [
            tile_bias(kid_ref, qidf_ref, tile, FINE_TILES, fine_windows(tile), FINE_LEVELS, fine_ref[...])
            for tile in tiles
        ]
        at_unit = lambda unit: (at(TILE * unit[0], TILE), pl.ds(QL * unit[1], QL))
        queries = [head_stack(q_ref[(0,) + at_unit(unit)], scaled) for unit in units]
        douts = [head_stack(dout_ref[(0,) + at_unit(unit)], mask) for unit in units]
        scores = []
        steers = []
        for index, (tile, quad) in enumerate(units):
            keys = gather_rows(kvp_ref, fine_windows(tile), pl.ds(QL * quad, QL))
            scores.append(dot_nt(keys, queries[index]))
            values = jnp.concatenate(
                [
                    gather_rows(kvp_ref, fine_windows(tile), pl.ds(512 + QL * quad, QL)),
                    oc_ref[0, at(16 * (tile // 2), 16), pl.ds(QL * quad, QL)],
                ],
                axis=0,
            )
            steers.append(dot_nt(values, douts[index]))
        shares = []
        grads = []
        for index, (tile, quad) in enumerate(units):
            lse = lse_ref[0, pl.ds(2 * tile + quad, 1), :]
            far_share = jnp.exp(lsex_ref[0, far_row(tile, quad), :] - lse)
            share = jnp.exp(level_sums(scores[index], FINE_LEVELS) + biases[index // 2] - lse)
            share = jnp.concatenate([share, jnp.where(own_cell(tile), far_share, 0.0)], axis=0)
            weighted = share * steers[index]
            delta = jnp.sum(weighted, axis=0, keepdims=True)
            delta_ref[far_row(tile, quad), :] = far_share * delta
            grad = weighted[0:FINE_KEYS] - share[0:FINE_KEYS] * delta
            grads.append(level_sums(grad, FINE_LEVELS).astype(BF16))
            shares.append(share.astype(BF16))
        dvalues = [dot_nn(share, dout) for share, dout in zip(shares, douts)]
        dkeys = [dot_nn(grad, query) for grad, query in zip(grads, queries)]
        dqueries = []
        for (tile, quad), grad in zip(units, grads):
            keys = gather_rows(kvp_ref, fine_windows(tile), pl.ds(QL * quad, QL))
            dqueries.append(dot_tn(grad, keys))
        for index, (tile, quad) in enumerate(units):
            lanes = pl.ds(QL * quad, QL)
            cells = at(16 * (tile // 2), 16)
            windows = fine_windows(tile)
            add_rows(acc_ref, windows, pl.ds(512 + QL * quad, QL), dvalues[index])
            dcell_ref[cells, lanes] = dcell_ref[cells, lanes] + dvalues[index][FINE_KEYS:]
            add_rows(acc_ref, windows, lanes, dkeys[index])
            dq_ref[(0,) + at_unit((tile, quad))] = (head_pick(dqueries[index]) * 0.125).astype(BF16)
        return carry

    lax.fori_loop(0, FINE_TILES // GROUP_BACK, fine_group, 0)

    units = [(tile, quad) for tile in range(COARSE_TILES) for quad in range(2)]
    biases = [
        tile_bias(kid_ref, qidc_ref, tile, 8, coarse_windows(tile), COARSE_LEVELS, coarse_ref[tile])
        for tile in range(COARSE_TILES)
    ]
    at_unit = lambda unit: (pl.ds(TILE * unit[0], TILE), pl.ds(QL * unit[1], QL))
    queries = [head_stack(q3_ref[(0,) + at_unit(unit)], scaled) for unit in units]
    douts = [head_stack(dcell_ref[at_unit(unit)].astype(BF16), mask) for unit in units]
    terms = dot_nn(jnp.concatenate(three_terms(delta_ref[...]), axis=0), spread_t_ref[...])
    terms = terms[0:64] + terms[64:128] + terms[128:192]
    deltas = lane_roll(terms[0:8], 0)
    for part in range(1, 8):
        deltas = deltas + lane_roll(terms[8 * part : 8 * part + 8], 8 * part)
    steers = []
    scores = []
    for (tile, quad), dout, query in zip(units, douts, queries):
        values = gather_rows(kvp_ref, coarse_windows(tile), pl.ds(512 + QL * quad, QL))
        steers.append(dot_nt(values, dout))
        keys = gather_rows(kvp_ref, coarse_windows(tile), pl.ds(QL * quad, QL))
        scores.append(dot_nt(keys, query))
    shares = []
    grads = []
    for index, (tile, quad) in enumerate(units):
        score = level_sums(scores[index], COARSE_LEVELS) + biases[index // 2]
        share = jnp.exp(score - lsec_ref[0, pl.ds(index, 1), :])
        delta = deltas[index : index + 1]
        grads.append(level_sums(share * (steers[index] - delta), COARSE_LEVELS).astype(BF16))
        shares.append(share.astype(BF16))
    dvalues = [dot_nn(share, dout) for share, dout in zip(shares, douts)]
    dkeys = [dot_nn(grad, query) for grad, query in zip(grads, queries)]
    dqueries = []
    for (tile, quad), grad in zip(units, grads):
        keys = gather_rows(kvp_ref, coarse_windows(tile), pl.ds(QL * quad, QL))
        dqueries.append(dot_tn(grad, keys))
    for index, (tile, quad) in enumerate(units):
        windows = coarse_windows(tile)
        add_rows(acc_ref, windows, pl.ds(512 + QL * quad, QL), dvalues[index])
        add_rows(acc_ref, windows, pl.ds(QL * quad, QL), dkeys[index])
        dq3_ref[(0,) + at_unit((tile, quad))] = (head_pick(dqueries[index]) * 0.125).astype(BF16)

    key_lane = lax.broadcasted_iota(jnp.int32, (1, acc_ref.shape[1]), 1) < 512

    def scale(level):
        return jnp.where(key_lane, 0.5 ** STEP[level], 1.0)

    def low(level, start, count):
        return (acc_ref[pl.ds(start, count), :] * scale(level)).astype(BF16)

    def edges(left_ref, right_ref):
        for level in range(LEVELS - 1):
            base = POFF[level]
            edge = pl.ds(HALO * level, HALO)
            left_ref[0, edge, :] = low(level, base, HALO)
            right_ref[0, edge, :] = low(level, base + HALO + CELLS[level], HALO)

    piece = where_ref[0]
    pl.when(piece % 2 == 0)(lambda: edges(far_ref, near_ref))
    pl.when(piece % 2 == 1)(lambda: edges(near_ref, far_ref))
    for level in range(LEVELS - 1):
        dkv_ref[0, pl.ds(OFF[level], CELLS[level]), :] = low(level, POFF[level] + HALO, CELLS[level])
    dkv_ref[0, pl.ds(OFF[7], 16), :] = jnp.zeros((16, acc_ref.shape[1]), BF16)
    blank = jnp.zeros((PIECE7, acc_ref.shape[1]), F32)

    def high(index):
        rows = pl.ds(pl.multiple_of(POFF[7] + PIECE7 * index, PIECE7), PIECE7)
        return jnp.concatenate([acc_ref[rows, :] * scale(7), blank], axis=0).astype(BF16)

    ends_ref[0] = high(3 - piece)
    across_ref[0] = high((piece + 2) % 4)


def attend_back(where, cells, received, stats, dout, ids, const):
    micro, _, width = dout.shape
    shape = jax.ShapeDtypeStruct
    outs = cell_shapes(width) + edge_shapes(width) + edge_shapes(width)[2:]
    ins = list(cells) + list(received) + list(stats) + [dout]
    return pl.pallas_call(
        attend_back_kernel,
        grid=(micro,),
        in_specs=[SCALAR]
        + [each_of(value.shape[1:]) for value in ins]
        + id_specs(each_of)
        + [whole((QL, QL))],
        out_specs=[each_of(out) for out in outs],
        out_shape=[shape((micro,) + out, BF16) for out in outs],
        scratch_shapes=[
            pltpu.VMEM((PADDED, 2 * width), F32),
            pltpu.VMEM((ROWS // 8, width), F32),
            pltpu.VMEM((64, QL), F32),
            pltpu.VMEM((PADDED, 2 * width), BF16),
        ],
        compiler_params=params(),
        cost_estimate=timing(38),
        name="attend_back",
    )(where, *ins, *id_args(ids, const), const["spread_t"])


MID_ROWS = 512
FF_CHUNK = 512
ROOT = math.sqrt(2.0 / math.pi)


def give(send_ref, start, piece_of):
    for index in range(send_ref.shape[0]):
        piece = piece_of(index)
        send_ref[index, pl.ds(start, piece.shape[0]), :] = piece


def row_piece(ref, shard):
    def piece_of(index):
        return ref[pl.ds(pl.multiple_of(shard * index, shard), shard), :].astype(BF16)

    return piece_of


def middle_kernel(
    where_ref,
    tok_ref,
    cot_ref,
    mixed_ref,
    vec_ref,
    mine_ref,
    other_ref,
    out_ref,
    dmid_ref,
    dmix_ref,
    send_ref,
    wo_ref,
    wi_ref,
    wd_ref,
    acc_o,
    acc_i,
    acc_d,
    acc_b,
    acc_s,
    activ_ref,
    grad_ref,
):
    step = pl.program_id(0)
    core = where_ref[1]
    parts = wi_ref.shape[0]
    shard = wo_ref.shape[2]

    @pl.when(step == 0)
    def _():
        acc_o[...] = jnp.zeros(acc_o.shape, F32)
        acc_i[...] = jnp.zeros(acc_i.shape, F32)
        acc_d[...] = jnp.zeros(acc_d.shape, F32)
        acc_b[...] = jnp.zeros(acc_b.shape, F32)
        acc_s[...] = jnp.zeros(acc_s.shape, F32)
        take_weight(wo_ref, 0, mine_ref, other_ref, core, 0)
        for part in range(parts):
            take_weight(wi_ref, part, mine_ref, other_ref, core, shard * (1 + part))
        take_weight(wd_ref, 0, mine_ref, other_ref, core, shard * (1 + parts))

    wo = weight_of(wo_ref, 0)
    pieces = FF_CHUNK // wd_ref.shape[2]
    wi = [weight_of(wi_ref, part) for part in range(parts)]
    wd = [
        wd_ref[0, pieces * part : pieces * (part + 1)].reshape(FF_CHUNK, wo.shape[1])
        for part in range(parts)
    ]
    cot = cot_ref[...]
    top = cot.astype(BF16)
    mixed = mixed_ref[...]
    middle = tok_ref[...] + dot_nn(mixed, wo)
    unit, rate = normalised(middle)
    second = (unit * vec_ref[1:2] + vec_ref[3:4]).astype(BF16)
    result = middle + vec_ref[4:5]
    back = jnp.zeros(cot.shape, F32)
    pres = {}

    def first(part):
        pres[part] = (dot_nn(second, wi[part]) + vec_ref[5 + part : 6 + part], dot_nt(top, wd[part]))

    first(0)
    for part in range(parts):
        if part + 1 < parts:
            first(part + 1)
        pre, grad = pres.pop(part)
        square = pre * pre
        tanh = jnp.tanh(pre * (ROOT + (ROOT * 0.044715) * square))
        half = 0.5 + 0.5 * tanh
        activ = (pre * half).astype(BF16)
        slope = half + (pre * (0.5 - 0.5 * (tanh * tanh))) * (
            ROOT + (ROOT * 3 * 0.044715) * square
        )
        grad = (grad * slope).astype(BF16)
        cols = pl.ds(FF_CHUNK * part, FF_CHUNK)
        activ_ref[:, cols] = activ
        grad_ref[:, cols] = grad
        acc_b[:, cols] = acc_b[:, cols] + fold_rows(grad.astype(F32))
        result = result + dot_nn(activ, wd[part])
        back = back + dot_nt(grad, wi[part])
    out_ref[...] = result
    acc_d[...] = acc_d[...] + dot_tn(activ_ref[...], top)
    for part in range(parts):
        acc_i[part] = acc_i[part] + dot_tn(second, grad_ref[:, pl.ds(FF_CHUNK * part, FF_CHUNK)])
    dmid = cot + norm_back(back * vec_ref[1:2], unit, rate)
    dmid_ref[...] = dmid
    branch = dmid.astype(BF16)
    dmix_ref[...] = dot_nt(branch, wo).astype(BF16)
    acc_o[...] = acc_o[...] + dot_tn(mixed, branch)
    acc_s[0:8, :] = acc_s[0:8, :] + fold_rows(top.astype(F32))
    acc_s[8:16, :] = acc_s[8:16, :] + fold_rows(back * unit)
    acc_s[16:24, :] = acc_s[16:24, :] + fold_rows(back)

    @pl.when(step == pl.num_programs(0) - 1)
    def _():
        give(send_ref, 0, row_piece(acc_o, shard))
        for part in range(parts):
            give(send_ref, shard * (1 + part), row_piece(acc_i.at[part], shard))
        give(send_ref, shard * (1 + parts), row_piece(acc_d, shard * parts))
        total = lambda value: jnp.sum(value, axis=0, keepdims=True)
        lines = [total(acc_s[8 * index : 8 * index + 8, :]) for index in range(3)]
        for part in range(parts):
            lines.append(total(acc_b[:, pl.ds(FF_CHUNK * part, FF_CHUNK)]))
        lines.append(jnp.zeros((16 - len(lines), lines[0].shape[1]), F32))
        lines = jnp.concatenate(lines, axis=0).astype(BF16)
        give(send_ref, shard * (1 + 2 * parts), lambda index: lines)


def middle_part(where, tokens, cot, mixed, vec, mine, other):
    rows, width = tokens.shape
    chips, lines, _ = mine.shape
    shard = width // (2 * chips)
    parts = (lines // shard - 1) // 2
    hidden = parts * FF_CHUNK
    shape = jax.ShapeDtypeStruct
    tiled = pl.BlockSpec((MID_ROWS, width), lambda r: (r, 0))
    shared = shape((2 * chips, lines + 16, width), BF16)
    single = lambda dims: pl.BlockSpec(
        dims, lambda *_: (0,) * len(dims), pipeline_mode=pl.Buffered(1)
    )
    return pl.pallas_call(
        middle_kernel,
        grid=(rows // MID_ROWS,),
        in_specs=[SCALAR, tiled, tiled, tiled, whole(vec.shape), single(mine.shape), single(mine.shape)],
        out_specs=[tiled, tiled, tiled, single(shared.shape)],
        out_shape=[
            shape((rows, width), F32),
            shape((rows, width), F32),
            shape((rows, width), BF16),
            shared,
        ],
        scratch_shapes=[
            pltpu.VMEM((1, 2 * chips, shard, width), BF16),
            pltpu.VMEM((parts, 2 * chips, shard, FF_CHUNK), BF16),
            pltpu.VMEM((1, 2 * chips, shard * parts, width), BF16),
            pltpu.VMEM((width, width), F32),
            pltpu.VMEM((parts, width, FF_CHUNK), F32),
            pltpu.VMEM((hidden, width), F32),
            pltpu.VMEM((8, hidden), F32),
            pltpu.VMEM((24, width), F32),
            pltpu.VMEM((MID_ROWS, hidden), BF16),
            pltpu.VMEM((MID_ROWS, hidden), BF16),
        ],
        compiler_params=params(),
        cost_estimate=timing(40),
        name="middle",
    )(where, tokens, cot, mixed, vec, mine, other)


def collect_kernel(
    where_ref,
    tok_ref,
    dq_ref,
    dq3_ref,
    dkv_ref,
    near_ref,
    far_ref,
    across_ref,
    ends_ref,
    low_ref,
    high_ref,
    vec_ref,
    mine_ref,
    other_ref,
    dp_ref,
    send_ref,
    cells_ref,
    norm_ref,
    gw_ref,
    sum_ref,
    w_ref,
):
    @pl.when(pl.program_id(0) == 0)
    def _():
        gw_ref[...] = jnp.zeros(gw_ref.shape, F32)
        sum_ref[...] = jnp.zeros(sum_ref.shape, F32)

    piece, core = where_ref[0], where_ref[1]
    cells_ref[...] = dkv_ref[0]

    def add(start, value):
        rows = pl.ds(start, HALO)
        cells_ref[rows, :] = (cells_ref[rows, :].astype(F32) + value.astype(F32)).astype(BF16)

    def edges(left_ref, right_ref):
        for level in range(LEVELS - 1):
            edge = pl.ds(HALO * level, HALO)

            @pl.when(piece > 0)
            def _():
                add(OFF[level], left_ref[0, edge, :])

            @pl.when(piece < 3)
            def _():
                add(OFF[level] + CELLS[level] - HALO, right_ref[0, edge, :])

    pl.when(piece % 2 == 0)(lambda: edges(far_ref, near_ref))
    pl.when(piece % 2 == 1)(lambda: edges(near_ref, far_ref))
    add(OFF[7], across_ref[0].astype(F32) + ends_ref[0].astype(F32))

    sums = [jnp.zeros((8, 512), F32), jnp.zeros((8, 1024), F32)]
    for chunk in range(ROWS // 256):
        rows = pl.ds(256 * chunk, 256)
        norm_ref[rows, :] = normalised(tok_ref[0, rows, :])[0].astype(BF16)
        cells = jnp.concatenate(
            [
                cells_ref[pl.ds(OFF[level] + (256 >> level) * chunk, 256 >> level), :]
                for level in range(1, 5)
            ],
            axis=0,
        )
        dkv = (
            cells_ref[rows, :].astype(F32)
            + dot_nn(low_ref[...], cells)
            + dot_nn(high_ref[rows, :], cells_ref[pl.ds(OFF[5], 64), :])
        ).astype(BF16)
        dq = (
            dq_ref[0, rows, :].astype(F32)
            + dot_nn(low_ref[:, 192:224], dq3_ref[0, pl.ds(32 * chunk, 32), :])
        ).astype(BF16)
        dp_ref[0, rows, pl.ds(0, 512)] = dq
        dp_ref[0, rows, pl.ds(512, 1024)] = dkv
        sums = [old + fold_rows(new.astype(F32)) for old, new in zip(sums, (dq, dkv))]
    sum_ref[...] = sum_ref[...] + jnp.concatenate(sums, axis=1)
    for index in range(3):
        grad = dot_tn(norm_ref[...], dp_ref[0, :, pl.ds(512 * index, 512)])
        gw_ref[index] = gw_ref[index] + grad

    @pl.when(pl.program_id(0) == pl.num_programs(0) - 1)
    def _():
        shard = w_ref.shape[2]
        row = lax.broadcasted_iota(jnp.int32, (VEC, 512), 0)
        lines = vec_ref[...].astype(BF16)
        gain = dot_tn(lines, jnp.where(row == 0, 1.0, 0.0).astype(BF16))
        offset = dot_tn(lines, jnp.where(row == 2, 1.0, 0.0).astype(BF16))
        ones = jnp.ones((8, 512), BF16)
        grad_gain = jnp.zeros((8, 512), F32)
        grad_offset = jnp.zeros((8, 512), F32)
        for index in range(3):
            take_weight(w_ref, index, mine_ref, other_ref, core, shard * index)
            grad = gw_ref[index]
            total = jnp.sum(sum_ref[:, pl.ds(512 * index, 512)], axis=0, keepdims=True)
            gw_ref[index] = gain * grad + offset * total
            weight = weight_of(w_ref, index)
            high, middle, _ = three_terms(weight.astype(F32) * grad)
            grad_gain = grad_gain + dot_nt(ones, high) + dot_nt(ones, middle)
            high, middle, low = three_terms(total)
            terms = jnp.concatenate([high, middle, low] + [jnp.zeros_like(low)] * 5, axis=0)
            grad_offset = grad_offset + dot_nt(terms, weight)
            give(send_ref, shard * index, row_piece(gw_ref.at[index], shard))
        grad_offset = jnp.sum(grad_offset, axis=0, keepdims=True)
        blank = jnp.zeros((VEC - 2, 512), F32)
        lines = jnp.concatenate([grad_gain[0:1], grad_offset, blank], axis=0).astype(BF16)
        give(send_ref, 3 * shard, lambda index: lines)


def collect(where, tokens, grads, received, vec, mine, other, const):
    micro, _, width = tokens.shape
    chips, lines, _ = mine.shape
    shard = width // (2 * chips)
    shape = jax.ShapeDtypeStruct
    moved = [tokens] + list(grads) + list(received)
    ins = [const["low_t"], const["high_t"], vec, mine, other]
    return pl.pallas_call(
        collect_kernel,
        grid=(micro,),
        in_specs=[SCALAR]
        + [each_of(value.shape[1:]) for value in moved]
        + [whole(value.shape) for value in ins],
        out_specs=[each_of((ROWS, 3 * width)), whole((2 * chips, lines, width))],
        out_shape=[
            shape((micro, ROWS, 3 * width), BF16),
            shape((2 * chips, lines, width), BF16),
        ],
        scratch_shapes=[
            pltpu.VMEM((2 * ROWS, 2 * width), BF16),
            pltpu.VMEM((ROWS, width), BF16),
            pltpu.VMEM((3, width, width), F32),
            pltpu.VMEM((8, 3 * width), F32),
            pltpu.VMEM((3, 2 * chips, shard, width), BF16),
        ],
        compiler_params=params(),
        cost_estimate=timing(17),
        name="collect",
    )(where, *moved, *ins)


FIN_ROWS = 512


def finish_kernel(
    where_ref, tok_ref, dmid_ref, dp_ref, vec_ref, mine_ref, other_ref, grad_ref, w_ref
):
    core = where_ref[1]

    @pl.when(pl.program_id(0) == 0)
    def _():
        for index in range(3):
            take_weight(w_ref, index, mine_ref, other_ref, core, w_ref.shape[2] * index)

    back = dot_nt(dp_ref[:, pl.ds(0, 512)], weight_of(w_ref, 0))
    for index in range(1, 3):
        back = back + dot_nt(dp_ref[:, pl.ds(512 * index, 512)], weight_of(w_ref, index))
    unit, rate = normalised(tok_ref[...])
    grad_ref[...] = dmid_ref[...] + norm_back(back * vec_ref[0:1], unit, rate)


def finish(where, tokens, dmid, dproj, vec, mine, other):
    rows, width = tokens.shape
    dp = 2 * mine.shape[0]
    chunk = lambda lanes: pl.BlockSpec((FIN_ROWS, lanes), lambda r: (r, 0))
    return pl.pallas_call(
        finish_kernel,
        grid=(rows // FIN_ROWS,),
        in_specs=[
            SCALAR,
            chunk(width),
            chunk(width),
            chunk(3 * width),
            whole(vec.shape),
            whole(mine.shape),
            whole(other.shape),
        ],
        out_specs=chunk(width),
        out_shape=jax.ShapeDtypeStruct(tokens.shape, F32),
        scratch_shapes=[pltpu.VMEM((3, dp, width // dp, width), BF16)],
        compiler_params=params(),
        cost_estimate=timing(13),
        name="finish",
    )(where, tokens, dmid, dproj, vec, mine, other)


def twice(chunk):
    lane = lax.broadcasted_iota(jnp.int32, chunk.shape, 1)
    other = pltpu.roll(chunk, 64, 1)
    halves = jnp.where(lane < 64, chunk, other), jnp.where(lane < 64, other, chunk)
    return [jnp.concatenate([half, half], axis=1)[0:1] for half in halves]


def lane_pairs(value, size, merge):
    halves = []
    for half in range(2):
        part = value[:, 128 * half : 128 * (half + 1)]
        lane = lax.broadcasted_iota(jnp.int32, part.shape, 1)
        first = (lane & size) == 0
        pair = jnp.where(first, pltpu.roll(part, 128 - size, 1), pltpu.roll(part, size, 1))
        halves.append(merge(part, pair))
    return jnp.concatenate(halves, axis=1)


def documents_kernel(where_ref, seg_ref, own_ref, kid_ref, qidf_ref, qidc_ref, row_ref):
    piece = where_ref[0]
    length = seg_ref.shape[2]
    margin = (row_ref.shape[0] - length) // 2
    ones = jnp.ones((16, 128), BF16)

    def only_first(row):
        index = lax.broadcasted_iota(jnp.int32, (16, row.shape[1]), 0)
        return jnp.where(index == 0, row.astype(F32), 0.0).astype(BF16)

    outside = jnp.full((margin, 128), -3.0, F32)
    row_ref[pl.ds(0, margin), :] = outside
    row_ref[pl.ds(margin + length, margin), :] = outside
    row_ref[pl.ds(margin, length), :] = dot_tn(only_first(seg_ref[0]), ones)
    for level in range(LEVELS):
        cell = 1 << level
        if level < LEVELS - 1:
            start = ROWS * piece + margin - HALO * cell
            count = CELLS[level] + 2 * HALO
        else:
            start = margin
            count = 4 * PIECE7
        if level == 0:
            key = row_ref[at(start, count), :]
        else:
            lowest = row_ref[pl.ds(start, count, stride=cell), :]
            highest = row_ref[pl.ds(start + cell - 1, count, stride=cell), :]
            key = jnp.where(lowest == highest, lowest, -2.0)
        if level == LEVELS - 1:
            owner = lax.broadcasted_iota(jnp.int32, key.shape, 0) // PIECE7
            counted = (jnp.abs(owner // 2 - piece // 2) == 1) & (jnp.abs(owner - piece) >= 2)
            key = jnp.where(counted, key, -3.0)
        kid_ref[0, pl.ds(POFF[level], count), :] = key.astype(BF16)

    own = own_ref[0].astype(F32)
    rows = []
    for chunk in range(ROWS // 128):
        rows += twice(jnp.broadcast_to(own[:, 128 * chunk : 128 * (chunk + 1)], (8, 128)))
    low = high = jnp.concatenate(rows, axis=0)
    for level in range(FINE):
        if level > 0:
            low = lane_pairs(low, 1 << (level - 1), jnp.minimum)
            high = lane_pairs(high, 1 << (level - 1), jnp.maximum)
        qidf_ref[0, pl.ds(FINE_TILES * level, FINE_TILES), :] = jnp.where(low == high, low, -1.0)

    token = lax.broadcasted_iota(jnp.int32, (ROWS, ROWS // 8), 0)
    cells = lax.broadcasted_iota(jnp.int32, (ROWS, ROWS // 8), 1)
    ends = []
    for step in (0, 7):
        pick = jnp.where(token == 8 * cells + step, 1.0, 0.0).astype(BF16)
        value = dot_nn(only_first(own), pick)[0:1]
        rows = twice(jnp.broadcast_to(value, (8, 128)))
        ends.append(jnp.concatenate(rows + [rows[1]] * 6, axis=0))
    low, high = ends
    for index in range(LEVELS - FINE):
        if index > 0:
            low = lane_pairs(low, 1 << (index - 1), jnp.minimum)
            high = lane_pairs(high, 1 << (index - 1), jnp.maximum)
        qidc_ref[0, pl.ds(8 * index, 8), :] = jnp.where(low == high, low, -1.0)


def cell_documents(where, segments, piece):
    micro, _, length = segments.shape
    shape = jax.ShapeDtypeStruct
    own = lax.dynamic_slice_in_dim(segments, piece * ROWS, ROWS, axis=2)
    outs = [((PADDED, 128), BF16), ((FINE * FINE_TILES, QL), F32), ((8 * (LEVELS - FINE), QL), F32)]
    key, fine, coarse = pl.pallas_call(
        documents_kernel,
        grid=(micro,),
        in_specs=[SCALAR, each_of((1, length)), each_of((1, ROWS))],
        out_specs=[each_of(dims) for dims, _ in outs],
        out_shape=[shape((micro,) + dims, kind) for dims, kind in outs],
        scratch_shapes=[pltpu.VMEM((length + 2 * ROWS, 128), F32)],
        compiler_params=params(),
        cost_estimate=timing(5),
        name="documents",
    )(where, segments, own)
    return dict(key=key, fine=fine, coarse=coarse)


def same_core(chips):
    return [[2 * chip + core for chip in range(chips)] for core in range(2)]


def core_swap(value, chips):
    pairs = [(place, place ^ 1) for place in range(2 * chips)]
    return lax.ppermute(value, "dp", pairs)


def chip_exchange(value, chips):
    return lax.all_to_all(value, "dp", 0, 0, axis_index_groups=same_core(chips), tiled=True)


def after(value, *done):
    return lax.optimization_barrier((value,) + done)[0]


def add(left, right):
    return left.astype(F32) + right.astype(F32)


def body(
    tokens,
    segment_ids,
    norm_gains,
    norm_biases,
    qkv_weight,
    out_weight,
    in_weight,
    in_bias,
    down_weight,
    down_bias,
    cotangent,
):
    micro, _, row_count, width = tokens.shape
    pieces = lax.axis_size("sp")
    piece = lax.axis_index("sp")
    assert row_count == ROWS and pieces == 4 and micro == 2
    const = constants()
    tokens = tokens[:, 0]
    cotangent = cotangent[:, 0]
    dp = lax.axis_size("dp")
    place = lax.axis_index("dp")
    chips = dp // 2
    shard = width // dp
    hidden = in_weight.shape[1]
    parts = hidden // FF_CHUNK
    where = jnp.stack([piece, place % 2]).astype(jnp.int32)
    swap = lambda value, bits: lax.ppermute(value, "sp", [(p, p ^ bits) for p in range(pieces)])
    spread = lambda value: chip_exchange(
        jnp.broadcast_to(value[None], (chips,) + value.shape), chips
    )

    def placed(value, start):
        lines = jnp.zeros((value.shape[0], start * value.shape[1]), BF16)
        return lax.dynamic_update_slice(lines, value, (0, place * value.shape[1])).reshape(-1, width)

    small = placed(jnp.concatenate([norm_gains, norm_biases, down_bias[None]]), dp)
    small = jnp.concatenate([small, placed(in_bias[None], dp)])
    small = jnp.pad(small, ((0, VEC - small.shape[0]), (0, 0)))
    mine = spread(jnp.concatenate([qkv_weight.reshape(3 * shard, width), small]))
    ids = cell_documents(where, segment_ids, piece)
    where, mine = lax.optimization_barrier((after(where, ids["coarse"]), mine))
    other = core_swap(mine, chips)
    rest = jnp.concatenate(
        [
            out_weight,
            in_weight.reshape(shard, parts, FF_CHUNK).swapaxes(0, 1).reshape(-1, width),
            down_weight,
        ]
    )
    rest_mine = spread(after(rest, other))

    def halo(near, far, across, ends):
        middle = lax.ppermute(far, "sp", [(1, 2), (2, 1)])
        return swap(near, 1), middle, swap(across, 2), lax.ppermute(ends, "sp", [(0, 3), (3, 0)])

    q, q3, kv, near, far, top, vec = project(where, tokens, mine, other, const)
    cells = (q, q3, kv)
    received = halo(near, far, top, top)
    rest_mine = after(rest_mine, *received)
    rest_other = core_swap(rest_mine, chips)
    mixed, *stats = attend(after(where, rest_mine), cells, received, ids, const)
    rest_other = after(rest_other, mixed)

    flat = lambda value: value.reshape(micro * ROWS, width)
    split = lambda value: value.reshape(micro, ROWS, width)
    outputs, dmid, dmix, send = middle_part(
        where, flat(tokens), flat(cotangent), flat(mixed), vec, rest_mine, rest_other
    )
    come = lax.all_to_all(send, "dp", 0, 0, tiled=True)
    dq, dq3, dkv, *edges = attend_back(where, cells, received, stats, split(dmix), ids, const)
    grads = (dq, dq3, dkv)
    back = halo(*edges)
    odd = piece % 2 == 1
    total = jnp.sum(after(come, *back).astype(F32), axis=0).astype(BF16)
    come = swap(total, 1)
    dproj, send = collect(
        after(where, total), tokens, grads, back, vec, mine, other, const
    )
    qkv_come = lax.all_to_all(send, "dp", 0, 0, tiled=True)
    total = add(total, after(come, send)).astype(BF16)
    half = jnp.where(odd, total[:, width // 2 :], total[:, : width // 2])
    come = swap(half, 2)
    input_grad = finish(
        after(where, half), flat(tokens), dmid, dproj.reshape(micro * ROWS, -1), vec, mine, other
    )
    half = add(half, after(come, input_grad)).astype(BF16)
    come = swap(half, 1)
    total = jnp.sum(after(qkv_come, half).astype(F32), axis=0).astype(BF16)
    qkv_come = swap(total, 1)
    come = after(come, total)
    rest = jnp.where(
        odd, jnp.concatenate([come, half], axis=1), jnp.concatenate([half, come], axis=1)
    ).astype(F32)
    total = add(total, qkv_come).astype(BF16)
    total = add(total, swap(total, 2))

    own = lambda value, size: lax.dynamic_slice_in_dim(value, place * size, size, axis=-1)
    small_two = rest[shard * (1 + 2 * parts) :]
    small_one = total[3 * shard :]
    gin = rest[shard : shard * (1 + parts)].reshape(parts, shard, FF_CHUNK).swapaxes(0, 1)
    return (
        outputs.reshape(micro, 1, ROWS, width),
        input_grad.reshape(micro, 1, ROWS, width),
        own(jnp.stack([small_one[0], small_two[1]]), shard),
        own(jnp.stack([small_one[1], small_two[2]]), shard),
        total[: 3 * shard].reshape(3, shard, width),
        rest[:shard],
        gin.reshape(shard, hidden),
        own(small_two[3 : 3 + parts].reshape(hidden), hidden // dp),
        rest[shard * (1 + parts) : shard * (1 + 2 * parts)],
        own(small_two[0], shard),
    )


def solution(mesh):
    in_specs = (
        P(None, "dp", "sp", None),
        P(None, "dp", None),
        P(None, "dp"),
        P(None, "dp"),
        P(None, "dp", None),
        P("dp", None),
        P("dp", None),
        P("dp"),
        P("dp", None),
        P("dp"),
        P(None, "dp", "sp", None),
    )
    out_specs = (
        P(None, "dp", "sp", None),
        P(None, "dp", "sp", None),
        P(None, "dp"),
        P(None, "dp"),
        P(None, "dp", None),
        P("dp", None),
        P("dp", None),
        P("dp"),
        P("dp", None),
        P("dp"),
    )
    return jax.shard_map(body, mesh=mesh, in_specs=in_specs, out_specs=out_specs, check_vma=False)
```

```python
import math

import jax
import jax.numpy as jnp
from jax import lax
from jax.experimental import pallas as pl
from jax.experimental.pallas import tpu as pltpu
from jax.sharding import PartitionSpec as P

HEADS = 8
HEAD_DIM = 64
BLOCK = 16
LEVELS = 8
HALO = 16
TILE = 64
QUAD = 4
QL = QUAD * HEAD_DIM
NEG = -1e30
FINE = 3
ROWS = 1024
EDGE = 112
VEC = 16
GROUP = 4
GROUP_BACK = 2
F32 = jnp.float32
BF16 = jnp.bfloat16

CELLS = [ROWS >> level for level in range(LEVELS)]
OFF = [2 * ROWS - (2 * ROWS >> level) for level in range(LEVELS)]
POFF = []
_at = 0
for _level in range(LEVELS - 1):
    POFF.append(_at)
    _at += CELLS[_level] + 2 * HALO
POFF.append(_at)
PIECE7 = CELLS[LEVELS - 1]
PADDED = _at + 4 * PIECE7
FINE_TILES = ROWS // TILE
COARSE_TILES = ROWS // 8 // TILE
FINE_KEYS = 192
COARSE_KEYS = 256
LN_EPS = 1e-05
VMEM_LIMIT = 62 * 1024 * 1024


STEP = [0, 1, 2, 0, 1, 2, 3, 4]


def places(shape):
    return [lax.broadcasted_iota(jnp.int32, shape, axis) for axis in range(2)]


def counted_pairs(level, query, key):
    near = jnp.abs((query >> 4) - (key >> 4))
    if level == 0:
        return near <= 1
    return (near == 1) & (jnp.abs((query >> 3) - (key >> 3)) >= 2)


def score_offsets(parts):
    out = []
    for level, count, window, query_of in parts:
        key, lane = places((count, 2 * TILE))
        query = query_of(lane & (TILE - 1))
        if window == "all":
            allowed = jnp.full(key.shape, True)
        else:
            split = window == "sides"
            key = jnp.where(key < 16, key - 16, key) if split else key - 16
            allowed = counted_pairs(level, query, key)
        out.append(jnp.where(allowed, level * math.log(2.0), NEG))
    return jnp.concatenate(out, axis=0)


def fine_offsets():
    return score_offsets(
        [
            (0, 96, "span", lambda token: token),
            (1, 64, "span", lambda token: token >> 1),
            (2, 32, "sides", lambda token: token >> 2),
        ]
    )


def coarse_offsets(tile):
    return score_offsets(
        [
            (3, 96, "span", lambda cell: cell),
            (4, 64, "span", lambda cell: cell >> 1),
            (5, 32, "sides", lambda cell: cell >> 2),
            (6, 32, "sides", lambda cell: 8 * tile + (cell >> 3)),
            (7, 4 * PIECE7, "all", lambda cell: cell),
        ]
    )


def mean_table(shape, cell_axis, levels, scale_of):
    index = places(shape)
    cell, token = index[cell_axis], index[1 - cell_axis]
    out = jnp.zeros(shape, F32)
    start = 0
    for level in levels:
        weight = scale_of(level) / (1 << level)
        out = out + jnp.where((token >> level) + start == cell, weight, 0.0)
        start += shape[1 - cell_axis] >> level
    return out.astype(BF16)


def head_table():
    row, col = places((QL, QL))
    return jnp.where((row >> 6) == (col >> 6), 1.0, 0.0).astype(BF16)


def spread_table(cell_axis):
    index = places((QL, QL))
    cell, token = index[cell_axis], index[1 - cell_axis]
    same = ((cell >> 6) == (token >> 6)) & ((cell & 63) == ((token & 63) >> 3))
    return jnp.where(same, 1.0, 0.0).astype(BF16)


def attention_tables(fine_ref, coarse_ref, mask_ref, spread_ref, cell_axis):
    fine_ref[...] = fine_offsets()
    for tile in range(COARSE_TILES):
        coarse_ref[tile] = coarse_offsets(tile)
    mask_ref[...] = head_table()
    spread_ref[...] = spread_table(cell_axis)


def table_shapes():
    return [
        pltpu.VMEM((FINE_KEYS, QL // 2), F32),
        pltpu.VMEM((COARSE_TILES, COARSE_KEYS, QL // 2), F32),
        pltpu.VMEM((QL, QL), BF16),
        pltpu.VMEM((QL, QL), BF16),
    ]


def dot_nn(left, right):
    return jnp.dot(left, right, preferred_element_type=F32)


def dot_nt(left, right):
    return lax.dot_general(left, right, (((1,), (1,)), ((), ())), preferred_element_type=F32)


def dot_tn(left, right):
    return lax.dot_general(left, right, (((0,), (0,)), ((), ())), preferred_element_type=F32)


def at(start, size):
    return pl.ds(pl.multiple_of(start, 16), size)


def whole(shape):
    zeros = (0,) * len(shape)
    return pl.BlockSpec(shape, lambda *_: zeros)


def one_of(shape, micro):
    zeros = (0,) * len(shape)
    return pl.BlockSpec((1,) + shape, lambda *_: (micro,) + zeros)


def each_of(shape):
    zeros = (0,) * len(shape)
    return pl.BlockSpec((1,) + shape, lambda step: (step,) + zeros)


SCALAR = pl.BlockSpec(memory_space=pltpu.SMEM)
KEPT = pl.BlockSpec(memory_space=pl.ANY)


def timing(micros):
    return pl.CostEstimate(
        flops=int(micros * 4e8), bytes_accessed=int(micros * 3e6), transcendentals=0
    )


def params():
    return pltpu.CompilerParams(
        dimension_semantics=("arbitrary",), vmem_limit_bytes=VMEM_LIMIT
    )


def normalised(rows):
    center = rows - jnp.mean(rows, axis=-1, keepdims=True)
    spread = jnp.mean(center * center, axis=-1, keepdims=True)
    rate = lax.rsqrt(spread + LN_EPS)
    return center * rate, rate


def norm_back(grad, unit, rate):
    mean_grad = jnp.mean(grad, axis=-1, keepdims=True)
    mean_dot = jnp.mean(grad * unit, axis=-1, keepdims=True)
    return rate * (grad - mean_grad - unit * mean_dot)


def fold_rows(value):
    return jnp.sum(value.reshape(-1, 8, value.shape[-1]), axis=0)


def take_weight(target, index, mine, other, core, start):
    chips, shard = mine.shape[0], target.shape[2]
    for chip in range(chips):
        target[index, 2 * chip + core] = mine[chip, pl.ds(start, shard), :]
        target[index, 2 * chip + 1 - core] = other[chip, pl.ds(start, shard), :]


def weight_of(ref, index):
    return ref[index].reshape(ref.shape[1] * ref.shape[2], ref.shape[3])


def project_kernel(
    where_ref,
    tok_ref,
    mine_ref,
    other_ref,
    q_ref,
    q3_ref,
    kv_ref,
    near_ref,
    far_ref,
    top_ref,
    vec_ref,
    w_ref,
    norm_ref,
    low_ref,
    high_ref,
):
    piece, core = where_ref[0], where_ref[1]
    shard = w_ref.shape[2]

    @pl.when(pl.program_id(0) == 0)
    def _():
        for index in range(3):
            take_weight(w_ref, index, mine_ref, other_ref, core, shard * index)
        vec = jnp.zeros(vec_ref.shape, F32)
        for chip in range(mine_ref.shape[0]):
            for ref in (mine_ref, other_ref):
                vec = vec + ref[chip, pl.ds(3 * shard, VEC), :].astype(F32)
        vec_ref[...] = vec
        for part, scale_of in enumerate((lambda level: 0.5 ** STEP[level], lambda level: 1.0)):
            low_ref[part] = mean_table((240, 256), 0, range(1, 5), scale_of)
            high_ref[part] = mean_table((64, ROWS), 0, range(5, 8), scale_of)

    for chunk in range(ROWS // 256):
        rows = pl.ds(256 * chunk, 256)
        unit, _ = normalised(tok_ref[0, rows, :])
        norm_ref[rows, :] = (unit * vec_ref[0:1] + vec_ref[2:3]).astype(BF16)
    for half in range(2):
        rows = pl.ds(512 * half, 512)
        for index in range(3):
            value = dot_nn(norm_ref[rows, :], weight_of(w_ref, index)).astype(BF16)
            if index == 0:
                q_ref[0, rows, :] = value
            else:
                kv_ref[0, rows, pl.ds(512 * (index - 1), 512)] = value
    for chunk in range(ROWS // 256):
        rows = pl.ds(256 * chunk, 256)
        q3_ref[0, pl.ds(32 * chunk, 32), :] = dot_nn(
            low_ref[1, 192:224, :], q_ref[0, rows, :]
        ).astype(BF16)
        for part in range(2):
            lanes = pl.ds(512 * part, 512)
            cells = dot_nn(low_ref[part], kv_ref[0, rows, lanes]).astype(BF16)
            start = 0
            for level in range(1, 5):
                count = 256 >> level
                kv_ref[0, pl.ds(OFF[level] + count * chunk, count), lanes] = cells[
                    start : start + count
                ]
                start += count
    for part in range(2):
        lanes = pl.ds(512 * part, 512)
        kv_ref[0, pl.ds(OFF[5], 64), lanes] = dot_nn(
            high_ref[part], kv_ref[0, pl.ds(0, ROWS), lanes]
        ).astype(BF16)

    def edges(left_ref, right_ref):
        for level in range(LEVELS - 1):
            edge = pl.ds(HALO * level, HALO)
            left_ref[0, edge, :] = kv_ref[0, pl.ds(OFF[level], HALO), :]
            right_ref[0, edge, :] = kv_ref[0, pl.ds(OFF[level] + CELLS[level] - HALO, HALO), :]

    pl.when(piece % 2 == 0)(lambda: edges(far_ref, near_ref))
    pl.when(piece % 2 == 1)(lambda: edges(near_ref, far_ref))
    top_ref[0] = kv_ref[0, pl.ds(OFF[7], 16), :]


def cell_shapes(width):
    return [(ROWS, width), (ROWS // 8, width), (2 * ROWS, 2 * width)]


def edge_shapes(width):
    return [(EDGE, 2 * width), (EDGE, 2 * width), (16, 2 * width)]


def project(where, tokens, mine, other):
    micro, _, width = tokens.shape
    shape = jax.ShapeDtypeStruct
    shard = width // (2 * mine.shape[0])
    outs = cell_shapes(width) + edge_shapes(width)
    return pl.pallas_call(
        project_kernel,
        grid=(micro,),
        in_specs=[
            SCALAR,
            each_of((ROWS, width)),
            whole(mine.shape),
            whole(other.shape),
        ],
        out_specs=[each_of(out) for out in outs] + [whole((VEC, width))],
        out_shape=[shape((micro,) + out, BF16) for out in outs] + [shape((VEC, width), F32)],
        scratch_shapes=[
            pltpu.VMEM((3, width // shard, shard, width), BF16),
            pltpu.VMEM((ROWS, width), BF16),
            pltpu.VMEM((2, 240, 256), BF16),
            pltpu.VMEM((2, 64, ROWS), BF16),
        ],
        compiler_params=params(),
        cost_estimate=timing(13),
        name="project",
    )(where, tokens, mine, other)


def fine_windows(tile):
    return [
        (POFF[0] + 64 * tile, 96),
        (POFF[1] + 32 * tile, 64),
        (POFF[2] + 16 * tile, 16),
        (POFF[2] + 16 * tile + 32, 16),
    ]


def coarse_windows(tile):
    return [
        (POFF[3] + 64 * tile, 96),
        (POFF[4] + 32 * tile, 64),
        (POFF[5] + 16 * tile, 16),
        (POFF[5] + 16 * tile + 32, 16),
        (POFF[6], 16),
        (POFF[6] + 32, 16),
        (POFF[7], 32),
    ]


FINE_LEVELS = [96, 64, 32]
COARSE_LEVELS = [96, 64, 32, 32, 32]


def gather_rows(ref, windows, lanes):
    return jnp.concatenate([ref[at(start, size), lanes] for start, size in windows], axis=0)


def tile_bias(kid_ref, qid_ref, tile, tiles, windows, levels, bias):
    keys = jnp.concatenate([kid_ref[0, at(start, size), :] for start, size in windows], axis=0)
    keys = keys.astype(F32)
    keys = jnp.concatenate([keys, keys], axis=1)
    bias = jnp.concatenate([bias, bias], axis=1)
    out = []
    start = 0
    for index, count in enumerate(levels):
        part = slice(start, start + count)
        owner = qid_ref[0, pl.ds(tiles * index + tile, 1), :]
        out.append(jnp.where(keys[part] == owner, bias[part], NEG))
        start += count
    return jnp.concatenate(out, axis=0)


def lane_sums(value, steps):
    halves = []
    for half in range(2):
        part = value[:, 128 * half : 128 * (half + 1)]
        lane = lax.broadcasted_iota(jnp.int32, part.shape, 1)
        for step in range(steps):
            size = 1 << step
            first = (lane & size) == 0
            part = part + jnp.where(
                first, pltpu.roll(part, 128 - size, 1), pltpu.roll(part, size, 1)
            )
        halves.append(part)
    return jnp.concatenate(halves, axis=1)


def lane_roll(value, shift):
    if shift == 0:
        return value
    halves = [value[:, 128 * half : 128 * (half + 1)] for half in range(2)]
    return jnp.concatenate([pltpu.roll(part, shift % 128, 1) for part in halves], axis=1)


def far_row(tile, quad):
    return pl.ds(8 * (tile % 8) + 2 * (tile // 8) + quad, 1)


def level_sums(value, levels):
    out = [value[0 : levels[0]]]
    start = levels[0]
    for index, count in enumerate(levels[1:]):
        out.append(lane_sums(value[start : start + count], index + 1))
        start += count
    return jnp.concatenate(out, axis=0)


def head_stack(value, mask):
    return jnp.concatenate([value] * QUAD, axis=0) * mask


def head_pick(stacked):
    lane = lax.broadcasted_iota(jnp.int32, (TILE, QL), 1) // HEAD_DIM
    out = stacked[0:TILE]
    for head in range(1, QUAD):
        out = jnp.where(lane == head, stacked[TILE * head : TILE * (head + 1)], out)
    return out


def three_terms(row):
    high = row.astype(BF16)
    rest = row - high.astype(F32)
    middle = rest.astype(BF16)
    low = (rest - middle.astype(F32)).astype(BF16)
    return high, middle, low


def own_cell(tile):
    cell = lax.broadcasted_iota(jnp.int32, (16, QL), 0)
    token = lax.broadcasted_iota(jnp.int32, (16, QL), 1) % TILE
    return cell == 8 * (tile % 2) + token // 8


def lay_out(piece, kv_ref, near_ref, far_ref, across_ref, ends_ref, kvp_ref):
    def edges(left_ref, right_ref):
        for level in range(LEVELS - 1):
            base = POFF[level]
            edge = pl.ds(HALO * level, HALO)
            kvp_ref[pl.ds(base, HALO), :] = left_ref[0, edge, :]
            kvp_ref[pl.ds(base + HALO + CELLS[level], HALO), :] = right_ref[0, edge, :]

    pl.when(piece % 2 == 0)(lambda: edges(far_ref, near_ref))
    pl.when(piece % 2 == 1)(lambda: edges(near_ref, far_ref))
    for level in range(LEVELS - 1):
        count = CELLS[level]
        kvp_ref[pl.ds(POFF[level] + HALO, count), :] = kv_ref[0, pl.ds(OFF[level], count), :]
    across = across_ref[0].astype(F32)[0:PIECE7]
    ends = ends_ref[0].astype(F32)[0:PIECE7]
    tops = []
    for owner in range(4):
        top = jnp.where(owner == (piece + 2) % 4, across, jnp.where(owner == 3 - piece, ends, 0.0))
        tops.append(top)
    kvp_ref[pl.ds(POFF[7], 4 * PIECE7), :] = jnp.concatenate(tops, axis=0).astype(BF16)


def attend_kernel(
    where_ref,
    q_ref,
    q3_ref,
    kv_ref,
    near_ref,
    far_ref,
    across_ref,
    ends_ref,
    kid_ref,
    qidf_ref,
    qidc_ref,
    mixed_ref,
    lse_ref,
    lsec_ref,
    lsex_ref,
    oc_ref,
    kvp_ref,
    fine_ref,
    coarse_ref,
    mask_ref,
    spread_ref,
):
    @pl.when(pl.program_id(0) == 0)
    def _():
        attention_tables(fine_ref, coarse_ref, mask_ref, spread_ref, 0)

    lay_out(where_ref[0], kv_ref, near_ref, far_ref, across_ref, ends_ref, kvp_ref)
    mask = mask_ref[...]
    scaled = mask * jnp.asarray(0.125, BF16)

    units = [(tile, quad) for tile in range(COARSE_TILES) for quad in range(2)]
    biases = [
        tile_bias(kid_ref, qidc_ref, tile, 8, coarse_windows(tile), COARSE_LEVELS, coarse_ref[tile])
        for tile in range(COARSE_TILES)
    ]
    scores = []
    for tile, quad in units:
        lanes = pl.ds(QL * quad, QL)
        query = head_stack(q3_ref[0, pl.ds(TILE * tile, TILE), lanes], scaled)
        scores.append(dot_nt(gather_rows(kvp_ref, coarse_windows(tile), lanes), query))
    shares = []
    lines = []
    for index, (tile, quad) in enumerate(units):
        score = level_sums(scores[index], COARSE_LEVELS) + biases[index // 2]
        top = jnp.max(score, axis=0, keepdims=True)
        share = jnp.exp(score - top)
        total = jnp.sum(share, axis=0, keepdims=True)
        lse = top + jnp.log(total)
        lsec_ref[0, pl.ds(index, 1), :] = lse
        lines.append(lse)
        shares.append((share * (1.0 / total)).astype(BF16))
    results = []
    for (tile, quad), share in zip(units, shares):
        values = gather_rows(kvp_ref, coarse_windows(tile), pl.ds(512 + QL * quad, QL))
        results.append(dot_tn(share, values))
    lines = three_terms(jnp.concatenate(lines * 2, axis=0))
    lines = jnp.concatenate([line.astype(F32) for line in lines], axis=0)
    terms = [lane_roll(lines, -8 * part) for part in range(8)]
    terms = dot_nn(jnp.concatenate(terms, axis=0).astype(BF16), spread_ref[...])
    for part in range(8):
        rows = [terms[24 * part + 8 * index : 24 * part + 8 * index + 8] for index in range(3)]
        lsex_ref[0, pl.ds(8 * part, 8), :] = rows[0] + rows[1] + rows[2]
    for index, (tile, quad) in enumerate(units):
        oc_ref[0, pl.ds(TILE * tile, TILE), pl.ds(QL * quad, QL)] = head_pick(
            results[index]
        ).astype(BF16)

    def fine_group(group, carry):
        tiles = [GROUP * group + index for index in range(GROUP)]
        units = [(tile, quad) for tile in tiles for quad in range(2)]
        biases = [
            tile_bias(kid_ref, qidf_ref, tile, FINE_TILES, fine_windows(tile), FINE_LEVELS, fine_ref[...])
            for tile in tiles
        ]
        scores = []
        for tile, quad in units:
            lanes = pl.ds(QL * quad, QL)
            query = head_stack(q_ref[0, at(TILE * tile, TILE), lanes], scaled)
            scores.append(dot_nt(gather_rows(kvp_ref, fine_windows(tile), lanes), query))
        shares = []
        for index, (tile, quad) in enumerate(units):
            score = level_sums(scores[index], FINE_LEVELS) + biases[index // 2]
            far = lsex_ref[0, far_row(tile, quad), :]
            top = jnp.maximum(jnp.max(score, axis=0, keepdims=True), far)
            share = jnp.exp(score - top)
            far_share = jnp.exp(far - top)
            total = jnp.sum(share, axis=0, keepdims=True) + far_share
            lse_ref[0, pl.ds(2 * tile + quad, 1), :] = top + jnp.log(total)
            inverse = 1.0 / total
            shares.append(
                jnp.concatenate(
                    [share * inverse, jnp.where(own_cell(tile), far_share * inverse, 0.0)], axis=0
                ).astype(BF16)
            )
        results = []
        for (tile, quad), share in zip(units, shares):
            values = jnp.concatenate(
                [
                    gather_rows(kvp_ref, fine_windows(tile), pl.ds(512 + QL * quad, QL)),
                    oc_ref[0, at(16 * (tile // 2), 16), pl.ds(QL * quad, QL)],
                ],
                axis=0,
            )
            results.append(dot_tn(share, values))
        for (tile, quad), result in zip(units, results):
            mixed_ref[0, at(TILE * tile, TILE), pl.ds(QL * quad, QL)] = head_pick(result).astype(
                BF16
            )
        return carry

    lax.fori_loop(0, FINE_TILES // GROUP, fine_group, 0)


def stat_shapes(width):
    return [
        ((2 * FINE_TILES, QL), F32),
        ((2 * COARSE_TILES, QL), F32),
        ((64, QL), F32),
        ((ROWS // 8, width), BF16),
    ]


def id_specs(spec):
    return [
        spec((PADDED, 128)),
        spec((FINE * FINE_TILES, QL)),
        spec((8 * (LEVELS - FINE), QL)),
    ]


def attend(where, cells, received, ids):
    micro, _, width = cells[0].shape
    outs = [((ROWS, width), BF16)] + stat_shapes(width)
    ins = list(cells) + list(received)
    return pl.pallas_call(
        attend_kernel,
        grid=(micro,),
        in_specs=[SCALAR]
        + [each_of(value.shape[1:]) for value in ins]
        + id_specs(each_of),
        out_specs=[each_of(dims) for dims, _ in outs],
        out_shape=[jax.ShapeDtypeStruct((micro,) + dims, kind) for dims, kind in outs],
        scratch_shapes=[pltpu.VMEM((PADDED, 2 * width), BF16)] + table_shapes(),
        compiler_params=params(),
        cost_estimate=timing(23),
        name="attend",
    )(where, *ins, *ids)


def add_rows(ref, windows, lanes, value):
    start = 0
    for base, count in windows:
        rows = at(base, count)
        ref[rows, lanes] = ref[rows, lanes] + value[start : start + count]
        start += count


def attend_back_kernel(
    where_ref,
    q_ref,
    q3_ref,
    kv_ref,
    near_in_ref,
    far_in_ref,
    across_in_ref,
    ends_in_ref,
    lse_ref,
    lsec_ref,
    lsex_ref,
    oc_ref,
    dout_ref,
    kid_ref,
    qidf_ref,
    qidc_ref,
    dq_ref,
    dq3_ref,
    dkv_ref,
    near_ref,
    far_ref,
    across_ref,
    ends_ref,
    acc_ref,
    dcell_ref,
    delta_ref,
    kvp_ref,
    fine_ref,
    coarse_ref,
    mask_ref,
    spread_t_ref,
):
    @pl.when(pl.program_id(0) == 0)
    def _():
        attention_tables(fine_ref, coarse_ref, mask_ref, spread_t_ref, 1)

    lay_out(where_ref[0], kv_ref, near_in_ref, far_in_ref, across_in_ref, ends_in_ref, kvp_ref)
    delta_ref[...] = jnp.zeros(delta_ref.shape, F32)
    acc_ref[...] = jnp.zeros(acc_ref.shape, F32)
    dcell_ref[...] = jnp.zeros(dcell_ref.shape, F32)
    mask = mask_ref[...]
    scaled = mask * jnp.asarray(0.125, BF16)

    def fine_group(group, carry):
        tiles = [GROUP_BACK * group + index for index in range(GROUP_BACK)]
        units = [(tile, quad) for tile in tiles for quad in range(2)]
        biases = [
            tile_bias(kid_ref, qidf_ref, tile, FINE_TILES, fine_windows(tile), FINE_LEVELS, fine_ref[...])
            for tile in tiles
        ]
        at_unit = lambda unit: (at(TILE * unit[0], TILE), pl.ds(QL * unit[1], QL))
        queries = [head_stack(q_ref[(0,) + at_unit(unit)], scaled) for unit in units]
        douts = [head_stack(dout_ref[(0,) + at_unit(unit)], mask) for unit in units]
        scores = []
        steers = []
        for index, (tile, quad) in enumerate(units):
            keys = gather_rows(kvp_ref, fine_windows(tile), pl.ds(QL * quad, QL))
            scores.append(dot_nt(keys, queries[index]))
            values = jnp.concatenate(
                [
                    gather_rows(kvp_ref, fine_windows(tile), pl.ds(512 + QL * quad, QL)),
                    oc_ref[0, at(16 * (tile // 2), 16), pl.ds(QL * quad, QL)],
                ],
                axis=0,
            )
            steers.append(dot_nt(values, douts[index]))
        shares = []
        grads = []
        for index, (tile, quad) in enumerate(units):
            lse = lse_ref[0, pl.ds(2 * tile + quad, 1), :]
            far_share = jnp.exp(lsex_ref[0, far_row(tile, quad), :] - lse)
            share = jnp.exp(level_sums(scores[index], FINE_LEVELS) + biases[index // 2] - lse)
            share = jnp.concatenate([share, jnp.where(own_cell(tile), far_share, 0.0)], axis=0)
            weighted = share * steers[index]
            delta = jnp.sum(weighted, axis=0, keepdims=True)
            delta_ref[far_row(tile, quad), :] = far_share * delta
            grad = weighted[0:FINE_KEYS] - share[0:FINE_KEYS] * delta
            grads.append(level_sums(grad, FINE_LEVELS).astype(BF16))
            shares.append(share.astype(BF16))
        dvalues = [dot_nn(share, dout) for share, dout in zip(shares, douts)]
        dkeys = [dot_nn(grad, query) for grad, query in zip(grads, queries)]
        dqueries = []
        for (tile, quad), grad in zip(units, grads):
            keys = gather_rows(kvp_ref, fine_windows(tile), pl.ds(QL * quad, QL))
            dqueries.append(dot_tn(grad, keys))
        for index, (tile, quad) in enumerate(units):
            lanes = pl.ds(QL * quad, QL)
            cells = at(16 * (tile // 2), 16)
            windows = fine_windows(tile)
            add_rows(acc_ref, windows, pl.ds(512 + QL * quad, QL), dvalues[index])
            dcell_ref[cells, lanes] = dcell_ref[cells, lanes] + dvalues[index][FINE_KEYS:]
            add_rows(acc_ref, windows, lanes, dkeys[index])
            dq_ref[(0,) + at_unit((tile, quad))] = (head_pick(dqueries[index]) * 0.125).astype(BF16)
        return carry

    lax.fori_loop(0, FINE_TILES // GROUP_BACK, fine_group, 0)

    units = [(tile, quad) for tile in range(COARSE_TILES) for quad in range(2)]
    biases = [
        tile_bias(kid_ref, qidc_ref, tile, 8, coarse_windows(tile), COARSE_LEVELS, coarse_ref[tile])
        for tile in range(COARSE_TILES)
    ]
    at_unit = lambda unit: (pl.ds(TILE * unit[0], TILE), pl.ds(QL * unit[1], QL))
    queries = [head_stack(q3_ref[(0,) + at_unit(unit)], scaled) for unit in units]
    douts = [head_stack(dcell_ref[at_unit(unit)].astype(BF16), mask) for unit in units]
    terms = dot_nn(jnp.concatenate(three_terms(delta_ref[...]), axis=0), spread_t_ref[...])
    terms = terms[0:64] + terms[64:128] + terms[128:192]
    deltas = lane_roll(terms[0:8], 0)
    for part in range(1, 8):
        deltas = deltas + lane_roll(terms[8 * part : 8 * part + 8], 8 * part)
    steers = []
    scores = []
    for (tile, quad), dout, query in zip(units, douts, queries):
        values = gather_rows(kvp_ref, coarse_windows(tile), pl.ds(512 + QL * quad, QL))
        steers.append(dot_nt(values, dout))
        keys = gather_rows(kvp_ref, coarse_windows(tile), pl.ds(QL * quad, QL))
        scores.append(dot_nt(keys, query))
    shares = []
    grads = []
    for index, (tile, quad) in enumerate(units):
        score = level_sums(scores[index], COARSE_LEVELS) + biases[index // 2]
        share = jnp.exp(score - lsec_ref[0, pl.ds(index, 1), :])
        delta = deltas[index : index + 1]
        grads.append(level_sums(share * (steers[index] - delta), COARSE_LEVELS).astype(BF16))
        shares.append(share.astype(BF16))
    dvalues = [dot_nn(share, dout) for share, dout in zip(shares, douts)]
    dkeys = [dot_nn(grad, query) for grad, query in zip(grads, queries)]
    dqueries = []
    for (tile, quad), grad in zip(units, grads):
        keys = gather_rows(kvp_ref, coarse_windows(tile), pl.ds(QL * quad, QL))
        dqueries.append(dot_tn(grad, keys))
    for index, (tile, quad) in enumerate(units):
        windows = coarse_windows(tile)
        add_rows(acc_ref, windows, pl.ds(512 + QL * quad, QL), dvalues[index])
        add_rows(acc_ref, windows, pl.ds(QL * quad, QL), dkeys[index])
        dq3_ref[(0,) + at_unit((tile, quad))] = (head_pick(dqueries[index]) * 0.125).astype(BF16)

    key_lane = lax.broadcasted_iota(jnp.int32, (1, acc_ref.shape[1]), 1) < 512

    def scale(level):
        return jnp.where(key_lane, 0.5 ** STEP[level], 1.0)

    def low(level, start, count):
        return (acc_ref[pl.ds(start, count), :] * scale(level)).astype(BF16)

    def edges(left_ref, right_ref):
        for level in range(LEVELS - 1):
            base = POFF[level]
            edge = pl.ds(HALO * level, HALO)
            left_ref[0, edge, :] = low(level, base, HALO)
            right_ref[0, edge, :] = low(level, base + HALO + CELLS[level], HALO)

    piece = where_ref[0]
    pl.when(piece % 2 == 0)(lambda: edges(far_ref, near_ref))
    pl.when(piece % 2 == 1)(lambda: edges(near_ref, far_ref))
    for level in range(LEVELS - 1):
        dkv_ref[0, pl.ds(OFF[level], CELLS[level]), :] = low(level, POFF[level] + HALO, CELLS[level])
    dkv_ref[0, pl.ds(OFF[7], 16), :] = jnp.zeros((16, acc_ref.shape[1]), BF16)
    blank = jnp.zeros((PIECE7, acc_ref.shape[1]), F32)

    def high(index):
        rows = pl.ds(pl.multiple_of(POFF[7] + PIECE7 * index, PIECE7), PIECE7)
        return jnp.concatenate([acc_ref[rows, :] * scale(7), blank], axis=0).astype(BF16)

    ends_ref[0] = high(3 - piece)
    across_ref[0] = high((piece + 2) % 4)


def attend_back(where, cells, received, stats, dout, ids):
    micro, _, width = dout.shape
    shape = jax.ShapeDtypeStruct
    outs = cell_shapes(width) + edge_shapes(width) + edge_shapes(width)[2:]
    ins = list(cells) + list(received) + list(stats) + [dout]
    return pl.pallas_call(
        attend_back_kernel,
        grid=(micro,),
        in_specs=[SCALAR]
        + [each_of(value.shape[1:]) for value in ins]
        + id_specs(each_of),
        out_specs=[each_of(out) for out in outs],
        out_shape=[shape((micro,) + out, BF16) for out in outs],
        scratch_shapes=[
            pltpu.VMEM((PADDED, 2 * width), F32),
            pltpu.VMEM((ROWS // 8, width), F32),
            pltpu.VMEM((64, QL), F32),
            pltpu.VMEM((PADDED, 2 * width), BF16),
        ]
        + table_shapes(),
        compiler_params=params(),
        cost_estimate=timing(38),
        name="attend_back",
    )(where, *ins, *ids)


MID_ROWS = 512
FF_CHUNK = 512
ROOT = math.sqrt(2.0 / math.pi)


def give(send_ref, start, piece_of):
    for index in range(send_ref.shape[0]):
        piece = piece_of(index)
        send_ref[index, pl.ds(start, piece.shape[0]), :] = piece


def row_piece(ref, shard):
    def piece_of(index):
        return ref[pl.ds(pl.multiple_of(shard * index, shard), shard), :].astype(BF16)

    return piece_of


def middle_kernel(
    where_ref,
    tok_ref,
    cot_ref,
    mixed_ref,
    vec_ref,
    mine_ref,
    other_ref,
    out_ref,
    dmid_ref,
    dmix_ref,
    send_ref,
    wo_ref,
    wi_ref,
    wd_ref,
    acc_o,
    acc_i,
    acc_d,
    acc_b,
    acc_s,
    activ_ref,
    grad_ref,
):
    step = pl.program_id(0)
    core = where_ref[1]
    parts = wi_ref.shape[0]
    shard = wo_ref.shape[2]

    @pl.when(step == 0)
    def _():
        acc_o[...] = jnp.zeros(acc_o.shape, F32)
        acc_i[...] = jnp.zeros(acc_i.shape, F32)
        acc_d[...] = jnp.zeros(acc_d.shape, F32)
        acc_b[...] = jnp.zeros(acc_b.shape, F32)
        acc_s[...] = jnp.zeros(acc_s.shape, F32)
        take_weight(wo_ref, 0, mine_ref, other_ref, core, 0)
        for part in range(parts):
            take_weight(wi_ref, part, mine_ref, other_ref, core, shard * (1 + part))
        take_weight(wd_ref, 0, mine_ref, other_ref, core, shard * (1 + parts))

    wo = weight_of(wo_ref, 0)
    pieces = FF_CHUNK // wd_ref.shape[2]
    wi = [weight_of(wi_ref, part) for part in range(parts)]
    wd = [
        wd_ref[0, pieces * part : pieces * (part + 1)].reshape(FF_CHUNK, wo.shape[1])
        for part in range(parts)
    ]
    cot = cot_ref[...]
    top = cot.astype(BF16)
    mixed = mixed_ref[...]
    middle = tok_ref[...] + dot_nn(mixed, wo)
    unit, rate = normalised(middle)
    second = (unit * vec_ref[1:2] + vec_ref[3:4]).astype(BF16)
    result = middle + vec_ref[4:5]
    back = jnp.zeros(cot.shape, F32)
    pres = {}

    def first(part):
        pres[part] = (dot_nn(second, wi[part]) + vec_ref[5 + part : 6 + part], dot_nt(top, wd[part]))

    first(0)
    for part in range(parts):
        if part + 1 < parts:
            first(part + 1)
        pre, grad = pres.pop(part)
        square = pre * pre
        tanh = jnp.tanh(pre * (ROOT + (ROOT * 0.044715) * square))
        half = 0.5 + 0.5 * tanh
        activ = (pre * half).astype(BF16)
        slope = half + (pre * (0.5 - 0.5 * (tanh * tanh))) * (
            ROOT + (ROOT * 3 * 0.044715) * square
        )
        grad = (grad * slope).astype(BF16)
        cols = pl.ds(FF_CHUNK * part, FF_CHUNK)
        activ_ref[:, cols] = activ
        grad_ref[:, cols] = grad
        acc_b[:, cols] = acc_b[:, cols] + fold_rows(grad.astype(F32))
        result = result + dot_nn(activ, wd[part])
        back = back + dot_nt(grad, wi[part])
    out_ref[...] = result
    acc_d[...] = acc_d[...] + dot_tn(activ_ref[...], top)
    for part in range(parts):
        acc_i[part] = acc_i[part] + dot_tn(second, grad_ref[:, pl.ds(FF_CHUNK * part, FF_CHUNK)])
    dmid = cot + norm_back(back * vec_ref[1:2], unit, rate)
    dmid_ref[...] = dmid
    branch = dmid.astype(BF16)
    dmix_ref[...] = dot_nt(branch, wo).astype(BF16)
    acc_o[...] = acc_o[...] + dot_tn(mixed, branch)
    acc_s[0:8, :] = acc_s[0:8, :] + fold_rows(top.astype(F32))
    acc_s[8:16, :] = acc_s[8:16, :] + fold_rows(back * unit)
    acc_s[16:24, :] = acc_s[16:24, :] + fold_rows(back)

    @pl.when(step == pl.num_programs(0) - 1)
    def _():
        give(send_ref, 0, row_piece(acc_o, shard))
        for part in range(parts):
            give(send_ref, shard * (1 + part), row_piece(acc_i.at[part], shard))
        give(send_ref, shard * (1 + parts), row_piece(acc_d, shard * parts))
        total = lambda value: jnp.sum(value, axis=0, keepdims=True)
        lines = [total(acc_s[8 * index : 8 * index + 8, :]) for index in range(3)]
        for part in range(parts):
            lines.append(total(acc_b[:, pl.ds(FF_CHUNK * part, FF_CHUNK)]))
        lines.append(jnp.zeros((16 - len(lines), lines[0].shape[1]), F32))
        lines = jnp.concatenate(lines, axis=0).astype(BF16)
        give(send_ref, shard * (1 + 2 * parts), lambda index: lines)


def middle_part(where, tokens, cot, mixed, vec, mine, other):
    rows, width = tokens.shape
    chips, lines, _ = mine.shape
    shard = width // (2 * chips)
    parts = (lines // shard - 1) // 2
    hidden = parts * FF_CHUNK
    shape = jax.ShapeDtypeStruct
    tiled = pl.BlockSpec((MID_ROWS, width), lambda r: (r, 0))
    shared = shape((2 * chips, lines + 16, width), BF16)
    single = lambda dims: pl.BlockSpec(
        dims, lambda *_: (0,) * len(dims), pipeline_mode=pl.Buffered(1)
    )
    return pl.pallas_call(
        middle_kernel,
        grid=(rows // MID_ROWS,),
        in_specs=[SCALAR, tiled, tiled, tiled, whole(vec.shape), single(mine.shape), single(mine.shape)],
        out_specs=[tiled, tiled, tiled, single(shared.shape)],
        out_shape=[
            shape((rows, width), F32),
            shape((rows, width), F32),
            shape((rows, width), BF16),
            shared,
        ],
        scratch_shapes=[
            pltpu.VMEM((1, 2 * chips, shard, width), BF16),
            pltpu.VMEM((parts, 2 * chips, shard, FF_CHUNK), BF16),
            pltpu.VMEM((1, 2 * chips, shard * parts, width), BF16),
            pltpu.VMEM((width, width), F32),
            pltpu.VMEM((parts, width, FF_CHUNK), F32),
            pltpu.VMEM((hidden, width), F32),
            pltpu.VMEM((8, hidden), F32),
            pltpu.VMEM((24, width), F32),
            pltpu.VMEM((MID_ROWS, hidden), BF16),
            pltpu.VMEM((MID_ROWS, hidden), BF16),
        ],
        compiler_params=params(),
        cost_estimate=timing(40),
        name="middle",
    )(where, tokens, cot, mixed, vec, mine, other)


def collect_kernel(
    where_ref,
    tok_ref,
    dq_ref,
    dq3_ref,
    dkv_ref,
    near_ref,
    far_ref,
    across_ref,
    ends_ref,
    vec_ref,
    mine_ref,
    other_ref,
    dp_ref,
    send_ref,
    cells_ref,
    norm_ref,
    gw_ref,
    sum_ref,
    w_ref,
    low_ref,
    high_ref,
):
    @pl.when(pl.program_id(0) == 0)
    def _():
        gw_ref[...] = jnp.zeros(gw_ref.shape, F32)
        sum_ref[...] = jnp.zeros(sum_ref.shape, F32)
        low_ref[...] = mean_table((256, 240), 1, range(1, 5), lambda level: 1.0)
        high_ref[...] = mean_table((ROWS, 64), 1, range(5, 8), lambda level: 1.0)

    piece, core = where_ref[0], where_ref[1]
    cells_ref[...] = dkv_ref[0]

    def add(start, value):
        rows = pl.ds(start, HALO)
        cells_ref[rows, :] = (cells_ref[rows, :].astype(F32) + value.astype(F32)).astype(BF16)

    def edges(left_ref, right_ref):
        for level in range(LEVELS - 1):
            edge = pl.ds(HALO * level, HALO)

            @pl.when(piece > 0)
            def _():
                add(OFF[level], left_ref[0, edge, :])

            @pl.when(piece < 3)
            def _():
                add(OFF[level] + CELLS[level] - HALO, right_ref[0, edge, :])

    pl.when(piece % 2 == 0)(lambda: edges(far_ref, near_ref))
    pl.when(piece % 2 == 1)(lambda: edges(near_ref, far_ref))
    add(OFF[7], across_ref[0].astype(F32) + ends_ref[0].astype(F32))

    def expand(chunk, sums):
        rows = at(256 * chunk, 256)
        norm_ref[rows, :] = normalised(tok_ref[0, rows, :])[0].astype(BF16)
        cells = jnp.concatenate(
            [
                cells_ref[at(OFF[level] + (256 >> level) * chunk, 256 >> level), :]
                for level in range(1, 5)
            ],
            axis=0,
        )
        dkv = (
            cells_ref[rows, :].astype(F32)
            + dot_nn(low_ref[...], cells)
            + dot_nn(high_ref[rows, :], cells_ref[pl.ds(OFF[5], 64), :])
        ).astype(BF16)
        dq = (
            dq_ref[0, rows, :].astype(F32)
            + dot_nn(low_ref[:, 192:224], dq3_ref[0, at(32 * chunk, 32), :])
        ).astype(BF16)
        dp_ref[0, rows, pl.ds(0, 512)] = dq
        dp_ref[0, rows, pl.ds(512, 1024)] = dkv
        return [old + fold_rows(new.astype(F32)) for old, new in zip(sums, (dq, dkv))]

    sums = [jnp.zeros((8, 512), F32), jnp.zeros((8, 1024), F32)]
    sums = lax.fori_loop(0, ROWS // 256, expand, sums)
    sum_ref[...] = sum_ref[...] + jnp.concatenate(sums, axis=1)
    for index in range(3):
        grad = dot_tn(norm_ref[...], dp_ref[0, :, pl.ds(512 * index, 512)])
        gw_ref[index] = gw_ref[index] + grad

    @pl.when(pl.program_id(0) == pl.num_programs(0) - 1)
    def _():
        shard = w_ref.shape[2]
        row = lax.broadcasted_iota(jnp.int32, (VEC, 512), 0)
        lines = vec_ref[...].astype(BF16)
        gain = dot_tn(lines, jnp.where(row == 0, 1.0, 0.0).astype(BF16))
        offset = dot_tn(lines, jnp.where(row == 2, 1.0, 0.0).astype(BF16))
        ones = jnp.ones((8, 512), BF16)
        grad_gain = jnp.zeros((8, 512), F32)
        grad_offset = jnp.zeros((8, 512), F32)
        for index in range(3):
            take_weight(w_ref, index, mine_ref, other_ref, core, shard * index)
            grad = gw_ref[index]
            total = jnp.sum(sum_ref[:, pl.ds(512 * index, 512)], axis=0, keepdims=True)
            gw_ref[index] = gain * grad + offset * total
            weight = weight_of(w_ref, index)
            high, middle, _ = three_terms(weight.astype(F32) * grad)
            grad_gain = grad_gain + dot_nt(ones, high) + dot_nt(ones, middle)
            high, middle, low = three_terms(total)
            terms = jnp.concatenate([high, middle, low] + [jnp.zeros_like(low)] * 5, axis=0)
            grad_offset = grad_offset + dot_nt(terms, weight)
            give(send_ref, shard * index, row_piece(gw_ref.at[index], shard))
        grad_offset = jnp.sum(grad_offset, axis=0, keepdims=True)
        blank = jnp.zeros((VEC - 2, 512), F32)
        lines = jnp.concatenate([grad_gain[0:1], grad_offset, blank], axis=0).astype(BF16)
        give(send_ref, 3 * shard, lambda index: lines)


def collect(where, tokens, grads, received, vec, mine, other):
    micro, _, width = tokens.shape
    chips, lines, _ = mine.shape
    shard = width // (2 * chips)
    shape = jax.ShapeDtypeStruct
    moved = [tokens] + list(grads) + list(received)
    ins = [vec, mine, other]
    return pl.pallas_call(
        collect_kernel,
        grid=(micro,),
        in_specs=[SCALAR]
        + [each_of(value.shape[1:]) for value in moved]
        + [whole(value.shape) for value in ins],
        out_specs=[each_of((ROWS, 3 * width)), whole((2 * chips, lines, width))],
        out_shape=[
            shape((micro, ROWS, 3 * width), BF16),
            shape((2 * chips, lines, width), BF16),
        ],
        scratch_shapes=[
            pltpu.VMEM((2 * ROWS, 2 * width), BF16),
            pltpu.VMEM((ROWS, width), BF16),
            pltpu.VMEM((3, width, width), F32),
            pltpu.VMEM((8, 3 * width), F32),
            pltpu.VMEM((3, 2 * chips, shard, width), BF16),
            pltpu.VMEM((256, 240), BF16),
            pltpu.VMEM((ROWS, 64), BF16),
        ],
        compiler_params=params(),
        cost_estimate=timing(17),
        name="collect",
    )(where, *moved, *ins)


FIN_ROWS = 256


def finish_kernel(
    where_ref, tok_ref, dmid_ref, dp_ref, vec_ref, mine_ref, other_ref, grad_ref, w_ref
):
    core = where_ref[1]

    @pl.when(pl.program_id(0) == 0)
    def _():
        for index in range(3):
            take_weight(w_ref, index, mine_ref, other_ref, core, w_ref.shape[2] * index)

    back = dot_nt(dp_ref[:, pl.ds(0, 512)], weight_of(w_ref, 0))
    for index in range(1, 3):
        back = back + dot_nt(dp_ref[:, pl.ds(512 * index, 512)], weight_of(w_ref, index))
    unit, rate = normalised(tok_ref[...])
    grad_ref[...] = dmid_ref[...] + norm_back(back * vec_ref[0:1], unit, rate)


def finish(where, tokens, dmid, dproj, vec, mine, other):
    rows, width = tokens.shape
    dp = 2 * mine.shape[0]
    chunk = lambda lanes: pl.BlockSpec((FIN_ROWS, lanes), lambda r: (r, 0))
    return pl.pallas_call(
        finish_kernel,
        grid=(rows // FIN_ROWS,),
        in_specs=[
            SCALAR,
            chunk(width),
            chunk(width),
            chunk(3 * width),
            whole(vec.shape),
            whole(mine.shape),
            whole(other.shape),
        ],
        out_specs=chunk(width),
        out_shape=jax.ShapeDtypeStruct(tokens.shape, F32),
        scratch_shapes=[pltpu.VMEM((3, dp, width // dp, width), BF16)],
        compiler_params=params(),
        cost_estimate=timing(13),
        name="finish",
    )(where, tokens, dmid, dproj, vec, mine, other)


def twice(chunk):
    lane = lax.broadcasted_iota(jnp.int32, chunk.shape, 1)
    other = pltpu.roll(chunk, 64, 1)
    halves = jnp.where(lane < 64, chunk, other), jnp.where(lane < 64, other, chunk)
    return [jnp.concatenate([half, half], axis=1)[0:1] for half in halves]


def lane_pairs(value, size, merge):
    halves = []
    for half in range(2):
        part = value[:, 128 * half : 128 * (half + 1)]
        lane = lax.broadcasted_iota(jnp.int32, part.shape, 1)
        first = (lane & size) == 0
        pair = jnp.where(first, pltpu.roll(part, 128 - size, 1), pltpu.roll(part, size, 1))
        halves.append(merge(part, pair))
    return jnp.concatenate(halves, axis=1)


def documents_kernel(where_ref, seg_ref, own_ref, kid_ref, qidf_ref, qidc_ref, row_ref):
    piece = where_ref[0]
    length = seg_ref.shape[2]
    margin = (row_ref.shape[0] - length) // 2
    ones = jnp.ones((16, 128), BF16)

    def only_first(row):
        index = lax.broadcasted_iota(jnp.int32, (16, row.shape[1]), 0)
        return jnp.where(index == 0, row.astype(F32), 0.0).astype(BF16)

    outside = jnp.full((margin, 128), -3.0, F32)
    row_ref[pl.ds(0, margin), :] = outside
    row_ref[pl.ds(margin + length, margin), :] = outside
    row_ref[pl.ds(margin, length), :] = dot_tn(only_first(seg_ref[0]), ones)
    for level in range(LEVELS):
        cell = 1 << level
        if level < LEVELS - 1:
            start = ROWS * piece + margin - HALO * cell
            count = CELLS[level] + 2 * HALO
        else:
            start = margin
            count = 4 * PIECE7
        if level == 0:
            key = row_ref[at(start, count), :]
        else:
            lowest = row_ref[pl.ds(start, count, stride=cell), :]
            highest = row_ref[pl.ds(start + cell - 1, count, stride=cell), :]
            key = jnp.where(lowest == highest, lowest, -2.0)
        if level == LEVELS - 1:
            owner = lax.broadcasted_iota(jnp.int32, key.shape, 0) // PIECE7
            counted = (jnp.abs(owner // 2 - piece // 2) == 1) & (jnp.abs(owner - piece) >= 2)
            key = jnp.where(counted, key, -3.0)
        kid_ref[0, pl.ds(POFF[level], count), :] = key.astype(BF16)

    own = own_ref[0].astype(F32)
    rows = []
    for chunk in range(ROWS // 128):
        rows += twice(jnp.broadcast_to(own[:, 128 * chunk : 128 * (chunk + 1)], (8, 128)))
    low = high = jnp.concatenate(rows, axis=0)
    for level in range(FINE):
        if level > 0:
            low = lane_pairs(low, 1 << (level - 1), jnp.minimum)
            high = lane_pairs(high, 1 << (level - 1), jnp.maximum)
        qidf_ref[0, pl.ds(FINE_TILES * level, FINE_TILES), :] = jnp.where(low == high, low, -1.0)

    token = lax.broadcasted_iota(jnp.int32, (ROWS, ROWS // 8), 0)
    cells = lax.broadcasted_iota(jnp.int32, (ROWS, ROWS // 8), 1)
    ends = []
    for step in (0, 7):
        pick = jnp.where(token == 8 * cells + step, 1.0, 0.0).astype(BF16)
        value = dot_nn(only_first(own), pick)[0:1]
        rows = twice(jnp.broadcast_to(value, (8, 128)))
        ends.append(jnp.concatenate(rows + [rows[1]] * 6, axis=0))
    low, high = ends
    for index in range(LEVELS - FINE):
        if index > 0:
            low = lane_pairs(low, 1 << (index - 1), jnp.minimum)
            high = lane_pairs(high, 1 << (index - 1), jnp.maximum)
        qidc_ref[0, pl.ds(8 * index, 8), :] = jnp.where(low == high, low, -1.0)


def cell_documents(where, segments, piece):
    micro, _, length = segments.shape
    shape = jax.ShapeDtypeStruct
    own = lax.dynamic_slice_in_dim(segments, piece * ROWS, ROWS, axis=2)
    outs = [((PADDED, 128), BF16), ((FINE * FINE_TILES, QL), F32), ((8 * (LEVELS - FINE), QL), F32)]
    key, fine, coarse = pl.pallas_call(
        documents_kernel,
        grid=(micro,),
        in_specs=[SCALAR, each_of((1, length)), each_of((1, ROWS))],
        out_specs=[each_of(dims) for dims, _ in outs],
        out_shape=[shape((micro,) + dims, kind) for dims, kind in outs],
        scratch_shapes=[pltpu.VMEM((length + 2 * ROWS, 128), F32)],
        compiler_params=params(),
        cost_estimate=timing(5),
        name="documents",
    )(where, segments, own)
    return key, fine, coarse


def same_core(chips):
    return [[2 * chip + core for chip in range(chips)] for core in range(2)]


def core_swap(value, chips):
    pairs = [(place, place ^ 1) for place in range(2 * chips)]
    return lax.ppermute(value, "dp", pairs)


def chip_exchange(value, chips):
    return lax.all_to_all(value, "dp", 0, 0, axis_index_groups=same_core(chips), tiled=True)


def after(value, *done):
    return lax.optimization_barrier((value,) + done)[0]


def add(left, right):
    return left.astype(F32) + right.astype(F32)


def body(
    tokens,
    segment_ids,
    norm_gains,
    norm_biases,
    qkv_weight,
    out_weight,
    in_weight,
    in_bias,
    down_weight,
    down_bias,
    cotangent,
):
    micro, _, row_count, width = tokens.shape
    pieces = lax.axis_size("sp")
    piece = lax.axis_index("sp")
    assert row_count == ROWS and pieces == 4 and micro == 2
    tokens = tokens[:, 0]
    cotangent = cotangent[:, 0]
    dp = lax.axis_size("dp")
    place = lax.axis_index("dp")
    chips = dp // 2
    shard = width // dp
    hidden = in_weight.shape[1]
    parts = hidden // FF_CHUNK
    where = jnp.stack([piece, place % 2]).astype(jnp.int32)
    swap = lambda value, bits: lax.ppermute(value, "sp", [(p, p ^ bits) for p in range(pieces)])
    spread = lambda value: chip_exchange(
        jnp.broadcast_to(value[None], (chips,) + value.shape), chips
    )

    def placed(value, start):
        lines = jnp.zeros((value.shape[0], start * value.shape[1]), BF16)
        return lax.dynamic_update_slice(lines, value, (0, place * value.shape[1])).reshape(-1, width)

    small = placed(jnp.concatenate([norm_gains, norm_biases, down_bias[None]]), dp)
    small = jnp.concatenate([small, placed(in_bias[None], dp)])
    small = jnp.pad(small, ((0, VEC - small.shape[0]), (0, 0)))
    mine = spread(jnp.concatenate([qkv_weight.reshape(3 * shard, width), small]))
    ids = cell_documents(where, segment_ids, piece)
    where, mine = lax.optimization_barrier((after(where, ids[2]), mine))
    other = core_swap(mine, chips)
    rest = jnp.concatenate(
        [
            out_weight,
            in_weight.reshape(shard, parts, FF_CHUNK).swapaxes(0, 1).reshape(-1, width),
            down_weight,
        ]
    )
    rest_mine = spread(after(rest, other))

    def halo(near, far, across, ends):
        middle = lax.ppermute(far, "sp", [(1, 2), (2, 1)])
        return swap(near, 1), middle, swap(across, 2), lax.ppermute(ends, "sp", [(0, 3), (3, 0)])

    q, q3, kv, near, far, top, vec = project(where, tokens, mine, other)
    cells = (q, q3, kv)
    received = halo(near, far, top, top)
    rest_mine = after(rest_mine, *received)
    rest_other = core_swap(rest_mine, chips)
    mixed, *stats = attend(after(where, rest_mine), cells, received, ids)
    rest_other = after(rest_other, mixed)

    flat = lambda value: value.reshape(micro * ROWS, width)
    split = lambda value: value.reshape(micro, ROWS, width)
    outputs, dmid, dmix, send = middle_part(
        where, flat(tokens), flat(cotangent), flat(mixed), vec, rest_mine, rest_other
    )
    come = lax.all_to_all(send, "dp", 0, 0, tiled=True)
    dq, dq3, dkv, *edges = attend_back(where, cells, received, stats, split(dmix), ids)
    grads = (dq, dq3, dkv)
    back = halo(*edges)
    odd = piece % 2 == 1
    total = jnp.sum(after(come, *back).astype(F32), axis=0).astype(BF16)
    come = swap(total, 1)
    dproj, send = collect(
        after(where, total), tokens, grads, back, vec, mine, other
    )
    total = add(total, after(come, send)).astype(BF16)
    half = jnp.where(odd, total[:, width // 2 :], total[:, : width // 2])
    come = swap(half, 2)
    qkv_come = lax.all_to_all(after(send, half), "dp", 0, 0, tiled=True)
    input_grad = finish(
        after(where, half), flat(tokens), dmid, dproj.reshape(micro * ROWS, -1), vec, mine, other
    )
    half = add(half, after(come, input_grad)).astype(BF16)
    come = swap(half, 1)
    total = jnp.sum(after(qkv_come, half).astype(F32), axis=0).astype(BF16)
    qkv_come = swap(total, 1)
    come = after(come, total)
    rest = jnp.where(
        odd, jnp.concatenate([come, half], axis=1), jnp.concatenate([half, come], axis=1)
    ).astype(F32)
    total = add(total, qkv_come).astype(BF16)
    total = add(total, swap(total, 2))

    own = lambda value, size: lax.dynamic_slice_in_dim(value, place * size, size, axis=-1)
    small_two = rest[shard * (1 + 2 * parts) :]
    small_one = total[3 * shard :]
    gin = rest[shard : shard * (1 + parts)].reshape(parts, shard, FF_CHUNK).swapaxes(0, 1)
    return (
        outputs.reshape(micro, 1, ROWS, width),
        input_grad.reshape(micro, 1, ROWS, width),
        own(jnp.stack([small_one[0], small_two[1]]), shard),
        own(jnp.stack([small_one[1], small_two[2]]), shard),
        total[: 3 * shard].reshape(3, shard, width),
        rest[:shard],
        gin.reshape(shard, hidden),
        own(small_two[3 : 3 + parts].reshape(hidden), hidden // dp),
        rest[shard * (1 + parts) : shard * (1 + 2 * parts)],
        own(small_two[0], shard),
    )


def solution(mesh):
    in_specs = (
        P(None, "dp", "sp", None),
        P(None, "dp", None),
        P(None, "dp"),
        P(None, "dp"),
        P(None, "dp", None),
        P("dp", None),
        P("dp", None),
        P("dp"),
        P("dp", None),
        P("dp"),
        P(None, "dp", "sp", None),
    )
    out_specs = (
        P(None, "dp", "sp", None),
        P(None, "dp", "sp", None),
        P(None, "dp"),
        P(None, "dp"),
        P(None, "dp", None),
        P("dp", None),
        P("dp", None),
        P("dp"),
        P("dp", None),
        P("dp"),
    )
    return jax.shard_map(body, mesh=mesh, in_specs=in_specs, out_specs=out_specs, check_vma=False)
```

```python
import math

import jax
import jax.numpy as jnp
from jax import lax
from jax.experimental import pallas as pl
from jax.experimental.pallas import tpu as pltpu
from jax.sharding import PartitionSpec as P

HEADS = 8
HEAD_DIM = 64
BLOCK = 16
LEVELS = 8
HALO = 16
TILE = 64
QUAD = 4
QL = QUAD * HEAD_DIM
NEG = -1e30
FINE = 3
ROWS = 1024
EDGE = 112
VEC = 16
GROUP = 4
GROUP_BACK = 2
F32 = jnp.float32
BF16 = jnp.bfloat16

CELLS = [ROWS >> level for level in range(LEVELS)]
OFF = [2 * ROWS - (2 * ROWS >> level) for level in range(LEVELS)]
POFF = []
_at = 0
for _level in range(LEVELS - 1):
    POFF.append(_at)
    _at += CELLS[_level] + 2 * HALO
POFF.append(_at)
PIECE7 = CELLS[LEVELS - 1]
PADDED = _at + 4 * PIECE7
FINE_TILES = ROWS // TILE
COARSE_TILES = ROWS // 8 // TILE
FINE_KEYS = 192
COARSE_KEYS = 256
LN_EPS = 1e-05
VMEM_LIMIT = 62 * 1024 * 1024


STEP = [0, 1, 2, 0, 1, 2, 3, 4]


def places(shape):
    return [lax.broadcasted_iota(jnp.int32, shape, axis) for axis in range(2)]


def counted_pairs(level, query, key):
    near = jnp.abs((query >> 4) - (key >> 4))
    if level == 0:
        return near <= 1
    return (near == 1) & (jnp.abs((query >> 3) - (key >> 3)) >= 2)


def score_offsets(parts):
    out = []
    for level, count, window, query_of in parts:
        key, lane = places((count, 2 * TILE))
        query = query_of(lane & (TILE - 1))
        if window == "all":
            allowed = jnp.full(key.shape, True)
        else:
            split = window == "sides"
            key = jnp.where(key < 16, key - 16, key) if split else key - 16
            allowed = counted_pairs(level, query, key)
        out.append(jnp.where(allowed, level * math.log(2.0), NEG))
    return jnp.concatenate(out, axis=0)


def fine_offsets():
    return score_offsets(
        [
            (0, 96, "span", lambda token: token),
            (1, 64, "span", lambda token: token >> 1),
            (2, 32, "sides", lambda token: token >> 2),
        ]
    )


def coarse_offsets(tile):
    return score_offsets(
        [
            (3, 96, "span", lambda cell: cell),
            (4, 64, "span", lambda cell: cell >> 1),
            (5, 32, "sides", lambda cell: cell >> 2),
            (6, 32, "sides", lambda cell: 8 * tile + (cell >> 3)),
            (7, 4 * PIECE7, "all", lambda cell: cell),
        ]
    )


def mean_table(shape, cell_axis, levels, scale_of):
    index = places(shape)
    cell, token = index[cell_axis], index[1 - cell_axis]
    out = jnp.zeros(shape, F32)
    start = 0
    for level in levels:
        weight = scale_of(level) / (1 << level)
        out = out + jnp.where((token >> level) + start == cell, weight, 0.0)
        start += shape[1 - cell_axis] >> level
    return out.astype(BF16)


def head_table():
    row, col = places((QL, QL))
    return jnp.where((row >> 6) == (col >> 6), 1.0, 0.0).astype(BF16)


def spread_table(cell_axis):
    index = places((QL, QL))
    cell, token = index[cell_axis], index[1 - cell_axis]
    same = ((cell >> 6) == (token >> 6)) & ((cell & 63) == ((token & 63) >> 3))
    return jnp.where(same, 1.0, 0.0).astype(BF16)


def attention_tables(fine_ref, coarse_ref, mask_ref, spread_ref, cell_axis):
    fine_ref[...] = fine_offsets()
    for tile in range(COARSE_TILES):
        coarse_ref[tile] = coarse_offsets(tile)
    mask_ref[...] = head_table()
    spread_ref[...] = spread_table(cell_axis)


def table_shapes():
    return [
        pltpu.VMEM((FINE_KEYS, QL // 2), F32),
        pltpu.VMEM((COARSE_TILES, COARSE_KEYS, QL // 2), F32),
        pltpu.VMEM((QL, QL), BF16),
        pltpu.VMEM((QL, QL), BF16),
    ]


def dot_nn(left, right):
    return jnp.dot(left, right, preferred_element_type=F32)


def dot_nt(left, right):
    return lax.dot_general(left, right, (((1,), (1,)), ((), ())), preferred_element_type=F32)


def dot_tn(left, right):
    return lax.dot_general(left, right, (((0,), (0,)), ((), ())), preferred_element_type=F32)


def at(start, size):
    return pl.ds(pl.multiple_of(start, 16), size)


def whole(shape):
    zeros = (0,) * len(shape)
    return pl.BlockSpec(shape, lambda *_: zeros)


def one_of(shape, micro):
    zeros = (0,) * len(shape)
    return pl.BlockSpec((1,) + shape, lambda *_: (micro,) + zeros)


def each_of(shape):
    zeros = (0,) * len(shape)
    return pl.BlockSpec((1,) + shape, lambda step: (step,) + zeros)


SCALAR = pl.BlockSpec(memory_space=pltpu.SMEM)
KEPT = pl.BlockSpec(memory_space=pl.ANY)


def timing(micros):
    return pl.CostEstimate(
        flops=int(micros * 4e8), bytes_accessed=int(micros * 3e6), transcendentals=0
    )


def params():
    return pltpu.CompilerParams(
        dimension_semantics=("arbitrary",), vmem_limit_bytes=VMEM_LIMIT
    )


def normalised(rows):
    center = rows - jnp.mean(rows, axis=-1, keepdims=True)
    spread = jnp.mean(center * center, axis=-1, keepdims=True)
    rate = lax.rsqrt(spread + LN_EPS)
    return center * rate, rate


def norm_back(grad, unit, rate):
    mean_grad = jnp.mean(grad, axis=-1, keepdims=True)
    mean_dot = jnp.mean(grad * unit, axis=-1, keepdims=True)
    return rate * (grad - mean_grad - unit * mean_dot)


def fold_rows(value):
    return jnp.sum(value.reshape(-1, 8, value.shape[-1]), axis=0)


def take_weight(target, index, mine, other, core, start):
    chips, shard = mine.shape[0], target.shape[2]
    for chip in range(chips):
        target[index, 2 * chip + core] = mine[chip, pl.ds(start, shard), :]
        target[index, 2 * chip + 1 - core] = other[chip, pl.ds(start, shard), :]


def weight_of(ref, index):
    return ref[index].reshape(ref.shape[1] * ref.shape[2], ref.shape[3])


def project_kernel(
    where_ref,
    tok_ref,
    mine_ref,
    other_ref,
    q_ref,
    q3_ref,
    kv_ref,
    near_ref,
    far_ref,
    top_ref,
    vec_ref,
    w_ref,
    norm_ref,
    low_ref,
    high_ref,
):
    piece, core = where_ref[0], where_ref[1]
    shard = w_ref.shape[2]

    @pl.when(pl.program_id(0) == 0)
    def _():
        for index in range(3):
            take_weight(w_ref, index, mine_ref, other_ref, core, shard * index)
        vec = jnp.zeros(vec_ref.shape, F32)
        for chip in range(mine_ref.shape[0]):
            for ref in (mine_ref, other_ref):
                vec = vec + ref[chip, pl.ds(3 * shard, VEC), :].astype(F32)
        vec_ref[...] = vec
        for part, scale_of in enumerate((lambda level: 0.5 ** STEP[level], lambda level: 1.0)):
            low_ref[part] = mean_table((240, 256), 0, range(1, 5), scale_of)
            high_ref[part] = mean_table((64, ROWS), 0, range(5, 8), scale_of)

    for chunk in range(ROWS // 256):
        rows = pl.ds(256 * chunk, 256)
        unit, _ = normalised(tok_ref[0, rows, :])
        norm_ref[rows, :] = (unit * vec_ref[0:1] + vec_ref[2:3]).astype(BF16)
    for half in range(2):
        rows = pl.ds(512 * half, 512)
        for index in range(3):
            value = dot_nn(norm_ref[rows, :], weight_of(w_ref, index)).astype(BF16)
            if index == 0:
                q_ref[0, rows, :] = value
            else:
                kv_ref[0, rows, pl.ds(512 * (index - 1), 512)] = value
    for chunk in range(ROWS // 256):
        rows = pl.ds(256 * chunk, 256)
        q3_ref[0, pl.ds(32 * chunk, 32), :] = dot_nn(
            low_ref[1, 192:224, :], q_ref[0, rows, :]
        ).astype(BF16)
        for part in range(2):
            lanes = pl.ds(512 * part, 512)
            cells = dot_nn(low_ref[part], kv_ref[0, rows, lanes]).astype(BF16)
            start = 0
            for level in range(1, 5):
                count = 256 >> level
                kv_ref[0, pl.ds(OFF[level] + count * chunk, count), lanes] = cells[
                    start : start + count
                ]
                start += count
    for part in range(2):
        lanes = pl.ds(512 * part, 512)
        kv_ref[0, pl.ds(OFF[5], 64), lanes] = dot_nn(
            high_ref[part], kv_ref[0, pl.ds(0, ROWS), lanes]
        ).astype(BF16)

    def edges(left_ref, right_ref):
        for level in range(LEVELS - 1):
            edge = pl.ds(HALO * level, HALO)
            left_ref[0, edge, :] = kv_ref[0, pl.ds(OFF[level], HALO), :]
            right_ref[0, edge, :] = kv_ref[0, pl.ds(OFF[level] + CELLS[level] - HALO, HALO), :]

    pl.when(piece % 2 == 0)(lambda: edges(far_ref, near_ref))
    pl.when(piece % 2 == 1)(lambda: edges(near_ref, far_ref))
    top_ref[0] = kv_ref[0, pl.ds(OFF[7], 16), :]


def cell_shapes(width):
    return [(ROWS, width), (ROWS // 8, width), (2 * ROWS, 2 * width)]


def edge_shapes(width):
    return [(EDGE, 2 * width), (EDGE, 2 * width), (16, 2 * width)]


def project(where, tokens, mine, other):
    micro, _, width = tokens.shape
    shape = jax.ShapeDtypeStruct
    shard = width // (2 * mine.shape[0])
    outs = cell_shapes(width) + edge_shapes(width)
    return pl.pallas_call(
        project_kernel,
        grid=(micro,),
        in_specs=[
            SCALAR,
            each_of((ROWS, width)),
            whole(mine.shape),
            whole(other.shape),
        ],
        out_specs=[each_of(out) for out in outs] + [whole((VEC, width))],
        out_shape=[shape((micro,) + out, BF16) for out in outs] + [shape((VEC, width), F32)],
        scratch_shapes=[
            pltpu.VMEM((3, width // shard, shard, width), BF16),
            pltpu.VMEM((ROWS, width), BF16),
            pltpu.VMEM((2, 240, 256), BF16),
            pltpu.VMEM((2, 64, ROWS), BF16),
        ],
        compiler_params=params(),
        cost_estimate=timing(13),
        name="project",
    )(where, tokens, mine, other)


def fine_windows(tile):
    return [
        (POFF[0] + 64 * tile, 96),
        (POFF[1] + 32 * tile, 64),
        (POFF[2] + 16 * tile, 16),
        (POFF[2] + 16 * tile + 32, 16),
    ]


def coarse_windows(tile):
    return [
        (POFF[3] + 64 * tile, 96),
        (POFF[4] + 32 * tile, 64),
        (POFF[5] + 16 * tile, 16),
        (POFF[5] + 16 * tile + 32, 16),
        (POFF[6], 16),
        (POFF[6] + 32, 16),
        (POFF[7], 32),
    ]


FINE_LEVELS = [96, 64, 32]
COARSE_LEVELS = [96, 64, 32, 32, 32]


def gather_rows(ref, windows, lanes):
    return jnp.concatenate([ref[at(start, size), lanes] for start, size in windows], axis=0)


def tile_bias(kid_ref, qid_ref, tile, tiles, windows, levels, bias):
    keys = jnp.concatenate([kid_ref[0, at(start, size), :] for start, size in windows], axis=0)
    keys = keys.astype(F32)
    keys = jnp.concatenate([keys, keys], axis=1)
    bias = jnp.concatenate([bias, bias], axis=1)
    out = []
    start = 0
    for index, count in enumerate(levels):
        part = slice(start, start + count)
        owner = qid_ref[0, pl.ds(tiles * index + tile, 1), :]
        out.append(jnp.where(keys[part] == owner, bias[part], NEG))
        start += count
    return jnp.concatenate(out, axis=0)


def lane_sums(value, steps):
    halves = []
    for half in range(2):
        part = value[:, 128 * half : 128 * (half + 1)]
        lane = lax.broadcasted_iota(jnp.int32, part.shape, 1)
        for step in range(steps):
            size = 1 << step
            first = (lane & size) == 0
            part = part + jnp.where(
                first, pltpu.roll(part, 128 - size, 1), pltpu.roll(part, size, 1)
            )
        halves.append(part)
    return jnp.concatenate(halves, axis=1)


def lane_roll(value, shift):
    if shift == 0:
        return value
    halves = [value[:, 128 * half : 128 * (half + 1)] for half in range(2)]
    return jnp.concatenate([pltpu.roll(part, shift % 128, 1) for part in halves], axis=1)


def far_row(tile, quad):
    return pl.ds(8 * (tile % 8) + 2 * (tile // 8) + quad, 1)


def level_sums(value, levels):
    out = [value[0 : levels[0]]]
    start = levels[0]
    for index, count in enumerate(levels[1:]):
        out.append(lane_sums(value[start : start + count], index + 1))
        start += count
    return jnp.concatenate(out, axis=0)


def head_stack(value, mask):
    return jnp.concatenate([value] * QUAD, axis=0) * mask


def head_pick(stacked):
    lane = lax.broadcasted_iota(jnp.int32, (TILE, QL), 1) // HEAD_DIM
    out = stacked[0:TILE]
    for head in range(1, QUAD):
        out = jnp.where(lane == head, stacked[TILE * head : TILE * (head + 1)], out)
    return out


def three_terms(row):
    high = row.astype(BF16)
    rest = row - high.astype(F32)
    middle = rest.astype(BF16)
    low = (rest - middle.astype(F32)).astype(BF16)
    return high, middle, low


def own_cell(tile):
    cell = lax.broadcasted_iota(jnp.int32, (16, QL), 0)
    token = lax.broadcasted_iota(jnp.int32, (16, QL), 1) % TILE
    return cell == 8 * (tile % 2) + token // 8


def lay_out(piece, kv_ref, near_ref, far_ref, across_ref, ends_ref, kvp_ref):
    def edges(left_ref, right_ref):
        for level in range(LEVELS - 1):
            base = POFF[level]
            edge = pl.ds(HALO * level, HALO)
            kvp_ref[pl.ds(base, HALO), :] = left_ref[0, edge, :]
            kvp_ref[pl.ds(base + HALO + CELLS[level], HALO), :] = right_ref[0, edge, :]

    pl.when(piece % 2 == 0)(lambda: edges(far_ref, near_ref))
    pl.when(piece % 2 == 1)(lambda: edges(near_ref, far_ref))
    for level in range(LEVELS - 1):
        count = CELLS[level]
        kvp_ref[pl.ds(POFF[level] + HALO, count), :] = kv_ref[0, pl.ds(OFF[level], count), :]
    across = across_ref[0].astype(F32)[0:PIECE7]
    ends = ends_ref[0].astype(F32)[0:PIECE7]
    tops = []
    for owner in range(4):
        top = jnp.where(owner == (piece + 2) % 4, across, jnp.where(owner == 3 - piece, ends, 0.0))
        tops.append(top)
    kvp_ref[pl.ds(POFF[7], 4 * PIECE7), :] = jnp.concatenate(tops, axis=0).astype(BF16)


def attend_kernel(
    where_ref,
    q_ref,
    q3_ref,
    kv_ref,
    near_ref,
    far_ref,
    across_ref,
    ends_ref,
    kid_ref,
    qidf_ref,
    qidc_ref,
    mixed_ref,
    lse_ref,
    lsec_ref,
    lsex_ref,
    oc_ref,
    kvp_ref,
    fine_ref,
    coarse_ref,
    mask_ref,
    spread_ref,
):
    @pl.when(pl.program_id(0) == 0)
    def _():
        attention_tables(fine_ref, coarse_ref, mask_ref, spread_ref, 0)

    lay_out(where_ref[0], kv_ref, near_ref, far_ref, across_ref, ends_ref, kvp_ref)
    mask = mask_ref[...]
    scaled = mask * jnp.asarray(0.125, BF16)

    units = [(tile, quad) for tile in range(COARSE_TILES) for quad in range(2)]
    biases = [
        tile_bias(kid_ref, qidc_ref, tile, 8, coarse_windows(tile), COARSE_LEVELS, coarse_ref[tile])
        for tile in range(COARSE_TILES)
    ]
    scores = []
    for tile, quad in units:
        lanes = pl.ds(QL * quad, QL)
        query = head_stack(q3_ref[0, pl.ds(TILE * tile, TILE), lanes], scaled)
        scores.append(dot_nt(gather_rows(kvp_ref, coarse_windows(tile), lanes), query))
    shares = []
    lines = []
    for index, (tile, quad) in enumerate(units):
        score = level_sums(scores[index], COARSE_LEVELS) + biases[index // 2]
        top = jnp.max(score, axis=0, keepdims=True)
        share = jnp.exp(score - top)
        total = jnp.sum(share, axis=0, keepdims=True)
        lse = top + jnp.log(total)
        lsec_ref[0, pl.ds(index, 1), :] = lse
        lines.append(lse)
        shares.append((share * (1.0 / total)).astype(BF16))
    results = []
    for (tile, quad), share in zip(units, shares):
        values = gather_rows(kvp_ref, coarse_windows(tile), pl.ds(512 + QL * quad, QL))
        results.append(dot_tn(share, values))
    lines = three_terms(jnp.concatenate(lines * 2, axis=0))
    lines = jnp.concatenate([line.astype(F32) for line in lines], axis=0)
    terms = [lane_roll(lines, -8 * part) for part in range(8)]
    terms = dot_nn(jnp.concatenate(terms, axis=0).astype(BF16), spread_ref[...])
    for part in range(8):
        rows = [terms[24 * part + 8 * index : 24 * part + 8 * index + 8] for index in range(3)]
        lsex_ref[0, pl.ds(8 * part, 8), :] = rows[0] + rows[1] + rows[2]
    for index, (tile, quad) in enumerate(units):
        oc_ref[0, pl.ds(TILE * tile, TILE), pl.ds(QL * quad, QL)] = head_pick(
            results[index]
        ).astype(BF16)

    def fine_group(group, carry):
        tiles = [GROUP * group + index for index in range(GROUP)]
        units = [(tile, quad) for tile in tiles for quad in range(2)]
        biases = [
            tile_bias(kid_ref, qidf_ref, tile, FINE_TILES, fine_windows(tile), FINE_LEVELS, fine_ref[...])
            for tile in tiles
        ]
        scores = []
        for tile, quad in units:
            lanes = pl.ds(QL * quad, QL)
            query = head_stack(q_ref[0, at(TILE * tile, TILE), lanes], scaled)
            scores.append(dot_nt(gather_rows(kvp_ref, fine_windows(tile), lanes), query))
        shares = []
        for index, (tile, quad) in enumerate(units):
            score = level_sums(scores[index], FINE_LEVELS) + biases[index // 2]
            far = lsex_ref[0, far_row(tile, quad), :]
            top = jnp.maximum(jnp.max(score, axis=0, keepdims=True), far)
            share = jnp.exp(score - top)
            far_share = jnp.exp(far - top)
            total = jnp.sum(share, axis=0, keepdims=True) + far_share
            lse_ref[0, pl.ds(2 * tile + quad, 1), :] = top + jnp.log(total)
            inverse = 1.0 / total
            shares.append(
                jnp.concatenate(
                    [share * inverse, jnp.where(own_cell(tile), far_share * inverse, 0.0)], axis=0
                ).astype(BF16)
            )
        results = []
        for (tile, quad), share in zip(units, shares):
            values = jnp.concatenate(
                [
                    gather_rows(kvp_ref, fine_windows(tile), pl.ds(512 + QL * quad, QL)),
                    oc_ref[0, at(16 * (tile // 2), 16), pl.ds(QL * quad, QL)],
                ],
                axis=0,
            )
            results.append(dot_tn(share, values))
        for (tile, quad), result in zip(units, results):
            mixed_ref[0, at(TILE * tile, TILE), pl.ds(QL * quad, QL)] = head_pick(result).astype(
                BF16
            )
        return carry

    lax.fori_loop(0, FINE_TILES // GROUP, fine_group, 0)


def stat_shapes(width):
    return [
        ((2 * FINE_TILES, QL), F32),
        ((2 * COARSE_TILES, QL), F32),
        ((64, QL), F32),
        ((ROWS // 8, width), BF16),
    ]


def id_specs(spec):
    return [
        spec((PADDED, 128)),
        spec((FINE * FINE_TILES, QL)),
        spec((8 * (LEVELS - FINE), QL)),
    ]


def attend(where, cells, received, ids):
    micro, _, width = cells[0].shape
    outs = [((ROWS, width), BF16)] + stat_shapes(width)
    ins = list(cells) + list(received)
    return pl.pallas_call(
        attend_kernel,
        grid=(micro,),
        in_specs=[SCALAR]
        + [each_of(value.shape[1:]) for value in ins]
        + id_specs(each_of),
        out_specs=[each_of(dims) for dims, _ in outs],
        out_shape=[jax.ShapeDtypeStruct((micro,) + dims, kind) for dims, kind in outs],
        scratch_shapes=[pltpu.VMEM((PADDED, 2 * width), BF16)] + table_shapes(),
        compiler_params=params(),
        cost_estimate=timing(23),
        name="attend",
    )(where, *ins, *ids)


def add_rows(ref, windows, lanes, value):
    start = 0
    for base, count in windows:
        rows = at(base, count)
        ref[rows, lanes] = ref[rows, lanes] + value[start : start + count]
        start += count


def attend_back_kernel(
    where_ref,
    q_ref,
    q3_ref,
    kv_ref,
    near_in_ref,
    far_in_ref,
    across_in_ref,
    ends_in_ref,
    lse_ref,
    lsec_ref,
    lsex_ref,
    oc_ref,
    dout_ref,
    kid_ref,
    qidf_ref,
    qidc_ref,
    dq_ref,
    dq3_ref,
    dkv_ref,
    near_ref,
    far_ref,
    across_ref,
    ends_ref,
    acc_ref,
    dcell_ref,
    delta_ref,
    kvp_ref,
    fine_ref,
    coarse_ref,
    mask_ref,
    spread_t_ref,
):
    @pl.when(pl.program_id(0) == 0)
    def _():
        attention_tables(fine_ref, coarse_ref, mask_ref, spread_t_ref, 1)

    lay_out(where_ref[0], kv_ref, near_in_ref, far_in_ref, across_in_ref, ends_in_ref, kvp_ref)
    delta_ref[...] = jnp.zeros(delta_ref.shape, F32)
    acc_ref[...] = jnp.zeros(acc_ref.shape, F32)
    dcell_ref[...] = jnp.zeros(dcell_ref.shape, F32)
    mask = mask_ref[...]
    scaled = mask * jnp.asarray(0.125, BF16)

    def fine_group(group, carry):
        tiles = [GROUP_BACK * group + index for index in range(GROUP_BACK)]
        units = [(tile, quad) for tile in tiles for quad in range(2)]
        biases = [
            tile_bias(kid_ref, qidf_ref, tile, FINE_TILES, fine_windows(tile), FINE_LEVELS, fine_ref[...])
            for tile in tiles
        ]
        at_unit = lambda unit: (at(TILE * unit[0], TILE), pl.ds(QL * unit[1], QL))
        queries = [head_stack(q_ref[(0,) + at_unit(unit)], scaled) for unit in units]
        douts = [head_stack(dout_ref[(0,) + at_unit(unit)], mask) for unit in units]
        scores = []
        steers = []
        for index, (tile, quad) in enumerate(units):
            keys = gather_rows(kvp_ref, fine_windows(tile), pl.ds(QL * quad, QL))
            scores.append(dot_nt(keys, queries[index]))
            values = jnp.concatenate(
                [
                    gather_rows(kvp_ref, fine_windows(tile), pl.ds(512 + QL * quad, QL)),
                    oc_ref[0, at(16 * (tile // 2), 16), pl.ds(QL * quad, QL)],
                ],
                axis=0,
            )
            steers.append(dot_nt(values, douts[index]))
        shares = []
        grads = []
        for index, (tile, quad) in enumerate(units):
            lse = lse_ref[0, pl.ds(2 * tile + quad, 1), :]
            far_share = jnp.exp(lsex_ref[0, far_row(tile, quad), :] - lse)
            share = jnp.exp(level_sums(scores[index], FINE_LEVELS) + biases[index // 2] - lse)
            share = jnp.concatenate([share, jnp.where(own_cell(tile), far_share, 0.0)], axis=0)
            weighted = share * steers[index]
            delta = jnp.sum(weighted, axis=0, keepdims=True)
            delta_ref[far_row(tile, quad), :] = far_share * delta
            grad = weighted[0:FINE_KEYS] - share[0:FINE_KEYS] * delta
            grads.append(level_sums(grad, FINE_LEVELS).astype(BF16))
            shares.append(share.astype(BF16))
        dvalues = [dot_nn(share, dout) for share, dout in zip(shares, douts)]
        dkeys = [dot_nn(grad, query) for grad, query in zip(grads, queries)]
        dqueries = []
        for (tile, quad), grad in zip(units, grads):
            keys = gather_rows(kvp_ref, fine_windows(tile), pl.ds(QL * quad, QL))
            dqueries.append(dot_tn(grad, keys))
        for index, (tile, quad) in enumerate(units):
            lanes = pl.ds(QL * quad, QL)
            cells = at(16 * (tile // 2), 16)
            windows = fine_windows(tile)
            add_rows(acc_ref, windows, pl.ds(512 + QL * quad, QL), dvalues[index])
            dcell_ref[cells, lanes] = dcell_ref[cells, lanes] + dvalues[index][FINE_KEYS:]
            add_rows(acc_ref, windows, lanes, dkeys[index])
            dq_ref[(0,) + at_unit((tile, quad))] = (head_pick(dqueries[index]) * 0.125).astype(BF16)
        return carry

    lax.fori_loop(0, FINE_TILES // GROUP_BACK, fine_group, 0)

    units = [(tile, quad) for tile in range(COARSE_TILES) for quad in range(2)]
    biases = [
        tile_bias(kid_ref, qidc_ref, tile, 8, coarse_windows(tile), COARSE_LEVELS, coarse_ref[tile])
        for tile in range(COARSE_TILES)
    ]
    at_unit = lambda unit: (pl.ds(TILE * unit[0], TILE), pl.ds(QL * unit[1], QL))
    queries = [head_stack(q3_ref[(0,) + at_unit(unit)], scaled) for unit in units]
    douts = [head_stack(dcell_ref[at_unit(unit)].astype(BF16), mask) for unit in units]
    terms = dot_nn(jnp.concatenate(three_terms(delta_ref[...]), axis=0), spread_t_ref[...])
    terms = terms[0:64] + terms[64:128] + terms[128:192]
    deltas = lane_roll(terms[0:8], 0)
    for part in range(1, 8):
        deltas = deltas + lane_roll(terms[8 * part : 8 * part + 8], 8 * part)
    steers = []
    scores = []
    for (tile, quad), dout, query in zip(units, douts, queries):
        values = gather_rows(kvp_ref, coarse_windows(tile), pl.ds(512 + QL * quad, QL))
        steers.append(dot_nt(values, dout))
        keys = gather_rows(kvp_ref, coarse_windows(tile), pl.ds(QL * quad, QL))
        scores.append(dot_nt(keys, query))
    shares = []
    grads = []
    for index, (tile, quad) in enumerate(units):
        score = level_sums(scores[index], COARSE_LEVELS) + biases[index // 2]
        share = jnp.exp(score - lsec_ref[0, pl.ds(index, 1), :])
        delta = deltas[index : index + 1]
        grads.append(level_sums(share * (steers[index] - delta), COARSE_LEVELS).astype(BF16))
        shares.append(share.astype(BF16))
    dvalues = [dot_nn(share, dout) for share, dout in zip(shares, douts)]
    dkeys = [dot_nn(grad, query) for grad, query in zip(grads, queries)]
    dqueries = []
    for (tile, quad), grad in zip(units, grads):
        keys = gather_rows(kvp_ref, coarse_windows(tile), pl.ds(QL * quad, QL))
        dqueries.append(dot_tn(grad, keys))
    for index, (tile, quad) in enumerate(units):
        windows = coarse_windows(tile)
        add_rows(acc_ref, windows, pl.ds(512 + QL * quad, QL), dvalues[index])
        add_rows(acc_ref, windows, pl.ds(QL * quad, QL), dkeys[index])
        dq3_ref[(0,) + at_unit((tile, quad))] = (head_pick(dqueries[index]) * 0.125).astype(BF16)

    key_lane = lax.broadcasted_iota(jnp.int32, (1, acc_ref.shape[1]), 1) < 512

    def scale(level):
        return jnp.where(key_lane, 0.5 ** STEP[level], 1.0)

    def low(level, start, count):
        return (acc_ref[pl.ds(start, count), :] * scale(level)).astype(BF16)

    def edges(left_ref, right_ref):
        for level in range(LEVELS - 1):
            base = POFF[level]
            edge = pl.ds(HALO * level, HALO)
            left_ref[0, edge, :] = low(level, base, HALO)
            right_ref[0, edge, :] = low(level, base + HALO + CELLS[level], HALO)

    piece = where_ref[0]
    pl.when(piece % 2 == 0)(lambda: edges(far_ref, near_ref))
    pl.when(piece % 2 == 1)(lambda: edges(near_ref, far_ref))
    for level in range(LEVELS - 1):
        dkv_ref[0, pl.ds(OFF[level], CELLS[level]), :] = low(level, POFF[level] + HALO, CELLS[level])
    dkv_ref[0, pl.ds(OFF[7], 16), :] = jnp.zeros((16, acc_ref.shape[1]), BF16)
    blank = jnp.zeros((PIECE7, acc_ref.shape[1]), F32)

    def high(index):
        rows = pl.ds(pl.multiple_of(POFF[7] + PIECE7 * index, PIECE7), PIECE7)
        return jnp.concatenate([acc_ref[rows, :] * scale(7), blank], axis=0).astype(BF16)

    ends_ref[0] = high(3 - piece)
    across_ref[0] = high((piece + 2) % 4)


def attend_back(where, cells, received, stats, dout, ids):
    micro, _, width = dout.shape
    shape = jax.ShapeDtypeStruct
    outs = cell_shapes(width) + edge_shapes(width) + edge_shapes(width)[2:]
    ins = list(cells) + list(received) + list(stats) + [dout]
    return pl.pallas_call(
        attend_back_kernel,
        grid=(micro,),
        in_specs=[SCALAR]
        + [each_of(value.shape[1:]) for value in ins]
        + id_specs(each_of),
        out_specs=[each_of(out) for out in outs],
        out_shape=[shape((micro,) + out, BF16) for out in outs],
        scratch_shapes=[
            pltpu.VMEM((PADDED, 2 * width), F32),
            pltpu.VMEM((ROWS // 8, width), F32),
            pltpu.VMEM((64, QL), F32),
            pltpu.VMEM((PADDED, 2 * width), BF16),
        ]
        + table_shapes(),
        compiler_params=params(),
        cost_estimate=timing(38),
        name="attend_back",
    )(where, *ins, *ids)


MID_ROWS = 512
FF_CHUNK = 512
ROOT = math.sqrt(2.0 / math.pi)


def give(send_ref, start, piece_of):
    for index in range(send_ref.shape[0]):
        piece = piece_of(index)
        send_ref[index, pl.ds(start, piece.shape[0]), :] = piece


def row_piece(ref, shard):
    def piece_of(index):
        return ref[pl.ds(pl.multiple_of(shard * index, shard), shard), :].astype(BF16)

    return piece_of


def middle_kernel(
    where_ref,
    tok_ref,
    cot_ref,
    mixed_ref,
    vec_ref,
    mine_ref,
    other_ref,
    out_ref,
    dmid_ref,
    dmix_ref,
    send_ref,
    wo_ref,
    wi_ref,
    wd_ref,
    acc_o,
    acc_i,
    acc_d,
    acc_b,
    acc_s,
    activ_ref,
    grad_ref,
    sems,
):
    step = pl.program_id(0)
    core = where_ref[1]
    parts = wi_ref.shape[0]
    shard = wo_ref.shape[2]

    def fetch(target, index, start, sem):
        size = target.shape[2]
        for chip in range(mine_ref.shape[0]):
            for ref, place in ((mine_ref, 2 * chip + core), (other_ref, 2 * chip + 1 - core)):
                source = ref.at[chip, pl.ds(start, size), :]
                pltpu.make_async_copy(source, target.at[index, place], sems.at[sem]).start()

    def arrived(target, sem):
        @pl.when(step == 0)
        def _():
            pltpu.make_async_copy(target, target, sems.at[sem]).wait()

    @pl.when(step == 0)
    def _():
        fetch(wo_ref, 0, 0, 0)
        for part in range(parts):
            fetch(wi_ref, part, shard * (1 + part), 1)
        fetch(wd_ref, 0, shard * (1 + parts), 2)
        acc_o[...] = jnp.zeros(acc_o.shape, F32)
        acc_i[...] = jnp.zeros(acc_i.shape, F32)
        acc_d[...] = jnp.zeros(acc_d.shape, F32)
        acc_b[...] = jnp.zeros(acc_b.shape, F32)
        acc_s[...] = jnp.zeros(acc_s.shape, F32)

    arrived(wo_ref, 0)
    wo = weight_of(wo_ref, 0)
    cot = cot_ref[...]
    top = cot.astype(BF16)
    mixed = mixed_ref[...]
    middle = tok_ref[...] + dot_nn(mixed, wo)
    unit, rate = normalised(middle)
    second = (unit * vec_ref[1:2] + vec_ref[3:4]).astype(BF16)
    arrived(wi_ref, 1)
    arrived(wd_ref, 2)
    pieces = FF_CHUNK // wd_ref.shape[2]
    wi = [weight_of(wi_ref, part) for part in range(parts)]
    wd = [
        wd_ref[0, pieces * part : pieces * (part + 1)].reshape(FF_CHUNK, wo.shape[1])
        for part in range(parts)
    ]
    result = middle + vec_ref[4:5]
    back = jnp.zeros(cot.shape, F32)
    pres = {}

    def first(part):
        pres[part] = (dot_nn(second, wi[part]) + vec_ref[5 + part : 6 + part], dot_nt(top, wd[part]))

    first(0)
    for part in range(parts):
        if part + 1 < parts:
            first(part + 1)
        pre, grad = pres.pop(part)
        square = pre * pre
        tanh = jnp.tanh(pre * (ROOT + (ROOT * 0.044715) * square))
        half = 0.5 + 0.5 * tanh
        activ = (pre * half).astype(BF16)
        slope = half + (pre * (0.5 - 0.5 * (tanh * tanh))) * (
            ROOT + (ROOT * 3 * 0.044715) * square
        )
        grad = (grad * slope).astype(BF16)
        cols = pl.ds(FF_CHUNK * part, FF_CHUNK)
        activ_ref[:, cols] = activ
        grad_ref[:, cols] = grad
        acc_b[:, cols] = acc_b[:, cols] + fold_rows(grad.astype(F32))
        result = result + dot_nn(activ, wd[part])
        back = back + dot_nt(grad, wi[part])
    out_ref[...] = result
    acc_d[...] = acc_d[...] + dot_tn(activ_ref[...], top)
    for part in range(parts):
        acc_i[part] = acc_i[part] + dot_tn(second, grad_ref[:, pl.ds(FF_CHUNK * part, FF_CHUNK)])
    dmid = cot + norm_back(back * vec_ref[1:2], unit, rate)
    dmid_ref[...] = dmid
    branch = dmid.astype(BF16)
    dmix_ref[...] = dot_nt(branch, wo).astype(BF16)
    acc_o[...] = acc_o[...] + dot_tn(mixed, branch)
    acc_s[0:8, :] = acc_s[0:8, :] + fold_rows(top.astype(F32))
    acc_s[8:16, :] = acc_s[8:16, :] + fold_rows(back * unit)
    acc_s[16:24, :] = acc_s[16:24, :] + fold_rows(back)

    @pl.when(step == pl.num_programs(0) - 1)
    def _():
        give(send_ref, 0, row_piece(acc_o, shard))
        for part in range(parts):
            give(send_ref, shard * (1 + part), row_piece(acc_i.at[part], shard))
        give(send_ref, shard * (1 + parts), row_piece(acc_d, shard * parts))
        total = lambda value: jnp.sum(value, axis=0, keepdims=True)
        lines = [total(acc_s[8 * index : 8 * index + 8, :]) for index in range(3)]
        for part in range(parts):
            lines.append(total(acc_b[:, pl.ds(FF_CHUNK * part, FF_CHUNK)]))
        lines.append(jnp.zeros((16 - len(lines), lines[0].shape[1]), F32))
        lines = jnp.concatenate(lines, axis=0).astype(BF16)
        give(send_ref, shard * (1 + 2 * parts), lambda index: lines)


def middle_part(where, tokens, cot, mixed, vec, mine, other):
    rows, width = tokens.shape
    chips, lines, _ = mine.shape
    shard = width // (2 * chips)
    parts = (lines // shard - 1) // 2
    hidden = parts * FF_CHUNK
    shape = jax.ShapeDtypeStruct
    tiled = pl.BlockSpec((MID_ROWS, width), lambda r: (r, 0))
    shared = shape((2 * chips, lines + 16, width), BF16)
    single = lambda dims: pl.BlockSpec(
        dims, lambda *_: (0,) * len(dims), pipeline_mode=pl.Buffered(1)
    )
    return pl.pallas_call(
        middle_kernel,
        grid=(rows // MID_ROWS,),
        in_specs=[SCALAR, tiled, tiled, tiled, whole(vec.shape), KEPT, KEPT],
        out_specs=[tiled, tiled, tiled, single(shared.shape)],
        out_shape=[
            shape((rows, width), F32),
            shape((rows, width), F32),
            shape((rows, width), BF16),
            shared,
        ],
        scratch_shapes=[
            pltpu.VMEM((1, 2 * chips, shard, width), BF16),
            pltpu.VMEM((parts, 2 * chips, shard, FF_CHUNK), BF16),
            pltpu.VMEM((1, 2 * chips, shard * parts, width), BF16),
            pltpu.VMEM((width, width), F32),
            pltpu.VMEM((parts, width, FF_CHUNK), F32),
            pltpu.VMEM((hidden, width), F32),
            pltpu.VMEM((8, hidden), F32),
            pltpu.VMEM((24, width), F32),
            pltpu.VMEM((MID_ROWS, hidden), BF16),
            pltpu.VMEM((MID_ROWS, hidden), BF16),
            pltpu.SemaphoreType.DMA((3,)),
        ],
        compiler_params=params(),
        cost_estimate=timing(40),
        name="middle",
    )(where, tokens, cot, mixed, vec, mine, other)


def collect_kernel(
    where_ref,
    tok_ref,
    dq_ref,
    dq3_ref,
    dkv_ref,
    near_ref,
    far_ref,
    across_ref,
    ends_ref,
    vec_ref,
    mine_ref,
    other_ref,
    dp_ref,
    send_ref,
    cells_ref,
    norm_ref,
    gw_ref,
    sum_ref,
    w_ref,
    low_ref,
    high_ref,
):
    @pl.when(pl.program_id(0) == 0)
    def _():
        gw_ref[...] = jnp.zeros(gw_ref.shape, F32)
        sum_ref[...] = jnp.zeros(sum_ref.shape, F32)
        low_ref[...] = mean_table((256, 240), 1, range(1, 5), lambda level: 1.0)
        high_ref[...] = mean_table((ROWS, 64), 1, range(5, 8), lambda level: 1.0)

    piece, core = where_ref[0], where_ref[1]
    cells_ref[...] = dkv_ref[0]

    def add(start, value):
        rows = pl.ds(start, HALO)
        cells_ref[rows, :] = (cells_ref[rows, :].astype(F32) + value.astype(F32)).astype(BF16)

    def edges(left_ref, right_ref):
        for level in range(LEVELS - 1):
            edge = pl.ds(HALO * level, HALO)

            @pl.when(piece > 0)
            def _():
                add(OFF[level], left_ref[0, edge, :])

            @pl.when(piece < 3)
            def _():
                add(OFF[level] + CELLS[level] - HALO, right_ref[0, edge, :])

    pl.when(piece % 2 == 0)(lambda: edges(far_ref, near_ref))
    pl.when(piece % 2 == 1)(lambda: edges(near_ref, far_ref))
    add(OFF[7], across_ref[0].astype(F32) + ends_ref[0].astype(F32))

    def expand(chunk, sums):
        rows = at(256 * chunk, 256)
        norm_ref[rows, :] = normalised(tok_ref[0, rows, :])[0].astype(BF16)
        cells = jnp.concatenate(
            [
                cells_ref[at(OFF[level] + (256 >> level) * chunk, 256 >> level), :]
                for level in range(1, 5)
            ],
            axis=0,
        )
        dkv = (
            cells_ref[rows, :].astype(F32)
            + dot_nn(low_ref[...], cells)
            + dot_nn(high_ref[rows, :], cells_ref[pl.ds(OFF[5], 64), :])
        ).astype(BF16)
        dq = (
            dq_ref[0, rows, :].astype(F32)
            + dot_nn(low_ref[:, 192:224], dq3_ref[0, at(32 * chunk, 32), :])
        ).astype(BF16)
        dp_ref[0, rows, pl.ds(0, 512)] = dq
        dp_ref[0, rows, pl.ds(512, 1024)] = dkv
        return [old + fold_rows(new.astype(F32)) for old, new in zip(sums, (dq, dkv))]

    sums = [jnp.zeros((8, 512), F32), jnp.zeros((8, 1024), F32)]
    sums = lax.fori_loop(0, ROWS // 256, expand, sums)
    sum_ref[...] = sum_ref[...] + jnp.concatenate(sums, axis=1)
    for index in range(3):
        grad = dot_tn(norm_ref[...], dp_ref[0, :, pl.ds(512 * index, 512)])
        gw_ref[index] = gw_ref[index] + grad

    @pl.when(pl.program_id(0) == pl.num_programs(0) - 1)
    def _():
        shard = w_ref.shape[2]
        row = lax.broadcasted_iota(jnp.int32, (VEC, 512), 0)
        lines = vec_ref[...].astype(BF16)
        gain = dot_tn(lines, jnp.where(row == 0, 1.0, 0.0).astype(BF16))
        offset = dot_tn(lines, jnp.where(row == 2, 1.0, 0.0).astype(BF16))
        ones = jnp.ones((8, 512), BF16)
        grad_gain = jnp.zeros((8, 512), F32)
        grad_offset = jnp.zeros((8, 512), F32)
        for index in range(3):
            take_weight(w_ref, index, mine_ref, other_ref, core, shard * index)
            grad = gw_ref[index]
            total = jnp.sum(sum_ref[:, pl.ds(512 * index, 512)], axis=0, keepdims=True)
            gw_ref[index] = gain * grad + offset * total
            weight = weight_of(w_ref, index)
            high, middle, _ = three_terms(weight.astype(F32) * grad)
            grad_gain = grad_gain + dot_nt(ones, high) + dot_nt(ones, middle)
            high, middle, low = three_terms(total)
            terms = jnp.concatenate([high, middle, low] + [jnp.zeros_like(low)] * 5, axis=0)
            grad_offset = grad_offset + dot_nt(terms, weight)
            give(send_ref, shard * index, row_piece(gw_ref.at[index], shard))
        grad_offset = jnp.sum(grad_offset, axis=0, keepdims=True)
        blank = jnp.zeros((VEC - 2, 512), F32)
        lines = jnp.concatenate([grad_gain[0:1], grad_offset, blank], axis=0).astype(BF16)
        give(send_ref, 3 * shard, lambda index: lines)


def collect(where, tokens, grads, received, vec, mine, other):
    micro, _, width = tokens.shape
    chips, lines, _ = mine.shape
    shard = width // (2 * chips)
    shape = jax.ShapeDtypeStruct
    moved = [tokens] + list(grads) + list(received)
    ins = [vec, mine, other]
    return pl.pallas_call(
        collect_kernel,
        grid=(micro,),
        in_specs=[SCALAR]
        + [each_of(value.shape[1:]) for value in moved]
        + [whole(value.shape) for value in ins],
        out_specs=[each_of((ROWS, 3 * width)), whole((2 * chips, lines, width))],
        out_shape=[
            shape((micro, ROWS, 3 * width), BF16),
            shape((2 * chips, lines, width), BF16),
        ],
        scratch_shapes=[
            pltpu.VMEM((2 * ROWS, 2 * width), BF16),
            pltpu.VMEM((ROWS, width), BF16),
            pltpu.VMEM((3, width, width), F32),
            pltpu.VMEM((8, 3 * width), F32),
            pltpu.VMEM((3, 2 * chips, shard, width), BF16),
            pltpu.VMEM((256, 240), BF16),
            pltpu.VMEM((ROWS, 64), BF16),
        ],
        compiler_params=params(),
        cost_estimate=timing(17),
        name="collect",
    )(where, *moved, *ins)


FIN_ROWS = 256


def finish_kernel(
    where_ref, tok_ref, dmid_ref, dp_ref, vec_ref, mine_ref, other_ref, grad_ref, w_ref
):
    core = where_ref[1]

    @pl.when(pl.program_id(0) == 0)
    def _():
        for index in range(3):
            take_weight(w_ref, index, mine_ref, other_ref, core, w_ref.shape[2] * index)

    back = dot_nt(dp_ref[:, pl.ds(0, 512)], weight_of(w_ref, 0))
    for index in range(1, 3):
        back = back + dot_nt(dp_ref[:, pl.ds(512 * index, 512)], weight_of(w_ref, index))
    unit, rate = normalised(tok_ref[...])
    grad_ref[...] = dmid_ref[...] + norm_back(back * vec_ref[0:1], unit, rate)


def finish(where, tokens, dmid, dproj, vec, mine, other):
    rows, width = tokens.shape
    dp = 2 * mine.shape[0]
    chunk = lambda lanes: pl.BlockSpec((FIN_ROWS, lanes), lambda r: (r, 0))
    return pl.pallas_call(
        finish_kernel,
        grid=(rows // FIN_ROWS,),
        in_specs=[
            SCALAR,
            chunk(width),
            chunk(width),
            chunk(3 * width),
            whole(vec.shape),
            whole(mine.shape),
            whole(other.shape),
        ],
        out_specs=chunk(width),
        out_shape=jax.ShapeDtypeStruct(tokens.shape, F32),
        scratch_shapes=[pltpu.VMEM((3, dp, width // dp, width), BF16)],
        compiler_params=params(),
        cost_estimate=timing(13),
        name="finish",
    )(where, tokens, dmid, dproj, vec, mine, other)


def twice(chunk):
    lane = lax.broadcasted_iota(jnp.int32, chunk.shape, 1)
    other = pltpu.roll(chunk, 64, 1)
    halves = jnp.where(lane < 64, chunk, other), jnp.where(lane < 64, other, chunk)
    return [jnp.concatenate([half, half], axis=1)[0:1] for half in halves]


def lane_pairs(value, size, merge):
    halves = []
    for half in range(2):
        part = value[:, 128 * half : 128 * (half + 1)]
        lane = lax.broadcasted_iota(jnp.int32, part.shape, 1)
        first = (lane & size) == 0
        pair = jnp.where(first, pltpu.roll(part, 128 - size, 1), pltpu.roll(part, size, 1))
        halves.append(merge(part, pair))
    return jnp.concatenate(halves, axis=1)


def documents_kernel(where_ref, seg_ref, own_ref, kid_ref, qidf_ref, qidc_ref, row_ref):
    piece = where_ref[0]
    length = seg_ref.shape[2]
    margin = (row_ref.shape[0] - length) // 2
    ones = jnp.ones((16, 128), BF16)

    def only_first(row):
        index = lax.broadcasted_iota(jnp.int32, (16, row.shape[1]), 0)
        return jnp.where(index == 0, row.astype(F32), 0.0).astype(BF16)

    outside = jnp.full((margin, 128), -3.0, F32)
    row_ref[pl.ds(0, margin), :] = outside
    row_ref[pl.ds(margin + length, margin), :] = outside
    row_ref[pl.ds(margin, length), :] = dot_tn(only_first(seg_ref[0]), ones)
    for level in range(LEVELS):
        cell = 1 << level
        if level < LEVELS - 1:
            start = ROWS * piece + margin - HALO * cell
            count = CELLS[level] + 2 * HALO
        else:
            start = margin
            count = 4 * PIECE7
        if level == 0:
            key = row_ref[at(start, count), :]
        else:
            lowest = row_ref[pl.ds(start, count, stride=cell), :]
            highest = row_ref[pl.ds(start + cell - 1, count, stride=cell), :]
            key = jnp.where(lowest == highest, lowest, -2.0)
        if level == LEVELS - 1:
            owner = lax.broadcasted_iota(jnp.int32, key.shape, 0) // PIECE7
            counted = (jnp.abs(owner // 2 - piece // 2) == 1) & (jnp.abs(owner - piece) >= 2)
            key = jnp.where(counted, key, -3.0)
        kid_ref[0, pl.ds(POFF[level], count), :] = key.astype(BF16)

    own = own_ref[0].astype(F32)
    rows = []
    for chunk in range(ROWS // 128):
        rows += twice(jnp.broadcast_to(own[:, 128 * chunk : 128 * (chunk + 1)], (8, 128)))
    low = high = jnp.concatenate(rows, axis=0)
    for level in range(FINE):
        if level > 0:
            low = lane_pairs(low, 1 << (level - 1), jnp.minimum)
            high = lane_pairs(high, 1 << (level - 1), jnp.maximum)
        qidf_ref[0, pl.ds(FINE_TILES * level, FINE_TILES), :] = jnp.where(low == high, low, -1.0)

    token = lax.broadcasted_iota(jnp.int32, (ROWS, ROWS // 8), 0)
    cells = lax.broadcasted_iota(jnp.int32, (ROWS, ROWS // 8), 1)
    ends = []
    for step in (0, 7):
        pick = jnp.where(token == 8 * cells + step, 1.0, 0.0).astype(BF16)
        value = dot_nn(only_first(own), pick)[0:1]
        rows = twice(jnp.broadcast_to(value, (8, 128)))
        ends.append(jnp.concatenate(rows + [rows[1]] * 6, axis=0))
    low, high = ends
    for index in range(LEVELS - FINE):
        if index > 0:
            low = lane_pairs(low, 1 << (index - 1), jnp.minimum)
            high = lane_pairs(high, 1 << (index - 1), jnp.maximum)
        qidc_ref[0, pl.ds(8 * index, 8), :] = jnp.where(low == high, low, -1.0)


def cell_documents(where, segments, piece):
    micro, _, length = segments.shape
    shape = jax.ShapeDtypeStruct
    own = lax.dynamic_slice_in_dim(segments, piece * ROWS, ROWS, axis=2)
    outs = [((PADDED, 128), BF16), ((FINE * FINE_TILES, QL), F32), ((8 * (LEVELS - FINE), QL), F32)]
    key, fine, coarse = pl.pallas_call(
        documents_kernel,
        grid=(micro,),
        in_specs=[SCALAR, each_of((1, length)), each_of((1, ROWS))],
        out_specs=[each_of(dims) for dims, _ in outs],
        out_shape=[shape((micro,) + dims, kind) for dims, kind in outs],
        scratch_shapes=[pltpu.VMEM((length + 2 * ROWS, 128), F32)],
        compiler_params=params(),
        cost_estimate=timing(5),
        name="documents",
    )(where, segments, own)
    return key, fine, coarse


def same_core(chips):
    return [[2 * chip + core for chip in range(chips)] for core in range(2)]


def core_swap(value, chips):
    pairs = [(place, place ^ 1) for place in range(2 * chips)]
    return lax.ppermute(value, "dp", pairs)


def chip_exchange(value, chips):
    return lax.all_to_all(value, "dp", 0, 0, axis_index_groups=same_core(chips), tiled=True)


def after(value, *done):
    return lax.optimization_barrier((value,) + done)[0]


def add(left, right):
    return left.astype(F32) + right.astype(F32)


def body(
    tokens,
    segment_ids,
    norm_gains,
    norm_biases,
    qkv_weight,
    out_weight,
    in_weight,
    in_bias,
    down_weight,
    down_bias,
    cotangent,
):
    micro, _, row_count, width = tokens.shape
    pieces = lax.axis_size("sp")
    piece = lax.axis_index("sp")
    assert row_count == ROWS and pieces == 4 and micro == 2
    tokens = tokens[:, 0]
    cotangent = cotangent[:, 0]
    dp = lax.axis_size("dp")
    place = lax.axis_index("dp")
    chips = dp // 2
    shard = width // dp
    hidden = in_weight.shape[1]
    parts = hidden // FF_CHUNK
    where = jnp.stack([piece, place % 2]).astype(jnp.int32)
    swap = lambda value, bits: lax.ppermute(value, "sp", [(p, p ^ bits) for p in range(pieces)])
    spread = lambda value: chip_exchange(
        jnp.broadcast_to(value[None], (chips,) + value.shape), chips
    )

    def placed(value, start):
        lines = jnp.zeros((value.shape[0], start * value.shape[1]), BF16)
        return lax.dynamic_update_slice(lines, value, (0, place * value.shape[1])).reshape(-1, width)

    small = placed(jnp.concatenate([norm_gains, norm_biases, down_bias[None]]), dp)
    small = jnp.concatenate([small, placed(in_bias[None], dp)])
    small = jnp.pad(small, ((0, VEC - small.shape[0]), (0, 0)))
    mine = spread(jnp.concatenate([qkv_weight.reshape(3 * shard, width), small]))
    ids = cell_documents(where, segment_ids, piece)
    where, mine = lax.optimization_barrier((after(where, ids[2]), mine))
    other = core_swap(mine, chips)
    rest = jnp.concatenate(
        [
            out_weight,
            in_weight.reshape(shard, parts, FF_CHUNK).swapaxes(0, 1).reshape(-1, width),
            down_weight,
        ]
    )
    rest_mine = spread(after(rest, other))

    def halo(near, far, across, ends):
        middle = lax.ppermute(far, "sp", [(1, 2), (2, 1)])
        return swap(near, 1), middle, swap(across, 2), lax.ppermute(ends, "sp", [(0, 3), (3, 0)])

    q, q3, kv, near, far, top, vec = project(where, tokens, mine, other)
    cells = (q, q3, kv)
    received = halo(near, far, top, top)
    rest_mine = after(rest_mine, *received)
    rest_other = core_swap(rest_mine, chips)
    mixed, *stats = attend(after(where, rest_mine), cells, received, ids)
    rest_other = after(rest_other, mixed)

    flat = lambda value: value.reshape(micro * ROWS, width)
    split = lambda value: value.reshape(micro, ROWS, width)
    outputs, dmid, dmix, send = middle_part(
        where, flat(tokens), flat(cotangent), flat(mixed), vec, rest_mine, rest_other
    )
    come = lax.all_to_all(send, "dp", 0, 0, tiled=True)
    dq, dq3, dkv, *edges = attend_back(where, cells, received, stats, split(dmix), ids)
    grads = (dq, dq3, dkv)
    back = halo(*edges)
    odd = piece % 2 == 1
    total = jnp.sum(after(come, *back).astype(F32), axis=0).astype(BF16)
    come = swap(total, 1)
    dproj, send = collect(
        after(where, total), tokens, grads, back, vec, mine, other
    )
    total = add(total, after(come, send)).astype(BF16)
    half = jnp.where(odd, total[:, width // 2 :], total[:, : width // 2])
    come = swap(half, 2)
    qkv_come = lax.all_to_all(after(send, half), "dp", 0, 0, tiled=True)
    input_grad = finish(
        after(where, half), flat(tokens), dmid, dproj.reshape(micro * ROWS, -1), vec, mine, other
    )
    half = add(half, after(come, input_grad)).astype(BF16)
    come = swap(half, 1)
    total = jnp.sum(after(qkv_come, half).astype(F32), axis=0).astype(BF16)
    qkv_come = swap(total, 1)
    come = after(come, total)
    rest = jnp.where(
        odd, jnp.concatenate([come, half], axis=1), jnp.concatenate([half, come], axis=1)
    ).astype(F32)
    total = add(total, qkv_come).astype(BF16)
    total = add(total, swap(total, 2))

    own = lambda value, size: lax.dynamic_slice_in_dim(value, place * size, size, axis=-1)
    small_two = rest[shard * (1 + 2 * parts) :]
    small_one = total[3 * shard :]
    gin = rest[shard : shard * (1 + parts)].reshape(parts, shard, FF_CHUNK).swapaxes(0, 1)
    return (
        outputs.reshape(micro, 1, ROWS, width),
        input_grad.reshape(micro, 1, ROWS, width),
        own(jnp.stack([small_one[0], small_two[1]]), shard),
        own(jnp.stack([small_one[1], small_two[2]]), shard),
        total[: 3 * shard].reshape(3, shard, width),
        rest[:shard],
        gin.reshape(shard, hidden),
        own(small_two[3 : 3 + parts].reshape(hidden), hidden // dp),
        rest[shard * (1 + parts) : shard * (1 + 2 * parts)],
        own(small_two[0], shard),
    )


def solution(mesh):
    in_specs = (
        P(None, "dp", "sp", None),
        P(None, "dp", None),
        P(None, "dp"),
        P(None, "dp"),
        P(None, "dp", None),
        P("dp", None),
        P("dp", None),
        P("dp"),
        P("dp", None),
        P("dp"),
        P(None, "dp", "sp", None),
    )
    out_specs = (
        P(None, "dp", "sp", None),
        P(None, "dp", "sp", None),
        P(None, "dp"),
        P(None, "dp"),
        P(None, "dp", None),
        P("dp", None),
        P("dp", None),
        P("dp"),
        P("dp", None),
        P("dp"),
    )
    return jax.shard_map(body, mesh=mesh, in_specs=in_specs, out_specs=out_specs, check_vma=False)
```

```python
import math

import jax
import jax.numpy as jnp
from jax import lax
from jax.experimental import pallas as pl
from jax.experimental.pallas import tpu as pltpu
from jax.sharding import PartitionSpec as P

HEADS = 8
HEAD_DIM = 64
BLOCK = 16
LEVELS = 8
HALO = 16
TILE = 64
QUAD = 4
QL = QUAD * HEAD_DIM
NEG = -1e30
FINE = 3
ROWS = 1024
EDGE = 112
VEC = 16
GROUP = 4
GROUP_BACK = 4
F32 = jnp.float32
BF16 = jnp.bfloat16

CELLS = [ROWS >> level for level in range(LEVELS)]
OFF = [2 * ROWS - (2 * ROWS >> level) for level in range(LEVELS)]
POFF = []
_at = 0
for _level in range(LEVELS - 1):
    POFF.append(_at)
    _at += CELLS[_level] + 2 * HALO
POFF.append(_at)
PIECE7 = CELLS[LEVELS - 1]
PADDED = _at + 4 * PIECE7
FINE_TILES = ROWS // TILE
COARSE_TILES = ROWS // 8 // TILE
FINE_KEYS = 192
COARSE_KEYS = 256
LN_EPS = 1e-05
VMEM_LIMIT = 62 * 1024 * 1024


STEP = [0, 1, 2, 0, 1, 2, 3, 4]


def places(shape):
    return [lax.broadcasted_iota(jnp.int32, shape, axis) for axis in range(2)]


def counted_pairs(level, query, key):
    near = jnp.abs((query >> 4) - (key >> 4))
    if level == 0:
        return near <= 1
    return (near == 1) & (jnp.abs((query >> 3) - (key >> 3)) >= 2)


def score_offsets(parts):
    out = []
    for level, count, window, query_of in parts:
        key, lane = places((count, 2 * TILE))
        query = query_of(lane & (TILE - 1))
        if window == "all":
            allowed = jnp.full(key.shape, True)
        else:
            split = window == "sides"
            key = jnp.where(key < 16, key - 16, key) if split else key - 16
            allowed = counted_pairs(level, query, key)
        out.append(jnp.where(allowed, level * math.log(2.0), NEG))
    return jnp.concatenate(out, axis=0)


def fine_offsets():
    return score_offsets(
        [
            (0, 96, "span", lambda token: token),
            (1, 64, "span", lambda token: token >> 1),
            (2, 32, "sides", lambda token: token >> 2),
        ]
    )


def coarse_offsets(tile):
    return score_offsets(
        [
            (3, 96, "span", lambda cell: cell),
            (4, 64, "span", lambda cell: cell >> 1),
            (5, 32, "sides", lambda cell: cell >> 2),
            (6, 32, "sides", lambda cell: 8 * tile + (cell >> 3)),
            (7, 4 * PIECE7, "all", lambda cell: cell),
        ]
    )


def mean_table(shape, cell_axis, levels, scale_of):
    index = places(shape)
    cell, token = index[cell_axis], index[1 - cell_axis]
    out = jnp.zeros(shape, F32)
    start = 0
    for level in levels:
        weight = scale_of(level) / (1 << level)
        out = out + jnp.where((token >> level) + start == cell, weight, 0.0)
        start += shape[1 - cell_axis] >> level
    return out.astype(BF16)


def head_table():
    row, col = places((QL, QL))
    return jnp.where((row >> 6) == (col >> 6), 1.0, 0.0).astype(BF16)


def spread_table(cell_axis):
    index = places((QL, QL))
    cell, token = index[cell_axis], index[1 - cell_axis]
    same = ((cell >> 6) == (token >> 6)) & ((cell & 63) == ((token & 63) >> 3))
    return jnp.where(same, 1.0, 0.0).astype(BF16)


def attention_tables(fine_ref, coarse_ref, mask_ref, spread_ref, cell_axis):
    fine_ref[...] = fine_offsets()
    for tile in range(COARSE_TILES):
        coarse_ref[tile] = coarse_offsets(tile)
    mask_ref[...] = head_table()
    spread_ref[...] = spread_table(cell_axis)


def table_shapes():
    return [
        pltpu.VMEM((FINE_KEYS, QL // 2), F32),
        pltpu.VMEM((COARSE_TILES, COARSE_KEYS, QL // 2), F32),
        pltpu.VMEM((QL, QL), BF16),
        pltpu.VMEM((QL, QL), BF16),
    ]


def dot_nn(left, right):
    return jnp.dot(left, right, preferred_element_type=F32)


def dot_nt(left, right):
    return lax.dot_general(left, right, (((1,), (1,)), ((), ())), preferred_element_type=F32)


def dot_tn(left, right):
    return lax.dot_general(left, right, (((0,), (0,)), ((), ())), preferred_element_type=F32)


def at(start, size):
    return pl.ds(pl.multiple_of(start, 16), size)


def whole(shape):
    zeros = (0,) * len(shape)
    return pl.BlockSpec(shape, lambda *_: zeros)


def one_of(shape, micro):
    zeros = (0,) * len(shape)
    return pl.BlockSpec((1,) + shape, lambda *_: (micro,) + zeros)


def each_of(shape):
    zeros = (0,) * len(shape)
    return pl.BlockSpec((1,) + shape, lambda step: (step,) + zeros)


SCALAR = pl.BlockSpec(memory_space=pltpu.SMEM)
KEPT = pl.BlockSpec(memory_space=pl.ANY)


def timing(micros):
    return pl.CostEstimate(
        flops=int(micros * 4e8), bytes_accessed=int(micros * 3e6), transcendentals=0
    )


def params():
    return pltpu.CompilerParams(
        dimension_semantics=("arbitrary",), vmem_limit_bytes=VMEM_LIMIT
    )


def normalised(rows):
    center = rows - jnp.mean(rows, axis=-1, keepdims=True)
    spread = jnp.mean(center * center, axis=-1, keepdims=True)
    rate = lax.rsqrt(spread + LN_EPS)
    return center * rate, rate


def norm_back(grad, unit, rate):
    mean_grad = jnp.mean(grad, axis=-1, keepdims=True)
    mean_dot = jnp.mean(grad * unit, axis=-1, keepdims=True)
    return rate * (grad - mean_grad - unit * mean_dot)


def fold_rows(value):
    return jnp.sum(value.reshape(-1, 8, value.shape[-1]), axis=0)


def take_weight(target, index, mine, other, core, start):
    chips, shard = mine.shape[0], target.shape[2]
    for chip in range(chips):
        target[index, 2 * chip + core] = mine[chip, pl.ds(start, shard), :]
        target[index, 2 * chip + 1 - core] = other[chip, pl.ds(start, shard), :]


def weight_of(ref, index):
    return ref[index].reshape(ref.shape[1] * ref.shape[2], ref.shape[3])


def project_kernel(
    where_ref,
    tok_ref,
    mine_ref,
    other_ref,
    q_ref,
    q3_ref,
    kv_ref,
    near_ref,
    far_ref,
    top_ref,
    vec_ref,
    w_ref,
    norm_ref,
    low_ref,
    high_ref,
):
    piece, core = where_ref[0], where_ref[1]
    shard = w_ref.shape[2]

    @pl.when(pl.program_id(0) == 0)
    def _():
        for index in range(3):
            take_weight(w_ref, index, mine_ref, other_ref, core, shard * index)
        vec = jnp.zeros(vec_ref.shape, F32)
        for chip in range(mine_ref.shape[0]):
            for ref in (mine_ref, other_ref):
                vec = vec + ref[chip, pl.ds(3 * shard, VEC), :].astype(F32)
        vec_ref[...] = vec
        for part, scale_of in enumerate((lambda level: 0.5 ** STEP[level], lambda level: 1.0)):
            low_ref[part] = mean_table((240, 256), 0, range(1, 5), scale_of)
            high_ref[part] = mean_table((64, ROWS), 0, range(5, 8), scale_of)

    def normalise(chunk, carry):
        rows = at(256 * chunk, 256)
        unit, _ = normalised(tok_ref[0, rows, :])
        norm_ref[rows, :] = (unit * vec_ref[0:1] + vec_ref[2:3]).astype(BF16)
        return carry

    lax.fori_loop(0, ROWS // 256, normalise, 0)
    for half in range(2):
        rows = pl.ds(512 * half, 512)
        for index in range(3):
            value = dot_nn(norm_ref[rows, :], weight_of(w_ref, index)).astype(BF16)
            if index == 0:
                q_ref[0, rows, :] = value
            else:
                kv_ref[0, rows, pl.ds(512 * (index - 1), 512)] = value

    def average(chunk, carry):
        rows = at(256 * chunk, 256)
        q3_ref[0, at(32 * chunk, 32), :] = dot_nn(
            low_ref[1, 192:224, :], q_ref[0, rows, :]
        ).astype(BF16)
        for part in range(2):
            lanes = pl.ds(512 * part, 512)
            cells = dot_nn(low_ref[part], kv_ref[0, rows, lanes]).astype(BF16)
            start = 0
            for level in range(1, 5):
                count = 256 >> level
                kv_ref[0, at(OFF[level] + count * chunk, count), lanes] = cells[
                    start : start + count
                ]
                start += count
        return carry

    lax.fori_loop(0, ROWS // 256, average, 0)
    for part in range(2):
        lanes = pl.ds(512 * part, 512)
        kv_ref[0, pl.ds(OFF[5], 64), lanes] = dot_nn(
            high_ref[part], kv_ref[0, pl.ds(0, ROWS), lanes]
        ).astype(BF16)

    def edges(left_ref, right_ref):
        for level in range(LEVELS - 1):
            edge = pl.ds(HALO * level, HALO)
            left_ref[0, edge, :] = kv_ref[0, pl.ds(OFF[level], HALO), :]
            right_ref[0, edge, :] = kv_ref[0, pl.ds(OFF[level] + CELLS[level] - HALO, HALO), :]

    pl.when(piece % 2 == 0)(lambda: edges(far_ref, near_ref))
    pl.when(piece % 2 == 1)(lambda: edges(near_ref, far_ref))
    top_ref[0] = kv_ref[0, pl.ds(OFF[7], PIECE7), :]


def cell_shapes(width):
    return [(ROWS, width), (ROWS // 8, width), (2 * ROWS, 2 * width)]


def edge_shapes(width):
    return [(EDGE, 2 * width), (EDGE, 2 * width), (PIECE7, 2 * width)]


def project(where, tokens, mine, other):
    micro, _, width = tokens.shape
    shape = jax.ShapeDtypeStruct
    shard = width // (2 * mine.shape[0])
    outs = cell_shapes(width) + edge_shapes(width)
    return pl.pallas_call(
        project_kernel,
        grid=(micro,),
        in_specs=[
            SCALAR,
            each_of((ROWS, width)),
            whole(mine.shape),
            whole(other.shape),
        ],
        out_specs=[each_of(out) for out in outs] + [whole((VEC, width))],
        out_shape=[shape((micro,) + out, BF16) for out in outs] + [shape((VEC, width), F32)],
        scratch_shapes=[
            pltpu.VMEM((3, width // shard, shard, width), BF16),
            pltpu.VMEM((ROWS, width), BF16),
            pltpu.VMEM((2, 240, 256), BF16),
            pltpu.VMEM((2, 64, ROWS), BF16),
        ],
        compiler_params=params(),
        cost_estimate=timing(13),
        name="project",
    )(where, tokens, mine, other)


def fine_windows(tile):
    return [
        (POFF[0] + 64 * tile, 96),
        (POFF[1] + 32 * tile, 64),
        (POFF[2] + 16 * tile, 16),
        (POFF[2] + 16 * tile + 32, 16),
    ]


def coarse_windows(tile):
    return [
        (POFF[3] + 64 * tile, 96),
        (POFF[4] + 32 * tile, 64),
        (POFF[5] + 16 * tile, 16),
        (POFF[5] + 16 * tile + 32, 16),
        (POFF[6], 16),
        (POFF[6] + 32, 16),
        (POFF[7], 32),
    ]


FINE_LEVELS = [96, 64, 32]
COARSE_LEVELS = [96, 64, 32, 32, 32]


def gather_rows(ref, windows, lanes):
    return jnp.concatenate([ref[at(start, size), lanes] for start, size in windows], axis=0)


def tile_bias(kid_ref, qid_ref, tile, tiles, windows, levels, bias):
    keys = jnp.concatenate([kid_ref[0, at(start, size), :] for start, size in windows], axis=0)
    keys = keys.astype(F32)
    keys = jnp.concatenate([keys, keys], axis=1)
    bias = jnp.concatenate([bias, bias], axis=1)
    out = []
    start = 0
    for index, count in enumerate(levels):
        part = slice(start, start + count)
        owner = qid_ref[0, pl.ds(tiles * index + tile, 1), :]
        out.append(jnp.where(keys[part] == owner, bias[part], NEG))
        start += count
    return jnp.concatenate(out, axis=0)


def lane_sums(value, steps):
    halves = []
    for half in range(2):
        part = value[:, 128 * half : 128 * (half + 1)]
        lane = lax.broadcasted_iota(jnp.int32, part.shape, 1)
        for step in range(steps):
            size = 1 << step
            first = (lane & size) == 0
            part = part + jnp.where(
                first, pltpu.roll(part, 128 - size, 1), pltpu.roll(part, size, 1)
            )
        halves.append(part)
    return jnp.concatenate(halves, axis=1)


def lane_roll(value, shift):
    if shift == 0:
        return value
    halves = [value[:, 128 * half : 128 * (half + 1)] for half in range(2)]
    return jnp.concatenate([pltpu.roll(part, shift % 128, 1) for part in halves], axis=1)


def far_row(tile, quad):
    return pl.ds(8 * (tile % 8) + 2 * (tile // 8) + quad, 1)


def level_sums(value, levels):
    out = [value[0 : levels[0]]]
    start = levels[0]
    for index, count in enumerate(levels[1:]):
        out.append(lane_sums(value[start : start + count], index + 1))
        start += count
    return jnp.concatenate(out, axis=0)


def head_stack(value, mask):
    return jnp.concatenate([value] * QUAD, axis=0) * mask


def head_pick(stacked):
    lane = lax.broadcasted_iota(jnp.int32, (TILE, QL), 1) // HEAD_DIM
    out = stacked[0:TILE]
    for head in range(1, QUAD):
        out = jnp.where(lane == head, stacked[TILE * head : TILE * (head + 1)], out)
    return out


def three_terms(row):
    high = row.astype(BF16)
    rest = row - high.astype(F32)
    middle = rest.astype(BF16)
    low = (rest - middle.astype(F32)).astype(BF16)
    return high, middle, low


def own_cell(tile):
    cell = lax.broadcasted_iota(jnp.int32, (16, QL), 0)
    token = lax.broadcasted_iota(jnp.int32, (16, QL), 1) % TILE
    return cell == 8 * (tile % 2) + token // 8


def lay_out(piece, kv_ref, near_ref, far_ref, across_ref, ends_ref, kvp_ref):
    def edges(left_ref, right_ref):
        for level in range(LEVELS - 1):
            base = POFF[level]
            edge = pl.ds(HALO * level, HALO)
            kvp_ref[pl.ds(base, HALO), :] = left_ref[0, edge, :]
            kvp_ref[pl.ds(base + HALO + CELLS[level], HALO), :] = right_ref[0, edge, :]

    pl.when(piece % 2 == 0)(lambda: edges(far_ref, near_ref))
    pl.when(piece % 2 == 1)(lambda: edges(near_ref, far_ref))
    for level in range(LEVELS - 1):
        count = CELLS[level]
        kvp_ref[pl.ds(POFF[level] + HALO, count), :] = kv_ref[0, pl.ds(OFF[level], count), :]
    across = across_ref[0].astype(F32)
    ends = ends_ref[0].astype(F32)
    tops = []
    for owner in range(4):
        top = jnp.where(owner == (piece + 2) % 4, across, jnp.where(owner == 3 - piece, ends, 0.0))
        tops.append(top)
    kvp_ref[pl.ds(POFF[7], 4 * PIECE7), :] = jnp.concatenate(tops, axis=0).astype(BF16)


def attend_kernel(
    where_ref,
    q_ref,
    q3_ref,
    kv_ref,
    near_ref,
    far_ref,
    across_ref,
    ends_ref,
    kid_ref,
    qidf_ref,
    qidc_ref,
    mixed_ref,
    lse_ref,
    lsec_ref,
    lsex_ref,
    oc_ref,
    kvp_ref,
    fine_ref,
    coarse_ref,
    mask_ref,
    spread_ref,
):
    @pl.when(pl.program_id(0) == 0)
    def _():
        attention_tables(fine_ref, coarse_ref, mask_ref, spread_ref, 0)

    lay_out(where_ref[0], kv_ref, near_ref, far_ref, across_ref, ends_ref, kvp_ref)
    mask = mask_ref[...]
    scaled = mask * jnp.asarray(0.125, BF16)

    units = [(tile, quad) for tile in range(COARSE_TILES) for quad in range(2)]
    biases = [
        tile_bias(kid_ref, qidc_ref, tile, 8, coarse_windows(tile), COARSE_LEVELS, coarse_ref[tile])
        for tile in range(COARSE_TILES)
    ]
    scores = []
    for tile, quad in units:
        lanes = pl.ds(QL * quad, QL)
        query = head_stack(q3_ref[0, pl.ds(TILE * tile, TILE), lanes], scaled)
        scores.append(dot_nt(gather_rows(kvp_ref, coarse_windows(tile), lanes), query))
    shares = []
    lines = []
    for index, (tile, quad) in enumerate(units):
        score = level_sums(scores[index], COARSE_LEVELS) + biases[index // 2]
        top = jnp.max(score, axis=0, keepdims=True)
        share = jnp.exp(score - top)
        total = jnp.sum(share, axis=0, keepdims=True)
        lse = top + jnp.log(total)
        lsec_ref[0, pl.ds(index, 1), :] = lse
        lines.append(lse)
        shares.append((share * (1.0 / total)).astype(BF16))
    results = []
    for (tile, quad), share in zip(units, shares):
        values = gather_rows(kvp_ref, coarse_windows(tile), pl.ds(512 + QL * quad, QL))
        results.append(dot_tn(share, values))
    lines = three_terms(jnp.concatenate(lines * 2, axis=0))
    lines = jnp.concatenate([line.astype(F32) for line in lines], axis=0)
    terms = [lane_roll(lines, -8 * part) for part in range(8)]
    terms = dot_nn(jnp.concatenate(terms, axis=0).astype(BF16), spread_ref[...])
    for part in range(8):
        rows = [terms[24 * part + 8 * index : 24 * part + 8 * index + 8] for index in range(3)]
        lsex_ref[0, pl.ds(8 * part, 8), :] = rows[0] + rows[1] + rows[2]
    for index, (tile, quad) in enumerate(units):
        oc_ref[0, pl.ds(TILE * tile, TILE), pl.ds(QL * quad, QL)] = head_pick(
            results[index]
        ).astype(BF16)

    def fine_group(group, carry):
        tiles = [GROUP * group + index for index in range(GROUP)]
        units = [(tile, quad) for tile in tiles for quad in range(2)]
        biases = [
            tile_bias(kid_ref, qidf_ref, tile, FINE_TILES, fine_windows(tile), FINE_LEVELS, fine_ref[...])
            for tile in tiles
        ]
        scores = []
        for tile, quad in units:
            lanes = pl.ds(QL * quad, QL)
            query = head_stack(q_ref[0, at(TILE * tile, TILE), lanes], scaled)
            scores.append(dot_nt(gather_rows(kvp_ref, fine_windows(tile), lanes), query))
        shares = []
        for index, (tile, quad) in enumerate(units):
            score = level_sums(scores[index], FINE_LEVELS) + biases[index // 2]
            far = lsex_ref[0, far_row(tile, quad), :]
            top = jnp.maximum(jnp.max(score, axis=0, keepdims=True), far)
            share = jnp.exp(score - top)
            far_share = jnp.exp(far - top)
            total = jnp.sum(share, axis=0, keepdims=True) + far_share
            lse_ref[0, pl.ds(2 * tile + quad, 1), :] = top + jnp.log(total)
            inverse = 1.0 / total
            shares.append(
                jnp.concatenate(
                    [share * inverse, jnp.where(own_cell(tile), far_share * inverse, 0.0)], axis=0
                ).astype(BF16)
            )
        results = []
        for (tile, quad), share in zip(units, shares):
            values = jnp.concatenate(
                [
                    gather_rows(kvp_ref, fine_windows(tile), pl.ds(512 + QL * quad, QL)),
                    oc_ref[0, at(16 * (tile // 2), 16), pl.ds(QL * quad, QL)],
                ],
                axis=0,
            )
            results.append(dot_tn(share, values))
        for (tile, quad), result in zip(units, results):
            mixed_ref[0, at(TILE * tile, TILE), pl.ds(QL * quad, QL)] = head_pick(result).astype(
                BF16
            )
        return carry

    lax.fori_loop(0, FINE_TILES // GROUP, fine_group, 0)


def stat_shapes(width):
    return [
        ((2 * FINE_TILES, QL), F32),
        ((2 * COARSE_TILES, QL), F32),
        ((64, QL), F32),
        ((ROWS // 8, width), BF16),
    ]


def id_specs(spec):
    return [
        spec((PADDED, 128)),
        spec((FINE * FINE_TILES, QL)),
        spec((8 * (LEVELS - FINE), QL)),
    ]


def attend(where, cells, received, ids):
    micro, _, width = cells[0].shape
    outs = [((ROWS, width), BF16)] + stat_shapes(width)
    ins = list(cells) + list(received)
    return pl.pallas_call(
        attend_kernel,
        grid=(micro,),
        in_specs=[SCALAR]
        + [each_of(value.shape[1:]) for value in ins]
        + id_specs(each_of),
        out_specs=[each_of(dims) for dims, _ in outs],
        out_shape=[jax.ShapeDtypeStruct((micro,) + dims, kind) for dims, kind in outs],
        scratch_shapes=[pltpu.VMEM((PADDED, 2 * width), BF16)] + table_shapes(),
        compiler_params=params(),
        cost_estimate=timing(23),
        name="attend",
    )(where, *ins, *ids)


def add_rows(ref, windows, lanes, value):
    start = 0
    for base, count in windows:
        rows = at(base, count)
        ref[rows, lanes] = ref[rows, lanes] + value[start : start + count]
        start += count


def attend_back_kernel(
    where_ref,
    q_ref,
    q3_ref,
    kv_ref,
    near_in_ref,
    far_in_ref,
    across_in_ref,
    ends_in_ref,
    lse_ref,
    lsec_ref,
    lsex_ref,
    oc_ref,
    dout_ref,
    kid_ref,
    qidf_ref,
    qidc_ref,
    dq_ref,
    dq3_ref,
    dkv_ref,
    near_ref,
    far_ref,
    across_ref,
    ends_ref,
    acc_ref,
    dcell_ref,
    delta_ref,
    kvp_ref,
    fine_ref,
    coarse_ref,
    mask_ref,
    spread_t_ref,
):
    @pl.when(pl.program_id(0) == 0)
    def _():
        attention_tables(fine_ref, coarse_ref, mask_ref, spread_t_ref, 1)

    lay_out(where_ref[0], kv_ref, near_in_ref, far_in_ref, across_in_ref, ends_in_ref, kvp_ref)
    delta_ref[...] = jnp.zeros(delta_ref.shape, F32)
    acc_ref[...] = jnp.zeros(acc_ref.shape, F32)
    dcell_ref[...] = jnp.zeros(dcell_ref.shape, F32)
    mask = mask_ref[...]
    scaled = mask * jnp.asarray(0.125, BF16)

    def fine_group(group, carry):
        tiles = [GROUP_BACK * group + index for index in range(GROUP_BACK)]
        units = [(tile, quad) for tile in tiles for quad in range(2)]
        biases = [
            tile_bias(kid_ref, qidf_ref, tile, FINE_TILES, fine_windows(tile), FINE_LEVELS, fine_ref[...])
            for tile in tiles
        ]
        at_unit = lambda unit: (at(TILE * unit[0], TILE), pl.ds(QL * unit[1], QL))
        queries = [head_stack(q_ref[(0,) + at_unit(unit)], scaled) for unit in units]
        douts = [head_stack(dout_ref[(0,) + at_unit(unit)], mask) for unit in units]
        scores = []
        steers = []
        for index, (tile, quad) in enumerate(units):
            keys = gather_rows(kvp_ref, fine_windows(tile), pl.ds(QL * quad, QL))
            scores.append(dot_nt(keys, queries[index]))
            values = jnp.concatenate(
                [
                    gather_rows(kvp_ref, fine_windows(tile), pl.ds(512 + QL * quad, QL)),
                    oc_ref[0, at(16 * (tile // 2), 16), pl.ds(QL * quad, QL)],
                ],
                axis=0,
            )
            steers.append(dot_nt(values, douts[index]))
        shares = []
        grads = []
        for index, (tile, quad) in enumerate(units):
            lse = lse_ref[0, pl.ds(2 * tile + quad, 1), :]
            far_share = jnp.exp(lsex_ref[0, far_row(tile, quad), :] - lse)
            share = jnp.exp(level_sums(scores[index], FINE_LEVELS) + biases[index // 2] - lse)
            share = jnp.concatenate([share, jnp.where(own_cell(tile), far_share, 0.0)], axis=0)
            weighted = share * steers[index]
            delta = jnp.sum(weighted, axis=0, keepdims=True)
            delta_ref[far_row(tile, quad), :] = far_share * delta
            grad = weighted[0:FINE_KEYS] - share[0:FINE_KEYS] * delta
            grads.append(level_sums(grad, FINE_LEVELS).astype(BF16))
            shares.append(share.astype(BF16))
        dvalues = [dot_nn(share, dout) for share, dout in zip(shares, douts)]
        dkeys = [dot_nn(grad, query) for grad, query in zip(grads, queries)]
        dqueries = []
        for (tile, quad), grad in zip(units, grads):
            keys = gather_rows(kvp_ref, fine_windows(tile), pl.ds(QL * quad, QL))
            dqueries.append(dot_tn(grad, keys))
        for index, (tile, quad) in enumerate(units):
            lanes = pl.ds(QL * quad, QL)
            cells = at(16 * (tile // 2), 16)
            windows = fine_windows(tile)
            add_rows(acc_ref, windows, pl.ds(512 + QL * quad, QL), dvalues[index])
            dcell_ref[cells, lanes] = dcell_ref[cells, lanes] + dvalues[index][FINE_KEYS:]
            add_rows(acc_ref, windows, lanes, dkeys[index])
            dq_ref[(0,) + at_unit((tile, quad))] = (head_pick(dqueries[index]) * 0.125).astype(BF16)
        return carry

    lax.fori_loop(0, FINE_TILES // GROUP_BACK, fine_group, 0)

    units = [(tile, quad) for tile in range(COARSE_TILES) for quad in range(2)]
    biases = [
        tile_bias(kid_ref, qidc_ref, tile, 8, coarse_windows(tile), COARSE_LEVELS, coarse_ref[tile])
        for tile in range(COARSE_TILES)
    ]
    at_unit = lambda unit: (pl.ds(TILE * unit[0], TILE), pl.ds(QL * unit[1], QL))
    queries = [head_stack(q3_ref[(0,) + at_unit(unit)], scaled) for unit in units]
    douts = [head_stack(dcell_ref[at_unit(unit)].astype(BF16), mask) for unit in units]
    terms = dot_nn(jnp.concatenate(three_terms(delta_ref[...]), axis=0), spread_t_ref[...])
    terms = terms[0:64] + terms[64:128] + terms[128:192]
    deltas = lane_roll(terms[0:8], 0)
    for part in range(1, 8):
        deltas = deltas + lane_roll(terms[8 * part : 8 * part + 8], 8 * part)
    steers = []
    scores = []
    for (tile, quad), dout, query in zip(units, douts, queries):
        values = gather_rows(kvp_ref, coarse_windows(tile), pl.ds(512 + QL * quad, QL))
        steers.append(dot_nt(values, dout))
        keys = gather_rows(kvp_ref, coarse_windows(tile), pl.ds(QL * quad, QL))
        scores.append(dot_nt(keys, query))
    shares = []
    grads = []
    for index, (tile, quad) in enumerate(units):
        score = level_sums(scores[index], COARSE_LEVELS) + biases[index // 2]
        share = jnp.exp(score - lsec_ref[0, pl.ds(index, 1), :])
        delta = deltas[index : index + 1]
        grads.append(level_sums(share * (steers[index] - delta), COARSE_LEVELS).astype(BF16))
        shares.append(share.astype(BF16))
    dvalues = [dot_nn(share, dout) for share, dout in zip(shares, douts)]
    dkeys = [dot_nn(grad, query) for grad, query in zip(grads, queries)]
    dqueries = []
    for (tile, quad), grad in zip(units, grads):
        keys = gather_rows(kvp_ref, coarse_windows(tile), pl.ds(QL * quad, QL))
        dqueries.append(dot_tn(grad, keys))
    for index, (tile, quad) in enumerate(units):
        windows = coarse_windows(tile)
        add_rows(acc_ref, windows, pl.ds(512 + QL * quad, QL), dvalues[index])
        add_rows(acc_ref, windows, pl.ds(QL * quad, QL), dkeys[index])
        dq3_ref[(0,) + at_unit((tile, quad))] = (head_pick(dqueries[index]) * 0.125).astype(BF16)

    key_lane = lax.broadcasted_iota(jnp.int32, (1, acc_ref.shape[1]), 1) < 512

    def scale(level):
        return jnp.where(key_lane, 0.5 ** STEP[level], 1.0)

    def low(level, start, count):
        return (acc_ref[pl.ds(start, count), :] * scale(level)).astype(BF16)

    def edges(left_ref, right_ref):
        for level in range(LEVELS - 1):
            base = POFF[level]
            edge = pl.ds(HALO * level, HALO)
            left_ref[0, edge, :] = low(level, base, HALO)
            right_ref[0, edge, :] = low(level, base + HALO + CELLS[level], HALO)

    piece = where_ref[0]
    pl.when(piece % 2 == 0)(lambda: edges(far_ref, near_ref))
    pl.when(piece % 2 == 1)(lambda: edges(near_ref, far_ref))
    for level in range(LEVELS - 1):
        dkv_ref[0, pl.ds(OFF[level], CELLS[level]), :] = low(level, POFF[level] + HALO, CELLS[level])
    dkv_ref[0, pl.ds(OFF[7], 16), :] = jnp.zeros((16, acc_ref.shape[1]), BF16)

    def high(index):
        rows = pl.ds(pl.multiple_of(POFF[7] + PIECE7 * index, PIECE7), PIECE7)
        return (acc_ref[rows, :] * scale(7)).astype(BF16)

    ends_ref[0] = high(3 - piece)
    across_ref[0] = high((piece + 2) % 4)


def attend_back(where, cells, received, stats, dout, ids):
    micro, _, width = dout.shape
    shape = jax.ShapeDtypeStruct
    outs = cell_shapes(width) + edge_shapes(width) + edge_shapes(width)[2:]
    ins = list(cells) + list(received) + list(stats) + [dout]
    return pl.pallas_call(
        attend_back_kernel,
        grid=(micro,),
        in_specs=[SCALAR]
        + [each_of(value.shape[1:]) for value in ins]
        + id_specs(each_of),
        out_specs=[each_of(out) for out in outs],
        out_shape=[shape((micro,) + out, BF16) for out in outs],
        scratch_shapes=[
            pltpu.VMEM((PADDED, 2 * width), F32),
            pltpu.VMEM((ROWS // 8, width), F32),
            pltpu.VMEM((64, QL), F32),
            pltpu.VMEM((PADDED, 2 * width), BF16),
        ]
        + table_shapes(),
        compiler_params=params(),
        cost_estimate=timing(38),
        name="attend_back",
    )(where, *ins, *ids)


MID_ROWS = 512
FF_CHUNK = 512
ROOT = math.sqrt(2.0 / math.pi)


def give(send_ref, start, piece_of):
    for index in range(send_ref.shape[0]):
        piece = piece_of(index)
        send_ref[index, pl.ds(start, piece.shape[0]), :] = piece


def row_piece(ref, shard):
    def piece_of(index):
        return ref[pl.ds(pl.multiple_of(shard * index, shard), shard), :].astype(BF16)

    return piece_of


def middle_kernel(
    where_ref,
    tok_ref,
    cot_ref,
    mixed_ref,
    vec_ref,
    mine_ref,
    other_ref,
    out_ref,
    dmid_ref,
    dmix_ref,
    send_ref,
    wo_ref,
    wi_ref,
    wd_ref,
    acc_o,
    acc_i,
    acc_d,
    acc_b,
    acc_s,
    activ_ref,
    grad_ref,
):
    step = pl.program_id(0)
    core = where_ref[1]
    parts = wi_ref.shape[0]
    shard = wo_ref.shape[2]

    @pl.when(step == 0)
    def _():
        acc_o[...] = jnp.zeros(acc_o.shape, F32)
        acc_i[...] = jnp.zeros(acc_i.shape, F32)
        acc_d[...] = jnp.zeros(acc_d.shape, F32)
        acc_b[...] = jnp.zeros(acc_b.shape, F32)
        acc_s[...] = jnp.zeros(acc_s.shape, F32)
        take_weight(wo_ref, 0, mine_ref, other_ref, core, 0)
        for part in range(parts):
            take_weight(wi_ref, part, mine_ref, other_ref, core, shard * (1 + part))
        take_weight(wd_ref, 0, mine_ref, other_ref, core, shard * (1 + parts))

    wo = weight_of(wo_ref, 0)
    pieces = FF_CHUNK // wd_ref.shape[2]
    wi = [weight_of(wi_ref, part) for part in range(parts)]
    wd = [
        wd_ref[0, pieces * part : pieces * (part + 1)].reshape(FF_CHUNK, wo.shape[1])
        for part in range(parts)
    ]
    cot = cot_ref[...]
    top = cot.astype(BF16)
    mixed = mixed_ref[...]
    middle = tok_ref[...] + dot_nn(mixed, wo)
    unit, rate = normalised(middle)
    second = (unit * vec_ref[1:2] + vec_ref[3:4]).astype(BF16)
    result = middle + vec_ref[4:5]
    back = jnp.zeros(cot.shape, F32)
    pres = {}

    def first(part):
        pres[part] = (dot_nn(second, wi[part]) + vec_ref[5 + part : 6 + part], dot_nt(top, wd[part]))

    first(0)
    for part in range(parts):
        if part + 1 < parts:
            first(part + 1)
        pre, grad = pres.pop(part)
        square = pre * pre
        tanh = jnp.tanh(pre * (ROOT + (ROOT * 0.044715) * square))
        half = 0.5 + 0.5 * tanh
        activ = (pre * half).astype(BF16)
        slope = half + (pre * (0.5 - 0.5 * (tanh * tanh))) * (
            ROOT + (ROOT * 3 * 0.044715) * square
        )
        grad = (grad * slope).astype(BF16)
        cols = pl.ds(FF_CHUNK * part, FF_CHUNK)
        activ_ref[:, cols] = activ
        grad_ref[:, cols] = grad
        acc_b[:, cols] = acc_b[:, cols] + fold_rows(grad.astype(F32))
        result = result + dot_nn(activ, wd[part])
        back = back + dot_nt(grad, wi[part])
    out_ref[...] = result
    acc_d[...] = acc_d[...] + dot_tn(activ_ref[...], top)
    for part in range(parts):
        acc_i[part] = acc_i[part] + dot_tn(second, grad_ref[:, pl.ds(FF_CHUNK * part, FF_CHUNK)])
    dmid = cot + norm_back(back * vec_ref[1:2], unit, rate)
    dmid_ref[...] = dmid
    branch = dmid.astype(BF16)
    dmix_ref[...] = dot_nt(branch, wo).astype(BF16)
    acc_o[...] = acc_o[...] + dot_tn(mixed, branch)
    acc_s[0:8, :] = acc_s[0:8, :] + fold_rows(top.astype(F32))
    acc_s[8:16, :] = acc_s[8:16, :] + fold_rows(back * unit)
    acc_s[16:24, :] = acc_s[16:24, :] + fold_rows(back)

    @pl.when(step == pl.num_programs(0) - 1)
    def _():
        give(send_ref, 0, row_piece(acc_o, shard))
        for part in range(parts):
            give(send_ref, shard * (1 + part), row_piece(acc_i.at[part], shard))
        give(send_ref, shard * (1 + parts), row_piece(acc_d, shard * parts))
        total = lambda value: jnp.sum(value, axis=0, keepdims=True)
        lines = [total(acc_s[8 * index : 8 * index + 8, :]) for index in range(3)]
        for part in range(parts):
            lines.append(total(acc_b[:, pl.ds(FF_CHUNK * part, FF_CHUNK)]))
        lines.append(jnp.zeros((16 - len(lines), lines[0].shape[1]), F32))
        lines = jnp.concatenate(lines, axis=0).astype(BF16)
        give(send_ref, shard * (1 + 2 * parts), lambda index: lines)


def middle_part(where, tokens, cot, mixed, vec, mine, other):
    rows, width = tokens.shape
    chips, lines, _ = mine.shape
    shard = width // (2 * chips)
    parts = (lines // shard - 1) // 2
    hidden = parts * FF_CHUNK
    shape = jax.ShapeDtypeStruct
    tiled = pl.BlockSpec((MID_ROWS, width), lambda r: (r, 0))
    shared = shape((2 * chips, lines + 16, width), BF16)
    single = lambda dims: pl.BlockSpec(
        dims, lambda *_: (0,) * len(dims), pipeline_mode=pl.Buffered(1)
    )
    return pl.pallas_call(
        middle_kernel,
        grid=(rows // MID_ROWS,),
        in_specs=[SCALAR, tiled, tiled, tiled, whole(vec.shape), single(mine.shape), single(mine.shape)],
        out_specs=[tiled, tiled, tiled, single(shared.shape)],
        out_shape=[
            shape((rows, width), F32),
            shape((rows, width), F32),
            shape((rows, width), BF16),
            shared,
        ],
        scratch_shapes=[
            pltpu.VMEM((1, 2 * chips, shard, width), BF16),
            pltpu.VMEM((parts, 2 * chips, shard, FF_CHUNK), BF16),
            pltpu.VMEM((1, 2 * chips, shard * parts, width), BF16),
            pltpu.VMEM((width, width), F32),
            pltpu.VMEM((parts, width, FF_CHUNK), F32),
            pltpu.VMEM((hidden, width), F32),
            pltpu.VMEM((8, hidden), F32),
            pltpu.VMEM((24, width), F32),
            pltpu.VMEM((MID_ROWS, hidden), BF16),
            pltpu.VMEM((MID_ROWS, hidden), BF16),
        ],
        compiler_params=params(),
        cost_estimate=timing(40),
        name="middle",
    )(where, tokens, cot, mixed, vec, mine, other)


def collect_kernel(
    where_ref,
    tok_ref,
    dq_ref,
    dq3_ref,
    dkv_ref,
    near_ref,
    far_ref,
    across_ref,
    ends_ref,
    vec_ref,
    mine_ref,
    other_ref,
    dp_ref,
    send_ref,
    cells_ref,
    norm_ref,
    gw_ref,
    sum_ref,
    w_ref,
    low_ref,
    high_ref,
):
    @pl.when(pl.program_id(0) == 0)
    def _():
        gw_ref[...] = jnp.zeros(gw_ref.shape, F32)
        sum_ref[...] = jnp.zeros(sum_ref.shape, F32)
        low_ref[...] = mean_table((256, 240), 1, range(1, 5), lambda level: 1.0)
        high_ref[...] = mean_table((ROWS, 64), 1, range(5, 8), lambda level: 1.0)

    piece, core = where_ref[0], where_ref[1]
    cells_ref[...] = dkv_ref[0]

    def add(start, value):
        rows = pl.ds(start, HALO)
        cells_ref[rows, :] = (cells_ref[rows, :].astype(F32) + value.astype(F32)).astype(BF16)

    def edges(left_ref, right_ref):
        for level in range(LEVELS - 1):
            edge = pl.ds(HALO * level, HALO)

            @pl.when(piece > 0)
            def _():
                add(OFF[level], left_ref[0, edge, :])

            @pl.when(piece < 3)
            def _():
                add(OFF[level] + CELLS[level] - HALO, right_ref[0, edge, :])

    pl.when(piece % 2 == 0)(lambda: edges(far_ref, near_ref))
    pl.when(piece % 2 == 1)(lambda: edges(near_ref, far_ref))
    high = across_ref[0].astype(F32) + ends_ref[0].astype(F32)
    add(OFF[7], jnp.concatenate([high, jnp.zeros_like(high)], axis=0))

    def expand(chunk, sums):
        rows = at(256 * chunk, 256)
        norm_ref[rows, :] = normalised(tok_ref[0, rows, :])[0].astype(BF16)
        cells = jnp.concatenate(
            [
                cells_ref[at(OFF[level] + (256 >> level) * chunk, 256 >> level), :]
                for level in range(1, 5)
            ],
            axis=0,
        )
        dkv = (
            cells_ref[rows, :].astype(F32)
            + dot_nn(low_ref[...], cells)
            + dot_nn(high_ref[rows, :], cells_ref[pl.ds(OFF[5], 64), :])
        ).astype(BF16)
        dq = (
            dq_ref[0, rows, :].astype(F32)
            + dot_nn(low_ref[:, 192:224], dq3_ref[0, at(32 * chunk, 32), :])
        ).astype(BF16)
        dp_ref[0, rows, pl.ds(0, 512)] = dq
        dp_ref[0, rows, pl.ds(512, 1024)] = dkv
        return [old + fold_rows(new.astype(F32)) for old, new in zip(sums, (dq, dkv))]

    sums = [jnp.zeros((8, 512), F32), jnp.zeros((8, 1024), F32)]
    sums = lax.fori_loop(0, ROWS // 256, expand, sums)
    sum_ref[...] = sum_ref[...] + jnp.concatenate(sums, axis=1)
    for index in range(3):
        grad = dot_tn(norm_ref[...], dp_ref[0, :, pl.ds(512 * index, 512)])
        gw_ref[index] = gw_ref[index] + grad

    @pl.when(pl.program_id(0) == pl.num_programs(0) - 1)
    def _():
        shard = w_ref.shape[2]
        row = lax.broadcasted_iota(jnp.int32, (VEC, 512), 0)
        lines = vec_ref[...].astype(BF16)
        gain = dot_tn(lines, jnp.where(row == 0, 1.0, 0.0).astype(BF16))
        offset = dot_tn(lines, jnp.where(row == 2, 1.0, 0.0).astype(BF16))
        ones = jnp.ones((8, 512), BF16)
        grad_gain = jnp.zeros((8, 512), F32)
        grad_offset = jnp.zeros((8, 512), F32)
        for index in range(3):
            take_weight(w_ref, index, mine_ref, other_ref, core, shard * index)
            grad = gw_ref[index]
            total = jnp.sum(sum_ref[:, pl.ds(512 * index, 512)], axis=0, keepdims=True)
            gw_ref[index] = gain * grad + offset * total
            weight = weight_of(w_ref, index)
            high, middle, _ = three_terms(weight.astype(F32) * grad)
            grad_gain = grad_gain + dot_nt(ones, high) + dot_nt(ones, middle)
            high, middle, low = three_terms(total)
            terms = jnp.concatenate([high, middle, low] + [jnp.zeros_like(low)] * 5, axis=0)
            grad_offset = grad_offset + dot_nt(terms, weight)
            give(send_ref, shard * index, row_piece(gw_ref.at[index], shard))
        grad_offset = jnp.sum(grad_offset, axis=0, keepdims=True)
        blank = jnp.zeros((VEC - 2, 512), F32)
        lines = jnp.concatenate([grad_gain[0:1], grad_offset, blank], axis=0).astype(BF16)
        give(send_ref, 3 * shard, lambda index: lines)


def collect(where, tokens, grads, received, vec, mine, other):
    micro, _, width = tokens.shape
    chips, lines, _ = mine.shape
    shard = width // (2 * chips)
    shape = jax.ShapeDtypeStruct
    moved = [tokens] + list(grads) + list(received)
    ins = [vec, mine, other]
    return pl.pallas_call(
        collect_kernel,
        grid=(micro,),
        in_specs=[SCALAR]
        + [each_of(value.shape[1:]) for value in moved]
        + [whole(value.shape) for value in ins],
        out_specs=[each_of((ROWS, 3 * width)), whole((2 * chips, lines, width))],
        out_shape=[
            shape((micro, ROWS, 3 * width), BF16),
            shape((2 * chips, lines, width), BF16),
        ],
        scratch_shapes=[
            pltpu.VMEM((2 * ROWS, 2 * width), BF16),
            pltpu.VMEM((ROWS, width), BF16),
            pltpu.VMEM((3, width, width), F32),
            pltpu.VMEM((8, 3 * width), F32),
            pltpu.VMEM((3, 2 * chips, shard, width), BF16),
            pltpu.VMEM((256, 240), BF16),
            pltpu.VMEM((ROWS, 64), BF16),
        ],
        compiler_params=params(),
        cost_estimate=timing(17),
        name="collect",
    )(where, *moved, *ins)


FIN_ROWS = 512


def finish_kernel(
    where_ref, tok_ref, dmid_ref, dp_ref, vec_ref, mine_ref, other_ref, grad_ref, w_ref
):
    core = where_ref[1]

    @pl.when(pl.program_id(0) == 0)
    def _():
        for index in range(3):
            take_weight(w_ref, index, mine_ref, other_ref, core, w_ref.shape[2] * index)

    back = dot_nt(dp_ref[:, pl.ds(0, 512)], weight_of(w_ref, 0))
    for index in range(1, 3):
        back = back + dot_nt(dp_ref[:, pl.ds(512 * index, 512)], weight_of(w_ref, index))
    unit, rate = normalised(tok_ref[...])
    grad_ref[...] = dmid_ref[...] + norm_back(back * vec_ref[0:1], unit, rate)


def finish(where, tokens, dmid, dproj, vec, mine, other):
    rows, width = tokens.shape
    dp = 2 * mine.shape[0]
    chunk = lambda lanes: pl.BlockSpec((FIN_ROWS, lanes), lambda r: (r, 0))
    return pl.pallas_call(
        finish_kernel,
        grid=(rows // FIN_ROWS,),
        in_specs=[
            SCALAR,
            chunk(width),
            chunk(width),
            chunk(3 * width),
            whole(vec.shape),
            whole(mine.shape),
            whole(other.shape),
        ],
        out_specs=chunk(width),
        out_shape=jax.ShapeDtypeStruct(tokens.shape, F32),
        scratch_shapes=[pltpu.VMEM((3, dp, width // dp, width), BF16)],
        compiler_params=params(),
        cost_estimate=timing(13),
        name="finish",
    )(where, tokens, dmid, dproj, vec, mine, other)


def twice(chunk):
    lane = lax.broadcasted_iota(jnp.int32, chunk.shape, 1)
    other = pltpu.roll(chunk, 64, 1)
    halves = jnp.where(lane < 64, chunk, other), jnp.where(lane < 64, other, chunk)
    return [jnp.concatenate([half, half], axis=1)[0:1] for half in halves]


def lane_pairs(value, size, merge):
    halves = []
    for half in range(2):
        part = value[:, 128 * half : 128 * (half + 1)]
        lane = lax.broadcasted_iota(jnp.int32, part.shape, 1)
        first = (lane & size) == 0
        pair = jnp.where(first, pltpu.roll(part, 128 - size, 1), pltpu.roll(part, size, 1))
        halves.append(merge(part, pair))
    return jnp.concatenate(halves, axis=1)


def documents_kernel(where_ref, seg_ref, own_ref, kid_ref, qidf_ref, qidc_ref, row_ref):
    piece = where_ref[0]
    length = seg_ref.shape[2]
    margin = (row_ref.shape[0] - length) // 2
    ones = jnp.ones((16, 128), BF16)

    def only_first(row):
        index = lax.broadcasted_iota(jnp.int32, (16, row.shape[1]), 0)
        return jnp.where(index == 0, row.astype(F32), 0.0).astype(BF16)

    outside = jnp.full((margin, 128), -3.0, F32)
    row_ref[pl.ds(0, margin), :] = outside
    row_ref[pl.ds(margin + length, margin), :] = outside

    def spread(part, carry):
        row = seg_ref[0, :, pl.ds(pl.multiple_of(ROWS * part, ROWS), ROWS)]
        row_ref[at(margin + ROWS * part, ROWS), :] = dot_tn(only_first(row), ones)
        return carry

    lax.fori_loop(0, length // ROWS, spread, 0)
    for level in range(LEVELS):
        cell = 1 << level
        if level < LEVELS - 1:
            start = ROWS * piece + margin - HALO * cell
            count = CELLS[level] + 2 * HALO
        else:
            start = margin
            count = 4 * PIECE7
        if level == 0:
            key = row_ref[at(start, count), :]
        else:
            lowest = row_ref[pl.ds(start, count, stride=cell), :]
            highest = row_ref[pl.ds(start + cell - 1, count, stride=cell), :]
            key = jnp.where(lowest == highest, lowest, -2.0)
        if level == LEVELS - 1:
            owner = lax.broadcasted_iota(jnp.int32, key.shape, 0) // PIECE7
            counted = (jnp.abs(owner // 2 - piece // 2) == 1) & (jnp.abs(owner - piece) >= 2)
            key = jnp.where(counted, key, -3.0)
        kid_ref[0, pl.ds(POFF[level], count), :] = key.astype(BF16)

    own = own_ref[0].astype(F32)
    rows = []
    for chunk in range(ROWS // 128):
        rows += twice(jnp.broadcast_to(own[:, 128 * chunk : 128 * (chunk + 1)], (8, 128)))
    low = high = jnp.concatenate(rows, axis=0)
    for level in range(FINE):
        if level > 0:
            low = lane_pairs(low, 1 << (level - 1), jnp.minimum)
            high = lane_pairs(high, 1 << (level - 1), jnp.maximum)
        qidf_ref[0, pl.ds(FINE_TILES * level, FINE_TILES), :] = jnp.where(low == high, low, -1.0)

    token = lax.broadcasted_iota(jnp.int32, (ROWS, ROWS // 8), 0)
    cells = lax.broadcasted_iota(jnp.int32, (ROWS, ROWS // 8), 1)
    ends = []
    for step in (0, 7):
        pick = jnp.where(token == 8 * cells + step, 1.0, 0.0).astype(BF16)
        value = dot_nn(only_first(own), pick)[0:1]
        rows = twice(jnp.broadcast_to(value, (8, 128)))
        ends.append(jnp.concatenate(rows + [rows[1]] * 6, axis=0))
    low, high = ends
    for index in range(LEVELS - FINE):
        if index > 0:
            low = lane_pairs(low, 1 << (index - 1), jnp.minimum)
            high = lane_pairs(high, 1 << (index - 1), jnp.maximum)
        qidc_ref[0, pl.ds(8 * index, 8), :] = jnp.where(low == high, low, -1.0)


def cell_documents(where, segments, piece):
    micro, _, length = segments.shape
    shape = jax.ShapeDtypeStruct
    own = lax.dynamic_slice_in_dim(segments, piece * ROWS, ROWS, axis=2)
    outs = [((PADDED, 128), BF16), ((FINE * FINE_TILES, QL), F32), ((8 * (LEVELS - FINE), QL), F32)]
    key, fine, coarse = pl.pallas_call(
        documents_kernel,
        grid=(micro,),
        in_specs=[SCALAR, each_of((1, length)), each_of((1, ROWS))],
        out_specs=[each_of(dims) for dims, _ in outs],
        out_shape=[shape((micro,) + dims, kind) for dims, kind in outs],
        scratch_shapes=[pltpu.VMEM((length + 2 * ROWS, 128), F32)],
        compiler_params=params(),
        cost_estimate=timing(5),
        name="documents",
    )(where, segments, own)
    return key, fine, coarse


def same_core(chips):
    return [[2 * chip + core for chip in range(chips)] for core in range(2)]


def core_swap(value, chips):
    pairs = [(place, place ^ 1) for place in range(2 * chips)]
    return lax.ppermute(value, "dp", pairs)


def chip_exchange(value, chips):
    return lax.all_to_all(value, "dp", 0, 0, axis_index_groups=same_core(chips), tiled=True)


def after(value, *done):
    return lax.optimization_barrier((value,) + done)[0]


def add(left, right):
    return left.astype(F32) + right.astype(F32)


def body(
    tokens,
    segment_ids,
    norm_gains,
    norm_biases,
    qkv_weight,
    out_weight,
    in_weight,
    in_bias,
    down_weight,
    down_bias,
    cotangent,
):
    micro, _, row_count, width = tokens.shape
    pieces = lax.axis_size("sp")
    piece = lax.axis_index("sp")
    assert row_count == ROWS and pieces == 4 and micro == 2
    tokens = tokens[:, 0]
    cotangent = cotangent[:, 0]
    dp = lax.axis_size("dp")
    place = lax.axis_index("dp")
    chips = dp // 2
    shard = width // dp
    hidden = in_weight.shape[1]
    parts = hidden // FF_CHUNK
    where = jnp.stack([piece, place % 2]).astype(jnp.int32)
    swap = lambda value, bits: lax.ppermute(value, "sp", [(p, p ^ bits) for p in range(pieces)])
    spread = lambda value: chip_exchange(
        jnp.broadcast_to(value[None], (chips,) + value.shape), chips
    )

    def placed(value, start):
        lines = jnp.zeros((value.shape[0], start * value.shape[1]), BF16)
        return lax.dynamic_update_slice(lines, value, (0, place * value.shape[1])).reshape(-1, width)

    small = placed(jnp.concatenate([norm_gains, norm_biases, down_bias[None]]), dp)
    small = jnp.concatenate([small, placed(in_bias[None], dp)])
    small = jnp.pad(small, ((0, VEC - small.shape[0]), (0, 0)))
    mine = spread(jnp.concatenate([qkv_weight.reshape(3 * shard, width), small]))
    ids = cell_documents(where, segment_ids, piece)
    where, mine = lax.optimization_barrier((after(where, ids[2]), mine))
    other = core_swap(mine, chips)
    rest = jnp.concatenate(
        [
            out_weight,
            in_weight.reshape(shard, parts, FF_CHUNK).swapaxes(0, 1).reshape(-1, width),
            down_weight,
        ]
    )
    rest_mine = spread(after(rest, other))

    def halo(near, far, across, ends):
        middle = lax.ppermute(far, "sp", [(1, 2), (2, 1)])
        return swap(near, 1), middle, swap(across, 2), lax.ppermute(ends, "sp", [(0, 3), (3, 0)])

    q, q3, kv, near, far, top, vec = project(where, tokens, mine, other)
    cells = (q, q3, kv)
    received = halo(near, far, top, top)
    rest_mine = after(rest_mine, *received)
    rest_other = core_swap(rest_mine, chips)
    mixed, *stats = attend(after(where, rest_mine), cells, received, ids)
    rest_other = after(rest_other, mixed)

    flat = lambda value: value.reshape(micro * ROWS, width)
    split = lambda value: value.reshape(micro, ROWS, width)
    outputs, dmid, dmix, send = middle_part(
        where, flat(tokens), flat(cotangent), flat(mixed), vec, rest_mine, rest_other
    )
    come = lax.all_to_all(send, "dp", 0, 0, tiled=True)
    dq, dq3, dkv, *edges = attend_back(where, cells, received, stats, split(dmix), ids)
    grads = (dq, dq3, dkv)
    back = halo(*edges)
    odd = piece % 2 == 1
    total = jnp.sum(after(come, *back).astype(F32), axis=0).astype(BF16)
    come = swap(total, 1)
    dproj, send = collect(
        after(where, total), tokens, grads, back, vec, mine, other
    )
    total = add(total, after(come, send)).astype(BF16)
    half = jnp.where(odd, total[:, width // 2 :], total[:, : width // 2])
    come = swap(half, 2)
    qkv_come = lax.all_to_all(after(send, half), "dp", 0, 0, tiled=True)
    input_grad = finish(
        after(where, half), flat(tokens), dmid, dproj.reshape(micro * ROWS, -1), vec, mine, other
    )
    half = add(half, after(come, input_grad)).astype(BF16)
    come = swap(half, 1)
    total = jnp.sum(after(qkv_come, half).astype(F32), axis=0).astype(BF16)
    qkv_come = swap(total, 1)
    come = after(come, total)
    rest = jnp.where(
        odd, jnp.concatenate([come, half], axis=1), jnp.concatenate([half, come], axis=1)
    ).astype(F32)
    total = add(total, qkv_come).astype(BF16)
    total = add(total, swap(total, 2))

    own = lambda value, size: lax.dynamic_slice_in_dim(value, place * size, size, axis=-1)
    small_two = rest[shard * (1 + 2 * parts) :]
    small_one = total[3 * shard :]
    gin = rest[shard : shard * (1 + parts)].reshape(parts, shard, FF_CHUNK).swapaxes(0, 1)
    return (
        outputs.reshape(micro, 1, ROWS, width),
        input_grad.reshape(micro, 1, ROWS, width),
        own(jnp.stack([small_one[0], small_two[1]]), shard),
        own(jnp.stack([small_one[1], small_two[2]]), shard),
        total[: 3 * shard].reshape(3, shard, width),
        rest[:shard],
        gin.reshape(shard, hidden),
        own(small_two[3 : 3 + parts].reshape(hidden), hidden // dp),
        rest[shard * (1 + parts) : shard * (1 + 2 * parts)],
        own(small_two[0], shard),
    )


def solution(mesh):
    in_specs = (
        P(None, "dp", "sp", None),
        P(None, "dp", None),
        P(None, "dp"),
        P(None, "dp"),
        P(None, "dp", None),
        P("dp", None),
        P("dp", None),
        P("dp"),
        P("dp", None),
        P("dp"),
        P(None, "dp", "sp", None),
    )
    out_specs = (
        P(None, "dp", "sp", None),
        P(None, "dp", "sp", None),
        P(None, "dp"),
        P(None, "dp"),
        P(None, "dp", None),
        P("dp", None),
        P("dp", None),
        P("dp"),
        P("dp", None),
        P("dp"),
    )
    return jax.shard_map(body, mesh=mesh, in_specs=in_specs, out_specs=out_specs, check_vma=False)
```

```python
import math

import jax
import jax.numpy as jnp
from jax import lax
from jax.experimental import pallas as pl
from jax.experimental.pallas import tpu as pltpu
from jax.sharding import PartitionSpec as P

HEADS = 8
HEAD_DIM = 64
BLOCK = 16
LEVELS = 8
HALO = 16
TILE = 64
QUAD = 4
QL = QUAD * HEAD_DIM
NEG = -1e30
FINE = 3
ROWS = 1024
EDGE = 112
VEC = 16
GROUP = 4
GROUP_BACK = 4
F32 = jnp.float32
BF16 = jnp.bfloat16

CELLS = [ROWS >> level for level in range(LEVELS)]
OFF = [2 * ROWS - (2 * ROWS >> level) for level in range(LEVELS)]
POFF = []
_at = 0
for _level in range(LEVELS - 1):
    POFF.append(_at)
    _at += CELLS[_level] + 2 * HALO
POFF.append(_at)
PIECE7 = CELLS[LEVELS - 1]
PADDED = _at + 4 * PIECE7
FINE_TILES = ROWS // TILE
COARSE_TILES = ROWS // 8 // TILE
FINE_KEYS = 192
COARSE_KEYS = 256
LN_EPS = 1e-05
VMEM_LIMIT = 62 * 1024 * 1024


STEP = [0, 1, 2, 0, 1, 2, 3, 4]


def places(shape):
    return [lax.broadcasted_iota(jnp.int32, shape, axis) for axis in range(2)]


def counted_pairs(level, query, key):
    near = jnp.abs((query >> 4) - (key >> 4))
    if level == 0:
        return near <= 1
    return (near == 1) & (jnp.abs((query >> 3) - (key >> 3)) >= 2)


def score_offsets(parts):
    out = []
    for level, count, window, query_of in parts:
        key, lane = places((count, 2 * TILE))
        query = query_of(lane & (TILE - 1))
        if window == "all":
            allowed = jnp.full(key.shape, True)
        else:
            split = window == "sides"
            key = jnp.where(key < 16, key - 16, key) if split else key - 16
            allowed = counted_pairs(level, query, key)
        out.append(jnp.where(allowed, level * math.log(2.0), NEG))
    return jnp.concatenate(out, axis=0)


def fine_offsets():
    return score_offsets(
        [
            (0, 96, "span", lambda token: token),
            (1, 64, "span", lambda token: token >> 1),
            (2, 32, "sides", lambda token: token >> 2),
        ]
    )


def coarse_offsets(tile):
    return score_offsets(
        [
            (3, 96, "span", lambda cell: cell),
            (4, 64, "span", lambda cell: cell >> 1),
            (5, 32, "sides", lambda cell: cell >> 2),
            (6, 32, "sides", lambda cell: 8 * tile + (cell >> 3)),
            (7, 4 * PIECE7, "all", lambda cell: cell),
        ]
    )


def mean_table(shape, cell_axis, levels, scale_of):
    index = places(shape)
    cell, token = index[cell_axis], index[1 - cell_axis]
    out = jnp.zeros(shape, F32)
    start = 0
    for level in levels:
        weight = scale_of(level) / (1 << level)
        out = out + jnp.where((token >> level) + start == cell, weight, 0.0)
        start += shape[1 - cell_axis] >> level
    return out.astype(BF16)


def head_table():
    row, col = places((QL, QL))
    return jnp.where((row >> 6) == (col >> 6), 1.0, 0.0).astype(BF16)


def spread_table(cell_axis):
    index = places((QL, QL))
    cell, token = index[cell_axis], index[1 - cell_axis]
    same = ((cell >> 6) == (token >> 6)) & ((cell & 63) == ((token & 63) >> 3))
    return jnp.where(same, 1.0, 0.0).astype(BF16)


def attention_tables(fine_ref, coarse_ref, mask_ref, spread_ref, cell_axis):
    fine_ref[...] = fine_offsets()
    for tile in range(COARSE_TILES):
        coarse_ref[tile] = coarse_offsets(tile)
    mask_ref[...] = head_table()
    spread_ref[...] = spread_table(cell_axis)


def table_shapes():
    return [
        pltpu.VMEM((FINE_KEYS, QL // 2), F32),
        pltpu.VMEM((COARSE_TILES, COARSE_KEYS, QL // 2), F32),
        pltpu.VMEM((QL, QL), BF16),
        pltpu.VMEM((QL, QL), BF16),
    ]


def dot_nn(left, right):
    return jnp.dot(left, right, preferred_element_type=F32)


def dot_nt(left, right):
    return lax.dot_general(left, right, (((1,), (1,)), ((), ())), preferred_element_type=F32)


def dot_tn(left, right):
    return lax.dot_general(left, right, (((0,), (0,)), ((), ())), preferred_element_type=F32)


def at(start, size):
    return pl.ds(pl.multiple_of(start, 16), size)


def whole(shape):
    zeros = (0,) * len(shape)
    return pl.BlockSpec(shape, lambda *_: zeros)


def one_of(shape, micro):
    zeros = (0,) * len(shape)
    return pl.BlockSpec((1,) + shape, lambda *_: (micro,) + zeros)


def each_of(shape):
    zeros = (0,) * len(shape)
    return pl.BlockSpec((1,) + shape, lambda step: (step,) + zeros)


SCALAR = pl.BlockSpec(memory_space=pltpu.SMEM)
KEPT = pl.BlockSpec(memory_space=pl.ANY)


def timing(micros):
    return pl.CostEstimate(
        flops=int(micros * 4e8), bytes_accessed=int(micros * 3e6), transcendentals=0
    )


def params():
    return pltpu.CompilerParams(
        dimension_semantics=("arbitrary",), vmem_limit_bytes=VMEM_LIMIT
    )


def normalised(rows):
    center = rows - jnp.mean(rows, axis=-1, keepdims=True)
    spread = jnp.mean(center * center, axis=-1, keepdims=True)
    rate = lax.rsqrt(spread + LN_EPS)
    return center * rate, rate


def norm_back(grad, unit, rate):
    mean_grad = jnp.mean(grad, axis=-1, keepdims=True)
    mean_dot = jnp.mean(grad * unit, axis=-1, keepdims=True)
    return rate * (grad - mean_grad - unit * mean_dot)


def fold_rows(value):
    return jnp.sum(value.reshape(-1, 8, value.shape[-1]), axis=0)


def take_weight(target, index, mine, other, core, start):
    shard = target.shape[2]

    def take(chip, carry):
        target[index, 2 * chip + core] = mine[chip, pl.ds(start, shard), :]
        target[index, 2 * chip + 1 - core] = other[chip, pl.ds(start, shard), :]
        return carry

    lax.fori_loop(0, mine.shape[0], take, 0)


def weight_of(ref, index):
    return ref[index].reshape(ref.shape[1] * ref.shape[2], ref.shape[3])


def project_kernel(
    where_ref,
    tok_ref,
    mine_ref,
    other_ref,
    q_ref,
    q3_ref,
    kv_ref,
    near_ref,
    far_ref,
    top_ref,
    vec_ref,
    w_ref,
    norm_ref,
    low_ref,
    high_ref,
):
    piece, core = where_ref[0], where_ref[1]
    shard = w_ref.shape[2]

    @pl.when(pl.program_id(0) == 0)
    def _():
        for index in range(3):
            take_weight(w_ref, index, mine_ref, other_ref, core, shard * index)
        vec = jnp.zeros(vec_ref.shape, F32)
        for chip in range(mine_ref.shape[0]):
            for ref in (mine_ref, other_ref):
                vec = vec + ref[chip, pl.ds(3 * shard, VEC), :].astype(F32)
        vec_ref[...] = vec
        for part, scale_of in enumerate((lambda level: 0.5 ** STEP[level], lambda level: 1.0)):
            low_ref[part] = mean_table((240, 256), 0, range(1, 5), scale_of)
            high_ref[part] = mean_table((64, ROWS), 0, range(5, 8), scale_of)

    for chunk in range(ROWS // 256):
        rows = pl.ds(256 * chunk, 256)
        unit, _ = normalised(tok_ref[0, rows, :])
        norm_ref[rows, :] = (unit * vec_ref[0:1] + vec_ref[2:3]).astype(BF16)
    for half in range(2):
        rows = pl.ds(512 * half, 512)
        for index in range(3):
            value = dot_nn(norm_ref[rows, :], weight_of(w_ref, index)).astype(BF16)
            if index == 0:
                q_ref[0, rows, :] = value
            else:
                kv_ref[0, rows, pl.ds(512 * (index - 1), 512)] = value
    for chunk in range(ROWS // 256):
        rows = pl.ds(256 * chunk, 256)
        q3_ref[0, pl.ds(32 * chunk, 32), :] = dot_nn(
            low_ref[1, 192:224, :], q_ref[0, rows, :]
        ).astype(BF16)
        for part in range(2):
            lanes = pl.ds(512 * part, 512)
            cells = dot_nn(low_ref[part], kv_ref[0, rows, lanes]).astype(BF16)
            start = 0
            for level in range(1, 5):
                count = 256 >> level
                kv_ref[0, pl.ds(OFF[level] + count * chunk, count), lanes] = cells[
                    start : start + count
                ]
                start += count
    for part in range(2):
        lanes = pl.ds(512 * part, 512)
        kv_ref[0, pl.ds(OFF[5], 64), lanes] = dot_nn(
            high_ref[part], kv_ref[0, pl.ds(0, ROWS), lanes]
        ).astype(BF16)

    def edges(left_ref, right_ref):
        for level in range(LEVELS - 1):
            edge = pl.ds(HALO * level, HALO)
            left_ref[0, edge, :] = kv_ref[0, pl.ds(OFF[level], HALO), :]
            right_ref[0, edge, :] = kv_ref[0, pl.ds(OFF[level] + CELLS[level] - HALO, HALO), :]

    pl.when(piece % 2 == 0)(lambda: edges(far_ref, near_ref))
    pl.when(piece % 2 == 1)(lambda: edges(near_ref, far_ref))
    top_ref[0] = kv_ref[0, pl.ds(OFF[7], PIECE7), :]


def cell_shapes(width):
    return [(ROWS, width), (ROWS // 8, width), (2 * ROWS, 2 * width)]


def edge_shapes(width):
    return [(EDGE, 2 * width), (EDGE, 2 * width), (PIECE7, 2 * width)]


def project(where, tokens, mine, other):
    micro, _, width = tokens.shape
    shape = jax.ShapeDtypeStruct
    shard = width // (2 * mine.shape[0])
    outs = cell_shapes(width) + edge_shapes(width)
    return pl.pallas_call(
        project_kernel,
        grid=(micro,),
        in_specs=[
            SCALAR,
            each_of((ROWS, width)),
            whole(mine.shape),
            whole(other.shape),
        ],
        out_specs=[each_of(out) for out in outs] + [whole((VEC, width))],
        out_shape=[shape((micro,) + out, BF16) for out in outs] + [shape((VEC, width), F32)],
        scratch_shapes=[
            pltpu.VMEM((3, width // shard, shard, width), BF16),
            pltpu.VMEM((ROWS, width), BF16),
            pltpu.VMEM((2, 240, 256), BF16),
            pltpu.VMEM((2, 64, ROWS), BF16),
        ],
        compiler_params=params(),
        cost_estimate=timing(13),
        name="project",
    )(where, tokens, mine, other)


def fine_windows(tile):
    return [
        (POFF[0] + 64 * tile, 96),
        (POFF[1] + 32 * tile, 64),
        (POFF[2] + 16 * tile, 16),
        (POFF[2] + 16 * tile + 32, 16),
    ]


def coarse_windows(tile):
    return [
        (POFF[3] + 64 * tile, 96),
        (POFF[4] + 32 * tile, 64),
        (POFF[5] + 16 * tile, 16),
        (POFF[5] + 16 * tile + 32, 16),
        (POFF[6], 16),
        (POFF[6] + 32, 16),
        (POFF[7], 32),
    ]


FINE_LEVELS = [96, 64, 32]
COARSE_LEVELS = [96, 64, 32, 32, 32]


def gather_rows(ref, windows, lanes):
    return jnp.concatenate([ref[at(start, size), lanes] for start, size in windows], axis=0)


def tile_bias(kid_ref, qid_ref, tile, tiles, windows, levels, bias):
    keys = jnp.concatenate([kid_ref[0, at(start, size), :] for start, size in windows], axis=0)
    keys = keys.astype(F32)
    keys = jnp.concatenate([keys, keys], axis=1)
    bias = jnp.concatenate([bias, bias], axis=1)
    out = []
    start = 0
    for index, count in enumerate(levels):
        part = slice(start, start + count)
        owner = qid_ref[0, pl.ds(tiles * index + tile, 1), :]
        out.append(jnp.where(keys[part] == owner, bias[part], NEG))
        start += count
    return jnp.concatenate(out, axis=0)


def lane_sums(value, steps):
    halves = []
    for half in range(2):
        part = value[:, 128 * half : 128 * (half + 1)]
        lane = lax.broadcasted_iota(jnp.int32, part.shape, 1)
        for step in range(steps):
            size = 1 << step
            first = (lane & size) == 0
            part = part + jnp.where(
                first, pltpu.roll(part, 128 - size, 1), pltpu.roll(part, size, 1)
            )
        halves.append(part)
    return jnp.concatenate(halves, axis=1)


def lane_roll(value, shift):
    if shift == 0:
        return value
    halves = [value[:, 128 * half : 128 * (half + 1)] for half in range(2)]
    return jnp.concatenate([pltpu.roll(part, shift % 128, 1) for part in halves], axis=1)


def far_row(tile, quad):
    return pl.ds(8 * (tile % 8) + 2 * (tile // 8) + quad, 1)


def level_sums(value, levels):
    out = [value[0 : levels[0]]]
    start = levels[0]
    for index, count in enumerate(levels[1:]):
        out.append(lane_sums(value[start : start + count], index + 1))
        start += count
    return jnp.concatenate(out, axis=0)


def head_stack(value, mask):
    return jnp.concatenate([value] * QUAD, axis=0) * mask


def head_pick(stacked):
    lane = lax.broadcasted_iota(jnp.int32, (TILE, QL), 1) // HEAD_DIM
    out = stacked[0:TILE]
    for head in range(1, QUAD):
        out = jnp.where(lane == head, stacked[TILE * head : TILE * (head + 1)], out)
    return out


def three_terms(row):
    high = row.astype(BF16)
    rest = row - high.astype(F32)
    middle = rest.astype(BF16)
    low = (rest - middle.astype(F32)).astype(BF16)
    return high, middle, low


def own_cell(tile):
    cell = lax.broadcasted_iota(jnp.int32, (16, QL), 0)
    token = lax.broadcasted_iota(jnp.int32, (16, QL), 1) % TILE
    return cell == 8 * (tile % 2) + token // 8


def lay_out(piece, kv_ref, near_ref, far_ref, across_ref, ends_ref, kvp_ref):
    def edges(left_ref, right_ref):
        for level in range(LEVELS - 1):
            base = POFF[level]
            edge = pl.ds(HALO * level, HALO)
            kvp_ref[pl.ds(base, HALO), :] = left_ref[0, edge, :]
            kvp_ref[pl.ds(base + HALO + CELLS[level], HALO), :] = right_ref[0, edge, :]

    pl.when(piece % 2 == 0)(lambda: edges(far_ref, near_ref))
    pl.when(piece % 2 == 1)(lambda: edges(near_ref, far_ref))
    for level in range(LEVELS - 1):
        count = CELLS[level]
        kvp_ref[pl.ds(POFF[level] + HALO, count), :] = kv_ref[0, pl.ds(OFF[level], count), :]
    across = across_ref[0].astype(F32)
    ends = ends_ref[0].astype(F32)
    tops = []
    for owner in range(4):
        top = jnp.where(owner == (piece + 2) % 4, across, jnp.where(owner == 3 - piece, ends, 0.0))
        tops.append(top)
    kvp_ref[pl.ds(POFF[7], 4 * PIECE7), :] = jnp.concatenate(tops, axis=0).astype(BF16)


def attend_kernel(
    where_ref,
    q_ref,
    q3_ref,
    kv_ref,
    near_ref,
    far_ref,
    across_ref,
    ends_ref,
    kid_ref,
    qidf_ref,
    qidc_ref,
    mixed_ref,
    lse_ref,
    lsec_ref,
    lsex_ref,
    oc_ref,
    kvp_ref,
    fine_ref,
    coarse_ref,
    mask_ref,
    spread_ref,
):
    @pl.when(pl.program_id(0) == 0)
    def _():
        attention_tables(fine_ref, coarse_ref, mask_ref, spread_ref, 0)

    lay_out(where_ref[0], kv_ref, near_ref, far_ref, across_ref, ends_ref, kvp_ref)
    mask = mask_ref[...]
    scaled = mask * jnp.asarray(0.125, BF16)

    units = [(tile, quad) for tile in range(COARSE_TILES) for quad in range(2)]
    biases = [
        tile_bias(kid_ref, qidc_ref, tile, 8, coarse_windows(tile), COARSE_LEVELS, coarse_ref[tile])
        for tile in range(COARSE_TILES)
    ]
    scores = []
    for tile, quad in units:
        lanes = pl.ds(QL * quad, QL)
        query = head_stack(q3_ref[0, pl.ds(TILE * tile, TILE), lanes], scaled)
        scores.append(dot_nt(gather_rows(kvp_ref, coarse_windows(tile), lanes), query))
    shares = []
    lines = []
    for index, (tile, quad) in enumerate(units):
        score = level_sums(scores[index], COARSE_LEVELS) + biases[index // 2]
        top = jnp.max(score, axis=0, keepdims=True)
        share = jnp.exp(score - top)
        total = jnp.sum(share, axis=0, keepdims=True)
        lse = top + jnp.log(total)
        lsec_ref[0, pl.ds(index, 1), :] = lse
        lines.append(lse)
        shares.append((share * (1.0 / total)).astype(BF16))
    results = []
    for (tile, quad), share in zip(units, shares):
        values = gather_rows(kvp_ref, coarse_windows(tile), pl.ds(512 + QL * quad, QL))
        results.append(dot_tn(share, values))
    lines = three_terms(jnp.concatenate(lines * 2, axis=0))
    lines = jnp.concatenate([line.astype(F32) for line in lines], axis=0)
    terms = [lane_roll(lines, -8 * part) for part in range(8)]
    terms = dot_nn(jnp.concatenate(terms, axis=0).astype(BF16), spread_ref[...])
    for part in range(8):
        rows = [terms[24 * part + 8 * index : 24 * part + 8 * index + 8] for index in range(3)]
        lsex_ref[0, pl.ds(8 * part, 8), :] = rows[0] + rows[1] + rows[2]
    for index, (tile, quad) in enumerate(units):
        oc_ref[0, pl.ds(TILE * tile, TILE), pl.ds(QL * quad, QL)] = head_pick(
            results[index]
        ).astype(BF16)

    def fine_group(group, carry):
        tiles = [GROUP * group + index for index in range(GROUP)]
        units = [(tile, quad) for tile in tiles for quad in range(2)]
        biases = [
            tile_bias(kid_ref, qidf_ref, tile, FINE_TILES, fine_windows(tile), FINE_LEVELS, fine_ref[...])
            for tile in tiles
        ]
        scores = []
        for tile, quad in units:
            lanes = pl.ds(QL * quad, QL)
            query = head_stack(q_ref[0, at(TILE * tile, TILE), lanes], scaled)
            scores.append(dot_nt(gather_rows(kvp_ref, fine_windows(tile), lanes), query))
        shares = []
        for index, (tile, quad) in enumerate(units):
            score = level_sums(scores[index], FINE_LEVELS) + biases[index // 2]
            far = lsex_ref[0, far_row(tile, quad), :]
            top = jnp.maximum(jnp.max(score, axis=0, keepdims=True), far)
            share = jnp.exp(score - top)
            far_share = jnp.exp(far - top)
            total = jnp.sum(share, axis=0, keepdims=True) + far_share
            lse_ref[0, pl.ds(2 * tile + quad, 1), :] = top + jnp.log(total)
            inverse = 1.0 / total
            shares.append(
                jnp.concatenate(
                    [share * inverse, jnp.where(own_cell(tile), far_share * inverse, 0.0)], axis=0
                ).astype(BF16)
            )
        results = []
        for (tile, quad), share in zip(units, shares):
            values = jnp.concatenate(
                [
                    gather_rows(kvp_ref, fine_windows(tile), pl.ds(512 + QL * quad, QL)),
                    oc_ref[0, at(16 * (tile // 2), 16), pl.ds(QL * quad, QL)],
                ],
                axis=0,
            )
            results.append(dot_tn(share, values))
        for (tile, quad), result in zip(units, results):
            mixed_ref[0, at(TILE * tile, TILE), pl.ds(QL * quad, QL)] = head_pick(result).astype(
                BF16
            )
        return carry

    lax.fori_loop(0, FINE_TILES // GROUP, fine_group, 0)


def stat_shapes(width):
    return [
        ((2 * FINE_TILES, QL), F32),
        ((2 * COARSE_TILES, QL), F32),
        ((64, QL), F32),
        ((ROWS // 8, width), BF16),
    ]


def id_specs(spec):
    return [
        spec((PADDED, 128)),
        spec((FINE * FINE_TILES, QL)),
        spec((8 * (LEVELS - FINE), QL)),
    ]


def attend(where, cells, received, ids):
    micro, _, width = cells[0].shape
    outs = [((ROWS, width), BF16)] + stat_shapes(width)
    ins = list(cells) + list(received)
    return pl.pallas_call(
        attend_kernel,
        grid=(micro,),
        in_specs=[SCALAR]
        + [each_of(value.shape[1:]) for value in ins]
        + id_specs(each_of),
        out_specs=[each_of(dims) for dims, _ in outs],
        out_shape=[jax.ShapeDtypeStruct((micro,) + dims, kind) for dims, kind in outs],
        scratch_shapes=[pltpu.VMEM((PADDED, 2 * width), BF16)] + table_shapes(),
        compiler_params=params(),
        cost_estimate=timing(23),
        name="attend",
    )(where, *ins, *ids)


def add_rows(ref, windows, lanes, value):
    start = 0
    for base, count in windows:
        rows = at(base, count)
        ref[rows, lanes] = ref[rows, lanes] + value[start : start + count]
        start += count


def attend_back_kernel(
    where_ref,
    q_ref,
    q3_ref,
    kv_ref,
    near_in_ref,
    far_in_ref,
    across_in_ref,
    ends_in_ref,
    lse_ref,
    lsec_ref,
    lsex_ref,
    oc_ref,
    dout_ref,
    kid_ref,
    qidf_ref,
    qidc_ref,
    dq_ref,
    dq3_ref,
    dkv_ref,
    near_ref,
    far_ref,
    across_ref,
    ends_ref,
    acc_ref,
    dcell_ref,
    delta_ref,
    kvp_ref,
    fine_ref,
    coarse_ref,
    mask_ref,
    spread_t_ref,
):
    @pl.when(pl.program_id(0) == 0)
    def _():
        attention_tables(fine_ref, coarse_ref, mask_ref, spread_t_ref, 1)

    lay_out(where_ref[0], kv_ref, near_in_ref, far_in_ref, across_in_ref, ends_in_ref, kvp_ref)
    delta_ref[...] = jnp.zeros(delta_ref.shape, F32)
    acc_ref[...] = jnp.zeros(acc_ref.shape, F32)
    dcell_ref[...] = jnp.zeros(dcell_ref.shape, F32)
    mask = mask_ref[...]
    scaled = mask * jnp.asarray(0.125, BF16)

    def fine_group(group, carry):
        tiles = [GROUP_BACK * group + index for index in range(GROUP_BACK)]
        units = [(tile, quad) for tile in tiles for quad in range(2)]
        biases = [
            tile_bias(kid_ref, qidf_ref, tile, FINE_TILES, fine_windows(tile), FINE_LEVELS, fine_ref[...])
            for tile in tiles
        ]
        at_unit = lambda unit: (at(TILE * unit[0], TILE), pl.ds(QL * unit[1], QL))
        queries = [head_stack(q_ref[(0,) + at_unit(unit)], scaled) for unit in units]
        douts = [head_stack(dout_ref[(0,) + at_unit(unit)], mask) for unit in units]
        scores = []
        steers = []
        for index, (tile, quad) in enumerate(units):
            keys = gather_rows(kvp_ref, fine_windows(tile), pl.ds(QL * quad, QL))
            scores.append(dot_nt(keys, queries[index]))
            values = jnp.concatenate(
                [
                    gather_rows(kvp_ref, fine_windows(tile), pl.ds(512 + QL * quad, QL)),
                    oc_ref[0, at(16 * (tile // 2), 16), pl.ds(QL * quad, QL)],
                ],
                axis=0,
            )
            steers.append(dot_nt(values, douts[index]))
        shares = []
        grads = []
        for index, (tile, quad) in enumerate(units):
            lse = lse_ref[0, pl.ds(2 * tile + quad, 1), :]
            far_share = jnp.exp(lsex_ref[0, far_row(tile, quad), :] - lse)
            share = jnp.exp(level_sums(scores[index], FINE_LEVELS) + biases[index // 2] - lse)
            share = jnp.concatenate([share, jnp.where(own_cell(tile), far_share, 0.0)], axis=0)
            weighted = share * steers[index]
            delta = jnp.sum(weighted, axis=0, keepdims=True)
            delta_ref[far_row(tile, quad), :] = far_share * delta
            grad = weighted[0:FINE_KEYS] - share[0:FINE_KEYS] * delta
            grads.append(level_sums(grad, FINE_LEVELS).astype(BF16))
            shares.append(share.astype(BF16))
        dvalues = [dot_nn(share, dout) for share, dout in zip(shares, douts)]
        dkeys = [dot_nn(grad, query) for grad, query in zip(grads, queries)]
        dqueries = []
        for (tile, quad), grad in zip(units, grads):
            keys = gather_rows(kvp_ref, fine_windows(tile), pl.ds(QL * quad, QL))
            dqueries.append(dot_tn(grad, keys))
        for index, (tile, quad) in enumerate(units):
            lanes = pl.ds(QL * quad, QL)
            cells = at(16 * (tile // 2), 16)
            windows = fine_windows(tile)
            add_rows(acc_ref, windows, pl.ds(512 + QL * quad, QL), dvalues[index])
            dcell_ref[cells, lanes] = dcell_ref[cells, lanes] + dvalues[index][FINE_KEYS:]
            add_rows(acc_ref, windows, lanes, dkeys[index])
            dq_ref[(0,) + at_unit((tile, quad))] = (head_pick(dqueries[index]) * 0.125).astype(BF16)
        return carry

    lax.fori_loop(0, FINE_TILES // GROUP_BACK, fine_group, 0)

    units = [(tile, quad) for tile in range(COARSE_TILES) for quad in range(2)]
    biases = [
        tile_bias(kid_ref, qidc_ref, tile, 8, coarse_windows(tile), COARSE_LEVELS, coarse_ref[tile])
        for tile in range(COARSE_TILES)
    ]
    at_unit = lambda unit: (pl.ds(TILE * unit[0], TILE), pl.ds(QL * unit[1], QL))
    queries = [head_stack(q3_ref[(0,) + at_unit(unit)], scaled) for unit in units]
    douts = [head_stack(dcell_ref[at_unit(unit)].astype(BF16), mask) for unit in units]
    terms = dot_nn(jnp.concatenate(three_terms(delta_ref[...]), axis=0), spread_t_ref[...])
    terms = terms[0:64] + terms[64:128] + terms[128:192]
    deltas = lane_roll(terms[0:8], 0)
    for part in range(1, 8):
        deltas = deltas + lane_roll(terms[8 * part : 8 * part + 8], 8 * part)
    steers = []
    scores = []
    for (tile, quad), dout, query in zip(units, douts, queries):
        values = gather_rows(kvp_ref, coarse_windows(tile), pl.ds(512 + QL * quad, QL))
        steers.append(dot_nt(values, dout))
        keys = gather_rows(kvp_ref, coarse_windows(tile), pl.ds(QL * quad, QL))
        scores.append(dot_nt(keys, query))
    shares = []
    grads = []
    for index, (tile, quad) in enumerate(units):
        score = level_sums(scores[index], COARSE_LEVELS) + biases[index // 2]
        share = jnp.exp(score - lsec_ref[0, pl.ds(index, 1), :])
        delta = deltas[index : index + 1]
        grads.append(level_sums(share * (steers[index] - delta), COARSE_LEVELS).astype(BF16))
        shares.append(share.astype(BF16))
    dvalues = [dot_nn(share, dout) for share, dout in zip(shares, douts)]
    dkeys = [dot_nn(grad, query) for grad, query in zip(grads, queries)]
    dqueries = []
    for (tile, quad), grad in zip(units, grads):
        keys = gather_rows(kvp_ref, coarse_windows(tile), pl.ds(QL * quad, QL))
        dqueries.append(dot_tn(grad, keys))
    for index, (tile, quad) in enumerate(units):
        windows = coarse_windows(tile)
        add_rows(acc_ref, windows, pl.ds(512 + QL * quad, QL), dvalues[index])
        add_rows(acc_ref, windows, pl.ds(QL * quad, QL), dkeys[index])
        dq3_ref[(0,) + at_unit((tile, quad))] = (head_pick(dqueries[index]) * 0.125).astype(BF16)

    key_lane = lax.broadcasted_iota(jnp.int32, (1, acc_ref.shape[1]), 1) < 512

    def scale(level):
        return jnp.where(key_lane, 0.5 ** STEP[level], 1.0)

    def low(level, start, count):
        return (acc_ref[pl.ds(start, count), :] * scale(level)).astype(BF16)

    def edges(left_ref, right_ref):
        for level in range(LEVELS - 1):
            base = POFF[level]
            edge = pl.ds(HALO * level, HALO)
            left_ref[0, edge, :] = low(level, base, HALO)
            right_ref[0, edge, :] = low(level, base + HALO + CELLS[level], HALO)

    piece = where_ref[0]
    pl.when(piece % 2 == 0)(lambda: edges(far_ref, near_ref))
    pl.when(piece % 2 == 1)(lambda: edges(near_ref, far_ref))
    for level in range(LEVELS - 1):
        dkv_ref[0, pl.ds(OFF[level], CELLS[level]), :] = low(level, POFF[level] + HALO, CELLS[level])
    dkv_ref[0, pl.ds(OFF[7], 16), :] = jnp.zeros((16, acc_ref.shape[1]), BF16)

    def high(index):
        rows = pl.ds(pl.multiple_of(POFF[7] + PIECE7 * index, PIECE7), PIECE7)
        return (acc_ref[rows, :] * scale(7)).astype(BF16)

    ends_ref[0] = high(3 - piece)
    across_ref[0] = high((piece + 2) % 4)


def attend_back(where, cells, received, stats, dout, ids):
    micro, _, width = dout.shape
    shape = jax.ShapeDtypeStruct
    outs = cell_shapes(width) + edge_shapes(width) + edge_shapes(width)[2:]
    ins = list(cells) + list(received) + list(stats) + [dout]
    return pl.pallas_call(
        attend_back_kernel,
        grid=(micro,),
        in_specs=[SCALAR]
        + [each_of(value.shape[1:]) for value in ins]
        + id_specs(each_of),
        out_specs=[each_of(out) for out in outs],
        out_shape=[shape((micro,) + out, BF16) for out in outs],
        scratch_shapes=[
            pltpu.VMEM((PADDED, 2 * width), F32),
            pltpu.VMEM((ROWS // 8, width), F32),
            pltpu.VMEM((64, QL), F32),
            pltpu.VMEM((PADDED, 2 * width), BF16),
        ]
        + table_shapes(),
        compiler_params=params(),
        cost_estimate=timing(38),
        name="attend_back",
    )(where, *ins, *ids)


MID_ROWS = 512
FF_CHUNK = 512
ROOT = math.sqrt(2.0 / math.pi)


def give(send_ref, start, piece_of):
    def store(index, carry):
        piece = piece_of(index)
        send_ref[index, pl.ds(start, piece.shape[0]), :] = piece
        return carry

    lax.fori_loop(0, send_ref.shape[0], store, 0)


def row_piece(ref, shard):
    def piece_of(index):
        return ref[pl.ds(pl.multiple_of(shard * index, shard), shard), :].astype(BF16)

    return piece_of


def middle_kernel(
    where_ref,
    tok_ref,
    cot_ref,
    mixed_ref,
    vec_ref,
    mine_ref,
    other_ref,
    out_ref,
    dmid_ref,
    dmix_ref,
    send_ref,
    wo_ref,
    wi_ref,
    wd_ref,
    acc_o,
    acc_i,
    acc_d,
    acc_b,
    acc_s,
    activ_ref,
    grad_ref,
):
    step = pl.program_id(0)
    core = where_ref[1]
    parts = wi_ref.shape[0]
    shard = wo_ref.shape[2]

    @pl.when(step == 0)
    def _():
        acc_o[...] = jnp.zeros(acc_o.shape, F32)
        acc_i[...] = jnp.zeros(acc_i.shape, F32)
        acc_d[...] = jnp.zeros(acc_d.shape, F32)
        acc_b[...] = jnp.zeros(acc_b.shape, F32)
        acc_s[...] = jnp.zeros(acc_s.shape, F32)
        take_weight(wo_ref, 0, mine_ref, other_ref, core, 0)
        for part in range(parts):
            take_weight(wi_ref, part, mine_ref, other_ref, core, shard * (1 + part))
        take_weight(wd_ref, 0, mine_ref, other_ref, core, shard * (1 + parts))

    wo = weight_of(wo_ref, 0)
    pieces = FF_CHUNK // wd_ref.shape[2]
    wi = [weight_of(wi_ref, part) for part in range(parts)]
    wd = [
        wd_ref[0, pieces * part : pieces * (part + 1)].reshape(FF_CHUNK, wo.shape[1])
        for part in range(parts)
    ]
    cot = cot_ref[...]
    top = cot.astype(BF16)
    mixed = mixed_ref[...]
    middle = tok_ref[...] + dot_nn(mixed, wo)
    unit, rate = normalised(middle)
    second = (unit * vec_ref[1:2] + vec_ref[3:4]).astype(BF16)
    result = middle + vec_ref[4:5]
    back = jnp.zeros(cot.shape, F32)
    pres = {}

    def first(part):
        pres[part] = (dot_nn(second, wi[part]) + vec_ref[5 + part : 6 + part], dot_nt(top, wd[part]))

    first(0)
    for part in range(parts):
        if part + 1 < parts:
            first(part + 1)
        pre, grad = pres.pop(part)
        square = pre * pre
        tanh = jnp.tanh(pre * (ROOT + (ROOT * 0.044715) * square))
        half = 0.5 + 0.5 * tanh
        activ = (pre * half).astype(BF16)
        slope = half + (pre * (0.5 - 0.5 * (tanh * tanh))) * (
            ROOT + (ROOT * 3 * 0.044715) * square
        )
        grad = (grad * slope).astype(BF16)
        cols = pl.ds(FF_CHUNK * part, FF_CHUNK)
        activ_ref[:, cols] = activ
        grad_ref[:, cols] = grad
        acc_b[:, cols] = acc_b[:, cols] + fold_rows(grad.astype(F32))
        result = result + dot_nn(activ, wd[part])
        back = back + dot_nt(grad, wi[part])
    out_ref[...] = result
    acc_d[...] = acc_d[...] + dot_tn(activ_ref[...], top)
    for part in range(parts):
        acc_i[part] = acc_i[part] + dot_tn(second, grad_ref[:, pl.ds(FF_CHUNK * part, FF_CHUNK)])
    dmid = cot + norm_back(back * vec_ref[1:2], unit, rate)
    dmid_ref[...] = dmid
    branch = dmid.astype(BF16)
    dmix_ref[...] = dot_nt(branch, wo).astype(BF16)
    acc_o[...] = acc_o[...] + dot_tn(mixed, branch)
    acc_s[0:8, :] = acc_s[0:8, :] + fold_rows(top.astype(F32))
    acc_s[8:16, :] = acc_s[8:16, :] + fold_rows(back * unit)
    acc_s[16:24, :] = acc_s[16:24, :] + fold_rows(back)

    @pl.when(step == pl.num_programs(0) - 1)
    def _():
        give(send_ref, 0, row_piece(acc_o, shard))
        for part in range(parts):
            give(send_ref, shard * (1 + part), row_piece(acc_i.at[part], shard))
        give(send_ref, shard * (1 + parts), row_piece(acc_d, shard * parts))
        total = lambda value: jnp.sum(value, axis=0, keepdims=True)
        lines = [total(acc_s[8 * index : 8 * index + 8, :]) for index in range(3)]
        for part in range(parts):
            lines.append(total(acc_b[:, pl.ds(FF_CHUNK * part, FF_CHUNK)]))
        lines.append(jnp.zeros((16 - len(lines), lines[0].shape[1]), F32))
        lines = jnp.concatenate(lines, axis=0).astype(BF16)
        give(send_ref, shard * (1 + 2 * parts), lambda index: lines)


def middle_part(where, tokens, cot, mixed, vec, mine, other):
    rows, width = tokens.shape
    chips, lines, _ = mine.shape
    shard = width // (2 * chips)
    parts = (lines // shard - 1) // 2
    hidden = parts * FF_CHUNK
    shape = jax.ShapeDtypeStruct
    tiled = pl.BlockSpec((MID_ROWS, width), lambda r: (r, 0))
    shared = shape((2 * chips, lines + 16, width), BF16)
    single = lambda dims: pl.BlockSpec(
        dims, lambda *_: (0,) * len(dims), pipeline_mode=pl.Buffered(1)
    )
    return pl.pallas_call(
        middle_kernel,
        grid=(rows // MID_ROWS,),
        in_specs=[SCALAR, tiled, tiled, tiled, whole(vec.shape), single(mine.shape), single(mine.shape)],
        out_specs=[tiled, tiled, tiled, single(shared.shape)],
        out_shape=[
            shape((rows, width), F32),
            shape((rows, width), F32),
            shape((rows, width), BF16),
            shared,
        ],
        scratch_shapes=[
            pltpu.VMEM((1, 2 * chips, shard, width), BF16),
            pltpu.VMEM((parts, 2 * chips, shard, FF_CHUNK), BF16),
            pltpu.VMEM((1, 2 * chips, shard * parts, width), BF16),
            pltpu.VMEM((width, width), F32),
            pltpu.VMEM((parts, width, FF_CHUNK), F32),
            pltpu.VMEM((hidden, width), F32),
            pltpu.VMEM((8, hidden), F32),
            pltpu.VMEM((24, width), F32),
            pltpu.VMEM((MID_ROWS, hidden), BF16),
            pltpu.VMEM((MID_ROWS, hidden), BF16),
        ],
        compiler_params=params(),
        cost_estimate=timing(40),
        name="middle",
    )(where, tokens, cot, mixed, vec, mine, other)


def collect_kernel(
    where_ref,
    tok_ref,
    dq_ref,
    dq3_ref,
    dkv_ref,
    near_ref,
    far_ref,
    across_ref,
    ends_ref,
    vec_ref,
    mine_ref,
    other_ref,
    dp_ref,
    send_ref,
    cells_ref,
    norm_ref,
    gw_ref,
    sum_ref,
    w_ref,
    low_ref,
    high_ref,
):
    @pl.when(pl.program_id(0) == 0)
    def _():
        gw_ref[...] = jnp.zeros(gw_ref.shape, F32)
        sum_ref[...] = jnp.zeros(sum_ref.shape, F32)
        low_ref[...] = mean_table((256, 240), 1, range(1, 5), lambda level: 1.0)
        high_ref[...] = mean_table((ROWS, 64), 1, range(5, 8), lambda level: 1.0)

    piece, core = where_ref[0], where_ref[1]
    cells_ref[...] = dkv_ref[0]

    def add(start, value):
        rows = pl.ds(start, HALO)
        cells_ref[rows, :] = (cells_ref[rows, :].astype(F32) + value.astype(F32)).astype(BF16)

    def edges(left_ref, right_ref):
        for level in range(LEVELS - 1):
            edge = pl.ds(HALO * level, HALO)

            @pl.when(piece > 0)
            def _():
                add(OFF[level], left_ref[0, edge, :])

            @pl.when(piece < 3)
            def _():
                add(OFF[level] + CELLS[level] - HALO, right_ref[0, edge, :])

    pl.when(piece % 2 == 0)(lambda: edges(far_ref, near_ref))
    pl.when(piece % 2 == 1)(lambda: edges(near_ref, far_ref))
    high = across_ref[0].astype(F32) + ends_ref[0].astype(F32)
    add(OFF[7], jnp.concatenate([high, jnp.zeros_like(high)], axis=0))

    def expand(chunk, sums):
        rows = at(256 * chunk, 256)
        norm_ref[rows, :] = normalised(tok_ref[0, rows, :])[0].astype(BF16)
        cells = jnp.concatenate(
            [
                cells_ref[at(OFF[level] + (256 >> level) * chunk, 256 >> level), :]
                for level in range(1, 5)
            ],
            axis=0,
        )
        dkv = (
            cells_ref[rows, :].astype(F32)
            + dot_nn(low_ref[...], cells)
            + dot_nn(high_ref[rows, :], cells_ref[pl.ds(OFF[5], 64), :])
        ).astype(BF16)
        dq = (
            dq_ref[0, rows, :].astype(F32)
            + dot_nn(low_ref[:, 192:224], dq3_ref[0, at(32 * chunk, 32), :])
        ).astype(BF16)
        dp_ref[0, rows, pl.ds(0, 512)] = dq
        dp_ref[0, rows, pl.ds(512, 1024)] = dkv
        return [old + fold_rows(new.astype(F32)) for old, new in zip(sums, (dq, dkv))]

    sums = [jnp.zeros((8, 512), F32), jnp.zeros((8, 1024), F32)]
    sums = lax.fori_loop(0, ROWS // 256, expand, sums)
    sum_ref[...] = sum_ref[...] + jnp.concatenate(sums, axis=1)
    for index in range(3):
        grad = dot_tn(norm_ref[...], dp_ref[0, :, pl.ds(512 * index, 512)])
        gw_ref[index] = gw_ref[index] + grad

    @pl.when(pl.program_id(0) == pl.num_programs(0) - 1)
    def _():
        shard = w_ref.shape[2]
        row = lax.broadcasted_iota(jnp.int32, (VEC, 512), 0)
        lines = vec_ref[...].astype(BF16)
        gain = dot_tn(lines, jnp.where(row == 0, 1.0, 0.0).astype(BF16))
        offset = dot_tn(lines, jnp.where(row == 2, 1.0, 0.0).astype(BF16))
        ones = jnp.ones((8, 512), BF16)
        grad_gain = jnp.zeros((8, 512), F32)
        grad_offset = jnp.zeros((8, 512), F32)
        for index in range(3):
            take_weight(w_ref, index, mine_ref, other_ref, core, shard * index)
            grad = gw_ref[index]
            total = jnp.sum(sum_ref[:, pl.ds(512 * index, 512)], axis=0, keepdims=True)
            gw_ref[index] = gain * grad + offset * total
            weight = weight_of(w_ref, index)
            high, middle, _ = three_terms(weight.astype(F32) * grad)
            grad_gain = grad_gain + dot_nt(ones, high) + dot_nt(ones, middle)
            high, middle, low = three_terms(total)
            terms = jnp.concatenate([high, middle, low] + [jnp.zeros_like(low)] * 5, axis=0)
            grad_offset = grad_offset + dot_nt(terms, weight)
            give(send_ref, shard * index, row_piece(gw_ref.at[index], shard))
        grad_offset = jnp.sum(grad_offset, axis=0, keepdims=True)
        blank = jnp.zeros((VEC - 2, 512), F32)
        lines = jnp.concatenate([grad_gain[0:1], grad_offset, blank], axis=0).astype(BF16)
        give(send_ref, 3 * shard, lambda index: lines)


def collect(where, tokens, grads, received, vec, mine, other):
    micro, _, width = tokens.shape
    chips, lines, _ = mine.shape
    shard = width // (2 * chips)
    shape = jax.ShapeDtypeStruct
    moved = [tokens] + list(grads) + list(received)
    ins = [vec, mine, other]
    return pl.pallas_call(
        collect_kernel,
        grid=(micro,),
        in_specs=[SCALAR]
        + [each_of(value.shape[1:]) for value in moved]
        + [whole(value.shape) for value in ins],
        out_specs=[each_of((ROWS, 3 * width)), whole((2 * chips, lines, width))],
        out_shape=[
            shape((micro, ROWS, 3 * width), BF16),
            shape((2 * chips, lines, width), BF16),
        ],
        scratch_shapes=[
            pltpu.VMEM((2 * ROWS, 2 * width), BF16),
            pltpu.VMEM((ROWS, width), BF16),
            pltpu.VMEM((3, width, width), F32),
            pltpu.VMEM((8, 3 * width), F32),
            pltpu.VMEM((3, 2 * chips, shard, width), BF16),
            pltpu.VMEM((256, 240), BF16),
            pltpu.VMEM((ROWS, 64), BF16),
        ],
        compiler_params=params(),
        cost_estimate=timing(17),
        name="collect",
    )(where, *moved, *ins)


FIN_ROWS = 512


def finish_kernel(
    where_ref, tok_ref, dmid_ref, dp_ref, vec_ref, mine_ref, other_ref, grad_ref, w_ref
):
    core = where_ref[1]

    @pl.when(pl.program_id(0) == 0)
    def _():
        for index in range(3):
            take_weight(w_ref, index, mine_ref, other_ref, core, w_ref.shape[2] * index)

    back = dot_nt(dp_ref[:, pl.ds(0, 512)], weight_of(w_ref, 0))
    for index in range(1, 3):
        back = back + dot_nt(dp_ref[:, pl.ds(512 * index, 512)], weight_of(w_ref, index))
    unit, rate = normalised(tok_ref[...])
    grad_ref[...] = dmid_ref[...] + norm_back(back * vec_ref[0:1], unit, rate)


def finish(where, tokens, dmid, dproj, vec, mine, other):
    rows, width = tokens.shape
    dp = 2 * mine.shape[0]
    chunk = lambda lanes: pl.BlockSpec((FIN_ROWS, lanes), lambda r: (r, 0))
    return pl.pallas_call(
        finish_kernel,
        grid=(rows // FIN_ROWS,),
        in_specs=[
            SCALAR,
            chunk(width),
            chunk(width),
            chunk(3 * width),
            whole(vec.shape),
            whole(mine.shape),
            whole(other.shape),
        ],
        out_specs=chunk(width),
        out_shape=jax.ShapeDtypeStruct(tokens.shape, F32),
        scratch_shapes=[pltpu.VMEM((3, dp, width // dp, width), BF16)],
        compiler_params=params(),
        cost_estimate=timing(13),
        name="finish",
    )(where, tokens, dmid, dproj, vec, mine, other)


def twice(chunk):
    lane = lax.broadcasted_iota(jnp.int32, chunk.shape, 1)
    other = pltpu.roll(chunk, 64, 1)
    halves = jnp.where(lane < 64, chunk, other), jnp.where(lane < 64, other, chunk)
    return [jnp.concatenate([half, half], axis=1)[0:1] for half in halves]


def lane_pairs(value, size, merge):
    halves = []
    for half in range(2):
        part = value[:, 128 * half : 128 * (half + 1)]
        lane = lax.broadcasted_iota(jnp.int32, part.shape, 1)
        first = (lane & size) == 0
        pair = jnp.where(first, pltpu.roll(part, 128 - size, 1), pltpu.roll(part, size, 1))
        halves.append(merge(part, pair))
    return jnp.concatenate(halves, axis=1)


def documents_kernel(where_ref, seg_ref, own_ref, kid_ref, qidf_ref, qidc_ref, row_ref):
    piece = where_ref[0]
    length = seg_ref.shape[2]
    margin = (row_ref.shape[0] - length) // 2
    ones = jnp.ones((16, 128), BF16)

    def only_first(row):
        index = lax.broadcasted_iota(jnp.int32, (16, row.shape[1]), 0)
        return jnp.where(index == 0, row.astype(F32), 0.0).astype(BF16)

    outside = jnp.full((margin, 128), -3.0, F32)
    row_ref[pl.ds(0, margin), :] = outside
    row_ref[pl.ds(margin + length, margin), :] = outside

    def spread(part, carry):
        row = seg_ref[0, :, pl.ds(pl.multiple_of(ROWS * part, ROWS), ROWS)]
        row_ref[at(margin + ROWS * part, ROWS), :] = dot_tn(only_first(row), ones)
        return carry

    lax.fori_loop(0, length // ROWS, spread, 0)
    for level in range(LEVELS):
        cell = 1 << level
        if level < LEVELS - 1:
            start = ROWS * piece + margin - HALO * cell
            count = CELLS[level] + 2 * HALO
        else:
            start = margin
            count = 4 * PIECE7
        if level == 0:
            key = row_ref[at(start, count), :]
        else:
            lowest = row_ref[pl.ds(start, count, stride=cell), :]
            highest = row_ref[pl.ds(start + cell - 1, count, stride=cell), :]
            key = jnp.where(lowest == highest, lowest, -2.0)
        if level == LEVELS - 1:
            owner = lax.broadcasted_iota(jnp.int32, key.shape, 0) // PIECE7
            counted = (jnp.abs(owner // 2 - piece // 2) == 1) & (jnp.abs(owner - piece) >= 2)
            key = jnp.where(counted, key, -3.0)
        kid_ref[0, pl.ds(POFF[level], count), :] = key.astype(BF16)

    own = own_ref[0].astype(F32)
    rows = []
    for chunk in range(ROWS // 128):
        rows += twice(jnp.broadcast_to(own[:, 128 * chunk : 128 * (chunk + 1)], (8, 128)))
    low = high = jnp.concatenate(rows, axis=0)
    for level in range(FINE):
        if level > 0:
            low = lane_pairs(low, 1 << (level - 1), jnp.minimum)
            high = lane_pairs(high, 1 << (level - 1), jnp.maximum)
        qidf_ref[0, pl.ds(FINE_TILES * level, FINE_TILES), :] = jnp.where(low == high, low, -1.0)

    token = lax.broadcasted_iota(jnp.int32, (ROWS, ROWS // 8), 0)
    cells = lax.broadcasted_iota(jnp.int32, (ROWS, ROWS // 8), 1)
    ends = []
    for step in (0, 7):
        pick = jnp.where(token == 8 * cells + step, 1.0, 0.0).astype(BF16)
        value = dot_nn(only_first(own), pick)[0:1]
        rows = twice(jnp.broadcast_to(value, (8, 128)))
        ends.append(jnp.concatenate(rows + [rows[1]] * 6, axis=0))
    low, high = ends
    for index in range(LEVELS - FINE):
        if index > 0:
            low = lane_pairs(low, 1 << (index - 1), jnp.minimum)
            high = lane_pairs(high, 1 << (index - 1), jnp.maximum)
        qidc_ref[0, pl.ds(8 * index, 8), :] = jnp.where(low == high, low, -1.0)


def cell_documents(where, segments, piece):
    micro, _, length = segments.shape
    shape = jax.ShapeDtypeStruct
    own = lax.dynamic_slice_in_dim(segments, piece * ROWS, ROWS, axis=2)
    outs = [((PADDED, 128), BF16), ((FINE * FINE_TILES, QL), F32), ((8 * (LEVELS - FINE), QL), F32)]
    key, fine, coarse = pl.pallas_call(
        documents_kernel,
        grid=(micro,),
        in_specs=[SCALAR, each_of((1, length)), each_of((1, ROWS))],
        out_specs=[each_of(dims) for dims, _ in outs],
        out_shape=[shape((micro,) + dims, kind) for dims, kind in outs],
        scratch_shapes=[pltpu.VMEM((length + 2 * ROWS, 128), F32)],
        compiler_params=params(),
        cost_estimate=timing(5),
        name="documents",
    )(where, segments, own)
    return key, fine, coarse


def same_core(chips):
    return [[2 * chip + core for chip in range(chips)] for core in range(2)]


def core_swap(value, chips):
    pairs = [(place, place ^ 1) for place in range(2 * chips)]
    return lax.ppermute(value, "dp", pairs)


def chip_exchange(value, chips):
    return lax.all_to_all(value, "dp", 0, 0, axis_index_groups=same_core(chips), tiled=True)


def after(value, *done):
    return lax.optimization_barrier((value,) + done)[0]


def add(left, right):
    return left.astype(F32) + right.astype(F32)


def body(
    tokens,
    segment_ids,
    norm_gains,
    norm_biases,
    qkv_weight,
    out_weight,
    in_weight,
    in_bias,
    down_weight,
    down_bias,
    cotangent,
):
    micro, _, row_count, width = tokens.shape
    pieces = lax.axis_size("sp")
    piece = lax.axis_index("sp")
    assert row_count == ROWS and pieces == 4 and micro == 2
    tokens = tokens[:, 0]
    cotangent = cotangent[:, 0]
    dp = lax.axis_size("dp")
    place = lax.axis_index("dp")
    chips = dp // 2
    shard = width // dp
    hidden = in_weight.shape[1]
    parts = hidden // FF_CHUNK
    where = jnp.stack([piece, place % 2]).astype(jnp.int32)
    swap = lambda value, bits: lax.ppermute(value, "sp", [(p, p ^ bits) for p in range(pieces)])
    spread = lambda value: chip_exchange(
        jnp.broadcast_to(value[None], (chips,) + value.shape), chips
    )

    def placed(value, start):
        lines = jnp.zeros((value.shape[0], start * value.shape[1]), BF16)
        return lax.dynamic_update_slice(lines, value, (0, place * value.shape[1])).reshape(-1, width)

    small = placed(jnp.concatenate([norm_gains, norm_biases, down_bias[None]]), dp)
    small = jnp.concatenate([small, placed(in_bias[None], dp)])
    small = jnp.pad(small, ((0, VEC - small.shape[0]), (0, 0)))
    mine = spread(jnp.concatenate([qkv_weight.reshape(3 * shard, width), small]))
    ids = cell_documents(where, segment_ids, piece)
    where, mine = lax.optimization_barrier((after(where, ids[2]), mine))
    other = core_swap(mine, chips)
    rest = jnp.concatenate(
        [
            out_weight,
            in_weight.reshape(shard, parts, FF_CHUNK).swapaxes(0, 1).reshape(-1, width),
            down_weight,
        ]
    )
    rest_mine = spread(after(rest, other))

    def halo(near, far, across, ends):
        middle = lax.ppermute(far, "sp", [(1, 2), (2, 1)])
        return swap(near, 1), middle, swap(across, 2), lax.ppermute(ends, "sp", [(0, 3), (3, 0)])

    q, q3, kv, near, far, top, vec = project(where, tokens, mine, other)
    cells = (q, q3, kv)
    received = halo(near, far, top, top)
    rest_mine = after(rest_mine, *received)
    rest_other = core_swap(rest_mine, chips)
    mixed, *stats = attend(after(where, rest_mine), cells, received, ids)
    rest_other = after(rest_other, mixed)

    flat = lambda value: value.reshape(micro * ROWS, width)
    split = lambda value: value.reshape(micro, ROWS, width)
    outputs, dmid, dmix, send = middle_part(
        where, flat(tokens), flat(cotangent), flat(mixed), vec, rest_mine, rest_other
    )
    come = lax.all_to_all(send, "dp", 0, 0, tiled=True)
    dq, dq3, dkv, *edges = attend_back(where, cells, received, stats, split(dmix), ids)
    grads = (dq, dq3, dkv)
    back = halo(*edges)
    odd = piece % 2 == 1
    total = jnp.sum(after(come, *back).astype(F32), axis=0).astype(BF16)
    come = swap(total, 1)
    dproj, send = collect(
        after(where, total), tokens, grads, back, vec, mine, other
    )
    total = add(total, after(come, send)).astype(BF16)
    half = jnp.where(odd, total[:, width // 2 :], total[:, : width // 2])
    come = swap(half, 2)
    qkv_come = lax.all_to_all(after(send, half), "dp", 0, 0, tiled=True)
    input_grad = finish(
        after(where, half), flat(tokens), dmid, dproj.reshape(micro * ROWS, -1), vec, mine, other
    )
    half = add(half, after(come, input_grad)).astype(BF16)
    come = swap(half, 1)
    total = jnp.sum(after(qkv_come, half).astype(F32), axis=0).astype(BF16)
    qkv_come = swap(total, 1)
    come = after(come, total)
    rest = jnp.where(
        odd, jnp.concatenate([come, half], axis=1), jnp.concatenate([half, come], axis=1)
    ).astype(F32)
    total = add(total, qkv_come).astype(BF16)
    total = add(total, swap(total, 2))

    own = lambda value, size: lax.dynamic_slice_in_dim(value, place * size, size, axis=-1)
    small_two = rest[shard * (1 + 2 * parts) :]
    small_one = total[3 * shard :]
    gin = rest[shard : shard * (1 + parts)].reshape(parts, shard, FF_CHUNK).swapaxes(0, 1)
    return (
        outputs.reshape(micro, 1, ROWS, width),
        input_grad.reshape(micro, 1, ROWS, width),
        own(jnp.stack([small_one[0], small_two[1]]), shard),
        own(jnp.stack([small_one[1], small_two[2]]), shard),
        total[: 3 * shard].reshape(3, shard, width),
        rest[:shard],
        gin.reshape(shard, hidden),
        own(small_two[3 : 3 + parts].reshape(hidden), hidden // dp),
        rest[shard * (1 + parts) : shard * (1 + 2 * parts)],
        own(small_two[0], shard),
    )


def solution(mesh):
    in_specs = (
        P(None, "dp", "sp", None),
        P(None, "dp", None),
        P(None, "dp"),
        P(None, "dp"),
        P(None, "dp", None),
        P("dp", None),
        P("dp", None),
        P("dp"),
        P("dp", None),
        P("dp"),
        P(None, "dp", "sp", None),
    )
    out_specs = (
        P(None, "dp", "sp", None),
        P(None, "dp", "sp", None),
        P(None, "dp"),
        P(None, "dp"),
        P(None, "dp", None),
        P("dp", None),
        P("dp", None),
        P("dp"),
        P("dp", None),
        P("dp"),
    )
    return jax.shard_map(body, mesh=mesh, in_specs=in_specs, out_specs=out_specs, check_vma=False)
```
